32 devices in a mesh: slab: 8 (over z, x), cross: 4 (over y, core).
Axes of the slice: x: 2, y: 2, z: 4, core: 2. Of those that a mesh axis runs over, the one named last changes fastest.
Arguments:
- les_state: float32 [54, 64, 16, 128], P(None, 'slab', 'cross'), may hold values from -6 to 6
- cmc_state: float32 [54, 128, 1024], P(None, 'cross', 'slab'), may hold values from -6 to 6
- cmc_map: int32 [64, 16, 128], P('slab', 'cross'), may hold values from 0 to 1023, as said below
- pdf_index: int32 [64, 16, 128], P('slab', 'cross'), may hold values from 0 to 127
- pdf_table: float32 [128, 128], replicated, may hold values from 0.001 to 0.05
- diffusion: float32 [54], replicated, may hold values from 0.02 to 0.15
- chem_matrix: float32 [54, 54], replicated, may hold values from -0.875 to 0.875
- dissipation: float32 [128, 1024], P('cross', 'slab'), may hold values from 0.05 to 0.2
- reaction_rate: float32 [128, 1024], P('cross', 'slab'), may hold values from 0.05 to 0.5
- substeps: int32 [1024], P('slab'), may hold values from 1 to 4
Outputs:
- les_out: float32 [54, 64, 16, 128], P(None, 'slab', 'cross')
- cmc_out: float32 [54, 128, 1024], P(None, 'cross', 'slab')
The draws below stay inside these ranges and needn't reach their ends.
Inputs may be any that keep to these rules, and one draw needn't show every extreme that they name: `cmc_map`: an LES cell in plane x along the jet axis maps to a CMC cell whose index divided by 128 differs from x divided by 8 (both rounded down) by at most one.
All inputs are finite; a program needn't handle non-finite values.
Results may differ from the reference program's by a relative error of at most 0.0001.
Values sent between devices are 32-bit elements; how exact they have to be, the bound alone decides.
A program may use at most 128 MiB of HBM per device.

```python
import math
import jax
import jax.numpy as jnp
from jax import lax

S = 54
NB = 128
NP = 128
CX = 8
CZ = 128
MC = 128
KMAX = 4
NX = 64
NY = 16
NCMC = 1024


def draw_cmc_map(key, part):
    plane = lax.broadcasted_iota(jnp.int32, (NX, NY, CZ), 0)
    base = plane // CX * MC + plane % CX * MC // CX
    jitter = jax.random.randint(key, (NX, NY, CZ), -MC, MC)
    return jnp.clip(base + jitter, 0, NCMC - 1).astype(jnp.int32)


def set_ends(values, own_key, low, top_value):
    shape = values.shape
    spot = [jax.random.randint(jax.random.fold_in(own_key, axis), (), 0, shape[axis]) for axis in range(len(shape))]
    values = values.at[tuple(spot)].set(low)
    longest = shape.index(max(shape))
    spot[longest] = (spot[longest] + 1) % shape[longest]
    return values.at[tuple(spot)].set(top_value)


def shard_levels(own_key, dims, cuts, least, largest):
    loudness, own = 1.0, jax.random.fold_in(own_key, 6)
    for position, shards_of in cuts:
        steps = jnp.exp(jax.random.uniform(jax.random.fold_in(own, position), (shards_of,), jnp.float32, least / len(cuts), largest / len(cuts)))
        loudness = loudness * jnp.repeat(steps, dims[position] // shards_of).reshape([-1 if axis == position else 1 for axis in range(len(dims))])
    return loudness


def gaussian(key, dims, scale, limit, split=(), held_as=jnp.bfloat16):
    array = jax.random.normal(key, dims, jnp.float32) * scale
    if len(split) > 0:
        array = shard_levels(key, dims, split, -0.22, 0.18) * array
    return jnp.clip(array, min=-limit, max=limit).astype(held_as)


def setup_inputs(seed: int = 0) -> dict:
    splits = jax.random.split(jax.random.key(seed), 11)
    les_state = gaussian(splits[0], (S, NX, NY, CZ), 1.0, 6.0, ((1, 8), (2, 4)), jnp.float32)
    cmc_state = gaussian(splits[1], (S, NB, NCMC), 1.0, 6.0, ((1, 4), (2, 8)), jnp.float32)
    cmc_map = draw_cmc_map(jax.random.fold_in(splits[10], 71), 0)
    pdf_index = set_ends(jax.random.randint(splits[3], (NX, NY, CZ), 0, NP), jax.random.fold_in(splits[3], 1), 0, NP - 1).astype(jnp.int32)
    pdf_table = jnp.clip(jnp.exp(jax.random.uniform(splits[4], (NP, NB), jnp.float32, math.log(0.001), math.log(0.05))), 0.001, 0.05)
    diffusion = jnp.clip(jnp.exp(jax.random.uniform(splits[5], (S,), jnp.float32, math.log(0.02), math.log(0.15))), 0.02, 0.15)
    chem_matrix = gaussian(splits[6], (S, S), S ** -0.5, 0.875, (), jnp.float32)
    dissipation = jnp.clip(0.05 + 0.15 * jax.random.uniform(splits[7], (NB, NCMC), jnp.float32) ** shard_levels(splits[7], (NB, NCMC), ((0, 4), (1, 8)), -0.2, 0.2), 0.05, 0.2)
    reaction_rate = jnp.clip(jnp.exp(math.log(0.5) - 2.3025851 * jax.random.uniform(splits[8], (NB, NCMC), jnp.float32) ** shard_levels(splits[8], (NB, NCMC), ((0, 4), (1, 8)), -0.2, 0.2)), 0.05, 0.5)
    substeps = set_ends(jax.random.randint(splits[9], (NCMC,), 1, KMAX + 1), jax.random.fold_in(splits[9], 1), 1, KMAX).astype(jnp.int32)
    return {"les_state": les_state, "cmc_state": cmc_state, "cmc_map": cmc_map, "pdf_index": pdf_index, "pdf_table": pdf_table, "diffusion": diffusion, "chem_matrix": chem_matrix, "dissipation": dissipation, "reaction_rate": reaction_rate, "substeps": substeps}


def reference(les_state, cmc_state, cmc_map, pdf_index, pdf_table, diffusion, chem_matrix, dissipation, reaction_rate, substeps):
    highest = lax.Precision.HIGHEST
    padded = jnp.pad(les_state, ((0, 0), (1, 1), (1, 1), (1, 1)))
    neighbours = padded[:, 2:, 1:-1, 1:-1] + padded[:, :-2, 1:-1, 1:-1]
    neighbours = neighbours + padded[:, 1:-1, 2:, 1:-1] + padded[:, 1:-1, :-2, 1:-1]
    neighbours = neighbours + padded[:, 1:-1, 1:-1, 2:] + padded[:, 1:-1, 1:-1, :-2]
    transported = les_state + diffusion[:, None, None, None] * (neighbours - 6.0 * les_state)
    species = transported.shape[0]
    flat = transported.reshape(species, -1)
    owner = cmc_map.reshape(-1).astype(jnp.int32)
    shape_id = pdf_index.reshape(-1).astype(jnp.int32)
    ncells = cmc_state.shape[2]
    nshape = pdf_table.shape[0]
    keys = owner * nshape + shape_id
    grouped = jax.ops.segment_sum(flat.T, keys, num_segments=ncells * nshape).reshape(ncells, nshape, species)
    counted = jax.ops.segment_sum(jnp.ones(owner.shape, jnp.float32), keys, num_segments=ncells * nshape).reshape(ncells, nshape)
    numer = jnp.einsum("mps,pb->sbm", grouped, pdf_table, precision=highest)
    denom = jnp.einsum("mp,pb->bm", counted, pdf_table, precision=highest)
    edged = jnp.pad(cmc_state, ((0, 0), (0, 0), (1, 1)))
    left_cells = edged[:, :, :-2]
    right_cells = edged[:, :, 2:]
    moved = cmc_state - 0.4 * (cmc_state - left_cells) + 0.1 * (right_cells - 2.0 * cmc_state + left_cells)
    blended = (numer + moved) / (denom[None] + 1.0)
    banded = jnp.pad(blended, ((0, 0), (1, 1), (0, 0)))
    state = blended + dissipation[None] * (banded[:, 2:] - 2.0 * blended + banded[:, :-2])
    for substep in range(KMAX):
        rate = jnp.dot(chem_matrix, state.reshape(species, -1), precision=highest).reshape(state.shape)
        active = (substep < substeps)[None, None, :]
        state = jnp.where(active, state + 0.5 * reaction_rate[None] * jnp.tanh(rate), state)
    projected = jnp.einsum("pb,sbm->spm", pdf_table, state, precision=highest).reshape(species, -1)
    conditional = jnp.take(projected, shape_id * ncells + owner, axis=1)
    weight_sum = jnp.sum(pdf_table, axis=1)
    conditional = conditional / weight_sum[shape_id][None, :]
    les_out = transported + 0.5 * (conditional.reshape(transported.shape) - transported)
    return les_out, state
```

```python
import functools

import jax
import jax.numpy as jnp
from jax import lax
from jax.experimental import pallas as pl
from jax.experimental.pallas import tpu as pltpu
from jax.sharding import PartitionSpec as P

KMAX = 4
F32 = jnp.float32
BF16 = jnp.bfloat16
NT = (((1,), (1,)), ((), ()))
NN = (((1,), (0,)), ((), ()))
LANES = 128
TILE = 256
HALF = 64
GROUP = 8
LIMIT = 56 << 20


def shift(array, axis, by):
    count = lax.axis_size(axis)
    return lax.ppermute(array, axis, [(i, i + by) for i in range(count) if 0 <= i + by < count])


def swap(array, axis, bit):
    count = lax.axis_size(axis)
    return lax.ppermute(array, axis, [(i, i ^ bit) for i in range(count)])


def hop(array, axis, outward):
    count = lax.axis_size(axis)
    step = lambda i: 2 if (i % 2 == 1) == outward else -2
    return lax.ppermute(array, axis, [(i, i + step(i)) for i in range(count) if 0 <= i + step(i) < count])


def halves(x):
    high = x.astype(BF16)
    return high, (x - high.astype(F32)).astype(BF16)


def padded_halves(x):
    gap = jnp.zeros((HALF - x.shape[0], x.shape[1]), F32)
    high = x.astype(BF16).astype(F32)
    return jnp.concatenate([high, gap, x - high, gap], axis=0).astype(BF16)


def rows_equal(targets, row):
    return jnp.where(targets == row, 1.0, 0.0).astype(BF16)


def whole(shape):
    return pl.BlockSpec(shape, lambda *_: (0,) * len(shape))


VMEM = pl.BlockSpec(memory_space=pltpu.VMEM)
SMEM = pl.BlockSpec(memory_space=pltpu.SMEM)


def params():
    return pltpu.CompilerParams(vmem_limit_bytes=LIMIT)


def rank_kernel(tiles, span, key_ref, rank_ref, table_ref):
    count = key_ref.shape[1]
    ids = lax.broadcasted_iota(jnp.int32, (tiles, TILE), 0).astype(F32)
    tile_of = lambda n: jnp.floor((key_ref[:, n * TILE : (n + 1) * TILE] + 0.5) * (1.0 / span))
    total = jnp.zeros((tiles, TILE), F32)
    for n in range(count // TILE):
        total = total + jnp.where(ids == tile_of(n), 1.0, 0.0)
    total = jnp.sum(total, axis=1, keepdims=True)
    total = jnp.broadcast_to(total, (tiles, LANES))
    big = jnp.floor(total * (1.0 / HALF))
    row = lax.broadcasted_iota(jnp.int32, (tiles, tiles), 0)
    below = rows_equal(jnp.where(lax.broadcasted_iota(jnp.int32, (tiles, tiles), 1) < row, 1, 0), 1)
    add = lambda part: lax.dot_general(below, part.astype(BF16), NN, preferred_element_type=F32)
    base = add(big) * HALF + add(total - big * HALF)
    order = lax.broadcasted_iota(jnp.int32, (tiles, LANES), 0).astype(F32)
    lane = lax.broadcasted_iota(jnp.int32, (tiles, LANES), 1).astype(F32)
    last = jnp.maximum(jnp.ceil((base + total) * (1.0 / LANES)) - 1.0, 0.0) + order
    passed = jnp.where((last < lane) & (order < tiles - 1), 1.0, 0.0)
    table_ref[...] = jnp.sum(passed, axis=0, keepdims=True)
    ahead = jnp.where(
        lax.broadcasted_iota(jnp.int32, (TILE, TILE), 0) < lax.broadcasted_iota(jnp.int32, (TILE, TILE), 1), 1.0, 0.0
    ).astype(BF16)
    carry = base[:, :1]
    for n in range(count // TILE):
        hot = jnp.where(ids == tile_of(n), 1.0, 0.0)
        before = lax.dot_general(hot.astype(BF16), ahead, NN, preferred_element_type=F32) + carry
        rank_ref[:, n * TILE : (n + 1) * TILE] = jnp.sum(hot * before, axis=0, keepdims=True)
        carry = carry + jnp.sum(hot, axis=1, keepdims=True)


def rank_call(key, tiles, span):
    count = key.shape[1]
    return pl.pallas_call(
        functools.partial(rank_kernel, tiles, span),
        out_shape=[jax.ShapeDtypeStruct((1, count), F32), jax.ShapeDtypeStruct((1, LANES), F32)],
        in_specs=[VMEM],
        out_specs=[VMEM] * 2,
        compiler_params=params(),
        cost_estimate=pl.CostEstimate(flops=2 * tiles * TILE * count, bytes_accessed=8 * count, transcendentals=0),
        name="rank",
    )(key)


def permute_kernel(back, x_ref, rank_ref, out_ref, parts):
    rows, count = x_ref.shape
    chunk = 2 * TILE

    @pl.when(pl.program_id(0) == 0)
    def _():
        x = x_ref[...]
        high = x.astype(BF16).astype(F32)
        parts[...] = jnp.concatenate([high, x - high], axis=0).astype(BF16)

    total = jnp.zeros((2 * rows, TILE), F32)
    here = pl.program_id(0) * TILE
    for n in range(count // chunk):
        piece = slice(n * chunk, (n + 1) * chunk)
        if back:
            ids = lax.broadcasted_iota(jnp.int32, (chunk, TILE), 0) + n * chunk
            hot = rows_equal(ids.astype(F32), rank_ref[:, pl.ds(pl.multiple_of(here, TILE), TILE)])
            total = total + lax.dot_general(parts[:, piece], hot, NN, preferred_element_type=F32)
        else:
            ids = lax.broadcasted_iota(jnp.int32, (TILE, chunk), 0) + here
            hot = rows_equal(ids.astype(F32), rank_ref[:, piece])
            total = total + lax.dot_general(parts[:, piece], hot, NT, preferred_element_type=F32)
    out_ref[...] = total[:rows] + total[rows:]


def permute_call(x, rank, back):
    rows, count = x.shape
    return pl.pallas_call(
        functools.partial(permute_kernel, back),
        grid=(count // TILE,),
        out_shape=jax.ShapeDtypeStruct((rows, count), F32),
        in_specs=[whole(x.shape), whole(rank.shape)],
        out_specs=pl.BlockSpec((rows, TILE), lambda i: (0, i)),
        scratch_shapes=[pltpu.VMEM((2 * rows, count), BF16)],
        compiler_params=params(),
        cost_estimate=pl.CostEstimate(flops=4 * rows * count * count, bytes_accessed=8 * rows * count, transcendentals=0),
        name="unsort" if back else "sort",
    )(x, rank)


def weights_of(key, table, bins, per_tile):
    nshape = table.shape[1]
    cell = jnp.floor((key + 0.5) * (1.0 / nshape))
    shape = key - cell * nshape
    tile = jnp.floor((cell + 0.5) * (1.0 / per_tile))
    within = cell - tile * per_tile
    ids = lax.broadcasted_iota(jnp.int32, (nshape, key.shape[1]), 0).astype(F32)
    picked = lax.dot_general(table, rows_equal(ids, shape), NN, preferred_element_type=F32)
    columns = []
    for part in (picked[:bins], picked[bins:]):
        columns.append(jnp.concatenate([jnp.where(within == m, part, 0.0) for m in range(per_tile)], axis=0))
    return jnp.concatenate(columns, axis=1).astype(BF16), tile


def split_table(table):
    high = table.astype(BF16).astype(F32)
    return jnp.concatenate([high, table - high], axis=0).astype(BF16)


def prepare_weights(source, index, key_row, table, bins, per_tile, weights, tiles):
    def step(n, _):
        key = source[key_row : key_row + 1, pl.ds(pl.multiple_of(n * LANES, LANES), LANES)]
        block, tile = weights_of(key, table, bins, per_tile)
        weights[index + n] = block
        tiles[index + n] = jnp.broadcast_to(tile, tiles.shape[1:])
        return 0

    lax.fori_loop(0, source.shape[1] // LANES, step, 0, unroll=2)


def collect_kernel(species, bins, per_tile, pairs, lists, first, *refs):
    sources, refs = refs[:lists], refs[lists:]
    table_ref, steps_ref, *refs = refs
    acc_ref = None if first else refs.pop(0)
    out_ref, weights, tiles, parts = refs
    rows, count = sources[0].shape
    blocks = count // LANES
    out_ref[...] = jnp.zeros_like(out_ref) if first else acc_ref[...]
    table = split_table(table_ref[...])
    line = lax.broadcasted_iota(jnp.int32, (rows, LANES), 0)
    for number, source in enumerate(sources):
        prepare_weights(source, number * blocks, species, table, bins, per_tile, weights, tiles)

        def split(n, _, source=source, number=number):
            x = source[:, pl.ds(pl.multiple_of(n * LANES, LANES), LANES)]
            x = jnp.where(line < species, x, jnp.where(line == species, 1.0, 0.0))
            parts[number * blocks + n] = padded_halves(x)
            return 0

        lax.fori_loop(0, blocks, split, 0, unroll=2)

    def step(n, _):
        for number in range(lists):
            for g in range(GROUP):
                k = n * GROUP + g
                tile = steps_ref[number, k]
                block = jnp.minimum(k - tile, blocks - 1) + number * blocks
                wanted = jnp.where(k < pairs, tile, -1).astype(F32)
                mask = jnp.where(tiles[block] == wanted, 1.0, 0.0).astype(BF16)
                mask = jnp.concatenate([mask] * (2 * HALF // mask.shape[0]), axis=0)
                x = parts[block] * mask
                both = jnp.concatenate([x, x], axis=1)
                got = lax.dot_general(both, weights[block], NT, preferred_element_type=F32)
                place = pl.ds(pl.multiple_of(tile * TILE, TILE), TILE)
                out_ref[:, place] += got[:rows] + got[HALF : HALF + rows]
        return 0

    lax.fori_loop(0, -(-pairs // GROUP), step, 0)


def collect_call(sources, table, steps, acc, species, bins, per_tile, ntiles):
    rows, count = sources[0].shape
    lists, blocks = len(sources), count // LANES
    pairs = blocks + ntiles - 1
    args = list(sources) + [table, steps]
    specs = [VMEM] * (lists + 1) + [SMEM]
    alias = {}
    if acc is not None:
        alias = {len(args): 0}
        args.append(acc)
        specs.append(VMEM)
    return pl.pallas_call(
        functools.partial(collect_kernel, species, bins, per_tile, pairs, lists, acc is None),
        out_shape=jax.ShapeDtypeStruct((rows, ntiles * TILE), F32),
        in_specs=specs,
        out_specs=VMEM,
        scratch_shapes=[
            pltpu.VMEM((lists * blocks, TILE, 2 * LANES), BF16),
            pltpu.VMEM((lists * blocks, 16, LANES), F32),
            pltpu.VMEM((lists * blocks, 2 * HALF, LANES), BF16),
        ],
        input_output_aliases=alias,
        compiler_params=params(),
        cost_estimate=pl.CostEstimate(flops=lists * pairs * 2 * LANES * TILE * TILE, bytes_accessed=0, transcendentals=0),
        name="collect",
    )(*args)


def project_kernel(bins, per_tile, pairs, lists, species, *refs):
    means, refs = refs[:3], refs[3:]
    keys_ref, table_ref, steps_ref, out_ref, weights, tiles, parts = refs
    rows = means[0].shape[0]
    count = keys_ref.shape[1]
    blocks = count // LANES
    per_mean = means[0].shape[1] // TILE
    for number, mean in enumerate(means):

        def split(n, _, number=number, mean=mean):
            parts[number * per_mean + n] = padded_halves(mean[:, pl.ds(pl.multiple_of(n * TILE, TILE), TILE)])
            return 0

        lax.fori_loop(0, per_mean, split, 0, unroll=2)
    table = split_table(table_ref[...])
    out_ref[...] = jnp.zeros_like(out_ref)
    for number in range(lists):
        prepare_weights(keys_ref.at[number : number + 1], number * blocks, 0, table, bins, per_tile, weights, tiles)

    def step(n, _):
        for number in range(lists):
            for g in range(GROUP):
                k = n * GROUP + g
                tile = steps_ref[number, k]
                local = jnp.minimum(k - tile, blocks - 1)
                block = local + number * blocks
                wanted = jnp.where(k < pairs, tile, -1).astype(F32)
                got = lax.dot_general(parts[tile], weights[block], NN, preferred_element_type=F32)
                got = got[:rows] + got[HALF : HALF + rows]
                got = got[:, :LANES] + got[:, LANES:]
                got = jnp.where(tiles[block][:1] == wanted, got, 0.0)
                place = pl.ds(pl.multiple_of(local * LANES, LANES), LANES)
                out_ref[number, :, place] += got
        return 0

    lax.fori_loop(0, -(-pairs // GROUP), step, 0)


def project_call(means, keys, table, steps, species, bins, per_tile, ntiles):
    rows = means[0].shape[0]
    lists, count = keys.shape
    blocks = count // LANES
    pairs = blocks + ntiles - 1
    return pl.pallas_call(
        functools.partial(project_kernel, bins, per_tile, pairs, lists, species),
        out_shape=jax.ShapeDtypeStruct((lists, rows, count), F32),
        in_specs=[VMEM] * 5 + [SMEM],
        out_specs=VMEM,
        scratch_shapes=[
            pltpu.VMEM((lists * blocks, TILE, 2 * LANES), BF16),
            pltpu.VMEM((lists * blocks, 16, LANES), F32),
            pltpu.VMEM((ntiles, 2 * HALF, TILE), BF16),
        ],
        compiler_params=params(),
        cost_estimate=pl.CostEstimate(flops=lists * pairs * 2 * LANES * TILE * TILE, bytes_accessed=0, transcendentals=0),
        name="project",
    )(*means, keys, table, steps)


def edge_rows(bins, chunk, cells, start):
    lane = lax.broadcasted_iota(jnp.int32, (cells, chunk), 1) + start
    cell = lax.broadcasted_iota(jnp.int32, (cells, chunk), 0)
    pick = lambda b: jnp.where(lane == cell * bins + b, 1.0, 0.0)
    return jnp.concatenate([pick(0), pick(bins - 1)], axis=0).astype(BF16)


def blend_kernel(species, bins, own_ref, got_ref, moved_ref, out_ref, edge_ref):
    rows, width = own_ref.shape
    cells = width // bins
    edge = jnp.zeros((2 * rows, 2 * cells), F32)
    for n in range(width // TILE):
        piece = slice(n * TILE, (n + 1) * TILE)
        total = own_ref[:, piece] + got_ref[:, piece]
        blended = (total + moved_ref[:, piece]) / (total[species : species + 1] + 1.0)
        out_ref[:, piece] = blended
        high = blended.astype(BF16).astype(F32)
        parts = jnp.concatenate([high, blended - high], axis=0).astype(BF16)
        edge = edge + lax.dot_general(parts, edge_rows(bins, TILE, cells, n * TILE), NT, preferred_element_type=F32)
    edge_ref[...] = edge[:rows] + edge[rows:]


def chem_kernel(species, bins, state_ref, edge_ref, diss_ref, rate_ref, count_ref, matrix_ref, out_ref):
    rows, width = state_ref.shape
    cells = width // bins
    third = matrix_ref.shape[1] // 3
    high, low = halves(matrix_ref[...])
    column = lax.broadcasted_iota(jnp.int32, matrix_ref.shape, 1)
    matrix = jnp.where(column < 2 * third, high.astype(F32), low.astype(F32)).astype(BF16)
    chunk = 2 * TILE
    line = lax.broadcasted_iota(jnp.int32, (rows, chunk), 0)
    slot = lax.broadcasted_iota(jnp.int32, (rows, chunk), 1) % bins
    gap = [jnp.zeros((third - rows, chunk), F32)] * (third > rows)
    edge = edge_ref[...]
    high = edge.astype(BF16).astype(F32)
    edges = jnp.concatenate([high, edge - high], axis=0).astype(BF16)
    for n in range(width // chunk):
        piece = slice(n * chunk, (n + 1) * chunk)
        here = state_ref[:, piece]
        outer = lax.dot_general(edges, edge_rows(bins, chunk, cells, n * chunk), NN, preferred_element_type=F32)
        outer = outer[:rows] + outer[rows:]
        before = jnp.where(slot == 0, outer, pltpu.roll(here, 1, 1))
        after = jnp.where(slot == bins - 1, outer, pltpu.roll(here, chunk - 1, 1))
        state = here + diss_ref[:, piece] * (after - 2.0 * here + before)
        half = 0.5 * rate_ref[:, piece]
        count = count_ref[:, piece]
        for k in range(KMAX):
            high, low = (part.astype(F32) for part in halves(state))
            stack = jnp.concatenate([high, *gap, low, *gap, high, *gap], axis=0).astype(BF16)
            rate = lax.dot_general(matrix, stack, NN, preferred_element_type=F32)
            state = jnp.where(k < count, state + half * jnp.tanh(rate), state)
        out_ref[:, piece] = jnp.where(line == species, 1.0, state)


def on_device(
    les_state, cmc_state, cmc_map, pdf_index, pdf_table, diffusion, chem_matrix, dissipation, reaction_rate, substeps
):
    species = les_state.shape[0]
    rows = -(-(species + 2) // 8) * 8
    bins, cells = cmc_state.shape[1:]
    nshape = pdf_table.shape[0]
    count = cmc_map.size
    ncross = lax.axis_size("cross")
    per_tile = TILE // bins
    ntiles = 3 * cells // per_tile
    width = cells * bins
    odd = lax.axis_index("slab") % 2 == 1

    below = shift(les_state[:, -1:], "slab", 1)
    above = shift(les_state[:, :1], "slab", -1)
    behind = shift(les_state[:, :, -1:], "cross", 1)
    ahead = shift(les_state[:, :, :1], "cross", -1)

    offset = cmc_map.reshape(1, count) - (lax.axis_index("slab") - 1) * cells
    block = offset // cells
    offset = jnp.where(odd, (2 - block) * cells + offset - block * cells, offset)
    key = (offset * nshape + pdf_index.reshape(1, count)).astype(F32)
    rank, steps = rank_call(key, ntiles, nshape * per_tile)

    xs = jnp.concatenate([below, les_state, above], axis=1)
    ys = jnp.concatenate([behind, les_state, ahead], axis=2)
    zs = jnp.pad(les_state, ((0, 0), (0, 0), (0, 0), (1, 1)))
    around = xs[:, 2:] + xs[:, :-2] + ys[:, :, 2:] + ys[:, :, :-2] + zs[..., 2:] + zs[..., :-2]
    transported = les_state + diffusion[:, None, None, None] * (around - 6.0 * les_state)
    flat = transported.reshape(species, count)
    fill = [jnp.zeros((rows - species - 1, count), F32)]
    mine = permute_call(jnp.concatenate([flat, key] + fill, axis=0), rank, False)
    mine = mine.at[rows - 1, :LANES].set(steps[0])

    table = lax.dynamic_slice_in_dim(pdf_table.T, lax.axis_index("cross") * bins, bins, axis=0)

    bits = [1 << k for k in range(ncross.bit_length() - 1)]
    sources = [mine]
    if bits:
        far_off = swap(mine, "cross", bits[-1])
        sources += [swap(mine, "cross", bit) for bit in bits[:-1]] + [far_off]
        sources += [swap(far_off, "cross", bit) for bit in bits[:-1]]
    steps_of = lambda group: jnp.stack([s[rows - 1, :LANES] for s in group]).astype(jnp.int32)

    spread = lambda a: a.transpose(0, 2, 1).reshape(a.shape[0], width)
    wide = lambda a: a.T.reshape(1, width)
    state = spread(cmc_state)
    left = jnp.concatenate([shift(state[:, -bins:], "slab", 1), state[:, :-bins]], axis=1)
    right = jnp.concatenate([state[:, bins:], shift(state[:, :bins], "slab", -1)], axis=1)
    moved = state - 0.4 * (state - left) + 0.1 * (right - 2.0 * state + left)
    moved = jnp.pad(moved, ((0, rows - species), (0, 0)))

    acc = None
    for source in sources:
        acc = collect_call([source], table, steps_of([source]), acc, species, bins, per_tile, ntiles)
    far, own, near = (acc[:, n * width : (n + 1) * width] for n in range(3))
    near = near + hop(far, "slab", True)
    got = swap(near, "slab", 1)

    blended, edge = pl.pallas_call(
        functools.partial(blend_kernel, species, bins),
        out_shape=[jax.ShapeDtypeStruct((rows, width), F32), jax.ShapeDtypeStruct((rows, 2 * cells), F32)],
        in_specs=[VMEM] * 3,
        out_specs=[VMEM] * 2,
        compiler_params=params(),
        name="blend",
    )(own, got, moved)
    edge = jnp.concatenate(
        [shift(edge[:, cells:], "cross", 1), shift(edge[:, :cells], "cross", -1)], axis=1
    )
    extra = rows - species
    fresh = pl.pallas_call(
        functools.partial(chem_kernel, species, bins),
        out_shape=jax.ShapeDtypeStruct((rows, width), F32),
        in_specs=[VMEM] * 6,
        out_specs=VMEM,
        compiler_params=params(),
        name="chem",
    )(
        blended, edge, wide(dissipation), wide(reaction_rate), jnp.repeat(substeps, bins)[None, :],
        jnp.tile(jnp.pad(chem_matrix, ((0, extra), (0, -(-rows // 16) * 16 - species))), (1, 3)),
    )
    cmc_out = fresh[:species].reshape(species, cells, bins).transpose(0, 2, 1)
    next_mean = swap(fresh, "slab", 1)
    far_mean = hop(next_mean, "slab", False)

    keys = jnp.concatenate([s[species : species + 1] for s in sources], axis=0)
    part = project_call(
        [far_mean, fresh, next_mean], keys, table, steps_of(sources), species, bins, per_tile, ntiles
    )
    part = [part[n] for n in range(len(sources))]
    if bits:
        half = len(part) // 2
        here, there = part[:half], part[half:]

        def gather(group):
            total = group[0]
            for bit, piece in zip(bits[:-1], group[1:]):
                total = total + swap(piece, "cross", bit)
            return total

        there = gather(there)
        part = [gather(here) + swap(there, "cross", bits[-1])]
    total = permute_call(part[0], rank, True)
    conditional = (total[:species] / total[species : species + 1]).reshape(transported.shape)
    les_out = transported + 0.5 * (conditional - transported)
    return (les_out, cmc_out)


def solution(mesh):
    return jax.shard_map(
        on_device,
        mesh=mesh,
        in_specs=(
            P(None, "slab", "cross", None),
            P(None, "cross", "slab"),
            P("slab", "cross", None),
            P("slab", "cross", None),
            P(),
            P(),
            P(),
            P("cross", "slab"),
            P("cross", "slab"),
            P("slab"),
        ),
        out_specs=(P(None, "slab", "cross", None), P(None, "cross", "slab")),
        check_vma=False,
    )
```

```python
import functools

import jax
import jax.numpy as jnp
from jax import lax
from jax.experimental import pallas as pl
from jax.experimental.pallas import tpu as pltpu
from jax.sharding import PartitionSpec as P

KMAX = 4
F32 = jnp.float32
BF16 = jnp.bfloat16
NT = (((1,), (1,)), ((), ()))
NN = (((1,), (0,)), ((), ()))
LANES = 128
TILE = 256
HALF = 64
GROUP = 8
LIMIT = 56 << 20
LAG = (2, 4, 6)


def shift(array, axis, by):
    count = lax.axis_size(axis)
    return lax.ppermute(array, axis, [(i, i + by) for i in range(count) if 0 <= i + by < count])


def swap(array, axis, bit):
    count = lax.axis_size(axis)
    return lax.ppermute(array, axis, [(i, i ^ bit) for i in range(count)])


def halves(x):
    high = x.astype(BF16)
    return high, (x - high.astype(F32)).astype(BF16)


def padded_halves(x):
    gap = jnp.zeros((HALF - x.shape[0], x.shape[1]), F32)
    high = x.astype(BF16).astype(F32)
    return jnp.concatenate([high, gap, x - high, gap], axis=0).astype(BF16)


def rows_equal(targets, row):
    return jnp.where(targets == row, 1.0, 0.0).astype(BF16)


def whole(shape):
    return pl.BlockSpec(shape, lambda *_: (0,) * len(shape))


VMEM = pl.BlockSpec(memory_space=pltpu.VMEM)
SMEM = pl.BlockSpec(memory_space=pltpu.SMEM)


def params():
    return pltpu.CompilerParams(vmem_limit_bytes=LIMIT)


def rank_kernel(tiles, span, key_ref, rank_ref, table_ref):
    count = key_ref.shape[1]
    ids = lax.broadcasted_iota(jnp.int32, (tiles, TILE), 0).astype(F32)
    tile_of = lambda n: jnp.floor((key_ref[:, n * TILE : (n + 1) * TILE] + 0.5) * (1.0 / span))
    total = jnp.zeros((tiles, TILE), F32)
    for n in range(count // TILE):
        total = total + jnp.where(ids == tile_of(n), 1.0, 0.0)
    total = jnp.sum(total, axis=1, keepdims=True)
    total = jnp.broadcast_to(total, (tiles, LANES))
    big = jnp.floor(total * (1.0 / HALF))
    row = lax.broadcasted_iota(jnp.int32, (tiles, tiles), 0)
    below = rows_equal(jnp.where(lax.broadcasted_iota(jnp.int32, (tiles, tiles), 1) < row, 1, 0), 1)
    add = lambda part: lax.dot_general(below, part.astype(BF16), NN, preferred_element_type=F32)
    base = add(big) * HALF + add(total - big * HALF)
    order = lax.broadcasted_iota(jnp.int32, (tiles, LANES), 0).astype(F32)
    lane = lax.broadcasted_iota(jnp.int32, (tiles, LANES), 1).astype(F32)
    last = jnp.maximum(jnp.ceil((base + total) * (1.0 / LANES)) - 1.0, 0.0) + order
    passed = jnp.where((last < lane) & (order < tiles - 1), 1.0, 0.0)
    table_ref[...] = jnp.sum(passed, axis=0, keepdims=True)
    ahead = jnp.where(
        lax.broadcasted_iota(jnp.int32, (TILE, TILE), 0) < lax.broadcasted_iota(jnp.int32, (TILE, TILE), 1), 1.0, 0.0
    ).astype(BF16)
    carry = base[:, :1]
    for n in range(count // TILE):
        hot = jnp.where(ids == tile_of(n), 1.0, 0.0)
        before = lax.dot_general(hot.astype(BF16), ahead, NN, preferred_element_type=F32) + carry
        rank_ref[:, n * TILE : (n + 1) * TILE] = jnp.sum(hot * before, axis=0, keepdims=True)
        carry = carry + jnp.sum(hot, axis=1, keepdims=True)


def rank_call(key, tiles, span):
    count = key.shape[1]
    return pl.pallas_call(
        functools.partial(rank_kernel, tiles, span),
        out_shape=[jax.ShapeDtypeStruct((1, count), F32), jax.ShapeDtypeStruct((1, LANES), F32)],
        in_specs=[VMEM],
        out_specs=[VMEM] * 2,
        compiler_params=params(),
        cost_estimate=pl.CostEstimate(flops=2 * tiles * TILE * count, bytes_accessed=8 * count, transcendentals=0),
        name="rank",
    )(key)


def permute_kernel(back, x_ref, rank_ref, out_ref, parts):
    rows, count = x_ref.shape
    chunk = 2 * TILE

    @pl.when(pl.program_id(0) == 0)
    def _():
        x = x_ref[...]
        high = x.astype(BF16).astype(F32)
        parts[...] = jnp.concatenate([high, x - high], axis=0).astype(BF16)

    total = jnp.zeros((2 * rows, TILE), F32)
    here = pl.program_id(0) * TILE
    for n in range(count // chunk):
        piece = slice(n * chunk, (n + 1) * chunk)
        if back:
            ids = lax.broadcasted_iota(jnp.int32, (chunk, TILE), 0) + n * chunk
            hot = rows_equal(ids.astype(F32), rank_ref[:, pl.ds(pl.multiple_of(here, TILE), TILE)])
            total = total + lax.dot_general(parts[:, piece], hot, NN, preferred_element_type=F32)
        else:
            ids = lax.broadcasted_iota(jnp.int32, (TILE, chunk), 0) + here
            hot = rows_equal(ids.astype(F32), rank_ref[:, piece])
            total = total + lax.dot_general(parts[:, piece], hot, NT, preferred_element_type=F32)
    out_ref[...] = total[:rows] + total[rows:]


def permute_call(x, rank, back):
    rows, count = x.shape
    return pl.pallas_call(
        functools.partial(permute_kernel, back),
        grid=(count // TILE,),
        out_shape=jax.ShapeDtypeStruct((rows, count), F32),
        in_specs=[whole(x.shape), whole(rank.shape)],
        out_specs=pl.BlockSpec((rows, TILE), lambda i: (0, i)),
        scratch_shapes=[pltpu.VMEM((2 * rows, count), BF16)],
        compiler_params=params(),
        cost_estimate=pl.CostEstimate(flops=4 * rows * count * count, bytes_accessed=8 * rows * count, transcendentals=0),
        name="unsort" if back else "sort",
    )(x, rank)


def weights_of(key, table, bins, per_tile):
    nshape = table.shape[1]
    cell = jnp.floor((key + 0.5) * (1.0 / nshape))
    shape = key - cell * nshape
    tile = jnp.floor((cell + 0.5) * (1.0 / per_tile))
    within = cell - tile * per_tile
    ids = lax.broadcasted_iota(jnp.int32, (nshape, key.shape[1]), 0).astype(F32)
    picked = lax.dot_general(table, rows_equal(ids, shape), NN, preferred_element_type=F32)
    columns = []
    for part in (picked[:bins], picked[bins:]):
        columns.append(jnp.concatenate([jnp.where(within == m, part, 0.0) for m in range(per_tile)], axis=0))
    return jnp.concatenate(columns, axis=1).astype(BF16), tile


def split_table(table):
    high = table.astype(BF16).astype(F32)
    return jnp.concatenate([high, table - high], axis=0).astype(BF16)


def prepare_weights(source, index, key_row, table, bins, per_tile, weights, tiles):
    def step(n, _):
        key = source[key_row : key_row + 1, pl.ds(pl.multiple_of(n * LANES, LANES), LANES)]
        block, tile = weights_of(key, table, bins, per_tile)
        weights[index + n] = block
        tiles[index + n] = jnp.broadcast_to(tile, tiles.shape[1:])
        return 0

    lax.fori_loop(0, source.shape[1] // LANES, step, 0, unroll=2)


def collect_kernel(species, bins, per_tile, pairs, lists, first, *refs):
    sources, refs = refs[:lists], refs[lists:]
    table_ref, steps_ref, *refs = refs
    acc_ref = None if first else refs.pop(0)
    out_ref, weights, tiles, parts = refs
    rows, count = sources[0].shape
    blocks = count // LANES
    out_ref[...] = jnp.zeros_like(out_ref) if first else acc_ref[...]
    table = split_table(table_ref[...])
    line = lax.broadcasted_iota(jnp.int32, (rows, LANES), 0)
    for number, source in enumerate(sources):
        prepare_weights(source, number * blocks, species, table, bins, per_tile, weights, tiles)

        def split(n, _, source=source, number=number):
            x = source[:, pl.ds(pl.multiple_of(n * LANES, LANES), LANES)]
            x = jnp.where(line < species, x, jnp.where(line == species, 1.0, 0.0))
            parts[number * blocks + n] = padded_halves(x)
            return 0

        lax.fori_loop(0, blocks, split, 0, unroll=2)

    def step(n, _):
        for number in range(lists):
            for g in range(GROUP):
                k = n * GROUP + g
                tile = steps_ref[number, k]
                block = jnp.minimum(k - tile, blocks - 1) + number * blocks
                wanted = jnp.where(k < pairs, tile, -1).astype(F32)
                mask = jnp.where(tiles[block] == wanted, 1.0, 0.0).astype(BF16)
                mask = jnp.concatenate([mask] * (2 * HALF // mask.shape[0]), axis=0)
                x = parts[block] * mask
                both = jnp.concatenate([x, x], axis=1)
                got = lax.dot_general(both, weights[block], NT, preferred_element_type=F32)
                place = pl.ds(pl.multiple_of(tile * TILE, TILE), TILE)
                out_ref[:, place] += got[:rows] + got[HALF : HALF + rows]
        return 0

    lax.fori_loop(0, -(-pairs // GROUP), step, 0)


def collect_call(sources, table, steps, acc, species, bins, per_tile, ntiles):
    rows, count = sources[0].shape
    lists, blocks = len(sources), count // LANES
    pairs = blocks + ntiles - 1
    args = list(sources) + [table, steps]
    specs = [VMEM] * (lists + 1) + [SMEM]
    alias = {}
    if acc is not None:
        alias = {len(args): 0}
        args.append(acc)
        specs.append(VMEM)
    return pl.pallas_call(
        functools.partial(collect_kernel, species, bins, per_tile, pairs, lists, acc is None),
        out_shape=jax.ShapeDtypeStruct((rows, ntiles * TILE), F32),
        in_specs=specs,
        out_specs=VMEM,
        scratch_shapes=[
            pltpu.VMEM((lists * blocks, TILE, 2 * LANES), BF16),
            pltpu.VMEM((lists * blocks, 16, LANES), F32),
            pltpu.VMEM((lists * blocks, 2 * HALF, LANES), BF16),
        ],
        input_output_aliases=alias,
        compiler_params=params(),
        cost_estimate=pl.CostEstimate(flops=lists * pairs * 2 * LANES * TILE * TILE, bytes_accessed=0, transcendentals=0),
        name="collect",
    )(*args)


def project_kernel(bins, per_tile, pairs, lists, species, *refs):
    means, refs = refs[:3], refs[3:]
    keys_ref, table_ref, steps_ref, out_ref, weights, tiles, parts = refs
    rows = means[0].shape[0]
    count = keys_ref.shape[1]
    blocks = count // LANES
    per_mean = means[0].shape[1] // TILE
    for number, mean in enumerate(means):

        def split(n, _, number=number, mean=mean):
            parts[number * per_mean + n] = padded_halves(mean[:, pl.ds(pl.multiple_of(n * TILE, TILE), TILE)])
            return 0

        lax.fori_loop(0, per_mean, split, 0, unroll=2)
    table = split_table(table_ref[...])
    out_ref[...] = jnp.zeros_like(out_ref)
    for number in range(lists):
        prepare_weights(keys_ref.at[number : number + 1], number * blocks, 0, table, bins, per_tile, weights, tiles)

    def step(n, _):
        for number in range(lists):
            for g in range(GROUP):
                k = n * GROUP + g
                tile = steps_ref[number, k]
                local = jnp.minimum(k - tile, blocks - 1)
                block = local + number * blocks
                wanted = jnp.where(k < pairs, tile, -1).astype(F32)
                got = lax.dot_general(parts[tile], weights[block], NN, preferred_element_type=F32)
                got = got[:rows] + got[HALF : HALF + rows]
                got = got[:, :LANES] + got[:, LANES:]
                got = jnp.where(tiles[block][:1] == wanted, got, 0.0)
                place = pl.ds(pl.multiple_of(local * LANES, LANES), LANES)
                out_ref[number, :, place] += got
        return 0

    lax.fori_loop(0, -(-pairs // GROUP), step, 0)


def project_call(means, keys, table, steps, species, bins, per_tile, ntiles):
    rows = means[0].shape[0]
    lists, count = keys.shape
    blocks = count // LANES
    pairs = blocks + ntiles - 1
    return pl.pallas_call(
        functools.partial(project_kernel, bins, per_tile, pairs, lists, species),
        out_shape=jax.ShapeDtypeStruct((lists, rows, count), F32),
        in_specs=[VMEM] * 5 + [SMEM],
        out_specs=VMEM,
        scratch_shapes=[
            pltpu.VMEM((lists * blocks, TILE, 2 * LANES), BF16),
            pltpu.VMEM((lists * blocks, 16, LANES), F32),
            pltpu.VMEM((ntiles, 2 * HALF, TILE), BF16),
        ],
        compiler_params=params(),
        cost_estimate=pl.CostEstimate(flops=lists * pairs * 2 * LANES * TILE * TILE, bytes_accessed=0, transcendentals=0),
        name="project",
    )(*means, keys, table, steps)


def middle_kernel(species, bins, chunk, refs_in, refs_out, scratch):
    acc_ref, moved_ref, diss_ref, rate_ref, count_ref, matrix_ref = refs_in
    fresh_ref, next_ref, far_ref = refs_out
    hopped, summed, got, state_ref, edge_out, edge_in, pick_ref, third_ref, send, recv = scratch
    rows, width = fresh_ref.shape
    steps = width // chunk
    per_chunk = chunk // bins
    slab, nslab = lax.axis_index("slab"), lax.axis_size("slab")
    cross, ncross = lax.axis_index("cross"), lax.axis_size("cross")
    parity = lax.rem(slab, 2)
    outer = slab + 4 * parity - 2
    inner = slab - 4 * parity + 2
    partner = slab + 1 - 2 * parity
    has_outer = (outer >= 0) & (outer < nslab)
    has_inner = (inner >= 0) & (inner < nslab)
    has_before, has_after = cross > 0, cross < ncross - 1
    mesh = pl.DeviceIdType.MESH

    @pl.when(jnp.logical_not(has_inner))
    def _():
        hopped[...] = jnp.zeros_like(hopped)

    @pl.when(jnp.logical_not(has_outer))
    def _():
        far_ref[...] = jnp.zeros_like(far_ref)

    @pl.when(jnp.logical_not(has_before))
    def _():
        edge_in[:, :, :LANES] = jnp.zeros(edge_in.shape[:2] + (LANES,), F32)

    @pl.when(jnp.logical_not(has_after))
    def _():
        edge_in[:, :, LANES:] = jnp.zeros(edge_in.shape[:2] + (LANES,), F32)

    barrier = pltpu.get_barrier_semaphore()
    greet = lambda where: pl.semaphore_signal(barrier, inc=1, device_id=where, device_id_type=mesh)
    greet({"slab": partner})
    pl.when(has_outer)(lambda: greet({"slab": outer}))
    pl.when(has_inner)(lambda: greet({"slab": inner}))
    pl.when(has_before)(lambda: greet({"cross": cross - 1}))
    pl.when(has_after)(lambda: greet({"cross": cross + 1}))
    number = lambda flag: jnp.where(flag, 1, 0)
    pl.semaphore_wait(barrier, 1 + number(has_outer) + number(has_inner) + number(has_before) + number(has_after))

    def lanes(c, base=0):
        return pl.ds(pl.multiple_of(base + c * chunk, chunk), chunk)

    def remote(kind, c, source, target, where):
        return pltpu.make_async_remote_copy(
            src_ref=source, dst_ref=target, send_sem=send.at[kind, c], recv_sem=recv.at[kind, c],
            device_id=where, device_id_type=mesh,
        )

    to_outer = lambda c: remote(0, c, acc_ref.at[:, lanes(c)], hopped.at[:, lanes(c)], {"slab": outer})
    to_partner = lambda c: remote(1, c, summed.at[:, lanes(c)], got.at[:, lanes(c)], {"slab": partner})
    to_after = lambda c: remote(2, c, edge_out.at[c, :, LANES:], edge_in.at[c, :, :LANES], {"cross": cross + 1})
    to_before = lambda c: remote(3, c, edge_out.at[c, :, :LANES], edge_in.at[c, :, LANES:], {"cross": cross - 1})
    give = lambda c: remote(4, c, fresh_ref.at[:, lanes(c)], next_ref.at[:, lanes(c)], {"slab": partner})
    pass_on = lambda c: remote(5, c, next_ref.at[:, lanes(c)], far_ref.at[:, lanes(c)], {"slab": inner})

    @pl.when(has_outer)
    def _():
        for c in range(steps):
            to_outer(c).start()

    lane = lax.broadcasted_iota(jnp.int32, (2 * LANES, chunk), 1)
    row = lax.broadcasted_iota(jnp.int32, (2 * LANES, chunk), 0)
    target = jnp.where(row < LANES, row * bins, (row - LANES) * bins + bins - 1)
    pick_ref[...] = rows_equal(target, lane)
    third = matrix_ref.shape[1] // 3
    high, low = halves(matrix_ref[...])
    column = lax.broadcasted_iota(jnp.int32, matrix_ref.shape, 1)
    third_ref[...] = jnp.where(column < 2 * third, high.astype(F32), low.astype(F32)).astype(BF16)
    line = lax.broadcasted_iota(jnp.int32, (rows, chunk), 0)
    slot = lax.broadcasted_iota(jnp.int32, (rows, chunk), 1) % bins
    gap = [jnp.zeros((third - rows, chunk), F32)] * (third > rows)

    def stacked(x):
        high = x.astype(BF16).astype(F32)
        return jnp.concatenate([high, x - high], axis=0).astype(BF16)

    def add_hop(c):
        pl.when(has_inner)(lambda: to_outer(c).wait_recv())
        summed[:, lanes(c)] = acc_ref[:, lanes(c, 2 * width)] + hopped[:, lanes(c)]

    def blend(c):
        total = acc_ref[:, lanes(c, width)] + got[:, lanes(c)]
        blended = (total + moved_ref[:, lanes(c)]) / (total[species : species + 1] + 1.0)
        state_ref[:, lanes(c)] = blended
        edge = lax.dot_general(stacked(blended), pick_ref[...], NT, preferred_element_type=F32)
        edge_out[c] = edge[:rows] + edge[rows:]

    def send_edges(c):
        pl.when(has_after)(lambda: to_after(c).start())
        pl.when(has_before)(lambda: to_before(c).start())

    def wait_edges(c):
        pl.when(has_before)(lambda: to_after(c).wait_recv())
        pl.when(has_after)(lambda: to_before(c).wait_recv())

    def react(c):
        here = state_ref[:, lanes(c)]
        around = lax.dot_general(stacked(edge_in[c]), pick_ref[...], NN, preferred_element_type=F32)
        around = around[:rows] + around[rows:]
        before = jnp.where(slot == 0, around, pltpu.roll(here, 1, 1))
        after = jnp.where(slot == bins - 1, around, pltpu.roll(here, chunk - 1, 1))
        state = here + diss_ref[:, lanes(c)] * (after - 2.0 * here + before)
        half = 0.5 * rate_ref[:, lanes(c)]
        count = count_ref[:, lanes(c)]
        for k in range(KMAX):
            high, low = (part.astype(F32) for part in halves(state))
            stack = jnp.concatenate([high, *gap, low, *gap, high, *gap], axis=0).astype(BF16)
            rate = lax.dot_general(third_ref[...], stack, NN, preferred_element_type=F32)
            state = jnp.where(k < count, state + half * jnp.tanh(rate), state)
        fresh_ref[:, lanes(c)] = jnp.where(line == species, 1.0, state)

    def step(t, _):
        def when(lag, body):
            c = t - lag
            pl.when((c >= 0) & (c < steps))(lambda: body(c))

        def second(c):
            to_partner(c).wait_recv()
            blend(c)

        def third_stage(c):
            wait_edges(c)
            react(c)

        def fourth(c):
            give(c).wait_recv()
            pl.when(has_inner)(lambda: pass_on(c).start())

        when(0, add_hop)
        when(LAG[0], second)
        when(0, lambda c: to_partner(c).start())
        when(LAG[1], third_stage)
        when(LAG[0], send_edges)
        when(LAG[2], fourth)
        when(LAG[1], lambda c: give(c).start())
        return 0

    lax.fori_loop(0, steps + LAG[2], step, 0)

    def finish(c, _):
        pl.when(has_outer)(lambda: to_outer(c).wait_send())
        to_partner(c).wait_send()
        pl.when(has_after)(lambda: to_after(c).wait_send())
        pl.when(has_before)(lambda: to_before(c).wait_send())
        give(c).wait_send()
        pl.when(has_inner)(lambda: pass_on(c).wait_send())
        pl.when(has_outer)(lambda: pass_on(c).wait_recv())
        return 0

    lax.fori_loop(0, steps, finish, 0)


def middle_call(acc, moved, diss, rate, count, matrix, species, bins, chunk=512):
    rows, width = moved.shape
    steps = width // chunk

    def kernel(*refs):
        middle_kernel(species, bins, chunk, refs[:6], refs[6:9], refs[9:])

    return pl.pallas_call(
        kernel,
        out_shape=[jax.ShapeDtypeStruct((rows, width), F32)] * 3,
        in_specs=[VMEM] * 6,
        out_specs=[VMEM] * 3,
        scratch_shapes=[pltpu.VMEM((rows, width), F32)] * 4
        + [pltpu.VMEM((steps, rows, 2 * LANES), F32)] * 2
        + [pltpu.VMEM((2 * LANES, chunk), BF16), pltpu.VMEM(matrix.shape, BF16)]
        + [pltpu.SemaphoreType.DMA((6, steps))] * 2,
        compiler_params=pltpu.CompilerParams(vmem_limit_bytes=LIMIT, collective_id=1, has_side_effects=True),
        name="middle",
    )(acc, moved, diss, rate, count, matrix)


def on_device(
    les_state, cmc_state, cmc_map, pdf_index, pdf_table, diffusion, chem_matrix, dissipation, reaction_rate, substeps
):
    species = les_state.shape[0]
    rows = -(-(species + 2) // 8) * 8
    bins, cells = cmc_state.shape[1:]
    nshape = pdf_table.shape[0]
    count = cmc_map.size
    ncross = lax.axis_size("cross")
    per_tile = TILE // bins
    ntiles = 3 * cells // per_tile
    width = cells * bins
    odd = lax.axis_index("slab") % 2 == 1

    below = shift(les_state[:, -1:], "slab", 1)
    above = shift(les_state[:, :1], "slab", -1)
    behind = shift(les_state[:, :, -1:], "cross", 1)
    ahead = shift(les_state[:, :, :1], "cross", -1)

    offset = cmc_map.reshape(1, count) - (lax.axis_index("slab") - 1) * cells
    block = offset // cells
    offset = jnp.where(odd, (2 - block) * cells + offset - block * cells, offset)
    key = (offset * nshape + pdf_index.reshape(1, count)).astype(F32)
    rank, steps = rank_call(key, ntiles, nshape * per_tile)

    xs = jnp.concatenate([below, les_state, above], axis=1)
    ys = jnp.concatenate([behind, les_state, ahead], axis=2)
    zs = jnp.pad(les_state, ((0, 0), (0, 0), (0, 0), (1, 1)))
    around = xs[:, 2:] + xs[:, :-2] + ys[:, :, 2:] + ys[:, :, :-2] + zs[..., 2:] + zs[..., :-2]
    transported = les_state + diffusion[:, None, None, None] * (around - 6.0 * les_state)
    flat = transported.reshape(species, count)
    fill = [jnp.zeros((rows - species - 1, count), F32)]
    mine = permute_call(jnp.concatenate([flat, key] + fill, axis=0), rank, False)
    mine = mine.at[rows - 1, :LANES].set(steps[0])

    table = lax.dynamic_slice_in_dim(pdf_table.T, lax.axis_index("cross") * bins, bins, axis=0)

    bits = [1 << k for k in range(ncross.bit_length() - 1)]
    sources = [mine]
    if bits:
        far_off = swap(mine, "cross", bits[-1])
        sources += [swap(mine, "cross", bit) for bit in bits[:-1]] + [far_off]
        sources += [None] * (len(bits) - 1)
    steps_of = lambda group: jnp.stack([s[rows - 1, :LANES] for s in group]).astype(jnp.int32)

    spread = lambda a: a.transpose(0, 2, 1).reshape(a.shape[0], width)
    wide = lambda a: a.T.reshape(1, width)
    state = spread(cmc_state)
    left = jnp.concatenate([shift(state[:, -bins:], "slab", 1), state[:, :-bins]], axis=1)
    right = jnp.concatenate([state[:, bins:], shift(state[:, :bins], "slab", -1)], axis=1)
    moved = state - 0.4 * (state - left) + 0.1 * (right - 2.0 * state + left)
    moved = jnp.pad(moved, ((0, rows - species), (0, 0)))

    acc = None
    for number, source in enumerate(sources):
        if number and number == len(sources) // 2:
            acc, far_off, moved = lax.optimization_barrier((acc, far_off, moved))
            sources[number] = source = far_off
            sources[number + 1 :] = [swap(far_off, "cross", bit) for bit in bits[:-1]]
        acc = collect_call([sources[number]], table, steps_of([sources[number]]), acc, species, bins, per_tile, ntiles)
    extra = rows - species
    matrix = jnp.tile(jnp.pad(chem_matrix, ((0, extra), (0, -(-rows // 16) * 16 - species))), (1, 3))
    fresh, next_mean, far_mean = middle_call(
        acc, moved, wide(dissipation), wide(reaction_rate), jnp.repeat(substeps, bins)[None, :], matrix, species, bins
    )
    cmc_out = fresh[:species].reshape(species, cells, bins).transpose(0, 2, 1)

    keys = jnp.concatenate([s[species : species + 1] for s in sources], axis=0)
    part = project_call(
        [far_mean, fresh, next_mean], keys, table, steps_of(sources), species, bins, per_tile, ntiles
    )
    part = [part[n] for n in range(len(sources))]
    if bits:
        half = len(part) // 2
        here, there = part[:half], part[half:]

        def gather(group):
            total = group[0]
            for bit, piece in zip(bits[:-1], group[1:]):
                total = total + swap(piece, "cross", bit)
            return total

        there = gather(there)
        part = [gather(here) + swap(there, "cross", bits[-1])]
    total = permute_call(part[0], rank, True)
    conditional = (total[:species] / total[species : species + 1]).reshape(transported.shape)
    les_out = transported + 0.5 * (conditional - transported)
    return (les_out, cmc_out)


def solution(mesh):
    return jax.shard_map(
        on_device,
        mesh=mesh,
        in_specs=(
            P(None, "slab", "cross", None),
            P(None, "cross", "slab"),
            P("slab", "cross", None),
            P("slab", "cross", None),
            P(),
            P(),
            P(),
            P("cross", "slab"),
            P("cross", "slab"),
            P("slab"),
        ),
        out_specs=(P(None, "slab", "cross", None), P(None, "cross", "slab")),
        check_vma=False,
    )
```

```python
import functools

import jax
import jax.numpy as jnp
from jax import lax
from jax.experimental import pallas as pl
from jax.experimental.pallas import tpu as pltpu
from jax.sharding import PartitionSpec as P

KMAX = 4
F32 = jnp.float32
BF16 = jnp.bfloat16
NT = (((1,), (1,)), ((), ()))
NN = (((1,), (0,)), ((), ()))
LANES = 128
TILE = 256
HALF = 64
GROUP = 16
LAG = (2, 4, 6)


def shift(array, axis, by):
    count = lax.axis_size(axis)
    return lax.ppermute(array, axis, [(i, i + by) for i in range(count) if 0 <= i + by < count])


def swap(array, axis, bit):
    count = lax.axis_size(axis)
    return lax.ppermute(array, axis, [(i, i ^ bit) for i in range(count)])


def halves(x):
    high = x.astype(BF16)
    return high, (x - high.astype(F32)).astype(BF16)


def padded_halves(x):
    gap = jnp.zeros((HALF - x.shape[0], x.shape[1]), F32)
    high = x.astype(BF16).astype(F32)
    return jnp.concatenate([high, gap, x - high, gap], axis=0).astype(BF16)


def rows_equal(targets, row):
    return jnp.where(targets == row, 1.0, 0.0).astype(BF16)


def whole(shape):
    return pl.BlockSpec(shape, lambda *_: (0,) * len(shape))


VMEM = pl.BlockSpec(memory_space=pltpu.VMEM)
SMEM = pl.BlockSpec(memory_space=pltpu.SMEM)


def params(mib):
    return pltpu.CompilerParams(vmem_limit_bytes=mib << 20)


def fetch_rows(sources, steps, sems, keys=None):
    rows = sources[0].shape[0]
    copies = []
    for number, source in enumerate(sources):
        last = source.at[rows - 8 : rows]
        copies.append(pltpu.make_async_copy(last.at[:, :LANES], steps.at[number], sems.at[0, number]))
        if keys is not None:
            copies.append(pltpu.make_async_copy(last, keys.at[number], sems.at[1, number]))
    for copy in copies:
        copy.start()
    return copies


def rank_kernel(tiles, span, key_ref, rank_ref, table_ref):
    count = key_ref.shape[1]
    ids = lax.broadcasted_iota(jnp.int32, (tiles, TILE), 0).astype(F32)
    tile_of = lambda n: jnp.floor((key_ref[:, n * TILE : (n + 1) * TILE] + 0.5) * (1.0 / span))
    total = jnp.zeros((tiles, TILE), F32)
    for n in range(count // TILE):
        total = total + jnp.where(ids == tile_of(n), 1.0, 0.0)
    total = jnp.sum(total, axis=1, keepdims=True)
    total = jnp.broadcast_to(total, (tiles, LANES))
    big = jnp.floor(total * (1.0 / HALF))
    row = lax.broadcasted_iota(jnp.int32, (tiles, tiles), 0)
    below = rows_equal(jnp.where(lax.broadcasted_iota(jnp.int32, (tiles, tiles), 1) < row, 1, 0), 1)
    add = lambda part: lax.dot_general(below, part.astype(BF16), NN, preferred_element_type=F32)
    base = add(big) * HALF + add(total - big * HALF)
    order = lax.broadcasted_iota(jnp.int32, (tiles, LANES), 0).astype(F32)
    lane = lax.broadcasted_iota(jnp.int32, (tiles, LANES), 1).astype(F32)
    last = jnp.maximum(jnp.ceil((base + total) * (1.0 / LANES)) - 1.0, 0.0) + order
    passed = jnp.where((last < lane) & (order < tiles - 1), 1.0, 0.0)
    table_ref[...] = jnp.sum(passed, axis=0, keepdims=True)
    ahead = jnp.where(
        lax.broadcasted_iota(jnp.int32, (TILE, TILE), 0) < lax.broadcasted_iota(jnp.int32, (TILE, TILE), 1), 1.0, 0.0
    ).astype(BF16)
    carry = base[:, :1]
    for n in range(count // TILE):
        hot = jnp.where(ids == tile_of(n), 1.0, 0.0)
        before = lax.dot_general(hot.astype(BF16), ahead, NN, preferred_element_type=F32) + carry
        rank_ref[:, n * TILE : (n + 1) * TILE] = jnp.sum(hot * before, axis=0, keepdims=True)
        carry = carry + jnp.sum(hot, axis=1, keepdims=True)


def rank_call(key, tiles, span):
    count = key.shape[1]
    return pl.pallas_call(
        functools.partial(rank_kernel, tiles, span),
        out_shape=[jax.ShapeDtypeStruct((1, count), F32), jax.ShapeDtypeStruct((1, LANES), F32)],
        in_specs=[VMEM],
        out_specs=[VMEM] * 2,
        compiler_params=params(8),
        cost_estimate=pl.CostEstimate(flops=2 * tiles * TILE * count, bytes_accessed=8 * count, transcendentals=0),
        name="rank",
    )(key)


def permute_kernel(back, count, rank_ref, *refs):
    xs, (out_ref, parts) = refs[:count], refs[count:]
    steps_ref = None
    if not back:
        xs, steps_ref = xs[:-1], xs[-1]
    rows, count = xs[0].shape
    chunk = 2 * TILE

    @pl.when(pl.program_id(0) == 0)
    def _():
        x = xs[0][...]
        for more in xs[1:]:
            x = x + more[...]
        high = x.astype(BF16).astype(F32)
        parts[...] = jnp.concatenate([high, x - high], axis=0).astype(BF16)

    total = jnp.zeros((2 * rows, TILE), F32)
    here = pl.program_id(0) * TILE
    for n in range(count // chunk):
        piece = slice(n * chunk, (n + 1) * chunk)
        if back:
            ids = lax.broadcasted_iota(jnp.int32, (chunk, TILE), 0) + n * chunk
            hot = rows_equal(ids.astype(F32), rank_ref[:, pl.ds(pl.multiple_of(here, TILE), TILE)])
            total = total + lax.dot_general(parts[:, piece], hot, NN, preferred_element_type=F32)
        else:
            ids = lax.broadcasted_iota(jnp.int32, (TILE, chunk), 0) + here
            hot = rows_equal(ids.astype(F32), rank_ref[:, piece])
            total = total + lax.dot_general(parts[:, piece], hot, NT, preferred_element_type=F32)
    total = total[:rows] + total[rows:]
    if back:
        out_ref[...] = total / total[rows - 2 : rows - 1]
    else:
        line = lax.broadcasted_iota(jnp.int32, (rows, TILE), 0)
        steps = jnp.concatenate([steps_ref[...]] * (TILE // LANES), axis=1)
        out_ref[...] = jnp.where(line == rows - 1, steps, total)


def permute_call(xs, rank, steps, back):
    rows, count = xs[0].shape
    args = list(xs) + ([] if back else [steps])
    return pl.pallas_call(
        functools.partial(permute_kernel, back, len(args)),
        grid=(count // TILE,),
        out_shape=jax.ShapeDtypeStruct((rows, count), F32),
        in_specs=[whole(rank.shape)] + [whole(x.shape) for x in args],
        out_specs=pl.BlockSpec((rows, TILE), lambda i: (0, i)),
        scratch_shapes=[pltpu.VMEM((2 * rows, count), BF16)],
        compiler_params=params(12),
        cost_estimate=pl.CostEstimate(flops=4 * rows * count * count, bytes_accessed=8 * rows * count, transcendentals=0),
        name="unsort" if back else "sort",
    )(rank, *args)


def weights_of(key, table, bins, per_tile):
    nshape = table.shape[1]
    cell = jnp.floor((key + 0.5) * (1.0 / nshape))
    shape = key - cell * nshape
    tile = jnp.floor((cell + 0.5) * (1.0 / per_tile))
    within = cell - tile * per_tile
    ids = lax.broadcasted_iota(jnp.int32, (nshape, key.shape[1]), 0).astype(F32)
    picked = lax.dot_general(table, rows_equal(ids, shape), NN, preferred_element_type=F32).astype(BF16)
    masks = [jnp.where(within == m, 1.0, 0.0).astype(BF16) for m in range(per_tile)]
    columns = []
    for part in (picked[:bins], picked[bins:]):
        columns.append(jnp.concatenate([part * mask for mask in masks], axis=0))
    return jnp.concatenate(columns, axis=1), tile


def split_table(table):
    high = table.astype(BF16).astype(F32)
    return jnp.concatenate([high, table - high], axis=0).astype(BF16)


def prepare_weights(source, index, key_row, table, bins, per_tile, weights, tiles):
    def step(n, _):
        key = source[key_row : key_row + 1, pl.ds(pl.multiple_of(n * LANES, LANES), LANES)]
        block, tile = weights_of(key, table, bins, per_tile)
        weights[index + n] = block
        tiles[index + n] = jnp.broadcast_to(tile, tiles.shape[1:])
        return 0

    lax.fori_loop(0, source.shape[1] // LANES, step, 0, unroll=4)


def collect_kernel(species, bins, per_tile, pairs, lists, first, *refs):
    sources, refs = refs[:lists], refs[lists:]
    table_ref, *refs = refs
    acc_ref = None if first else refs.pop(0)
    out_ref, weights, tiles, parts, steps, sems = refs
    copies = fetch_rows(sources, steps, sems)
    rows, count = sources[0].shape
    blocks = count // LANES
    out_ref[...] = jnp.zeros_like(out_ref) if first else acc_ref[...]
    table = split_table(table_ref[...])
    line = lax.broadcasted_iota(jnp.int32, (rows, LANES), 0)
    for number, source in enumerate(sources):
        prepare_weights(source, number * blocks, species, table, bins, per_tile, weights, tiles)

        def split(n, _, source=source, number=number):
            x = source[:, pl.ds(pl.multiple_of(n * LANES, LANES), LANES)]
            x = jnp.where(line < species, x, jnp.where(line == species, 1.0, 0.0))
            parts[number * blocks + n] = padded_halves(x)
            return 0

        lax.fori_loop(0, blocks, split, 0, unroll=2)

    for copy in copies:
        copy.wait()

    def step(n, _):
        for number in range(lists):
            for g in range(GROUP):
                k = n * GROUP + g
                tile = steps[number, 7, k].astype(jnp.int32)
                block = jnp.minimum(k - tile, blocks - 1) + number * blocks
                wanted = jnp.where(k < pairs, tile, -1).astype(F32)
                mask = jnp.where(tiles[block] == wanted, 1.0, 0.0).astype(BF16)
                mask = jnp.concatenate([mask] * (2 * HALF // mask.shape[0]), axis=0)
                x = parts[block] * mask
                both = jnp.concatenate([x, x], axis=1)
                got = lax.dot_general(both, weights[block], NT, preferred_element_type=F32)
                place = pl.ds(pl.multiple_of(tile * TILE, TILE), TILE)
                out_ref[:, place] += got[:rows] + got[HALF : HALF + rows]
        return 0

    lax.fori_loop(0, -(-pairs // GROUP), step, 0)


def collect_call(sources, table, acc, species, bins, per_tile, ntiles):
    rows, count = sources[0].shape
    lists, blocks = len(sources), count // LANES
    pairs = blocks + ntiles - 1
    args = list(sources) + [table]
    specs = [VMEM] * (lists + 1)
    alias = {}
    if acc is not None:
        alias = {len(args): 0}
        args.append(acc)
        specs.append(VMEM)
    return pl.pallas_call(
        functools.partial(collect_kernel, species, bins, per_tile, pairs, lists, acc is None),
        out_shape=jax.ShapeDtypeStruct((rows, ntiles * TILE), F32),
        in_specs=specs,
        out_specs=VMEM,
        scratch_shapes=[
            pltpu.VMEM((lists * blocks, TILE, 2 * LANES), BF16),
            pltpu.VMEM((lists * blocks, 16, LANES), F32),
            pltpu.VMEM((lists * blocks, 2 * HALF, LANES), BF16),
            pltpu.SMEM((lists, 8, LANES), F32),
            pltpu.SemaphoreType.DMA((2, lists)),
        ],
        input_output_aliases=alias,
        compiler_params=params(24),
        cost_estimate=pl.CostEstimate(flops=lists * pairs * 2 * LANES * TILE * TILE, bytes_accessed=0, transcendentals=0),
        name="collect",
    )(*args)


def project_kernel(bins, per_tile, pairs, lists, *refs):
    means, refs = refs[:3], refs[3:]
    sources, refs = refs[:lists], refs[lists:]
    table_ref, *refs = refs
    outs, (weights, tiles, parts, keys, steps, sems) = refs[:lists], refs[lists:]
    copies = fetch_rows(sources, steps, sems, keys)
    rows, count = outs[0].shape
    blocks = count // LANES
    per_mean = means[0].shape[1] // TILE
    for number, mean in enumerate(means):

        def split(n, _, number=number, mean=mean):
            parts[number * per_mean + n] = padded_halves(mean[:, pl.ds(pl.multiple_of(n * TILE, TILE), TILE)])
            return 0

        lax.fori_loop(0, per_mean, split, 0, unroll=2)
    table = split_table(table_ref[...])
    for copy in copies:
        copy.wait()
    for number in range(lists):
        outs[number][...] = jnp.zeros_like(outs[number])
        prepare_weights(keys.at[number], number * blocks, 6, table, bins, per_tile, weights, tiles)

    def step(n, _):
        for number in range(lists):
            for g in range(GROUP):
                k = n * GROUP + g
                tile = steps[number, 7, k].astype(jnp.int32)
                local = jnp.minimum(k - tile, blocks - 1)
                block = local + number * blocks
                wanted = jnp.where(k < pairs, tile, -1).astype(F32)
                got = lax.dot_general(parts[tile], weights[block], NN, preferred_element_type=F32)
                got = got[:rows] + got[HALF : HALF + rows]
                got = got[:, :LANES] + got[:, LANES:]
                got = jnp.where(tiles[block][:1] == wanted, got, 0.0)
                place = pl.ds(pl.multiple_of(local * LANES, LANES), LANES)
                outs[number][:, place] += got
        return 0

    lax.fori_loop(0, -(-pairs // GROUP), step, 0)


def project_call(means, sources, table, bins, per_tile, ntiles):
    rows, count = sources[0].shape
    lists = len(sources)
    blocks = count // LANES
    pairs = blocks + ntiles - 1
    return pl.pallas_call(
        functools.partial(project_kernel, bins, per_tile, pairs, lists),
        out_shape=[jax.ShapeDtypeStruct((rows, count), F32)] * lists,
        in_specs=[VMEM] * 3 + [pl.BlockSpec(memory_space=pl.ANY)] * lists + [VMEM],
        out_specs=[VMEM] * lists,
        scratch_shapes=[
            pltpu.VMEM((lists * blocks, TILE, 2 * LANES), BF16),
            pltpu.VMEM((lists * blocks, 16, LANES), F32),
            pltpu.VMEM((ntiles, 2 * HALF, TILE), BF16),
            pltpu.VMEM((lists, 8, count), F32),
            pltpu.SMEM((lists, 8, LANES), F32),
            pltpu.SemaphoreType.DMA((2, lists)),
        ],
        compiler_params=params(24),
        cost_estimate=pl.CostEstimate(flops=lists * pairs * 2 * LANES * TILE * TILE, bytes_accessed=0, transcendentals=0),
        name="project",
    )(*means, *sources, table)


def middle_kernel(species, bins, chunk, refs_in, refs_out, scratch):
    acc_ref, moved_ref, diss_ref, rate_ref, count_ref, matrix_ref = refs_in
    fresh_ref, next_ref, far_ref = refs_out
    hopped, summed, got, state_ref, edge_out, edge_in, pick_ref, third_ref, send, recv = scratch
    rows, width = fresh_ref.shape
    steps = width // chunk
    per_chunk = chunk // bins
    slab, nslab = lax.axis_index("slab"), lax.axis_size("slab")
    cross, ncross = lax.axis_index("cross"), lax.axis_size("cross")
    parity = lax.rem(slab, 2)
    outer = slab + 4 * parity - 2
    inner = slab - 4 * parity + 2
    partner = slab + 1 - 2 * parity
    has_outer = (outer >= 0) & (outer < nslab)
    has_inner = (inner >= 0) & (inner < nslab)
    has_before, has_after = cross > 0, cross < ncross - 1
    mesh = pl.DeviceIdType.MESH

    @pl.when(jnp.logical_not(has_inner))
    def _():
        hopped[...] = jnp.zeros_like(hopped)

    @pl.when(jnp.logical_not(has_outer))
    def _():
        far_ref[...] = jnp.zeros_like(far_ref)

    @pl.when(jnp.logical_not(has_before))
    def _():
        edge_in[:, :, :LANES] = jnp.zeros(edge_in.shape[:2] + (LANES,), F32)

    @pl.when(jnp.logical_not(has_after))
    def _():
        edge_in[:, :, LANES:] = jnp.zeros(edge_in.shape[:2] + (LANES,), F32)

    barrier = pltpu.get_barrier_semaphore()
    greet = lambda where: pl.semaphore_signal(barrier, inc=1, device_id=where, device_id_type=mesh)
    greet({"slab": partner})
    pl.when(has_outer)(lambda: greet({"slab": outer}))
    pl.when(has_inner)(lambda: greet({"slab": inner}))
    pl.when(has_before)(lambda: greet({"cross": cross - 1}))
    pl.when(has_after)(lambda: greet({"cross": cross + 1}))
    number = lambda flag: jnp.where(flag, 1, 0)
    pl.semaphore_wait(barrier, 1 + number(has_outer) + number(has_inner) + number(has_before) + number(has_after))

    def lanes(c, base=0):
        return pl.ds(pl.multiple_of(base + c * chunk, chunk), chunk)

    def remote(kind, c, source, target, where):
        return pltpu.make_async_remote_copy(
            src_ref=source, dst_ref=target, send_sem=send.at[kind, c], recv_sem=recv.at[kind, c],
            device_id=where, device_id_type=mesh,
        )

    to_outer = lambda c: remote(0, c, acc_ref.at[:, lanes(c)], hopped.at[:, lanes(c)], {"slab": outer})
    to_partner = lambda c: remote(1, c, summed.at[:, lanes(c)], got.at[:, lanes(c)], {"slab": partner})
    to_after = lambda c: remote(2, c, edge_out.at[c, :, LANES:], edge_in.at[c, :, :LANES], {"cross": cross + 1})
    to_before = lambda c: remote(3, c, edge_out.at[c, :, :LANES], edge_in.at[c, :, LANES:], {"cross": cross - 1})
    give = lambda c: remote(4, c, fresh_ref.at[:, lanes(c)], next_ref.at[:, lanes(c)], {"slab": partner})
    pass_on = lambda c: remote(5, c, next_ref.at[:, lanes(c)], far_ref.at[:, lanes(c)], {"slab": inner})

    @pl.when(has_outer)
    def _():
        for c in range(steps):
            to_outer(c).start()

    lane = lax.broadcasted_iota(jnp.int32, (2 * LANES, chunk), 1)
    row = lax.broadcasted_iota(jnp.int32, (2 * LANES, chunk), 0)
    target = jnp.where(row < LANES, row * bins, (row - LANES) * bins + bins - 1)
    pick_ref[...] = rows_equal(target, lane)
    third = matrix_ref.shape[1] // 3
    high, low = halves(matrix_ref[...])
    column = lax.broadcasted_iota(jnp.int32, matrix_ref.shape, 1)
    third_ref[...] = jnp.where(column < 2 * third, high.astype(F32), low.astype(F32)).astype(BF16)
    line = lax.broadcasted_iota(jnp.int32, (rows, chunk), 0)
    slot = lax.broadcasted_iota(jnp.int32, (rows, chunk), 1) % bins
    gap = [jnp.zeros((third - rows, chunk), F32)] * (third > rows)

    def stacked(x):
        high = x.astype(BF16).astype(F32)
        return jnp.concatenate([high, x - high], axis=0).astype(BF16)

    def add_hop(c):
        pl.when(has_inner)(lambda: to_outer(c).wait_recv())
        summed[:, lanes(c)] = acc_ref[:, lanes(c, 2 * width)] + hopped[:, lanes(c)]

    def blend(c):
        total = acc_ref[:, lanes(c, width)] + got[:, lanes(c)]
        blended = (total + moved_ref[:, lanes(c)]) / (total[species : species + 1] + 1.0)
        state_ref[:, lanes(c)] = blended
        edge = lax.dot_general(stacked(blended), pick_ref[...], NT, preferred_element_type=F32)
        edge_out[c] = edge[:rows] + edge[rows:]

    def send_edges(c):
        pl.when(has_after)(lambda: to_after(c).start())
        pl.when(has_before)(lambda: to_before(c).start())

    def wait_edges(c):
        pl.when(has_before)(lambda: to_after(c).wait_recv())
        pl.when(has_after)(lambda: to_before(c).wait_recv())

    def react(c):
        here = state_ref[:, lanes(c)]
        around = lax.dot_general(stacked(edge_in[c]), pick_ref[...], NN, preferred_element_type=F32)
        around = around[:rows] + around[rows:]
        before = jnp.where(slot == 0, around, pltpu.roll(here, 1, 1))
        after = jnp.where(slot == bins - 1, around, pltpu.roll(here, chunk - 1, 1))
        state = here + diss_ref[:, lanes(c)] * (after - 2.0 * here + before)
        half = 0.5 * rate_ref[:, lanes(c)]
        count = count_ref[:, lanes(c)]
        for k in range(KMAX):
            high, low = (part.astype(F32) for part in halves(state))
            stack = jnp.concatenate([high, *gap, low, *gap, high, *gap], axis=0).astype(BF16)
            rate = lax.dot_general(third_ref[...], stack, NN, preferred_element_type=F32)
            state = jnp.where(k < count, state + half * jnp.tanh(rate), state)
        fresh_ref[:, lanes(c)] = jnp.where(line == species, 1.0, state)

    def step(t, _):
        def when(lag, body):
            c = t - lag
            pl.when((c >= 0) & (c < steps))(lambda: body(c))

        def second(c):
            to_partner(c).wait_recv()
            blend(c)

        def third_stage(c):
            wait_edges(c)
            react(c)

        def fourth(c):
            give(c).wait_recv()
            pl.when(has_inner)(lambda: pass_on(c).start())

        when(0, add_hop)
        when(LAG[0], second)
        when(0, lambda c: to_partner(c).start())
        when(LAG[1], third_stage)
        when(LAG[0], send_edges)
        when(LAG[2], fourth)
        when(LAG[1], lambda c: give(c).start())
        return 0

    lax.fori_loop(0, steps + LAG[2], step, 0)

    def finish(c, _):
        pl.when(has_outer)(lambda: to_outer(c).wait_send())
        to_partner(c).wait_send()
        pl.when(has_after)(lambda: to_after(c).wait_send())
        pl.when(has_before)(lambda: to_before(c).wait_send())
        give(c).wait_send()
        pl.when(has_inner)(lambda: pass_on(c).wait_send())
        pl.when(has_outer)(lambda: pass_on(c).wait_recv())
        return 0

    lax.fori_loop(0, steps, finish, 0)


def middle_call(acc, moved, diss, rate, count, matrix, species, bins, chunk=512):
    rows, width = moved.shape
    steps = width // chunk

    def kernel(*refs):
        middle_kernel(species, bins, chunk, refs[:6], refs[6:9], refs[9:])

    return pl.pallas_call(
        kernel,
        out_shape=[jax.ShapeDtypeStruct((rows, width), F32)] * 3,
        in_specs=[VMEM] * 6,
        out_specs=[VMEM] * 3,
        scratch_shapes=[pltpu.VMEM((rows, width), F32)] * 4
        + [pltpu.VMEM((steps, rows, 2 * LANES), F32)] * 2
        + [pltpu.VMEM((2 * LANES, chunk), BF16), pltpu.VMEM(matrix.shape, BF16)]
        + [pltpu.SemaphoreType.DMA((6, steps))] * 2,
        compiler_params=pltpu.CompilerParams(vmem_limit_bytes=24 << 20, collective_id=1, has_side_effects=True),
        name="middle",
    )(acc, moved, diss, rate, count, matrix)


def on_device(
    les_state, cmc_state, cmc_map, pdf_index, pdf_table, diffusion, chem_matrix, dissipation, reaction_rate, substeps
):
    species = les_state.shape[0]
    rows = -(-(species + 2) // 8) * 8
    bins, cells = cmc_state.shape[1:]
    nshape = pdf_table.shape[0]
    count = cmc_map.size
    ncross = lax.axis_size("cross")
    per_tile = TILE // bins
    ntiles = 3 * cells // per_tile
    width = cells * bins
    odd = lax.axis_index("slab") % 2 == 1

    below = shift(les_state[:, -1:], "slab", 1)
    above = shift(les_state[:, :1], "slab", -1)
    behind = shift(les_state[:, :, -1:], "cross", 1)
    ahead = shift(les_state[:, :, :1], "cross", -1)

    offset = cmc_map.reshape(1, count) - (lax.axis_index("slab") - 1) * cells
    block = offset // cells
    offset = jnp.where(odd, (2 - block) * cells + offset - block * cells, offset)
    key = (offset * nshape + pdf_index.reshape(1, count)).astype(F32)
    rank, steps = rank_call(key, ntiles, nshape * per_tile)

    xs = jnp.concatenate([below, les_state, above], axis=1)
    ys = jnp.concatenate([behind, les_state, ahead], axis=2)
    zs = jnp.pad(les_state, ((0, 0), (0, 0), (0, 0), (1, 1)))
    around = xs[:, 2:] + xs[:, :-2] + ys[:, :, 2:] + ys[:, :, :-2] + zs[..., 2:] + zs[..., :-2]
    transported = les_state + diffusion[:, None, None, None] * (around - 6.0 * les_state)
    flat = transported.reshape(species, count)
    fill = [jnp.zeros((rows - species - 1, count), F32)]
    mine = permute_call([jnp.concatenate([flat, key] + fill, axis=0)], rank, steps, False)

    table = lax.dynamic_slice_in_dim(pdf_table.T, lax.axis_index("cross") * bins, bins, axis=0)

    mine, cmc_state, dissipation, reaction_rate, substeps, chem_matrix = lax.optimization_barrier(
        (mine, cmc_state, dissipation, reaction_rate, substeps, chem_matrix)
    )
    bits = [1 << k for k in range(ncross.bit_length() - 1)]
    near_lists, far_lists = [mine], []
    if bits:
        far_lists = [swap(mine, "cross", bits[-1])]
        near_lists += [swap(mine, "cross", bit) for bit in bits[:-1]]

    spread = lambda a: a.transpose(0, 2, 1).reshape(a.shape[0], width)
    wide = lambda a: a.T.reshape(1, width)
    state = spread(cmc_state)
    left = jnp.concatenate([shift(state[:, -bins:], "slab", 1), state[:, :-bins]], axis=1)
    right = jnp.concatenate([state[:, bins:], shift(state[:, :bins], "slab", -1)], axis=1)
    moved = state - 0.4 * (state - left) + 0.1 * (right - 2.0 * state + left)
    moved = jnp.pad(moved, ((0, rows - species), (0, 0)))

    extra = rows - species
    matrix = jnp.tile(jnp.pad(chem_matrix, ((0, extra), (0, -(-rows // 16) * 16 - species))), (1, 3))
    terms = (moved, wide(dissipation), wide(reaction_rate), jnp.repeat(substeps, bins)[None, :], matrix)
    acc = collect_call(near_lists, table, None, species, bins, per_tile, ntiles)
    if bits:
        acc, far_lists, terms = lax.optimization_barrier((acc, far_lists, terms))
        far_lists = list(far_lists) + [swap(far_lists[0], "cross", bit) for bit in bits[:-1]]
        acc = collect_call(far_lists, table, acc, species, bins, per_tile, ntiles)
    means = middle_call(acc, *terms, species, bins)
    fresh = means[0]
    means = [means[2], means[0], means[1]]
    cmc_out = fresh[:species].reshape(species, cells, bins).transpose(0, 2, 1)


    def gather(group):
        total = group[0]
        for bit, piece in zip(bits[:-1], group[1:]):
            total = total + swap(piece, "cross", bit)
        return total

    if bits:
        there = gather(project_call(means, far_lists, table, bins, per_tile, ntiles))
        there, means = lax.optimization_barrier((there, means))
        there = swap(there, "cross", bits[-1])
    here = project_call(means, near_lists, table, bins, per_tile, ntiles)
    total = [here[0]] + [swap(piece, "cross", bit) for bit, piece in zip(bits[:-1], here[1:])]
    conditional = permute_call(total + [there] * bool(bits), rank, None, True)
    conditional = conditional[:species].reshape(transported.shape)
    les_out = transported + 0.5 * (conditional - transported)
    return (les_out, cmc_out)


def solution(mesh):
    return jax.shard_map(
        on_device,
        mesh=mesh,
        in_specs=(
            P(None, "slab", "cross", None),
            P(None, "cross", "slab"),
            P("slab", "cross", None),
            P("slab", "cross", None),
            P(),
            P(),
            P(),
            P("cross", "slab"),
            P("cross", "slab"),
            P("slab"),
        ),
        out_specs=(P(None, "slab", "cross", None), P(None, "cross", "slab")),
        check_vma=False,
    )
```

```python
import functools


import jax
import jax.numpy as jnp
from jax import lax
from jax.experimental import pallas as pl
from jax.experimental.pallas import tpu as pltpu
from jax.sharding import PartitionSpec as P

KMAX = 4
F32 = jnp.float32
BF16 = jnp.bfloat16
NT = (((1,), (1,)), ((), ()))
NN = (((1,), (0,)), ((), ()))
LANES = 128
TILE = 256
HALF = 64
GROUP = 16
LAG = (2, 4, 6)


def swap(array, axis, bit):
    count = lax.axis_size(axis)
    return lax.ppermute(array, axis, [(i, i ^ bit) for i in range(count)])


def halves(x):
    high = x.astype(BF16)
    return high, (x - high.astype(F32)).astype(BF16)


def padded_halves(x):
    gap = jnp.zeros((HALF - x.shape[0], x.shape[1]), F32)
    high = x.astype(BF16).astype(F32)
    return jnp.concatenate([high, gap, x - high, gap], axis=0).astype(BF16)


def rows_equal(targets, row):
    return jnp.where(targets == row, 1.0, 0.0).astype(BF16)


def whole(shape):
    return pl.BlockSpec(shape, lambda *_: (0,) * len(shape))


VMEM = pl.BlockSpec(memory_space=pltpu.VMEM)
SMEM = pl.BlockSpec(memory_space=pltpu.SMEM)


def params(mib):
    return pltpu.CompilerParams(vmem_limit_bytes=mib << 20)


def fetch_rows(sources, steps, sems):
    copies = []
    for number, source in enumerate(sources):
        last = source.at[source.shape[0] - 8 : source.shape[0], :LANES]
        copies.append(pltpu.make_async_copy(last, steps.at[number], sems.at[number]))
        copies[-1].start()
    return copies


def ranks(tiles, span, key_ref, rank_ref, table_ref):
    count = rank_ref.shape[1]
    ids = lax.broadcasted_iota(jnp.int32, (tiles, TILE), 0).astype(F32)
    tile_of = lambda n: jnp.floor((key_ref[:1, n * TILE : (n + 1) * TILE] + 0.5) * (1.0 / span))
    total = jnp.zeros((tiles, TILE), F32)
    for n in range(count // TILE):
        total = total + jnp.where(ids == tile_of(n), 1.0, 0.0)
    total = jnp.sum(total, axis=1, keepdims=True)
    total = jnp.broadcast_to(total, (tiles, LANES))
    big = jnp.floor(total * (1.0 / HALF))
    row = lax.broadcasted_iota(jnp.int32, (tiles, tiles), 0)
    below = rows_equal(jnp.where(lax.broadcasted_iota(jnp.int32, (tiles, tiles), 1) < row, 1, 0), 1)
    add = lambda part: lax.dot_general(below, part.astype(BF16), NN, preferred_element_type=F32)
    base = add(big) * HALF + add(total - big * HALF)
    order = lax.broadcasted_iota(jnp.int32, (tiles, LANES), 0).astype(F32)
    lane = lax.broadcasted_iota(jnp.int32, (tiles, LANES), 1).astype(F32)
    last = jnp.maximum(jnp.ceil((base + total) * (1.0 / LANES)) - 1.0, 0.0) + order
    passed = jnp.where((last < lane) & (order < tiles - 1), 1.0, 0.0)
    table_ref[...] = jnp.sum(passed, axis=0, keepdims=True)
    ahead = jnp.where(
        lax.broadcasted_iota(jnp.int32, (TILE, TILE), 0) < lax.broadcasted_iota(jnp.int32, (TILE, TILE), 1), 1.0, 0.0
    ).astype(BF16)
    carry = base[:, :1]
    for n in range(count // TILE):
        hot = jnp.where(ids == tile_of(n), 1.0, 0.0)
        before = lax.dot_general(hot.astype(BF16), ahead, NN, preferred_element_type=F32) + carry
        rank_ref[:, n * TILE : (n + 1) * TILE] = jnp.sum(hot * before, axis=0, keepdims=True)
        carry = carry + jnp.sum(hot, axis=1, keepdims=True)


def head_kernel(grid_shape, cells, nshape, tiles, span, *refs):
    les_ref, map_ref, shape_ref, diff_ref, t_ref, rank_ref, table_ref, key_ref, *refs = refs
    faces, halos, (send, recv) = refs[:4], refs[4:8], refs[8:]
    species, nx, ny = grid_shape
    count = rank_ref.shape[1]
    slab, nslab = lax.axis_index("slab"), lax.axis_size("slab")
    cross, ncross = lax.axis_index("cross"), lax.axis_size("cross")
    mesh = pl.DeviceIdType.MESH
    sides = [
        (slab > 0, {"slab": slab - 1}),
        (slab < nslab - 1, {"slab": slab + 1}),
        (cross > 0, {"cross": cross - 1}),
        (cross < ncross - 1, {"cross": cross + 1}),
    ]
    barrier = pltpu.get_barrier_semaphore()
    for n, (there, where) in enumerate(sides):

        @pl.when(jnp.logical_not(there))
        def _(n=n):
            halos[n][...] = jnp.zeros_like(halos[n])

    line = lambda x, y: les_ref[pl.ds(x * ny + y, species, stride=nx * ny), :]
    for n, x in enumerate((0, nx - 1)):
        for y in range(ny):
            faces[n][y, :species] = line(x, y)
    for n, y in enumerate((0, ny - 1)):
        for x in range(nx):
            faces[2 + n][x, :species] = line(x, y)
    for there, where in sides:

        @pl.when(there)
        def _(where=where):
            pl.semaphore_signal(barrier, inc=1, device_id=where, device_id_type=mesh)

    pl.semaphore_wait(barrier, sum(jnp.where(there, 1, 0) for there, _ in sides))
    copies = []
    for n, (there, where) in enumerate(sides):
        copy = pltpu.make_async_remote_copy(
            src_ref=faces[n], dst_ref=halos[n ^ 1], send_sem=send.at[n], recv_sem=recv.at[n ^ 1],
            device_id=where, device_id_type=mesh,
        )
        pl.when(there)(copy.start)
        copies.append(copy)
    offset = map_ref[...] - (slab - 1) * cells
    block = jnp.where(offset >= cells, 1, 0) + jnp.where(offset >= 2 * cells, 1, 0)
    offset = jnp.where(lax.rem(slab, 2) == 1, (2 - block) * cells + offset - block * cells, offset)
    key = (offset * nshape + shape_ref[...]).astype(F32)
    key_ref[:1, :] = key
    t_ref[species:, :] = jnp.concatenate([key] + [jnp.zeros((t_ref.shape[0] - species - 1, count), F32)], axis=0)
    ranks(tiles, span, key_ref, rank_ref, table_ref)
    row = lax.broadcasted_iota(jnp.int32, (species, species), 0)
    number = jnp.where(row == lax.broadcasted_iota(jnp.int32, (species, species), 1), diff_ref[...], 0.0)
    number = jnp.sum(number, axis=1, keepdims=True)
    lane = lax.broadcasted_iota(jnp.int32, (species, LANES), 1)
    for n, (there, _) in enumerate(sides):
        pl.when(sides[n ^ 1][0])(copies[n].wait_recv)
    for x in range(nx):
        for y in range(ny):
            here = line(x, y)
            around = line(x + 1, y) if x < nx - 1 else halos[1][y, :species]
            around = around + (line(x - 1, y) if x else halos[0][y, :species])
            around = around + (line(x, y + 1) if y < ny - 1 else halos[3][x, :species])
            around = around + (line(x, y - 1) if y else halos[2][x, :species])
            around = around + jnp.where(lane < LANES - 1, pltpu.roll(here, LANES - 1, 1), 0.0)
            around = around + jnp.where(lane > 0, pltpu.roll(here, 1, 1), 0.0)
            place = (x * ny + y) * LANES
            t_ref[:species, place : place + LANES] = here + number * (around - 6.0 * here)
    for n, (there, _) in enumerate(sides):
        pl.when(there)(copies[n].wait_send)


def head_call(les_state, cmc_map, pdf_index, diffusion, rows, cells, nshape, tiles, span):
    species, nx, ny, nz = les_state.shape
    count = nx * ny * nz
    halo = [pltpu.VMEM((n, rows, LANES), F32) for n in (ny, ny, nx, nx)]
    return pl.pallas_call(
        functools.partial(head_kernel, (species, nx, ny), cells, nshape, tiles, span),
        out_shape=[
            jax.ShapeDtypeStruct((rows, count), F32),
            jax.ShapeDtypeStruct((1, count), F32),
            jax.ShapeDtypeStruct((1, LANES), F32),
        ],
        in_specs=[VMEM] * 4,
        out_specs=[VMEM] * 3,
        scratch_shapes=[pltpu.VMEM((8, count), F32)] + halo * 2 + [pltpu.SemaphoreType.DMA((4,))] * 2,
        compiler_params=pltpu.CompilerParams(vmem_limit_bytes=12 << 20, collective_id=2, has_side_effects=True),
        name="head",
    )(
        les_state.reshape(species * nx * ny, nz), cmc_map.reshape(1, count), pdf_index.reshape(1, count),
        diffusion.reshape(1, species),
    )


def permute_kernel(back, count, rank_ref, *refs):
    xs, (out_ref, parts) = refs[:count], refs[count:]
    xs, extra_ref = xs[:-1], xs[-1]
    rows, count = xs[0].shape
    chunk = 2 * TILE

    @pl.when(pl.program_id(0) == 0)
    def _():
        x = xs[0][...]
        for more in xs[1:]:
            x = x + more[...]
        high = x.astype(BF16).astype(F32)
        parts[...] = jnp.concatenate([high, x - high], axis=0).astype(BF16)

    total = jnp.zeros((2 * rows, TILE), F32)
    here = pl.program_id(0) * TILE
    for n in range(count // chunk):
        piece = slice(n * chunk, (n + 1) * chunk)
        if back:
            ids = lax.broadcasted_iota(jnp.int32, (chunk, TILE), 0) + n * chunk
            hot = rows_equal(ids.astype(F32), rank_ref[:, pl.ds(pl.multiple_of(here, TILE), TILE)])
            total = total + lax.dot_general(parts[:, piece], hot, NN, preferred_element_type=F32)
        else:
            ids = lax.broadcasted_iota(jnp.int32, (TILE, chunk), 0) + here
            hot = rows_equal(ids.astype(F32), rank_ref[:, piece])
            total = total + lax.dot_general(parts[:, piece], hot, NT, preferred_element_type=F32)
    total = total[:rows] + total[rows:]
    if back:
        species = rows - 2
        lines = count // LANES
        for n in range(TILE // LANES):
            piece = total[:, n * LANES : (n + 1) * LANES]
            moved = extra_ref[:species, pl.ds(pl.multiple_of(here + n * LANES, LANES), LANES)]
            piece = piece[:species] / piece[species : species + 1]
            line = pl.program_id(0) * (TILE // LANES) + n
            out_ref[pl.ds(line, species, stride=lines), :] = moved + 0.5 * (piece - moved)
    else:
        line = lax.broadcasted_iota(jnp.int32, (rows, TILE), 0)
        steps = jnp.concatenate([extra_ref[...]] * (TILE // LANES), axis=1)
        out_ref[...] = jnp.where(line == rows - 1, steps, total)


def permute_call(xs, rank, extra, back):
    rows, count = xs[0].shape
    args = list(xs) + [extra]
    lines = (rows - 2) * count // LANES
    out_shape, out_spec = (rows, count), pl.BlockSpec((rows, TILE), lambda i: (0, i))
    if back:
        out_shape, out_spec = (lines, LANES), whole((lines, LANES))
    return pl.pallas_call(
        functools.partial(permute_kernel, back, len(args)),
        grid=(count // TILE,),
        out_shape=jax.ShapeDtypeStruct(out_shape, F32),
        in_specs=[whole(rank.shape)] + [whole(x.shape) for x in args],
        out_specs=out_spec,
        scratch_shapes=[pltpu.VMEM((2 * rows, count), BF16)],
        compiler_params=params(12),
        cost_estimate=pl.CostEstimate(flops=4 * rows * count * count, bytes_accessed=8 * rows * count, transcendentals=0),
        name="unsort" if back else "sort",
    )(rank, *args)


def weights_of(key, table, bins, per_tile):
    nshape = table.shape[1]
    cell = jnp.floor((key + 0.5) * (1.0 / nshape))
    shape = key - cell * nshape
    tile = jnp.floor((cell + 0.5) * (1.0 / per_tile))
    within = cell - tile * per_tile
    ids = lax.broadcasted_iota(jnp.int32, (nshape, key.shape[1]), 0).astype(F32)
    picked = lax.dot_general(table, rows_equal(ids, shape), NN, preferred_element_type=F32).astype(BF16)
    masks = [jnp.where(within == m, 1.0, 0.0).astype(BF16) for m in range(per_tile)]
    columns = []
    for part in (picked[:bins], picked[bins:]):
        columns.append(jnp.concatenate([part * mask for mask in masks], axis=0))
    return jnp.concatenate(columns, axis=1), tile


def split_table(table):
    high = table.astype(BF16).astype(F32)
    return jnp.concatenate([high, table - high], axis=0).astype(BF16)


def prepare_weights(source, index, key_row, table, bins, per_tile, weights, tiles):
    def step(n, _):
        key = source[key_row : key_row + 1, pl.ds(pl.multiple_of(n * LANES, LANES), LANES)]
        block, tile = weights_of(key, table, bins, per_tile)
        weights[index + n] = block
        tiles[index + n] = jnp.broadcast_to(tile, tiles.shape[1:])
        return 0

    lax.fori_loop(0, source.shape[1] // LANES, step, 0, unroll=4)


def collect_kernel(species, bins, per_tile, pairs, lists, first, *refs):
    sources, refs = refs[:lists], refs[lists:]
    table_ref, *refs = refs
    acc_ref = None if first else refs.pop(0)
    out_ref, *refs = refs
    keys, (weights, tiles, parts, steps, sems) = refs[:lists], refs[lists:]
    copies = fetch_rows(sources, steps, sems)
    for key, source in zip(keys, sources):
        key[...] = source[source.shape[0] - 8 :, :]
    rows, count = sources[0].shape
    blocks = count // LANES
    out_ref[...] = jnp.zeros_like(out_ref) if first else acc_ref[...]
    table = split_table(table_ref[...])
    line = lax.broadcasted_iota(jnp.int32, (rows, LANES), 0)
    for number, source in enumerate(sources):
        prepare_weights(source, number * blocks, species, table, bins, per_tile, weights, tiles)

        def split(n, _, source=source, number=number):
            x = source[:, pl.ds(pl.multiple_of(n * LANES, LANES), LANES)]
            x = jnp.where(line < species, x, jnp.where(line == species, 1.0, 0.0))
            parts[number * blocks + n] = padded_halves(x)
            return 0

        lax.fori_loop(0, blocks, split, 0, unroll=2)

    for copy in copies:
        copy.wait()

    def step(n, _):
        for number in range(lists):
            for g in range(GROUP):
                k = n * GROUP + g
                tile = steps[number, 7, k].astype(jnp.int32)
                block = jnp.minimum(k - tile, blocks - 1) + number * blocks
                wanted = jnp.where(k < pairs, tile, -1).astype(F32)
                mask = jnp.where(tiles[block] == wanted, 1.0, 0.0).astype(BF16)
                mask = jnp.concatenate([mask] * (2 * HALF // mask.shape[0]), axis=0)
                x = parts[block] * mask
                both = jnp.concatenate([x, x], axis=1)
                got = lax.dot_general(both, weights[block], NT, preferred_element_type=F32)
                place = pl.ds(pl.multiple_of(tile * TILE, TILE), TILE)
                out_ref[:, place] += got[:rows] + got[HALF : HALF + rows]
        return 0

    lax.fori_loop(0, -(-pairs // GROUP), step, 0)


def collect_call(sources, table, acc, species, bins, per_tile, ntiles):
    rows, count = sources[0].shape
    lists, blocks = len(sources), count // LANES
    pairs = blocks + ntiles - 1
    args = list(sources) + [table]
    specs = [VMEM] * (lists + 1)
    alias = {}
    if acc is not None:
        alias = {len(args): 0}
        args.append(acc)
        specs.append(VMEM)
    return pl.pallas_call(
        functools.partial(collect_kernel, species, bins, per_tile, pairs, lists, acc is None),
        out_shape=[jax.ShapeDtypeStruct((rows, ntiles * TILE), F32)] + [jax.ShapeDtypeStruct((8, count), F32)] * lists,
        in_specs=specs,
        out_specs=[VMEM] * (lists + 1),
        scratch_shapes=[
            pltpu.VMEM((lists * blocks, TILE, 2 * LANES), BF16),
            pltpu.VMEM((lists * blocks, 16, LANES), F32),
            pltpu.VMEM((lists * blocks, 2 * HALF, LANES), BF16),
            pltpu.SMEM((lists, 8, LANES), F32),
            pltpu.SemaphoreType.DMA((lists,)),
        ],
        input_output_aliases=alias,
        compiler_params=params(19),
        cost_estimate=pl.CostEstimate(flops=lists * pairs * 2 * LANES * TILE * TILE, bytes_accessed=0, transcendentals=0),
        name="collect",
    )(*args)


def project_kernel(bins, per_tile, pairs, lists, *refs):
    means, refs = refs[:3], refs[3:]
    sources, refs = refs[:lists], refs[lists:]
    table_ref, *refs = refs
    outs, (weights, tiles, parts, steps, sems) = refs[:lists], refs[lists:]
    copies = fetch_rows(sources, steps, sems)
    rows, count = outs[0].shape
    blocks = count // LANES
    per_mean = means[0].shape[1] // TILE
    for number, mean in enumerate(means):

        def split(n, _, number=number, mean=mean):
            parts[number * per_mean + n] = padded_halves(mean[:, pl.ds(pl.multiple_of(n * TILE, TILE), TILE)])
            return 0

        lax.fori_loop(0, per_mean, split, 0, unroll=2)
    table = split_table(table_ref[...])
    for copy in copies:
        copy.wait()
    for number in range(lists):
        outs[number][...] = jnp.zeros_like(outs[number])
        prepare_weights(sources[number], number * blocks, 6, table, bins, per_tile, weights, tiles)

    def step(n, _):
        for number in range(lists):
            for g in range(GROUP):
                k = n * GROUP + g
                tile = steps[number, 7, k].astype(jnp.int32)
                local = jnp.minimum(k - tile, blocks - 1)
                block = local + number * blocks
                wanted = jnp.where(k < pairs, tile, -1).astype(F32)
                got = lax.dot_general(parts[tile], weights[block], NN, preferred_element_type=F32)
                got = got[:rows] + got[HALF : HALF + rows]
                got = got[:, :LANES] + got[:, LANES:]
                got = jnp.where(tiles[block][:1] == wanted, got, 0.0)
                place = pl.ds(pl.multiple_of(local * LANES, LANES), LANES)
                outs[number][:, place] += got
        return 0

    lax.fori_loop(0, -(-pairs // GROUP), step, 0)


def project_call(means, sources, table, bins, per_tile, ntiles):
    rows, count = means[0].shape[0], sources[0].shape[1]
    lists = len(sources)
    blocks = count // LANES
    pairs = blocks + ntiles - 1
    return pl.pallas_call(
        functools.partial(project_kernel, bins, per_tile, pairs, lists),
        out_shape=[jax.ShapeDtypeStruct((rows, count), F32)] * lists,
        in_specs=[VMEM] * (lists + 4),
        out_specs=[VMEM] * lists,
        scratch_shapes=[
            pltpu.VMEM((lists * blocks, TILE, 2 * LANES), BF16),
            pltpu.VMEM((lists * blocks, 16, LANES), F32),
            pltpu.VMEM((ntiles, 2 * HALF, TILE), BF16),
            pltpu.SMEM((lists, 8, LANES), F32),
            pltpu.SemaphoreType.DMA((lists,)),
        ],
        compiler_params=params(19),
        cost_estimate=pl.CostEstimate(flops=lists * pairs * 2 * LANES * TILE * TILE, bytes_accessed=0, transcendentals=0),
        name="project",
    )(*means, *sources, table)


def middle_kernel(species, bins, chunk, refs_in, refs_out, scratch):
    acc_ref, old_ref, diss_ref, rate_ref, count_ref, matrix_ref = refs_in
    fresh_ref, next_ref, far_ref = refs_out
    hopped, summed, got, state_ref, edge_out, edge_in, side_in, pick_ref, third_ref, send, recv, side_send, side_recv = scratch
    rows, width = fresh_ref.shape
    steps = width // chunk
    slab, nslab = lax.axis_index("slab"), lax.axis_size("slab")
    cross, ncross = lax.axis_index("cross"), lax.axis_size("cross")
    parity = lax.rem(slab, 2)
    outer = slab + 4 * parity - 2
    inner = slab - 4 * parity + 2
    partner = slab + 1 - 2 * parity
    has_outer = (outer >= 0) & (outer < nslab)
    has_inner = (inner >= 0) & (inner < nslab)
    has_before, has_after = cross > 0, cross < ncross - 1
    has_down, has_up = slab > 0, slab < nslab - 1
    mesh = pl.DeviceIdType.MESH

    @pl.when(jnp.logical_not(has_inner))
    def _():
        hopped[...] = jnp.zeros_like(hopped)

    @pl.when(jnp.logical_not(has_outer))
    def _():
        far_ref[...] = jnp.zeros_like(far_ref)

    @pl.when(jnp.logical_not(has_before))
    def _():
        edge_in[:, :, :LANES] = jnp.zeros(edge_in.shape[:2] + (LANES,), F32)

    @pl.when(jnp.logical_not(has_after))
    def _():
        edge_in[:, :, LANES:] = jnp.zeros(edge_in.shape[:2] + (LANES,), F32)

    @pl.when(jnp.logical_not(has_down))
    def _():
        side_in[0] = jnp.zeros(side_in.shape[1:], F32)

    @pl.when(jnp.logical_not(has_up))
    def _():
        side_in[1] = jnp.zeros(side_in.shape[1:], F32)

    barrier = pltpu.get_barrier_semaphore()
    greet = lambda where: pl.semaphore_signal(barrier, inc=1, device_id=where, device_id_type=mesh)
    pl.when(has_down)(lambda: greet({"slab": slab - 1}))
    pl.when(has_up)(lambda: greet({"slab": slab + 1}))
    pl.when(has_outer)(lambda: greet({"slab": outer}))
    pl.when(has_inner)(lambda: greet({"slab": inner}))
    pl.when(has_before)(lambda: greet({"cross": cross - 1}))
    pl.when(has_after)(lambda: greet({"cross": cross + 1}))
    number = lambda flag: jnp.where(flag, 1, 0)
    flags = (has_down, has_up, has_outer, has_inner, has_before, has_after)
    pl.semaphore_wait(barrier, sum(number(flag) for flag in flags))

    def lanes(c, base=0):
        return pl.ds(pl.multiple_of(base + c * chunk, chunk), chunk)

    def remote(kind, c, source, target, where):
        return pltpu.make_async_remote_copy(
            src_ref=source, dst_ref=target, send_sem=send.at[kind, c], recv_sem=recv.at[kind, c],
            device_id=where, device_id_type=mesh,
        )

    to_outer = lambda c: remote(0, c, acc_ref.at[:, lanes(c)], hopped.at[:, lanes(c)], {"slab": outer})
    to_partner = lambda c: remote(1, c, summed.at[:, lanes(c)], got.at[:, lanes(c)], {"slab": partner})
    to_after = lambda c: remote(2, c, edge_out.at[c, :, LANES:], edge_in.at[c, :, :LANES], {"cross": cross + 1})
    to_before = lambda c: remote(3, c, edge_out.at[c, :, :LANES], edge_in.at[c, :, LANES:], {"cross": cross - 1})
    give = lambda c: remote(4, c, fresh_ref.at[:, lanes(c)], next_ref.at[:, lanes(c)], {"slab": partner})
    pass_on = lambda c: remote(5, c, next_ref.at[:, lanes(c)], far_ref.at[:, lanes(c)], {"slab": inner})

    def side(n, source, where):
        return pltpu.make_async_remote_copy(
            src_ref=source, dst_ref=side_in.at[n], send_sem=side_send.at[n], recv_sem=side_recv.at[n],
            device_id=where, device_id_type=mesh,
        )

    to_up = side(0, old_ref.at[:, width - LANES : width], {"slab": slab + 1})
    to_down = side(1, old_ref.at[:, :LANES], {"slab": slab - 1})

    @pl.when(has_outer)
    def _():
        for c in range(steps):
            to_outer(c).start()

    pl.when(has_up)(to_up.start)
    pl.when(has_down)(to_down.start)

    lane = lax.broadcasted_iota(jnp.int32, (2 * LANES, chunk), 1)
    row = lax.broadcasted_iota(jnp.int32, (2 * LANES, chunk), 0)
    target = jnp.where(row < LANES, row * bins, (row - LANES) * bins + bins - 1)
    pick_ref[...] = rows_equal(target, lane)
    third = matrix_ref.shape[1] // 3
    high, low = halves(matrix_ref[...])
    column = lax.broadcasted_iota(jnp.int32, matrix_ref.shape, 1)
    third_ref[...] = jnp.where(column < 2 * third, high.astype(F32), low.astype(F32)).astype(BF16)
    line = lax.broadcasted_iota(jnp.int32, (rows, chunk), 0)
    slot = lax.broadcasted_iota(jnp.int32, (rows, chunk), 1) % bins
    gap = [jnp.zeros((third - rows, chunk), F32)] * (third > rows)

    def stacked(x):
        high = x.astype(BF16).astype(F32)
        return jnp.concatenate([high, x - high], axis=0).astype(BF16)

    def add_hop(c):
        pl.when(has_inner)(lambda: to_outer(c).wait_recv())
        summed[:, lanes(c)] = acc_ref[:, lanes(c, 2 * width)] + hopped[:, lanes(c)]

    def advect(c):
        here = old_ref[:, lanes(c)]
        start = jnp.maximum(c * chunk - LANES, 0)
        stop = jnp.minimum((c + 1) * chunk, width - LANES)
        low = old_ref[:, pl.ds(pl.multiple_of(start, LANES), LANES)]
        high = old_ref[:, pl.ds(pl.multiple_of(stop, LANES), LANES)]
        low = jnp.where(c == 0, side_in[0], low)
        high = jnp.where(c == steps - 1, side_in[1], high)
        left = pltpu.roll(jnp.concatenate([low, here], axis=1), bins, 1)[:, LANES:]
        right = pltpu.roll(jnp.concatenate([here, high], axis=1), chunk + LANES - bins, 1)[:, :chunk]
        return here - 0.4 * (here - left) + 0.1 * (right - 2.0 * here + left)

    def blend(c):
        total = acc_ref[:, lanes(c, width)] + got[:, lanes(c)]
        blended = (total + advect(c)) / (total[species : species + 1] + 1.0)
        state_ref[:, lanes(c)] = blended
        edge = lax.dot_general(stacked(blended), pick_ref[...], NT, preferred_element_type=F32)
        edge_out[c] = edge[:rows] + edge[rows:]

    def send_edges(c):
        pl.when(has_after)(lambda: to_after(c).start())
        pl.when(has_before)(lambda: to_before(c).start())

    def wait_edges(c):
        pl.when(has_before)(lambda: to_after(c).wait_recv())
        pl.when(has_after)(lambda: to_before(c).wait_recv())

    def react(c):
        here = state_ref[:, lanes(c)]
        around = lax.dot_general(stacked(edge_in[c]), pick_ref[...], NN, preferred_element_type=F32)
        around = around[:rows] + around[rows:]
        before = jnp.where(slot == 0, around, pltpu.roll(here, 1, 1))
        after = jnp.where(slot == bins - 1, around, pltpu.roll(here, chunk - 1, 1))
        state = here + diss_ref[:, lanes(c)] * (after - 2.0 * here + before)
        half = 0.5 * rate_ref[:, lanes(c)]
        count = count_ref[:, lanes(c)]
        for k in range(KMAX):
            high, low = (part.astype(F32) for part in halves(state))
            stack = jnp.concatenate([high, *gap, low, *gap, high, *gap], axis=0).astype(BF16)
            rate = lax.dot_general(third_ref[...], stack, NN, preferred_element_type=F32)
            state = jnp.where(k < count, state + half * jnp.tanh(rate), state)
        fresh_ref[:, lanes(c)] = jnp.where(line == species, 1.0, state)

    def step(t, _):
        def when(lag, body):
            c = t - lag
            pl.when((c >= 0) & (c < steps))(lambda: body(c))

        def second(c):
            pl.when((c == 0) & has_down)(to_up.wait_recv)
            pl.when((c == 0) & has_up)(to_down.wait_recv)
            to_partner(c).wait_recv()
            blend(c)

        def third_stage(c):
            wait_edges(c)
            react(c)

        def fourth(c):
            give(c).wait_recv()
            pl.when(has_inner)(lambda: pass_on(c).start())

        when(0, add_hop)
        when(LAG[0], second)
        when(0, lambda c: to_partner(c).start())
        when(LAG[1], third_stage)
        when(LAG[0], send_edges)
        when(LAG[2], fourth)
        when(LAG[1], lambda c: give(c).start())
        return 0

    lax.fori_loop(0, steps + LAG[2], step, 0)

    def finish(c, _):
        pl.when(has_outer)(lambda: to_outer(c).wait_send())
        to_partner(c).wait_send()
        pl.when(has_after)(lambda: to_after(c).wait_send())
        pl.when(has_before)(lambda: to_before(c).wait_send())
        give(c).wait_send()
        pl.when(has_inner)(lambda: pass_on(c).wait_send())
        pl.when(has_outer)(lambda: pass_on(c).wait_recv())
        return 0

    lax.fori_loop(0, steps, finish, 0)
    pl.when(has_up)(to_up.wait_send)
    pl.when(has_down)(to_down.wait_send)


def middle_call(acc, old, diss, rate, count, matrix, species, bins, chunk=512):
    rows, width = old.shape
    steps = width // chunk

    def kernel(*refs):
        middle_kernel(species, bins, chunk, refs[:6], refs[6:9], refs[9:])

    return pl.pallas_call(
        kernel,
        out_shape=[jax.ShapeDtypeStruct((rows, width), F32)] * 3,
        in_specs=[VMEM] * 6,
        out_specs=[VMEM] * 3,
        scratch_shapes=[pltpu.VMEM((rows, width), F32)] * 4
        + [pltpu.VMEM((steps, rows, 2 * LANES), F32)] * 2
        + [pltpu.VMEM((2, rows, LANES), F32), pltpu.VMEM((2 * LANES, chunk), BF16), pltpu.VMEM(matrix.shape, BF16)]
        + [pltpu.SemaphoreType.DMA((6, steps))] * 2
        + [pltpu.SemaphoreType.DMA((2,))] * 2,
        compiler_params=pltpu.CompilerParams(vmem_limit_bytes=16 << 20, collective_id=1, has_side_effects=True),
        name="middle",
    )(acc, old, diss, rate, count, matrix)


def on_device(
    les_state, cmc_state, cmc_map, pdf_index, pdf_table, diffusion, chem_matrix, dissipation, reaction_rate, substeps
):
    species = les_state.shape[0]
    rows = -(-(species + 2) // 8) * 8
    bins, cells = cmc_state.shape[1:]
    nshape = pdf_table.shape[0]
    ncross = lax.axis_size("cross")
    per_tile = TILE // bins
    ntiles = 3 * cells // per_tile
    width = cells * bins
    flat, rank, steps = head_call(
        les_state, cmc_map, pdf_index, diffusion, rows, cells, nshape, ntiles, nshape * per_tile
    )
    mine = permute_call([flat], rank, steps, False)

    table = lax.dynamic_slice_in_dim(pdf_table.T, lax.axis_index("cross") * bins, bins, axis=0)

    mine, cmc_state, dissipation, reaction_rate, substeps, chem_matrix = lax.optimization_barrier(
        (mine, cmc_state, dissipation, reaction_rate, substeps, chem_matrix)
    )
    bits = [1 << k for k in range(ncross.bit_length() - 1)]
    near_lists, far_lists = [mine], []
    if bits:
        far_lists = [swap(mine, "cross", bits[-1])]
        near_lists += [swap(mine, "cross", bit) for bit in bits[:-1]]

    spread = lambda a: a.transpose(0, 2, 1).reshape(a.shape[0], width)
    wide = lambda a: a.T.reshape(1, width)
    state = spread(jnp.pad(cmc_state, ((0, rows - species), (0, 0), (0, 0))))
    extra = rows - species
    matrix = jnp.tile(jnp.pad(chem_matrix, ((0, extra), (0, -(-rows // 16) * 16 - species))), (1, 3))
    terms = (state, wide(dissipation), wide(reaction_rate), jnp.repeat(substeps, bins)[None, :], matrix)
    acc, *near_keys = collect_call(near_lists, table, None, species, bins, per_tile, ntiles)
    if bits:
        acc, far_lists, terms = lax.optimization_barrier((acc, far_lists, terms))
        far_lists = list(far_lists) + [swap(far_lists[0], "cross", bit) for bit in bits[:-1]]
        acc, *far_keys = collect_call(far_lists, table, acc, species, bins, per_tile, ntiles)
    means = middle_call(acc, *terms, species, bins)
    fresh = means[0]
    means = [means[2], means[0], means[1]]
    cmc_out = fresh[:species].reshape(species, cells, bins).transpose(0, 2, 1)


    def gather(group):
        total = group[0]
        for bit, piece in zip(bits[:-1], group[1:]):
            total = total + swap(piece, "cross", bit)
        return total

    if bits:
        there = gather(project_call(means, far_keys, table, bins, per_tile, ntiles))
        there, means = lax.optimization_barrier((there, means))
        there = swap(there, "cross", bits[-1])
    here = project_call(means, near_keys, table, bins, per_tile, ntiles)
    total = [here[0]] + [swap(piece, "cross", bit) for bit, piece in zip(bits[:-1], here[1:])]
    les_out = permute_call(total + [there] * bool(bits), rank, flat, True)
    return (les_out.reshape(les_state.shape), cmc_out)


def solution(mesh):
    return jax.shard_map(
        on_device,
        mesh=mesh,
        in_specs=(
            P(None, "slab", "cross", None),
            P(None, "cross", "slab"),
            P("slab", "cross", None),
            P("slab", "cross", None),
            P(),
            P(),
            P(),
            P("cross", "slab"),
            P("cross", "slab"),
            P("slab"),
        ),
        out_specs=(P(None, "slab", "cross", None), P(None, "cross", "slab")),
        check_vma=False,
    )
```

```python
import functools


import jax
import jax.numpy as jnp
from jax import lax
from jax.experimental import pallas as pl
from jax.experimental.pallas import tpu as pltpu
from jax.sharding import PartitionSpec as P

KMAX = 4
F32 = jnp.float32
BF16 = jnp.bfloat16
NT = (((1,), (1,)), ((), ()))
NN = (((1,), (0,)), ((), ()))
LANES = 128
TILE = 256
HALF = 64
GROUP = 16
LAG = (2, 4, 6)


def swap(array, axis, bit):
    count = lax.axis_size(axis)
    return lax.ppermute(array, axis, [(i, i ^ bit) for i in range(count)])


def halves(x):
    high = x.astype(BF16)
    return high, (x - high.astype(F32)).astype(BF16)


def padded_halves(x):
    gap = jnp.zeros((HALF - x.shape[0], x.shape[1]), F32)
    high = x.astype(BF16).astype(F32)
    return jnp.concatenate([high, gap, x - high, gap], axis=0).astype(BF16)


def rows_equal(targets, row):
    return jnp.where(targets == row, 1.0, 0.0).astype(BF16)


def whole(shape):
    return pl.BlockSpec(shape, lambda *_: (0,) * len(shape))


VMEM = pl.BlockSpec(memory_space=pltpu.VMEM)
SMEM = pl.BlockSpec(memory_space=pltpu.SMEM)


def params(mib):
    return pltpu.CompilerParams(vmem_limit_bytes=mib << 20)


def fetch_rows(sources, steps, sems):
    copies = []
    for number, source in enumerate(sources):
        last = source.at[source.shape[0] - 8 : source.shape[0], :LANES]
        copies.append(pltpu.make_async_copy(last, steps.at[number], sems.at[number]))
        copies[-1].start()
    return copies


def ranks(tiles, span, key_ref, rank_ref, table_ref):
    count = rank_ref.shape[1]
    ids = lax.broadcasted_iota(jnp.int32, (tiles, TILE), 0).astype(F32)
    tile_of = lambda n: jnp.floor((key_ref[:1, n * TILE : (n + 1) * TILE] + 0.5) * (1.0 / span))
    total = jnp.zeros((tiles, TILE), F32)
    for n in range(count // TILE):
        total = total + jnp.where(ids == tile_of(n), 1.0, 0.0)
    total = jnp.sum(total, axis=1, keepdims=True)
    total = jnp.broadcast_to(total, (tiles, LANES))
    big = jnp.floor(total * (1.0 / HALF))
    row = lax.broadcasted_iota(jnp.int32, (tiles, tiles), 0)
    below = rows_equal(jnp.where(lax.broadcasted_iota(jnp.int32, (tiles, tiles), 1) < row, 1, 0), 1)
    add = lambda part: lax.dot_general(below, part.astype(BF16), NN, preferred_element_type=F32)
    base = add(big) * HALF + add(total - big * HALF)
    order = lax.broadcasted_iota(jnp.int32, (tiles, LANES), 0).astype(F32)
    lane = lax.broadcasted_iota(jnp.int32, (tiles, LANES), 1).astype(F32)
    last = jnp.maximum(jnp.ceil((base + total) * (1.0 / LANES)) - 1.0, 0.0) + order
    passed = jnp.where((last < lane) & (order < tiles - 1), 1.0, 0.0)
    table_ref[...] = jnp.sum(passed, axis=0, keepdims=True)
    ahead = jnp.where(
        lax.broadcasted_iota(jnp.int32, (TILE, TILE), 0) < lax.broadcasted_iota(jnp.int32, (TILE, TILE), 1), 1.0, 0.0
    ).astype(BF16)
    carry = base[:, :1]
    for n in range(count // TILE):
        hot = jnp.where(ids == tile_of(n), 1.0, 0.0)
        before = lax.dot_general(hot.astype(BF16), ahead, NN, preferred_element_type=F32) + carry
        rank_ref[:, n * TILE : (n + 1) * TILE] = jnp.sum(hot * before, axis=0, keepdims=True)
        carry = carry + jnp.sum(hot, axis=1, keepdims=True)


def head_kernel(grid_shape, cells, nshape, tiles, span, *refs):
    given, (t_ref, rank_ref, table_ref), refs = refs[:4], refs[4:7], refs[7:]
    les_ref, map_ref, shape_ref, diff_ref, key_ref, *refs = refs
    faces, halos, (send, recv, load) = refs[:4], refs[4:8], refs[8:]
    loads = [
        pltpu.make_async_copy(source, target, load.at[n])
        for n, (source, target) in enumerate(zip(given, (les_ref, map_ref, shape_ref, diff_ref)))
    ]
    for copy in loads:
        copy.start()
    species, nx, ny = grid_shape
    count = rank_ref.shape[1]
    slab, nslab = lax.axis_index("slab"), lax.axis_size("slab")
    cross, ncross = lax.axis_index("cross"), lax.axis_size("cross")
    mesh = pl.DeviceIdType.MESH
    sides = [
        (slab > 0, {"slab": slab - 1}),
        (slab < nslab - 1, {"slab": slab + 1}),
        (cross > 0, {"cross": cross - 1}),
        (cross < ncross - 1, {"cross": cross + 1}),
    ]
    barrier = pltpu.get_barrier_semaphore()
    for n, (there, where) in enumerate(sides):

        @pl.when(jnp.logical_not(there))
        def _(n=n):
            halos[n][...] = jnp.zeros_like(halos[n])

    for copy in loads:
        copy.wait()
    line = lambda x, y: les_ref[pl.ds(x * ny + y, species, stride=nx * ny), :]
    for n, x in enumerate((0, nx - 1)):
        for y in range(ny):
            faces[n][y, :species] = line(x, y)
    for n, y in enumerate((0, ny - 1)):
        for x in range(nx):
            faces[2 + n][x, :species] = line(x, y)
    for there, where in sides:

        @pl.when(there)
        def _(where=where):
            pl.semaphore_signal(barrier, inc=1, device_id=where, device_id_type=mesh)

    pl.semaphore_wait(barrier, sum(jnp.where(there, 1, 0) for there, _ in sides))
    copies = []
    for n, (there, where) in enumerate(sides):
        copy = pltpu.make_async_remote_copy(
            src_ref=faces[n], dst_ref=halos[n ^ 1], send_sem=send.at[n], recv_sem=recv.at[n ^ 1],
            device_id=where, device_id_type=mesh,
        )
        pl.when(there)(copy.start)
        copies.append(copy)
    offset = map_ref[...] - (slab - 1) * cells
    block = jnp.where(offset >= cells, 1, 0) + jnp.where(offset >= 2 * cells, 1, 0)
    offset = jnp.where(lax.rem(slab, 2) == 1, (2 - block) * cells + offset - block * cells, offset)
    key = (offset * nshape + shape_ref[...]).astype(F32)
    key_ref[:1, :] = key
    t_ref[species:, :] = jnp.concatenate([key] + [jnp.zeros((t_ref.shape[0] - species - 1, count), F32)], axis=0)
    ranks(tiles, span, key_ref, rank_ref, table_ref)
    row = lax.broadcasted_iota(jnp.int32, (species, species), 0)
    number = jnp.where(row == lax.broadcasted_iota(jnp.int32, (species, species), 1), diff_ref[...], 0.0)
    number = jnp.sum(number, axis=1, keepdims=True)
    lane = lax.broadcasted_iota(jnp.int32, (species, LANES), 1)
    for n, (there, _) in enumerate(sides):
        pl.when(sides[n ^ 1][0])(copies[n].wait_recv)
    for x in range(nx):
        for y in range(ny):
            here = line(x, y)
            around = line(x + 1, y) if x < nx - 1 else halos[1][y, :species]
            around = around + (line(x - 1, y) if x else halos[0][y, :species])
            around = around + (line(x, y + 1) if y < ny - 1 else halos[3][x, :species])
            around = around + (line(x, y - 1) if y else halos[2][x, :species])
            around = around + jnp.where(lane < LANES - 1, pltpu.roll(here, LANES - 1, 1), 0.0)
            around = around + jnp.where(lane > 0, pltpu.roll(here, 1, 1), 0.0)
            place = (x * ny + y) * LANES
            t_ref[:species, place : place + LANES] = here + number * (around - 6.0 * here)
    for n, (there, _) in enumerate(sides):
        pl.when(there)(copies[n].wait_send)


def head_call(les_state, cmc_map, pdf_index, diffusion, rows, cells, nshape, tiles, span):
    species, nx, ny, nz = les_state.shape
    count = nx * ny * nz
    halo = [pltpu.VMEM((n, rows, LANES), F32) for n in (ny, ny, nx, nx)]
    return pl.pallas_call(
        functools.partial(head_kernel, (species, nx, ny), cells, nshape, tiles, span),
        out_shape=[
            jax.ShapeDtypeStruct((rows, count), F32),
            jax.ShapeDtypeStruct((1, count), F32),
            jax.ShapeDtypeStruct((1, LANES), F32),
        ],
        in_specs=[pl.BlockSpec(memory_space=pltpu.HBM)] * 4,
        out_specs=[VMEM] * 3,
        scratch_shapes=[
            pltpu.VMEM((species * nx * ny, nz), F32),
            pltpu.VMEM((1, count), jnp.int32),
            pltpu.VMEM((1, count), jnp.int32),
            pltpu.VMEM((1, species), F32),
            pltpu.VMEM((8, count), F32),
        ] + halo * 2 + [pltpu.SemaphoreType.DMA((4,))] * 3,
        compiler_params=pltpu.CompilerParams(vmem_limit_bytes=60 << 20, collective_id=2, has_side_effects=True),
        name="head",
    )(
        les_state.reshape(species * nx * ny, nz), cmc_map.reshape(1, count), pdf_index.reshape(1, count),
        diffusion.reshape(1, species),
    )


def permute_kernel(back, count, rank_ref, *refs):
    xs, (out_ref, parts) = refs[:count], refs[count:]
    xs, extra_ref = xs[:-1], xs[-1]
    rows, count = xs[0].shape
    chunk = 2 * TILE

    @pl.when(pl.program_id(0) == 0)
    def _():
        x = xs[0][...]
        for more in xs[1:]:
            x = x + more[...]
        high = x.astype(BF16).astype(F32)
        parts[...] = jnp.concatenate([high, x - high], axis=0).astype(BF16)

    total = jnp.zeros((2 * rows, TILE), F32)
    here = pl.program_id(0) * TILE
    for n in range(count // chunk):
        piece = slice(n * chunk, (n + 1) * chunk)
        if back:
            ids = lax.broadcasted_iota(jnp.int32, (chunk, TILE), 0) + n * chunk
            hot = rows_equal(ids.astype(F32), rank_ref[:, pl.ds(pl.multiple_of(here, TILE), TILE)])
            total = total + lax.dot_general(parts[:, piece], hot, NN, preferred_element_type=F32)
        else:
            ids = lax.broadcasted_iota(jnp.int32, (TILE, chunk), 0) + here
            hot = rows_equal(ids.astype(F32), rank_ref[:, piece])
            total = total + lax.dot_general(parts[:, piece], hot, NT, preferred_element_type=F32)
    total = total[:rows] + total[rows:]
    if back:
        species = rows - 2
        lines = count // LANES
        for n in range(TILE // LANES):
            piece = total[:, n * LANES : (n + 1) * LANES]
            moved = extra_ref[:species, pl.ds(pl.multiple_of(here + n * LANES, LANES), LANES)]
            piece = piece[:species] / piece[species : species + 1]
            line = pl.program_id(0) * (TILE // LANES) + n
            out_ref[pl.ds(line, species, stride=lines), :] = moved + 0.5 * (piece - moved)
    else:
        line = lax.broadcasted_iota(jnp.int32, (rows, TILE), 0)
        steps = jnp.concatenate([extra_ref[...]] * (TILE // LANES), axis=1)
        out_ref[...] = jnp.where(line == rows - 1, steps, total)


def permute_call(xs, rank, extra, back):
    rows, count = xs[0].shape
    args = list(xs) + [extra]
    lines = (rows - 2) * count // LANES
    out_shape, out_spec = (rows, count), pl.BlockSpec((rows, TILE), lambda i: (0, i))
    if back:
        out_shape, out_spec = (lines, LANES), whole((lines, LANES))
    return pl.pallas_call(
        functools.partial(permute_kernel, back, len(args)),
        grid=(count // TILE,),
        out_shape=jax.ShapeDtypeStruct(out_shape, F32),
        in_specs=[whole(rank.shape)] + [whole(x.shape) for x in args],
        out_specs=out_spec,
        scratch_shapes=[pltpu.VMEM((2 * rows, count), BF16)],
        compiler_params=params(12),
        cost_estimate=pl.CostEstimate(flops=4 * rows * count * count, bytes_accessed=8 * rows * count, transcendentals=0),
        name="unsort" if back else "sort",
    )(rank, *args)


def weights_of(key, table, bins, per_tile):
    nshape = table.shape[1]
    cell = jnp.floor((key + 0.5) * (1.0 / nshape))
    shape = key - cell * nshape
    tile = jnp.floor((cell + 0.5) * (1.0 / per_tile))
    within = cell - tile * per_tile
    ids = lax.broadcasted_iota(jnp.int32, (nshape, key.shape[1]), 0).astype(F32)
    picked = lax.dot_general(table, rows_equal(ids, shape), NN, preferred_element_type=F32).astype(BF16)
    masks = [jnp.where(within == m, 1.0, 0.0).astype(BF16) for m in range(per_tile)]
    columns = []
    for part in (picked[:bins], picked[bins:]):
        columns.append(jnp.concatenate([part * mask for mask in masks], axis=0))
    return jnp.concatenate(columns, axis=1), tile


def split_table(table):
    high = table.astype(BF16).astype(F32)
    return jnp.concatenate([high, table - high], axis=0).astype(BF16)


def prepare_weights(source, index, key_row, table, bins, per_tile, weights, tiles):
    def step(n, _):
        key = source[key_row : key_row + 1, pl.ds(pl.multiple_of(n * LANES, LANES), LANES)]
        block, tile = weights_of(key, table, bins, per_tile)
        weights[index + n] = block
        tiles[index + n] = jnp.broadcast_to(tile, tiles.shape[1:])
        return 0

    lax.fori_loop(0, source.shape[1] // LANES, step, 0, unroll=4)


def collect_kernel(species, bins, per_tile, pairs, lists, *refs):
    sources, refs = refs[:lists], refs[lists:]
    table_ref, out_ref, *refs = refs
    keys, (weights, tiles, parts, steps, sems) = refs[:lists], refs[lists:]
    copies = fetch_rows(sources, steps, sems)
    for key, source in zip(keys, sources):
        key[...] = source[source.shape[0] - 8 :, :]
    rows, count = sources[0].shape
    blocks = count // LANES
    out_ref[...] = jnp.zeros_like(out_ref)
    table = split_table(table_ref[...])
    line = lax.broadcasted_iota(jnp.int32, (rows, LANES), 0)
    for number, source in enumerate(sources):
        prepare_weights(source, number * blocks, species, table, bins, per_tile, weights, tiles)

        def split(n, _, source=source, number=number):
            x = source[:, pl.ds(pl.multiple_of(n * LANES, LANES), LANES)]
            x = jnp.where(line < species, x, jnp.where(line == species, 1.0, 0.0))
            parts[number * blocks + n] = padded_halves(x)
            return 0

        lax.fori_loop(0, blocks, split, 0, unroll=2)

    for copy in copies:
        copy.wait()

    def step(n, _):
        for number in range(lists):
            for g in range(GROUP):
                k = n * GROUP + g
                tile = steps[number, 7, k].astype(jnp.int32)
                block = jnp.minimum(k - tile, blocks - 1) + number * blocks
                wanted = jnp.where(k < pairs, tile, -1).astype(F32)
                mask = jnp.where(tiles[block] == wanted, 1.0, 0.0).astype(BF16)
                mask = jnp.concatenate([mask] * (2 * HALF // mask.shape[0]), axis=0)
                x = parts[block] * mask
                both = jnp.concatenate([x, x], axis=1)
                got = lax.dot_general(both, weights[block], NT, preferred_element_type=F32)
                place = pl.ds(pl.multiple_of(tile * TILE, TILE), TILE)
                out_ref[:, place] += got[:rows] + got[HALF : HALF + rows]
        return 0

    lax.fori_loop(0, -(-pairs // GROUP), step, 0)


def collect_call(sources, table, species, bins, per_tile, ntiles):
    rows, count = sources[0].shape
    lists, blocks = len(sources), count // LANES
    pairs = blocks + ntiles - 1
    args = list(sources) + [table]
    specs = [VMEM] * (lists + 1)
    return pl.pallas_call(
        functools.partial(collect_kernel, species, bins, per_tile, pairs, lists),
        out_shape=[jax.ShapeDtypeStruct((rows, ntiles * TILE), F32)] + [jax.ShapeDtypeStruct((8, count), F32)] * lists,
        in_specs=specs,
        out_specs=[VMEM] * (lists + 1),
        scratch_shapes=[
            pltpu.VMEM((lists * blocks, TILE, 2 * LANES), BF16),
            pltpu.VMEM((lists * blocks, 16, LANES), F32),
            pltpu.VMEM((lists * blocks, 2 * HALF, LANES), BF16),
            pltpu.SMEM((lists, 8, LANES), F32),
            pltpu.SemaphoreType.DMA((lists,)),
        ],
        compiler_params=params(19),
        cost_estimate=pl.CostEstimate(flops=lists * pairs * 2 * LANES * TILE * TILE, bytes_accessed=0, transcendentals=0),
        name="collect",
    )(*args)


def project_kernel(bins, per_tile, pairs, lists, *refs):
    means, refs = refs[:3], refs[3:]
    sources, refs = refs[:lists], refs[lists:]
    table_ref, *refs = refs
    outs, (weights, tiles, parts, steps, sems) = refs[:lists], refs[lists:]
    copies = fetch_rows(sources, steps, sems)
    rows, count = outs[0].shape
    blocks = count // LANES
    per_mean = means[0].shape[1] // TILE
    for number, mean in enumerate(means):

        def split(n, _, number=number, mean=mean):
            parts[number * per_mean + n] = padded_halves(mean[:, pl.ds(pl.multiple_of(n * TILE, TILE), TILE)])
            return 0

        lax.fori_loop(0, per_mean, split, 0, unroll=2)
    table = split_table(table_ref[...])
    for copy in copies:
        copy.wait()
    for number in range(lists):
        outs[number][...] = jnp.zeros_like(outs[number])
        prepare_weights(sources[number], number * blocks, 6, table, bins, per_tile, weights, tiles)

    def step(n, _):
        for number in range(lists):
            for g in range(GROUP):
                k = n * GROUP + g
                tile = steps[number, 7, k].astype(jnp.int32)
                local = jnp.minimum(k - tile, blocks - 1)
                block = local + number * blocks
                wanted = jnp.where(k < pairs, tile, -1).astype(F32)
                got = lax.dot_general(parts[tile], weights[block], NN, preferred_element_type=F32)
                got = got[:rows] + got[HALF : HALF + rows]
                got = got[:, :LANES] + got[:, LANES:]
                got = jnp.where(tiles[block][:1] == wanted, got, 0.0)
                place = pl.ds(pl.multiple_of(local * LANES, LANES), LANES)
                outs[number][:, place] += got
        return 0

    lax.fori_loop(0, -(-pairs // GROUP), step, 0)


def project_call(means, sources, table, bins, per_tile, ntiles):
    rows, count = means[0].shape[0], sources[0].shape[1]
    lists = len(sources)
    blocks = count // LANES
    pairs = blocks + ntiles - 1
    return pl.pallas_call(
        functools.partial(project_kernel, bins, per_tile, pairs, lists),
        out_shape=[jax.ShapeDtypeStruct((rows, count), F32)] * lists,
        in_specs=[VMEM] * (lists + 4),
        out_specs=[VMEM] * lists,
        scratch_shapes=[
            pltpu.VMEM((lists * blocks, TILE, 2 * LANES), BF16),
            pltpu.VMEM((lists * blocks, 16, LANES), F32),
            pltpu.VMEM((ntiles, 2 * HALF, TILE), BF16),
            pltpu.SMEM((lists, 8, LANES), F32),
            pltpu.SemaphoreType.DMA((lists,)),
        ],
        compiler_params=params(19),
        cost_estimate=pl.CostEstimate(flops=lists * pairs * 2 * LANES * TILE * TILE, bytes_accessed=0, transcendentals=0),
        name="project",
    )(*means, *sources, table)


def middle_kernel(species, bins, chunk, refs_in, refs_out, scratch):
    *accs, old_ref, diss_ref, rate_ref, count_ref, matrix_ref = refs_in
    fresh_ref, next_ref, far_ref = refs_out
    outward, hopped, summed, got, state_ref, edge_out, edge_in, side_in, pick_ref, third_ref, send, recv, side_send, side_recv = scratch
    rows, width = fresh_ref.shape
    steps = width // chunk
    slab, nslab = lax.axis_index("slab"), lax.axis_size("slab")
    cross, ncross = lax.axis_index("cross"), lax.axis_size("cross")
    parity = lax.rem(slab, 2)
    outer = slab + 4 * parity - 2
    inner = slab - 4 * parity + 2
    partner = slab + 1 - 2 * parity
    has_outer = (outer >= 0) & (outer < nslab)
    has_inner = (inner >= 0) & (inner < nslab)
    has_before, has_after = cross > 0, cross < ncross - 1
    has_down, has_up = slab > 0, slab < nslab - 1
    mesh = pl.DeviceIdType.MESH

    def partial_sum(piece):
        total = accs[0][:, piece]
        for more in accs[1:]:
            total = total + more[:, piece]
        return total

    outward[...] = partial_sum(slice(0, width))

    @pl.when(jnp.logical_not(has_inner))
    def _():
        hopped[...] = jnp.zeros_like(hopped)

    @pl.when(jnp.logical_not(has_outer))
    def _():
        far_ref[...] = jnp.zeros_like(far_ref)

    @pl.when(jnp.logical_not(has_before))
    def _():
        edge_in[:, :, :LANES] = jnp.zeros(edge_in.shape[:2] + (LANES,), F32)

    @pl.when(jnp.logical_not(has_after))
    def _():
        edge_in[:, :, LANES:] = jnp.zeros(edge_in.shape[:2] + (LANES,), F32)

    @pl.when(jnp.logical_not(has_down))
    def _():
        side_in[0] = jnp.zeros(side_in.shape[1:], F32)

    @pl.when(jnp.logical_not(has_up))
    def _():
        side_in[1] = jnp.zeros(side_in.shape[1:], F32)

    barrier = pltpu.get_barrier_semaphore()
    greet = lambda where: pl.semaphore_signal(barrier, inc=1, device_id=where, device_id_type=mesh)
    pl.when(has_down)(lambda: greet({"slab": slab - 1}))
    pl.when(has_up)(lambda: greet({"slab": slab + 1}))
    pl.when(has_outer)(lambda: greet({"slab": outer}))
    pl.when(has_inner)(lambda: greet({"slab": inner}))
    pl.when(has_before)(lambda: greet({"cross": cross - 1}))
    pl.when(has_after)(lambda: greet({"cross": cross + 1}))
    number = lambda flag: jnp.where(flag, 1, 0)
    flags = (has_down, has_up, has_outer, has_inner, has_before, has_after)
    pl.semaphore_wait(barrier, sum(number(flag) for flag in flags))

    def lanes(c, base=0):
        return pl.ds(pl.multiple_of(base + c * chunk, chunk), chunk)

    def remote(kind, c, source, target, where):
        return pltpu.make_async_remote_copy(
            src_ref=source, dst_ref=target, send_sem=send.at[kind, c], recv_sem=recv.at[kind, c],
            device_id=where, device_id_type=mesh,
        )

    to_outer = lambda c: remote(0, c, outward.at[:, lanes(c)], hopped.at[:, lanes(c)], {"slab": outer})
    to_partner = lambda c: remote(1, c, summed.at[:, lanes(c)], got.at[:, lanes(c)], {"slab": partner})
    to_after = lambda c: remote(2, c, edge_out.at[c, :, LANES:], edge_in.at[c, :, :LANES], {"cross": cross + 1})
    to_before = lambda c: remote(3, c, edge_out.at[c, :, :LANES], edge_in.at[c, :, LANES:], {"cross": cross - 1})
    give = lambda c: remote(4, c, fresh_ref.at[:, lanes(c)], next_ref.at[:, lanes(c)], {"slab": partner})
    pass_on = lambda c: remote(5, c, next_ref.at[:, lanes(c)], far_ref.at[:, lanes(c)], {"slab": inner})

    def side(n, source, where):
        return pltpu.make_async_remote_copy(
            src_ref=source, dst_ref=side_in.at[n], send_sem=side_send.at[n], recv_sem=side_recv.at[n],
            device_id=where, device_id_type=mesh,
        )

    to_up = side(0, old_ref.at[:, width - LANES : width], {"slab": slab + 1})
    to_down = side(1, old_ref.at[:, :LANES], {"slab": slab - 1})

    pl.when(has_up)(to_up.start)
    pl.when(has_down)(to_down.start)

    @pl.when(has_outer)
    def _():
        for c in range(steps):
            to_outer(c).start()

    lane = lax.broadcasted_iota(jnp.int32, (2 * LANES, chunk), 1)
    row = lax.broadcasted_iota(jnp.int32, (2 * LANES, chunk), 0)
    target = jnp.where(row < LANES, row * bins, (row - LANES) * bins + bins - 1)
    pick_ref[...] = rows_equal(target, lane)
    third = matrix_ref.shape[1] // 3
    high, low = halves(matrix_ref[...])
    column = lax.broadcasted_iota(jnp.int32, matrix_ref.shape, 1)
    third_ref[...] = jnp.where(column < 2 * third, high.astype(F32), low.astype(F32)).astype(BF16)
    line = lax.broadcasted_iota(jnp.int32, (rows, chunk), 0)
    slot = lax.broadcasted_iota(jnp.int32, (rows, chunk), 1) % bins
    gap = [jnp.zeros((third - rows, chunk), F32)] * (third > rows)

    def stacked(x):
        high = x.astype(BF16).astype(F32)
        return jnp.concatenate([high, x - high], axis=0).astype(BF16)

    def add_hop(c):
        pl.when(has_inner)(lambda: to_outer(c).wait_recv())
        summed[:, lanes(c)] = partial_sum(lanes(c, 2 * width)) + hopped[:, lanes(c)]

    def advect(c):
        here = old_ref[:, lanes(c)]
        start = jnp.maximum(c * chunk - LANES, 0)
        stop = jnp.minimum((c + 1) * chunk, width - LANES)
        low = old_ref[:, pl.ds(pl.multiple_of(start, LANES), LANES)]
        high = old_ref[:, pl.ds(pl.multiple_of(stop, LANES), LANES)]
        low = jnp.where(c == 0, side_in[0], low)
        high = jnp.where(c == steps - 1, side_in[1], high)
        left = pltpu.roll(jnp.concatenate([low, here], axis=1), bins, 1)[:, LANES:]
        right = pltpu.roll(jnp.concatenate([here, high], axis=1), chunk + LANES - bins, 1)[:, :chunk]
        return here - 0.4 * (here - left) + 0.1 * (right - 2.0 * here + left)

    def blend(c):
        total = partial_sum(lanes(c, width)) + got[:, lanes(c)]
        blended = (total + advect(c)) / (total[species : species + 1] + 1.0)
        state_ref[:, lanes(c)] = blended
        edge = lax.dot_general(stacked(blended), pick_ref[...], NT, preferred_element_type=F32)
        edge_out[c] = edge[:rows] + edge[rows:]

    def send_edges(c):
        pl.when(has_after)(lambda: to_after(c).start())
        pl.when(has_before)(lambda: to_before(c).start())

    def wait_edges(c):
        pl.when(has_before)(lambda: to_after(c).wait_recv())
        pl.when(has_after)(lambda: to_before(c).wait_recv())

    def react(c):
        here = state_ref[:, lanes(c)]
        around = lax.dot_general(stacked(edge_in[c]), pick_ref[...], NN, preferred_element_type=F32)
        around = around[:rows] + around[rows:]
        before = jnp.where(slot == 0, around, pltpu.roll(here, 1, 1))
        after = jnp.where(slot == bins - 1, around, pltpu.roll(here, chunk - 1, 1))
        state = here + diss_ref[:, lanes(c)] * (after - 2.0 * here + before)
        half = 0.5 * rate_ref[:, lanes(c)]
        count = count_ref[:, lanes(c)]
        for k in range(KMAX):
            high, low = (part.astype(F32) for part in halves(state))
            stack = jnp.concatenate([high, *gap, low, *gap, high, *gap], axis=0).astype(BF16)
            rate = lax.dot_general(third_ref[...], stack, NN, preferred_element_type=F32)
            state = jnp.where(k < count, state + half * jnp.tanh(rate), state)
        fresh_ref[:, lanes(c)] = jnp.where(line == species, 1.0, state)

    def step(t, _):
        def when(lag, body):
            c = t - lag
            pl.when((c >= 0) & (c < steps))(lambda: body(c))

        def second(c):
            pl.when((c == 0) & has_down)(to_up.wait_recv)
            pl.when((c == 0) & has_up)(to_down.wait_recv)
            to_partner(c).wait_recv()
            blend(c)

        def third_stage(c):
            wait_edges(c)
            react(c)

        def fourth(c):
            give(c).wait_recv()
            pl.when(has_inner)(lambda: pass_on(c).start())

        when(0, add_hop)
        when(LAG[0], second)
        when(0, lambda c: to_partner(c).start())
        when(LAG[1], third_stage)
        when(LAG[0], send_edges)
        when(LAG[2], fourth)
        when(LAG[1], lambda c: give(c).start())
        return 0

    lax.fori_loop(0, steps + LAG[2], step, 0)

    def finish(c, _):
        pl.when(has_outer)(lambda: to_outer(c).wait_send())
        to_partner(c).wait_send()
        pl.when(has_after)(lambda: to_after(c).wait_send())
        pl.when(has_before)(lambda: to_before(c).wait_send())
        give(c).wait_send()
        pl.when(has_inner)(lambda: pass_on(c).wait_send())
        pl.when(has_outer)(lambda: pass_on(c).wait_recv())
        return 0

    lax.fori_loop(0, steps, finish, 0)
    pl.when(has_up)(to_up.wait_send)
    pl.when(has_down)(to_down.wait_send)


def middle_call(accs, old, diss, rate, count, matrix, species, bins, chunk=512):
    rows, width = old.shape
    steps = width // chunk
    given = len(accs) + 5

    def kernel(*refs):
        middle_kernel(species, bins, chunk, refs[:given], refs[given : given + 3], refs[given + 3 :])

    return pl.pallas_call(
        kernel,
        out_shape=[jax.ShapeDtypeStruct((rows, width), F32)] * 3,
        in_specs=[VMEM] * given,
        out_specs=[VMEM] * 3,
        scratch_shapes=[pltpu.VMEM((rows, width), F32)] * 5
        + [pltpu.VMEM((steps, rows, 2 * LANES), F32)] * 2
        + [pltpu.VMEM((2, rows, LANES), F32), pltpu.VMEM((2 * LANES, chunk), BF16), pltpu.VMEM(matrix.shape, BF16)]
        + [pltpu.SemaphoreType.DMA((6, steps))] * 2
        + [pltpu.SemaphoreType.DMA((2,))] * 2,
        compiler_params=pltpu.CompilerParams(vmem_limit_bytes=20 << 20, collective_id=1, has_side_effects=True),
        name="middle",
    )(*accs, old, diss, rate, count, matrix)


def on_device(
    les_state, cmc_state, cmc_map, pdf_index, pdf_table, diffusion, chem_matrix, dissipation, reaction_rate, substeps
):
    species = les_state.shape[0]
    rows = -(-(species + 2) // 8) * 8
    bins, cells = cmc_state.shape[1:]
    nshape = pdf_table.shape[0]
    ncross = lax.axis_size("cross")
    per_tile = TILE // bins
    ntiles = 3 * cells // per_tile
    width = cells * bins
    flat, rank, steps = head_call(
        les_state, cmc_map, pdf_index, diffusion, rows, cells, nshape, ntiles, nshape * per_tile
    )
    mine = permute_call([flat], rank, steps, False)

    table = lax.dynamic_slice_in_dim(pdf_table.T, lax.axis_index("cross") * bins, bins, axis=0)

    mine, cmc_state, dissipation, reaction_rate, substeps, chem_matrix = lax.optimization_barrier(
        (mine, cmc_state, dissipation, reaction_rate, substeps, chem_matrix)
    )
    bits = [1 << k for k in range(ncross.bit_length() - 1)]
    near_lists, far_lists = [mine], []
    if bits:
        far_lists = [swap(mine, "cross", bits[-1])]
        near_lists += [swap(mine, "cross", bit) for bit in bits[:-1]]

    spread = lambda a: a.transpose(0, 2, 1).reshape(a.shape[0], width)
    wide = lambda a: a.T.reshape(1, width)
    state = spread(jnp.pad(cmc_state, ((0, rows - species), (0, 0), (0, 0))))
    extra = rows - species
    matrix = jnp.tile(jnp.pad(chem_matrix, ((0, extra), (0, -(-rows // 16) * 16 - species))), (1, 3))
    terms = (state, wide(dissipation), wide(reaction_rate), jnp.repeat(substeps, bins)[None, :], matrix)
    acc, *near_keys = collect_call(near_lists, table, species, bins, per_tile, ntiles)
    accs = [acc]
    if bits:
        accs, far_lists, terms = lax.optimization_barrier((accs, far_lists, terms))
        far_lists = list(far_lists) + [swap(far_lists[0], "cross", bit) for bit in bits[:-1]]
        acc, *far_keys = collect_call(far_lists, table, species, bins, per_tile, ntiles)
        accs = list(accs) + [acc]
    means = middle_call(accs, *terms, species, bins)
    fresh = means[0]
    means = [means[2], means[0], means[1]]
    cmc_out = fresh[:species].reshape(species, cells, bins).transpose(0, 2, 1)


    def gather(group):
        total = group[0]
        for bit, piece in zip(bits[:-1], group[1:]):
            total = total + swap(piece, "cross", bit)
        return total

    if bits:
        there = gather(project_call(means, far_keys, table, bins, per_tile, ntiles))
        there, means = lax.optimization_barrier((there, means))
        there = swap(there, "cross", bits[-1])
    here = project_call(means, near_keys, table, bins, per_tile, ntiles)
    total = [here[0]] + [swap(piece, "cross", bit) for bit, piece in zip(bits[:-1], here[1:])]
    les_out = permute_call(total + [there] * bool(bits), rank, flat, True)
    return (les_out.reshape(les_state.shape), cmc_out)


def solution(mesh):
    return jax.shard_map(
        on_device,
        mesh=mesh,
        in_specs=(
            P(None, "slab", "cross", None),
            P(None, "cross", "slab"),
            P("slab", "cross", None),
            P("slab", "cross", None),
            P(),
            P(),
            P(),
            P("cross", "slab"),
            P("cross", "slab"),
            P("slab"),
        ),
        out_specs=(P(None, "slab", "cross", None), P(None, "cross", "slab")),
        check_vma=False,
    )
```

```python
import functools


import jax
import jax.numpy as jnp
from jax import lax
from jax.experimental import pallas as pl
from jax.experimental.pallas import tpu as pltpu
from jax.sharding import PartitionSpec as P

KMAX = 4
F32 = jnp.float32
BF16 = jnp.bfloat16
NT = (((1,), (1,)), ((), ()))
NN = (((1,), (0,)), ((), ()))
LANES = 128
TILE = 256
HALF = 64
GROUP = 16
LAG = (2, 4, 6)


def swap(array, axis, bit):
    count = lax.axis_size(axis)
    return lax.ppermute(array, axis, [(i, i ^ bit) for i in range(count)])


def halves(x):
    high = x.astype(BF16)
    return high, (x - high.astype(F32)).astype(BF16)


def padded_halves(x):
    gap = jnp.zeros((HALF - x.shape[0], x.shape[1]), F32)
    high = x.astype(BF16).astype(F32)
    return jnp.concatenate([high, gap, x - high, gap], axis=0).astype(BF16)


def rows_equal(targets, row):
    return jnp.where(targets == row, 1.0, 0.0).astype(BF16)


def whole(shape):
    return pl.BlockSpec(shape, lambda *_: (0,) * len(shape))


VMEM = pl.BlockSpec(memory_space=pltpu.VMEM)
SMEM = pl.BlockSpec(memory_space=pltpu.SMEM)


def params(mib):
    return pltpu.CompilerParams(vmem_limit_bytes=mib << 20)


def fetch_rows(sources, steps, sems):
    copies = []
    for number, source in enumerate(sources):
        last = source.at[source.shape[0] - 8 : source.shape[0], :LANES]
        copies.append(pltpu.make_async_copy(last, steps.at[number], sems.at[number]))
        copies[-1].start()
    return copies


def ranks(tiles, span, key_ref, rank_ref, table_ref):
    count = rank_ref.shape[1]
    ids = lax.broadcasted_iota(jnp.int32, (tiles, TILE), 0).astype(F32)
    tile_of = lambda n: jnp.floor((key_ref[:1, n * TILE : (n + 1) * TILE] + 0.5) * (1.0 / span))
    total = jnp.zeros((tiles, TILE), F32)
    for n in range(count // TILE):
        total = total + jnp.where(ids == tile_of(n), 1.0, 0.0)
    total = jnp.sum(total, axis=1, keepdims=True)
    total = jnp.broadcast_to(total, (tiles, LANES))
    big = jnp.floor(total * (1.0 / HALF))
    row = lax.broadcasted_iota(jnp.int32, (tiles, tiles), 0)
    below = rows_equal(jnp.where(lax.broadcasted_iota(jnp.int32, (tiles, tiles), 1) < row, 1, 0), 1)
    add = lambda part: lax.dot_general(below, part.astype(BF16), NN, preferred_element_type=F32)
    base = add(big) * HALF + add(total - big * HALF)
    order = lax.broadcasted_iota(jnp.int32, (tiles, LANES), 0).astype(F32)
    lane = lax.broadcasted_iota(jnp.int32, (tiles, LANES), 1).astype(F32)
    last = jnp.maximum(jnp.ceil((base + total) * (1.0 / LANES)) - 1.0, 0.0) + order
    passed = jnp.where((last < lane) & (order < tiles - 1), 1.0, 0.0)
    table_ref[...] = jnp.sum(passed, axis=0, keepdims=True)
    ahead = jnp.where(
        lax.broadcasted_iota(jnp.int32, (TILE, TILE), 0) < lax.broadcasted_iota(jnp.int32, (TILE, TILE), 1), 1.0, 0.0
    ).astype(BF16)
    carry = base[:, :1]
    for n in range(count // TILE):
        hot = jnp.where(ids == tile_of(n), 1.0, 0.0)
        before = lax.dot_general(hot.astype(BF16), ahead, NN, preferred_element_type=F32) + carry
        rank_ref[:, n * TILE : (n + 1) * TILE] = jnp.sum(hot * before, axis=0, keepdims=True)
        carry = carry + jnp.sum(hot, axis=1, keepdims=True)


def head_kernel(grid_shape, cells, nshape, tiles, span, *refs):
    given, (t_ref, rank_ref, table_ref), refs = refs[:4], refs[4:7], refs[7:]
    les_ref, map_ref, shape_ref, diff_ref, key_ref, *refs = refs
    faces, halos, (send, recv, load) = refs[:4], refs[4:8], refs[8:]
    loads = [
        pltpu.make_async_copy(source, target, load.at[n])
        for n, (source, target) in enumerate(zip(given, (les_ref, map_ref, shape_ref, diff_ref)))
    ]
    for copy in loads:
        copy.start()
    species, nx, ny = grid_shape
    count = rank_ref.shape[1]
    slab, nslab = lax.axis_index("slab"), lax.axis_size("slab")
    cross, ncross = lax.axis_index("cross"), lax.axis_size("cross")
    mesh = pl.DeviceIdType.MESH
    sides = [
        (slab > 0, {"slab": slab - 1}),
        (slab < nslab - 1, {"slab": slab + 1}),
        (cross > 0, {"cross": cross - 1}),
        (cross < ncross - 1, {"cross": cross + 1}),
    ]
    barrier = pltpu.get_barrier_semaphore()
    for n, (there, where) in enumerate(sides):

        @pl.when(jnp.logical_not(there))
        def _(n=n):
            halos[n][...] = jnp.zeros_like(halos[n])

    for copy in loads:
        copy.wait()
    line = lambda x, y: les_ref[pl.ds(x * ny + y, species, stride=nx * ny), :]
    for n, x in enumerate((0, nx - 1)):
        for y in range(ny):
            faces[n][y, :species] = line(x, y)
    for n, y in enumerate((0, ny - 1)):
        for x in range(nx):
            faces[2 + n][x, :species] = line(x, y)
    for there, where in sides:

        @pl.when(there)
        def _(where=where):
            pl.semaphore_signal(barrier, inc=1, device_id=where, device_id_type=mesh)

    pl.semaphore_wait(barrier, sum(jnp.where(there, 1, 0) for there, _ in sides))
    copies = []
    for n, (there, where) in enumerate(sides):
        copy = pltpu.make_async_remote_copy(
            src_ref=faces[n], dst_ref=halos[n ^ 1], send_sem=send.at[n], recv_sem=recv.at[n ^ 1],
            device_id=where, device_id_type=mesh,
        )
        pl.when(there)(copy.start)
        copies.append(copy)
    offset = map_ref[...] - (slab - 1) * cells
    block = jnp.where(offset >= cells, 1, 0) + jnp.where(offset >= 2 * cells, 1, 0)
    offset = jnp.where(lax.rem(slab, 2) == 1, (2 - block) * cells + offset - block * cells, offset)
    key = (offset * nshape + shape_ref[...]).astype(F32)
    key_ref[:1, :] = key
    t_ref[species:, :] = jnp.concatenate([key] + [jnp.zeros((t_ref.shape[0] - species - 1, count), F32)], axis=0)
    ranks(tiles, span, key_ref, rank_ref, table_ref)
    row = lax.broadcasted_iota(jnp.int32, (species, species), 0)
    number = jnp.where(row == lax.broadcasted_iota(jnp.int32, (species, species), 1), diff_ref[...], 0.0)
    number = jnp.sum(number, axis=1, keepdims=True)
    lane = lax.broadcasted_iota(jnp.int32, (species, LANES), 1)
    for n, (there, _) in enumerate(sides):
        pl.when(sides[n ^ 1][0])(copies[n].wait_recv)
    for x in range(nx):
        for y in range(ny):
            here = line(x, y)
            around = line(x + 1, y) if x < nx - 1 else halos[1][y, :species]
            around = around + (line(x - 1, y) if x else halos[0][y, :species])
            around = around + (line(x, y + 1) if y < ny - 1 else halos[3][x, :species])
            around = around + (line(x, y - 1) if y else halos[2][x, :species])
            around = around + jnp.where(lane < LANES - 1, pltpu.roll(here, LANES - 1, 1), 0.0)
            around = around + jnp.where(lane > 0, pltpu.roll(here, 1, 1), 0.0)
            place = (x * ny + y) * LANES
            t_ref[:species, place : place + LANES] = here + number * (around - 6.0 * here)
    for n, (there, _) in enumerate(sides):
        pl.when(there)(copies[n].wait_send)


def head_call(les_state, cmc_map, pdf_index, diffusion, rows, cells, nshape, tiles, span):
    species, nx, ny, nz = les_state.shape
    count = nx * ny * nz
    halo = [pltpu.VMEM((n, rows, LANES), F32) for n in (ny, ny, nx, nx)]
    return pl.pallas_call(
        functools.partial(head_kernel, (species, nx, ny), cells, nshape, tiles, span),
        out_shape=[
            jax.ShapeDtypeStruct((rows, count), F32),
            jax.ShapeDtypeStruct((1, count), F32),
            jax.ShapeDtypeStruct((1, LANES), F32),
        ],
        in_specs=[pl.BlockSpec(memory_space=pltpu.HBM)] * 4,
        out_specs=[VMEM] * 3,
        scratch_shapes=[
            pltpu.VMEM((species * nx * ny, nz), F32),
            pltpu.VMEM((1, count), jnp.int32),
            pltpu.VMEM((1, count), jnp.int32),
            pltpu.VMEM((1, species), F32),
            pltpu.VMEM((8, count), F32),
        ] + halo * 2 + [pltpu.SemaphoreType.DMA((4,))] * 3,
        compiler_params=pltpu.CompilerParams(vmem_limit_bytes=60 << 20, collective_id=2, has_side_effects=True),
        name="head",
    )(
        les_state.reshape(species * nx * ny, nz), cmc_map.reshape(1, count), pdf_index.reshape(1, count),
        diffusion.reshape(1, species),
    )


def permute_kernel(back, count, rank_ref, *refs):
    xs, (out_ref, parts) = refs[:count], refs[count:]
    xs, extra_ref = xs[:-1], xs[-1]
    rows, count = xs[0].shape
    chunk = 2 * TILE

    @pl.when(pl.program_id(0) == 0)
    def _():
        x = xs[0][...]
        for more in xs[1:]:
            x = x + more[...]
        high = x.astype(BF16).astype(F32)
        parts[...] = jnp.concatenate([high, x - high], axis=0).astype(BF16)

    total = jnp.zeros((2 * rows, TILE), F32)
    here = pl.program_id(0) * TILE
    for n in range(count // chunk):
        piece = slice(n * chunk, (n + 1) * chunk)
        if back:
            ids = lax.broadcasted_iota(jnp.int32, (chunk, TILE), 0) + n * chunk
            hot = rows_equal(ids.astype(F32), rank_ref[:, pl.ds(pl.multiple_of(here, TILE), TILE)])
            total = total + lax.dot_general(parts[:, piece], hot, NN, preferred_element_type=F32)
        else:
            ids = lax.broadcasted_iota(jnp.int32, (TILE, chunk), 0) + here
            hot = rows_equal(ids.astype(F32), rank_ref[:, piece])
            total = total + lax.dot_general(parts[:, piece], hot, NT, preferred_element_type=F32)
    total = total[:rows] + total[rows:]
    if back:
        species = rows - 2
        lines = count // LANES
        for n in range(TILE // LANES):
            piece = total[:, n * LANES : (n + 1) * LANES]
            moved = extra_ref[:species, pl.ds(pl.multiple_of(here + n * LANES, LANES), LANES)]
            piece = piece[:species] / piece[species : species + 1]
            line = pl.program_id(0) * (TILE // LANES) + n
            out_ref[pl.ds(line, species, stride=lines), :] = moved + 0.5 * (piece - moved)
    else:
        line = lax.broadcasted_iota(jnp.int32, (rows, TILE), 0)
        steps = jnp.concatenate([extra_ref[...]] * (TILE // LANES), axis=1)
        out_ref[...] = jnp.where(line == rows - 1, steps, total)


def permute_call(xs, rank, extra, back):
    rows, count = xs[0].shape
    args = list(xs) + [extra]
    lines = (rows - 2) * count // LANES
    out_shape, out_spec = (rows, count), pl.BlockSpec((rows, TILE), lambda i: (0, i))
    if back:
        out_shape, out_spec = (lines, LANES), whole((lines, LANES))
    return pl.pallas_call(
        functools.partial(permute_kernel, back, len(args)),
        grid=(count // TILE,),
        out_shape=jax.ShapeDtypeStruct(out_shape, F32),
        in_specs=[whole(rank.shape)] + [whole(x.shape) for x in args],
        out_specs=out_spec,
        scratch_shapes=[pltpu.VMEM((2 * rows, count), BF16)],
        compiler_params=params(12),
        cost_estimate=pl.CostEstimate(flops=4 * rows * count * count, bytes_accessed=8 * rows * count, transcendentals=0),
        name="unsort" if back else "sort",
    )(rank, *args)


def weights_of(key, table, bins, per_tile):
    nshape = table.shape[1]
    cell = jnp.floor((key + 0.5) * (1.0 / nshape))
    shape = key - cell * nshape
    tile = jnp.floor((cell + 0.5) * (1.0 / per_tile))
    within = cell - tile * per_tile
    ids = lax.broadcasted_iota(jnp.int32, (nshape, key.shape[1]), 0).astype(F32)
    picked = lax.dot_general(table, rows_equal(ids, shape), NN, preferred_element_type=F32).astype(BF16)
    masks = [jnp.where(within == m, 1.0, 0.0).astype(BF16) for m in range(per_tile)]
    columns = []
    for part in (picked[:bins], picked[bins:]):
        columns.append(jnp.concatenate([part * mask for mask in masks], axis=0))
    return jnp.concatenate(columns, axis=1), tile


def split_table(table):
    high = table.astype(BF16).astype(F32)
    return jnp.concatenate([high, table - high], axis=0).astype(BF16)


def prepare_weights(source, index, key_row, table, bins, per_tile, weights, tiles):
    def step(n, _):
        key = source[key_row : key_row + 1, pl.ds(pl.multiple_of(n * LANES, LANES), LANES)]
        block, tile = weights_of(key, table, bins, per_tile)
        weights[index + n] = block
        tiles[index + n] = jnp.broadcast_to(tile, tiles.shape[1:])
        return 0

    lax.fori_loop(0, source.shape[1] // LANES, step, 0, unroll=4)


def collect_kernel(species, bins, per_tile, pairs, lists, *refs):
    sources, refs = refs[:lists], refs[lists:]
    table_ref, out_ref, *refs = refs
    keys, (weights, tiles, parts, steps, sems) = refs[:lists], refs[lists:]
    copies = fetch_rows(sources, steps, sems)
    for key, source in zip(keys, sources):
        key[...] = source[source.shape[0] - 8 :, :]
    rows, count = sources[0].shape
    blocks = count // LANES
    out_ref[...] = jnp.zeros_like(out_ref)
    table = split_table(table_ref[...])
    line = lax.broadcasted_iota(jnp.int32, (rows, LANES), 0)
    for number, source in enumerate(sources):
        prepare_weights(source, number * blocks, species, table, bins, per_tile, weights, tiles)

        def split(n, _, source=source, number=number):
            x = source[:, pl.ds(pl.multiple_of(n * LANES, LANES), LANES)]
            x = jnp.where(line < species, x, jnp.where(line == species, 1.0, 0.0))
            parts[number * blocks + n] = padded_halves(x)
            return 0

        lax.fori_loop(0, blocks, split, 0, unroll=2)

    for copy in copies:
        copy.wait()

    def step(n, _):
        for number in range(lists):
            for g in range(GROUP):
                k = n * GROUP + g
                tile = steps[number, 7, k].astype(jnp.int32)
                block = jnp.minimum(k - tile, blocks - 1) + number * blocks
                wanted = jnp.where(k < pairs, tile, -1).astype(F32)
                mask = jnp.where(tiles[block] == wanted, 1.0, 0.0).astype(BF16)
                mask = jnp.concatenate([mask] * (2 * HALF // mask.shape[0]), axis=0)
                x = parts[block] * mask
                both = jnp.concatenate([x, x], axis=1)
                got = lax.dot_general(both, weights[block], NT, preferred_element_type=F32)
                place = pl.ds(pl.multiple_of(tile * TILE, TILE), TILE)
                out_ref[:, place] += got[:rows] + got[HALF : HALF + rows]
        return 0

    lax.fori_loop(0, -(-pairs // GROUP), step, 0)


def collect_call(sources, table, species, bins, per_tile, ntiles):
    rows, count = sources[0].shape
    lists, blocks = len(sources), count // LANES
    pairs = blocks + ntiles - 1
    args = list(sources) + [table]
    specs = [VMEM] * (lists + 1)
    return pl.pallas_call(
        functools.partial(collect_kernel, species, bins, per_tile, pairs, lists),
        out_shape=[jax.ShapeDtypeStruct((rows, ntiles * TILE), F32)] + [jax.ShapeDtypeStruct((8, count), F32)] * lists,
        in_specs=specs,
        out_specs=[VMEM] * (lists + 1),
        scratch_shapes=[
            pltpu.VMEM((lists * blocks, TILE, 2 * LANES), BF16),
            pltpu.VMEM((lists * blocks, 16, LANES), F32),
            pltpu.VMEM((lists * blocks, 2 * HALF, LANES), BF16),
            pltpu.SMEM((lists, 8, LANES), F32),
            pltpu.SemaphoreType.DMA((lists,)),
        ],
        compiler_params=params(19),
        cost_estimate=pl.CostEstimate(flops=lists * pairs * 2 * LANES * TILE * TILE, bytes_accessed=0, transcendentals=0),
        name="collect",
    )(*args)


def turn_back(mean, out_ref, bins, quads, turned):
    rows, width = mean.shape
    lines = width // LANES
    fold = LANES // bins
    for q in range(lines):
        quads[pl.ds(q, rows, stride=lines), :] = mean[:, q * LANES : (q + 1) * LANES]
    blocked = lax.broadcasted_iota(jnp.int32, (lines, LANES), 1) // bins

    def turn(g):
        source = [quads[pl.ds(pl.multiple_of(g * LANES + k * lines, lines), lines), :] for k in range(fold)]
        for r in range(fold):
            out = source[r]
            for k in range(fold):
                if k != r:
                    out = jnp.where(blocked == k, pltpu.roll(source[k], (k - r) * bins % LANES, 1), out)
            turned[pl.ds(r, lines, stride=fold), :] = out
        return turned[...].T

    full, rest = out_ref.shape[0] // LANES, out_ref.shape[0] % LANES

    def step(g, _):
        out_ref[pl.ds(pl.multiple_of(g * LANES, LANES), LANES), :] = turn(g)
        return 0

    lax.fori_loop(0, full, step, 0)
    if rest:
        out_ref[full * LANES :, :] = turn(full)[:rest]


def project_kernel(bins, per_tile, pairs, lists, state_rows, *refs):
    means, refs = refs[:3], refs[3:]
    sources, refs = refs[:lists], refs[lists:]
    table_ref, *refs = refs
    outs, refs = refs[:lists], refs[lists:]
    state_ref = refs.pop(0) if state_rows else None
    weights, tiles, parts, steps, sems, *turning = refs
    copies = fetch_rows(sources, steps, sems)
    rows, count = outs[0].shape
    blocks = count // LANES
    per_mean = means[0].shape[1] // TILE
    for number, mean in enumerate(means):

        def split(n, _, number=number, mean=mean):
            parts[number * per_mean + n] = padded_halves(mean[:, pl.ds(pl.multiple_of(n * TILE, TILE), TILE)])
            return 0

        lax.fori_loop(0, per_mean, split, 0, unroll=2)
    if state_rows:
        turn_back(means[1], state_ref, bins, *turning)
    table = split_table(table_ref[...])
    for copy in copies:
        copy.wait()
    for number in range(lists):
        outs[number][...] = jnp.zeros_like(outs[number])
        prepare_weights(sources[number], number * blocks, 6, table, bins, per_tile, weights, tiles)

    def step(n, _):
        for number in range(lists):
            for g in range(GROUP):
                k = n * GROUP + g
                tile = steps[number, 7, k].astype(jnp.int32)
                local = jnp.minimum(k - tile, blocks - 1)
                block = local + number * blocks
                wanted = jnp.where(k < pairs, tile, -1).astype(F32)
                got = lax.dot_general(parts[tile], weights[block], NN, preferred_element_type=F32)
                got = got[:rows] + got[HALF : HALF + rows]
                got = got[:, :LANES] + got[:, LANES:]
                got = jnp.where(tiles[block][:1] == wanted, got, 0.0)
                place = pl.ds(pl.multiple_of(local * LANES, LANES), LANES)
                outs[number][:, place] += got
        return 0

    lax.fori_loop(0, -(-pairs // GROUP), step, 0)


def project_call(means, sources, table, bins, per_tile, ntiles, state_rows=0):
    rows, count = means[0].shape[0], sources[0].shape[1]
    lists = len(sources)
    blocks = count // LANES
    pairs = blocks + ntiles - 1
    return pl.pallas_call(
        functools.partial(project_kernel, bins, per_tile, pairs, lists, state_rows),
        out_shape=[jax.ShapeDtypeStruct((rows, count), F32)] * lists
        + [jax.ShapeDtypeStruct((state_rows, LANES), F32)] * bool(state_rows),
        in_specs=[VMEM] * (lists + 4),
        out_specs=[VMEM] * (lists + bool(state_rows)),
        scratch_shapes=[
            pltpu.VMEM((lists * blocks, TILE, 2 * LANES), BF16),
            pltpu.VMEM((lists * blocks, 16, LANES), F32),
            pltpu.VMEM((ntiles, 2 * HALF, TILE), BF16),
            pltpu.SMEM((lists, 8, LANES), F32),
            pltpu.SemaphoreType.DMA((lists,)),
        ] + [pltpu.VMEM((rows * means[0].shape[1] // LANES, LANES), F32), pltpu.VMEM((LANES, LANES), F32)] * bool(state_rows),
        compiler_params=params(19),
        cost_estimate=pl.CostEstimate(flops=lists * pairs * 2 * LANES * TILE * TILE, bytes_accessed=0, transcendentals=0),
        name="project",
    )(*means, *sources, table)


def middle_kernel(species, bins, chunk, refs_in, refs_out, scratch):
    *accs, cmc_ref, diss_ref, rate_ref, count_ref, matrix_ref = refs_in
    fresh_ref, next_ref, far_ref = refs_out
    nat, quads, turned, side_out, load, outward, hopped, summed, got, state_ref, edge_out, edge_in, side_in, pick_ref, third_ref, send, recv, side_send, side_recv = scratch
    rows, width = fresh_ref.shape
    steps = width // chunk
    slab, nslab = lax.axis_index("slab"), lax.axis_size("slab")
    cross, ncross = lax.axis_index("cross"), lax.axis_size("cross")
    parity = lax.rem(slab, 2)
    outer = slab + 4 * parity - 2
    inner = slab - 4 * parity + 2
    partner = slab + 1 - 2 * parity
    has_outer = (outer >= 0) & (outer < nslab)
    has_inner = (inner >= 0) & (inner < nslab)
    has_before, has_after = cross > 0, cross < ncross - 1
    has_down, has_up = slab > 0, slab < nslab - 1
    mesh = pl.DeviceIdType.MESH

    def partial_sum(piece):
        total = accs[0][:, piece]
        for more in accs[1:]:
            total = total + more[:, piece]
        return total

    loads, start = [], 0
    for n, source in enumerate((cmc_ref, diss_ref, rate_ref)):
        target = nat.at[start : start + source.shape[0]]
        loads.append(pltpu.make_async_copy(source, target, load.at[n]))
        loads[-1].start()
        start += source.shape[0]
    if start < nat.shape[0]:
        nat[start:, :] = jnp.zeros((nat.shape[0] - start, LANES), F32)
    outward[...] = partial_sum(slice(0, width))

    @pl.when(jnp.logical_not(has_inner))
    def _():
        hopped[...] = jnp.zeros_like(hopped)

    @pl.when(jnp.logical_not(has_outer))
    def _():
        far_ref[...] = jnp.zeros_like(far_ref)

    @pl.when(jnp.logical_not(has_before))
    def _():
        edge_in[:, :, :LANES] = jnp.zeros(edge_in.shape[:2] + (LANES,), F32)

    @pl.when(jnp.logical_not(has_after))
    def _():
        edge_in[:, :, LANES:] = jnp.zeros(edge_in.shape[:2] + (LANES,), F32)

    @pl.when(jnp.logical_not(has_down))
    def _():
        side_in[0] = jnp.zeros(side_in.shape[1:], F32)

    @pl.when(jnp.logical_not(has_up))
    def _():
        side_in[1] = jnp.zeros(side_in.shape[1:], F32)

    barrier = pltpu.get_barrier_semaphore()
    greet = lambda where: pl.semaphore_signal(barrier, inc=1, device_id=where, device_id_type=mesh)
    pl.when(has_down)(lambda: greet({"slab": slab - 1}))
    pl.when(has_up)(lambda: greet({"slab": slab + 1}))
    pl.when(has_outer)(lambda: greet({"slab": outer}))
    pl.when(has_inner)(lambda: greet({"slab": inner}))
    pl.when(has_before)(lambda: greet({"cross": cross - 1}))
    pl.when(has_after)(lambda: greet({"cross": cross + 1}))
    number = lambda flag: jnp.where(flag, 1, 0)
    flags = (has_down, has_up, has_outer, has_inner, has_before, has_after)
    pl.semaphore_wait(barrier, sum(number(flag) for flag in flags))

    def lanes(c, base=0):
        return pl.ds(pl.multiple_of(base + c * chunk, chunk), chunk)

    def remote(kind, c, source, target, where):
        return pltpu.make_async_remote_copy(
            src_ref=source, dst_ref=target, send_sem=send.at[kind, c], recv_sem=recv.at[kind, c],
            device_id=where, device_id_type=mesh,
        )

    to_outer = lambda c: remote(0, c, outward.at[:, lanes(c)], hopped.at[:, lanes(c)], {"slab": outer})
    to_partner = lambda c: remote(1, c, summed.at[:, lanes(c)], got.at[:, lanes(c)], {"slab": partner})
    to_after = lambda c: remote(2, c, edge_out.at[c, :, LANES:], edge_in.at[c, :, :LANES], {"cross": cross + 1})
    to_before = lambda c: remote(3, c, edge_out.at[c, :, :LANES], edge_in.at[c, :, LANES:], {"cross": cross - 1})
    give = lambda c: remote(4, c, fresh_ref.at[:, lanes(c)], next_ref.at[:, lanes(c)], {"slab": partner})
    pass_on = lambda c: remote(5, c, next_ref.at[:, lanes(c)], far_ref.at[:, lanes(c)], {"slab": inner})

    def side(n, source, where):
        return pltpu.make_async_remote_copy(
            src_ref=source, dst_ref=side_in.at[n], send_sem=side_send.at[n], recv_sem=side_recv.at[n],
            device_id=where, device_id_type=mesh,
        )

    to_up = side(0, side_out.at[0], {"slab": slab + 1})
    to_down = side(1, side_out.at[1], {"slab": slab - 1})

    def start_hops(chunks):
        @pl.when(has_outer)
        def _():
            for c in chunks:
                to_outer(c).start()

    start_hops(range(2))
    for copy in loads:
        copy.wait()
    lines = width // LANES
    fold = LANES // bins
    blocked = lax.broadcasted_iota(jnp.int32, (LANES // fold, LANES), 1) // bins

    def turn(g, _):
        turned[...] = nat[pl.ds(pl.multiple_of(g * LANES, LANES), LANES), :].T
        parts = [turned[pl.ds(r, LANES // fold, stride=fold), :] for r in range(fold)]
        for k in range(fold):
            out = parts[k]
            for r in range(fold):
                if r != k:
                    out = jnp.where(blocked == r, pltpu.roll(parts[r], (r - k) * bins % LANES, 1), out)
            place = pl.multiple_of(g * LANES + k * lines, lines)
            quads[pl.ds(place, lines), :] = out
        return 0

    lax.fori_loop(0, nat.shape[0] // LANES, turn, 0)
    tile = lambda q: quads[pl.ds(q, rows, stride=lines), :]
    side_out[0] = tile(lines - 1)
    side_out[1] = tile(0)

    lane = lax.broadcasted_iota(jnp.int32, (2 * LANES, chunk), 1)
    row = lax.broadcasted_iota(jnp.int32, (2 * LANES, chunk), 0)
    target = jnp.where(row < LANES, row * bins, (row - LANES) * bins + bins - 1)
    pick_ref[...] = rows_equal(target, lane)
    third = matrix_ref.shape[1] // 3
    high, low = halves(matrix_ref[...])
    column = lax.broadcasted_iota(jnp.int32, matrix_ref.shape, 1)
    third_ref[...] = jnp.where(column < 2 * third, high.astype(F32), low.astype(F32)).astype(BF16)
    line = lax.broadcasted_iota(jnp.int32, (rows, chunk), 0)
    slot = lax.broadcasted_iota(jnp.int32, (rows, chunk), 1) % bins
    gap = [jnp.zeros((third - rows, chunk), F32)] * (third > rows)

    pl.when(has_up)(to_up.start)
    pl.when(has_down)(to_down.start)
    start_hops(range(2, steps))

    def stacked(x):
        high = x.astype(BF16).astype(F32)
        return jnp.concatenate([high, x - high], axis=0).astype(BF16)

    def add_hop(c):
        pl.when(has_inner)(lambda: to_outer(c).wait_recv())
        summed[:, lanes(c)] = partial_sum(lanes(c, 2 * width)) + hopped[:, lanes(c)]

    per = chunk // LANES

    def advect(c):
        here = jnp.concatenate([tile(c * per + n) for n in range(per)], axis=1)
        low = jnp.where(c == 0, side_in[0], tile(jnp.maximum(c * per - 1, 0)))
        high = jnp.where(c == steps - 1, side_in[1], tile(jnp.minimum((c + 1) * per, lines - 1)))
        left = pltpu.roll(jnp.concatenate([low, here], axis=1), bins, 1)[:, LANES:]
        right = pltpu.roll(jnp.concatenate([here, high], axis=1), chunk + LANES - bins, 1)[:, :chunk]
        return here - 0.4 * (here - left) + 0.1 * (right - 2.0 * here + left)

    def cell_row(n, c):
        start = (species + n) * lines + c * per
        return jnp.concatenate([quads[pl.ds(start + k, 1), :] for k in range(per)], axis=1)

    def blend(c):
        total = partial_sum(lanes(c, width)) + got[:, lanes(c)]
        blended = (total + advect(c)) / (total[species : species + 1] + 1.0)
        state_ref[:, lanes(c)] = blended
        edge = lax.dot_general(stacked(blended), pick_ref[...], NT, preferred_element_type=F32)
        edge_out[c] = edge[:rows] + edge[rows:]

    def send_edges(c):
        pl.when(has_after)(lambda: to_after(c).start())
        pl.when(has_before)(lambda: to_before(c).start())

    def wait_edges(c):
        pl.when(has_before)(lambda: to_after(c).wait_recv())
        pl.when(has_after)(lambda: to_before(c).wait_recv())

    def react(c):
        here = state_ref[:, lanes(c)]
        around = lax.dot_general(stacked(edge_in[c]), pick_ref[...], NN, preferred_element_type=F32)
        around = around[:rows] + around[rows:]
        before = jnp.where(slot == 0, around, pltpu.roll(here, 1, 1))
        after = jnp.where(slot == bins - 1, around, pltpu.roll(here, chunk - 1, 1))
        state = here + cell_row(0, c) * (after - 2.0 * here + before)
        half = 0.5 * cell_row(1, c)
        count = count_ref[:, lanes(c)]
        for k in range(KMAX):
            high, low = (part.astype(F32) for part in halves(state))
            stack = jnp.concatenate([high, *gap, low, *gap, high, *gap], axis=0).astype(BF16)
            rate = lax.dot_general(third_ref[...], stack, NN, preferred_element_type=F32)
            state = jnp.where(k < count, state + half * jnp.tanh(rate), state)
        fresh_ref[:, lanes(c)] = jnp.where(line == species, 1.0, state)

    def step(t, _):
        def when(lag, body):
            c = t - lag
            pl.when((c >= 0) & (c < steps))(lambda: body(c))

        def second(c):
            pl.when((c == 0) & has_down)(to_up.wait_recv)
            pl.when((c == 0) & has_up)(to_down.wait_recv)
            to_partner(c).wait_recv()
            blend(c)

        def third_stage(c):
            wait_edges(c)
            react(c)

        def fourth(c):
            give(c).wait_recv()
            pl.when(has_inner)(lambda: pass_on(c).start())

        when(0, add_hop)
        when(LAG[0], second)
        when(0, lambda c: to_partner(c).start())
        when(LAG[1], third_stage)
        when(LAG[0], send_edges)
        when(LAG[2], fourth)
        when(LAG[1], lambda c: give(c).start())
        return 0

    lax.fori_loop(0, steps + LAG[2], step, 0)

    def finish(c, _):
        pl.when(has_outer)(lambda: to_outer(c).wait_send())
        to_partner(c).wait_send()
        pl.when(has_after)(lambda: to_after(c).wait_send())
        pl.when(has_before)(lambda: to_before(c).wait_send())
        give(c).wait_send()
        pl.when(has_inner)(lambda: pass_on(c).wait_send())
        pl.when(has_outer)(lambda: pass_on(c).wait_recv())
        return 0

    lax.fori_loop(0, steps, finish, 0)
    pl.when(has_up)(to_up.wait_send)
    pl.when(has_down)(to_down.wait_send)


def middle_call(accs, cmc, diss, rate, count, matrix, species, bins, chunk=512):
    rows, width = accs[0].shape[0], count.shape[1]
    steps = width // chunk
    given = len(accs) + 5

    def kernel(*refs):
        middle_kernel(species, bins, chunk, refs[:given], refs[given : given + 3], refs[given + 3 :])

    return pl.pallas_call(
        kernel,
        out_shape=[jax.ShapeDtypeStruct((rows, width), F32)] * 3,
        in_specs=[VMEM] * len(accs) + [pl.BlockSpec(memory_space=pl.ANY)] * 3 + [VMEM] * 2,
        out_specs=[VMEM] * 3,
        scratch_shapes=[pltpu.VMEM((rows * bins, LANES), F32), pltpu.VMEM((rows * width // LANES, LANES), F32)]
        + [pltpu.VMEM((LANES, LANES), F32), pltpu.VMEM((2, rows, LANES), F32), pltpu.SemaphoreType.DMA((3,))]
        + [pltpu.VMEM((rows, width), F32)] * 5
        + [pltpu.VMEM((steps, rows, 2 * LANES), F32)] * 2
        + [pltpu.VMEM((2, rows, LANES), F32), pltpu.VMEM((2 * LANES, chunk), BF16), pltpu.VMEM(matrix.shape, BF16)]
        + [pltpu.SemaphoreType.DMA((6, steps))] * 2
        + [pltpu.SemaphoreType.DMA((2,))] * 2,
        compiler_params=pltpu.CompilerParams(vmem_limit_bytes=20 << 20, collective_id=1, has_side_effects=True),
        name="middle",
    )(*accs, cmc, diss, rate, count, matrix)


def on_device(
    les_state, cmc_state, cmc_map, pdf_index, pdf_table, diffusion, chem_matrix, dissipation, reaction_rate, substeps
):
    species = les_state.shape[0]
    rows = -(-(species + 2) // 8) * 8
    bins, cells = cmc_state.shape[1:]
    nshape = pdf_table.shape[0]
    ncross = lax.axis_size("cross")
    per_tile = TILE // bins
    ntiles = 3 * cells // per_tile
    flat, rank, steps = head_call(
        les_state, cmc_map, pdf_index, diffusion, rows, cells, nshape, ntiles, nshape * per_tile
    )
    mine = permute_call([flat], rank, steps, False)

    table = lax.dynamic_slice_in_dim(pdf_table.T, lax.axis_index("cross") * bins, bins, axis=0)

    mine, cmc_state, dissipation, reaction_rate, substeps, chem_matrix = lax.optimization_barrier(
        (mine, cmc_state, dissipation, reaction_rate, substeps, chem_matrix)
    )
    bits = [1 << k for k in range(ncross.bit_length() - 1)]
    near_lists, far_lists = [mine], []
    if bits:
        far_lists = [swap(mine, "cross", bits[-1])]
        near_lists += [swap(mine, "cross", bit) for bit in bits[:-1]]

    extra = rows - species
    matrix = jnp.tile(jnp.pad(chem_matrix, ((0, extra), (0, -(-rows // 16) * 16 - species))), (1, 3))
    terms = (cmc_state.reshape(species * bins, cells), dissipation, reaction_rate, jnp.repeat(substeps, bins)[None, :], matrix)
    acc, *near_keys = collect_call(near_lists, table, species, bins, per_tile, ntiles)
    accs = [acc]
    if bits:
        accs, far_lists, terms = lax.optimization_barrier((accs, far_lists, terms))
        far_lists = list(far_lists) + [swap(far_lists[0], "cross", bit) for bit in bits[:-1]]
        acc, *far_keys = collect_call(far_lists, table, species, bins, per_tile, ntiles)
        accs = list(accs) + [acc]
    means = middle_call(accs, *terms, species, bins)
    means = [means[2], means[0], means[1]]

    def gather(group):
        total = group[0]
        for bit, piece in zip(bits[:-1], group[1:]):
            total = total + swap(piece, "cross", bit)
        return total

    if bits:
        there = gather(project_call(means, far_keys, table, bins, per_tile, ntiles))
        there, means = lax.optimization_barrier((there, means))
        there = swap(there, "cross", bits[-1])
    *here, cmc_out = project_call(means, near_keys, table, bins, per_tile, ntiles, species * bins)
    total = [here[0]] + [swap(piece, "cross", bit) for bit, piece in zip(bits[:-1], here[1:])]
    les_out = permute_call(total + [there] * bool(bits), rank, flat, True)
    return (les_out.reshape(les_state.shape), cmc_out.reshape(species, bins, cells))


def solution(mesh):
    return jax.shard_map(
        on_device,
        mesh=mesh,
        in_specs=(
            P(None, "slab", "cross", None),
            P(None, "cross", "slab"),
            P("slab", "cross", None),
            P("slab", "cross", None),
            P(),
            P(),
            P(),
            P("cross", "slab"),
            P("cross", "slab"),
            P("slab"),
        ),
        out_specs=(P(None, "slab", "cross", None), P(None, "cross", "slab")),
        check_vma=False,
    )
```

```python
import functools


import jax
import jax.numpy as jnp
from jax import lax
from jax.experimental import pallas as pl
from jax.experimental.pallas import tpu as pltpu
from jax.sharding import PartitionSpec as P

KMAX = 4
F32 = jnp.float32
BF16 = jnp.bfloat16
NT = (((1,), (1,)), ((), ()))
NN = (((1,), (0,)), ((), ()))
LANES = 128
TILE = 256
HALF = 64
GROUP = 16
LAG = (2, 4, 6)


def swap(array, axis, bit):
    count = lax.axis_size(axis)
    return lax.ppermute(array, axis, [(i, i ^ bit) for i in range(count)])


def halves(x):
    high = x.astype(BF16)
    return high, (x - high.astype(F32)).astype(BF16)


def padded_halves(x):
    gap = jnp.zeros((HALF - x.shape[0], x.shape[1]), F32)
    high = x.astype(BF16).astype(F32)
    return jnp.concatenate([high, gap, x - high, gap], axis=0).astype(BF16)


def rows_equal(targets, row):
    return jnp.where(targets == row, 1.0, 0.0).astype(BF16)


def whole(shape):
    return pl.BlockSpec(shape, lambda *_: (0,) * len(shape))


VMEM = pl.BlockSpec(memory_space=pltpu.VMEM)
SMEM = pl.BlockSpec(memory_space=pltpu.SMEM)


def params(mib):
    return pltpu.CompilerParams(vmem_limit_bytes=mib << 20)


def fetch_rows(sources, steps, sems):
    copies = []
    for number, source in enumerate(sources):
        last = source.at[source.shape[0] - 8 : source.shape[0], :LANES]
        copies.append(pltpu.make_async_copy(last, steps.at[number], sems.at[number]))
        copies[-1].start()
    return copies


def ranks(tiles, span, key_ref, rank_ref, table_ref):
    count = rank_ref.shape[1]
    ids = lax.broadcasted_iota(jnp.int32, (tiles, TILE), 0).astype(F32)
    tile_of = lambda n: jnp.floor((key_ref[:1, n * TILE : (n + 1) * TILE] + 0.5) * (1.0 / span))
    total = jnp.zeros((tiles, TILE), F32)
    for n in range(count // TILE):
        total = total + jnp.where(ids == tile_of(n), 1.0, 0.0)
    total = jnp.sum(total, axis=1, keepdims=True)
    total = jnp.broadcast_to(total, (tiles, LANES))
    big = jnp.floor(total * (1.0 / HALF))
    row = lax.broadcasted_iota(jnp.int32, (tiles, tiles), 0)
    below = rows_equal(jnp.where(lax.broadcasted_iota(jnp.int32, (tiles, tiles), 1) < row, 1, 0), 1)
    add = lambda part: lax.dot_general(below, part.astype(BF16), NN, preferred_element_type=F32)
    base = add(big) * HALF + add(total - big * HALF)
    order = lax.broadcasted_iota(jnp.int32, (tiles, LANES), 0).astype(F32)
    lane = lax.broadcasted_iota(jnp.int32, (tiles, LANES), 1).astype(F32)
    last = jnp.maximum(jnp.ceil((base + total) * (1.0 / LANES)) - 1.0, 0.0) + order
    passed = jnp.where((last < lane) & (order < tiles - 1), 1.0, 0.0)
    table_ref[...] = jnp.sum(passed, axis=0, keepdims=True)
    ahead = jnp.where(
        lax.broadcasted_iota(jnp.int32, (TILE, TILE), 0) < lax.broadcasted_iota(jnp.int32, (TILE, TILE), 1), 1.0, 0.0
    ).astype(BF16)
    carry = base[:, :1]
    for n in range(count // TILE):
        hot = jnp.where(ids == tile_of(n), 1.0, 0.0)
        before = lax.dot_general(hot.astype(BF16), ahead, NN, preferred_element_type=F32) + carry
        rank_ref[:, n * TILE : (n + 1) * TILE] = jnp.sum(hot * before, axis=0, keepdims=True)
        carry = carry + jnp.sum(hot, axis=1, keepdims=True)


def head_kernel(grid_shape, cells, nshape, tiles, span, *refs):
    given, (t_ref, rank_ref, parts_ref, half_ref), refs = refs[:4], refs[4:8], refs[8:]
    les_ref, map_ref, shape_ref, diff_ref, key_ref, table_ref, *refs = refs
    faces, halos, (send, recv, load) = refs[:4], refs[4:8], refs[8:]
    loads = [
        pltpu.make_async_copy(source, target, load.at[n])
        for n, (source, target) in enumerate(zip(given, (les_ref, map_ref, shape_ref, diff_ref)))
    ]
    for copy in loads:
        copy.start()
    species, nx, ny = grid_shape
    count = rank_ref.shape[1]
    slab, nslab = lax.axis_index("slab"), lax.axis_size("slab")
    cross, ncross = lax.axis_index("cross"), lax.axis_size("cross")
    mesh = pl.DeviceIdType.MESH
    sides = [
        (slab > 0, {"slab": slab - 1}),
        (slab < nslab - 1, {"slab": slab + 1}),
        (cross > 0, {"cross": cross - 1}),
        (cross < ncross - 1, {"cross": cross + 1}),
    ]
    barrier = pltpu.get_barrier_semaphore()
    for n, (there, where) in enumerate(sides):

        @pl.when(jnp.logical_not(there))
        def _(n=n):
            halos[n][...] = jnp.zeros_like(halos[n])

    for copy in loads:
        copy.wait()
    line = lambda x, y: les_ref[pl.ds(x * ny + y, species, stride=nx * ny), :]
    for n, x in enumerate((0, nx - 1)):
        for y in range(ny):
            faces[n][y, :species] = line(x, y)
    for n, y in enumerate((0, ny - 1)):
        for x in range(nx):
            faces[2 + n][x, :species] = line(x, y)
    for there, where in sides:

        @pl.when(there)
        def _(where=where):
            pl.semaphore_signal(barrier, inc=1, device_id=where, device_id_type=mesh)

    pl.semaphore_wait(barrier, sum(jnp.where(there, 1, 0) for there, _ in sides))
    copies = []
    for n, (there, where) in enumerate(sides):
        copy = pltpu.make_async_remote_copy(
            src_ref=faces[n], dst_ref=halos[n ^ 1], send_sem=send.at[n], recv_sem=recv.at[n ^ 1],
            device_id=where, device_id_type=mesh,
        )
        pl.when(there)(copy.start)
        copies.append(copy)
    offset = map_ref[...] - (slab - 1) * cells
    block = jnp.where(offset >= cells, 1, 0) + jnp.where(offset >= 2 * cells, 1, 0)
    offset = jnp.where(lax.rem(slab, 2) == 1, (2 - block) * cells + offset - block * cells, offset)
    key = (offset * nshape + shape_ref[...]).astype(F32)
    key_ref[:1, :] = key
    t_ref[species:, :] = jnp.concatenate([key] + [jnp.zeros((t_ref.shape[0] - species - 1, count), F32)], axis=0)
    ranks(tiles, span, key_ref, rank_ref, table_ref)
    row = lax.broadcasted_iota(jnp.int32, (species, species), 0)
    number = jnp.where(row == lax.broadcasted_iota(jnp.int32, (species, species), 1), diff_ref[...], 0.0)
    number = jnp.sum(number, axis=1, keepdims=True)
    lane = lax.broadcasted_iota(jnp.int32, (species, LANES), 1)
    for n, (there, _) in enumerate(sides):
        pl.when(sides[n ^ 1][0])(copies[n].wait_recv)
    for x in range(nx):
        for y in range(ny):
            here = line(x, y)
            around = line(x + 1, y) if x < nx - 1 else halos[1][y, :species]
            around = around + (line(x - 1, y) if x else halos[0][y, :species])
            around = around + (line(x, y + 1) if y < ny - 1 else halos[3][x, :species])
            around = around + (line(x, y - 1) if y else halos[2][x, :species])
            around = around + jnp.where(lane < LANES - 1, pltpu.roll(here, LANES - 1, 1), 0.0)
            around = around + jnp.where(lane > 0, pltpu.roll(here, 1, 1), 0.0)
            place = (x * ny + y) * LANES
            t_ref[:species, place : place + LANES] = here + number * (around - 6.0 * here)
    x = t_ref[...]
    high = x.astype(BF16).astype(F32)
    parts_ref[...] = jnp.concatenate([high, x - high], axis=0).astype(BF16)
    sort_tiles(parts_ref, rank_ref, table_ref[...], half_ref, 0)
    for n, (there, _) in enumerate(sides):
        pl.when(there)(copies[n].wait_send)


def head_call(les_state, cmc_map, pdf_index, diffusion, rows, cells, nshape, tiles, span):
    species, nx, ny, nz = les_state.shape
    count = nx * ny * nz
    halo = [pltpu.VMEM((n, rows, LANES), F32) for n in (ny, ny, nx, nx)]
    return pl.pallas_call(
        functools.partial(head_kernel, (species, nx, ny), cells, nshape, tiles, span),
        out_shape=[
            jax.ShapeDtypeStruct((rows, count), F32),
            jax.ShapeDtypeStruct((1, count), F32),
            jax.ShapeDtypeStruct((2 * rows, count), BF16),
            jax.ShapeDtypeStruct((rows, count // 2), F32),
        ],
        in_specs=[pl.BlockSpec(memory_space=pltpu.HBM)] * 4,
        out_specs=[VMEM] * 4,
        scratch_shapes=[
            pltpu.VMEM((species * nx * ny, nz), F32),
            pltpu.VMEM((1, count), jnp.int32),
            pltpu.VMEM((1, count), jnp.int32),
            pltpu.VMEM((1, species), F32),
            pltpu.VMEM((8, count), F32),
            pltpu.VMEM((1, LANES), F32),
        ] + halo * 2 + [pltpu.SemaphoreType.DMA((4,))] * 3,
        compiler_params=pltpu.CompilerParams(vmem_limit_bytes=60 << 20, collective_id=2, has_side_effects=True),
        name="head",
    )(
        les_state.reshape(species * nx * ny, nz), cmc_map.reshape(1, count), pdf_index.reshape(1, count),
        diffusion.reshape(1, species),
    )


CHUNK = 2 * TILE


def sort_tiles(parts, rank_ref, steps, out_ref, first):
    rows = out_ref.shape[0]
    count = rank_ref.shape[1]

    def step(n, _):
        here = (first + n) * TILE
        total = jnp.zeros((2 * rows, TILE), F32)
        for k in range(count // CHUNK):
            piece = slice(k * CHUNK, (k + 1) * CHUNK)
            ids = lax.broadcasted_iota(jnp.int32, (TILE, CHUNK), 0) + here
            hot = rows_equal(ids.astype(F32), rank_ref[:, piece])
            total = total + lax.dot_general(parts[:, piece], hot, NT, preferred_element_type=F32)
        total = total[:rows] + total[rows:]
        if steps is not None:
            line = lax.broadcasted_iota(jnp.int32, (rows, TILE), 0)
            total = jnp.where(line == rows - 1, jnp.concatenate([steps] * (TILE // LANES), axis=1), total)
        out_ref[:, pl.ds(pl.multiple_of(n * TILE, TILE), TILE)] = total
        return 0

    lax.fori_loop(0, out_ref.shape[1] // TILE, step, 0)


def sort_kernel(parts_ref, rank_ref, out_ref):
    sort_tiles(parts_ref, rank_ref, None, out_ref, out_ref.shape[1] // TILE)


def sort_call(parts, rank):
    rows, count = parts.shape[0] // 2, parts.shape[1]
    return pl.pallas_call(
        sort_kernel,
        out_shape=jax.ShapeDtypeStruct((rows, count // 2), F32),
        in_specs=[VMEM] * 2,
        out_specs=VMEM,
        compiler_params=params(8),
        cost_estimate=pl.CostEstimate(flops=2 * rows * count * count, bytes_accessed=4 * rows * count, transcendentals=0),
        name="sort",
    )(parts, rank)


def unsort_kernel(half, given, rank_ref, *refs):
    xs, refs = refs[:given], refs[given:]
    before, (flat_ref,) = (refs[:1], refs[1:2]) if half else ((), (None,))
    out_ref, parts = refs[-2:]
    rows, count = xs[0].shape[0], rank_ref.shape[1]
    width = xs[0].shape[1]

    @pl.when(pl.program_id(0) == 0)
    def _():
        x = xs[0][...]
        for more in xs[1:]:
            x = x + more[...]
        high = x.astype(BF16).astype(F32)
        parts[...] = jnp.concatenate([high, x - high], axis=0).astype(BF16)

    total = jnp.zeros((2 * rows, TILE), F32)
    for k in range(width // CHUNK):
        ids = lax.broadcasted_iota(jnp.int32, (CHUNK, TILE), 0) + (half * width + k * CHUNK)
        hot = rows_equal(ids.astype(F32), rank_ref[:, pl.ds(pl.multiple_of(pl.program_id(0) * TILE, TILE), TILE)])
        piece = parts[:, k * CHUNK : (k + 1) * CHUNK]
        total = total + lax.dot_general(piece, hot, NN, preferred_element_type=F32)
    total = total[:rows] + total[rows:]
    if not half:
        out_ref[...] = total
        return
    total = total + before[0][...]
    species = rows - 2
    ratio = 0.5 / total[species : species + 1]
    for n in range(TILE // LANES):
        piece = slice(n * LANES, (n + 1) * LANES)
        line = pl.program_id(0) * (TILE // LANES) + n
        value = 0.5 * flat_ref[:species, piece] + total[:species, piece] * ratio[:, piece]
        out_ref[pl.ds(line, species, stride=count // LANES), :] = value


def unsort_call(wholes, piece, rank, before, flat):
    half = int(before is not None)
    rows, count = wholes[0].shape
    part = pl.BlockSpec((rows, count // 2), lambda i: (0, half))
    column = pl.BlockSpec((rows, TILE), lambda i: (0, i))
    args = [rank, *wholes, piece]
    specs = [whole(rank.shape)] + [part] * len(wholes) + [whole(piece.shape)]
    out_shape, out_spec = (rows, count), column
    if half:
        args += [before, flat]
        specs += [column, column]
        lines = (rows - 2) * count // LANES
        out_shape, out_spec = (lines, LANES), whole((lines, LANES))
    return pl.pallas_call(
        functools.partial(unsort_kernel, half, len(wholes) + 1),
        grid=(count // TILE,),
        out_shape=jax.ShapeDtypeStruct(out_shape, F32),
        in_specs=specs,
        out_specs=out_spec,
        scratch_shapes=[pltpu.VMEM((2 * rows, count // 2), BF16)],
        compiler_params=params(12),
        cost_estimate=pl.CostEstimate(flops=2 * rows * count * count, bytes_accessed=4 * rows * count, transcendentals=0),
        name="unsort",
    )(*args)


def weights_of(key, table, bins, per_tile):
    nshape = table.shape[1]
    cell = jnp.floor((key + 0.5) * (1.0 / nshape))
    shape = key - cell * nshape
    tile = jnp.floor((cell + 0.5) * (1.0 / per_tile))
    within = cell - tile * per_tile
    ids = lax.broadcasted_iota(jnp.int32, (nshape, key.shape[1]), 0).astype(F32)
    picked = lax.dot_general(table, rows_equal(ids, shape), NN, preferred_element_type=F32).astype(BF16)
    masks = [jnp.where(within == m, 1.0, 0.0).astype(BF16) for m in range(per_tile)]
    columns = []
    for part in (picked[:bins], picked[bins:]):
        columns.append(jnp.concatenate([part * mask for mask in masks], axis=0))
    return jnp.concatenate(columns, axis=1), tile


def split_table(table):
    high = table.astype(BF16).astype(F32)
    return jnp.concatenate([high, table - high], axis=0).astype(BF16)


def prepare_weights(source, index, key_row, table, bins, per_tile, weights, tiles):
    def step(n, _):
        key = source[key_row : key_row + 1, pl.ds(pl.multiple_of(n * LANES, LANES), LANES)]
        block, tile = weights_of(key, table, bins, per_tile)
        weights[index + n] = block
        tiles[index + n] = jnp.broadcast_to(tile, tiles.shape[1:])
        return 0

    lax.fori_loop(0, source.shape[1] // LANES, step, 0, unroll=4)


def collect_kernel(species, bins, per_tile, pairs, lists, *refs):
    sources, refs = [refs[2 * n : 2 * n + 2] for n in range(lists)], refs[2 * lists :]
    table_ref, out_ref, *refs = refs
    keys, (weights, tiles, parts, steps, sems) = refs[:lists], refs[lists:]
    copies = fetch_rows([source[0] for source in sources], steps, sems)
    rows, part = sources[0][0].shape
    count = 2 * part
    for key, source in zip(keys, sources):
        key[:, :part] = source[0][rows - 8 :, :]
        key[:, part:] = source[1][rows - 8 :, :]
    blocks = count // LANES
    out_ref[...] = jnp.zeros_like(out_ref)
    table = split_table(table_ref[...])
    line = lax.broadcasted_iota(jnp.int32, (rows, LANES), 0)
    for number in range(2 * lists):
        source = sources[number // 2][number % 2]
        start = number * blocks // 2
        prepare_weights(source, start, species, table, bins, per_tile, weights, tiles)

        def split(n, _, source=source, start=start):
            x = source[:, pl.ds(pl.multiple_of(n * LANES, LANES), LANES)]
            x = jnp.where(line < species, x, jnp.where(line == species, 1.0, 0.0))
            parts[start + n] = padded_halves(x)
            return 0

        lax.fori_loop(0, blocks // 2, split, 0, unroll=4)

    for copy in copies:
        copy.wait()

    def step(n, _):
        for number in range(lists):
            for g in range(GROUP):
                k = n * GROUP + g
                tile = steps[number, 7, k].astype(jnp.int32)
                block = jnp.minimum(k - tile, blocks - 1) + number * blocks
                wanted = jnp.where(k < pairs, tile, -1).astype(F32)
                mask = jnp.where(tiles[block] == wanted, 1.0, 0.0).astype(BF16)
                mask = jnp.concatenate([mask] * (2 * HALF // mask.shape[0]), axis=0)
                x = parts[block] * mask
                both = jnp.concatenate([x, x], axis=1)
                got = lax.dot_general(both, weights[block], NT, preferred_element_type=F32)
                place = pl.ds(pl.multiple_of(tile * TILE, TILE), TILE)
                out_ref[:, place] += got[:rows] + got[HALF : HALF + rows]
        return 0

    lax.fori_loop(0, -(-pairs // GROUP), step, 0)


def collect_call(sources, table, species, bins, per_tile, ntiles):
    rows, count = sources[0][0].shape[0], 2 * sources[0][0].shape[1]
    lists, blocks = len(sources), count // LANES
    pairs = blocks + ntiles - 1
    args = [half for source in sources for half in source] + [table]
    specs = [VMEM] * (2 * lists + 1)
    return pl.pallas_call(
        functools.partial(collect_kernel, species, bins, per_tile, pairs, lists),
        out_shape=[jax.ShapeDtypeStruct((rows, ntiles * TILE), F32)] + [jax.ShapeDtypeStruct((8, count), F32)] * lists,
        in_specs=specs,
        out_specs=[VMEM] * (lists + 1),
        scratch_shapes=[
            pltpu.VMEM((lists * blocks, TILE, 2 * LANES), BF16),
            pltpu.VMEM((lists * blocks, 16, LANES), F32),
            pltpu.VMEM((lists * blocks, 2 * HALF, LANES), BF16),
            pltpu.SMEM((lists, 8, LANES), F32),
            pltpu.SemaphoreType.DMA((lists,)),
        ],
        compiler_params=params(19),
        cost_estimate=pl.CostEstimate(flops=lists * pairs * 2 * LANES * TILE * TILE, bytes_accessed=0, transcendentals=0),
        name="collect",
    )(*args)


def turn_back(mean, out_ref, bins, quads, turned):
    rows, width = mean.shape
    lines = width // LANES
    fold = LANES // bins
    for q in range(lines):
        quads[pl.ds(q, rows, stride=lines), :] = mean[:, q * LANES : (q + 1) * LANES]
    blocked = lax.broadcasted_iota(jnp.int32, (lines, LANES), 1) // bins

    def turn(g):
        source = [quads[pl.ds(pl.multiple_of(g * LANES + k * lines, lines), lines), :] for k in range(fold)]
        for r in range(fold):
            out = source[r]
            for k in range(fold):
                if k != r:
                    out = jnp.where(blocked == k, pltpu.roll(source[k], (k - r) * bins % LANES, 1), out)
            turned[pl.ds(r, lines, stride=fold), :] = out
        return turned[...].T

    full, rest = out_ref.shape[0] // LANES, out_ref.shape[0] % LANES

    def step(g, _):
        out_ref[pl.ds(pl.multiple_of(g * LANES, LANES), LANES), :] = turn(g)
        return 0

    lax.fori_loop(0, full, step, 0)
    if rest:
        out_ref[full * LANES :, :] = turn(full)[:rest]


def project_kernel(bins, per_tile, pairs, lists, state_rows, *refs):
    means, refs = refs[:3], refs[3:]
    sources, refs = refs[:lists], refs[lists:]
    table_ref, *refs = refs
    outs, refs = refs[:lists], refs[lists:]
    state_ref = refs.pop(0) if state_rows else None
    weights, tiles, parts, steps, sems, *turning = refs
    copies = fetch_rows(sources, steps, sems)
    rows, count = outs[0].shape
    blocks = count // LANES
    per_mean = means[0].shape[1] // TILE
    for number, mean in enumerate(means):

        def split(n, _, number=number, mean=mean):
            parts[number * per_mean + n] = padded_halves(mean[:, pl.ds(pl.multiple_of(n * TILE, TILE), TILE)])
            return 0

        lax.fori_loop(0, per_mean, split, 0, unroll=2)
    if state_rows:
        turn_back(means[1], state_ref, bins, *turning)
    table = split_table(table_ref[...])
    for copy in copies:
        copy.wait()
    for number in range(lists):
        outs[number][...] = jnp.zeros_like(outs[number])
        prepare_weights(sources[number], number * blocks, 6, table, bins, per_tile, weights, tiles)

    def step(n, _):
        for number in range(lists):
            for g in range(GROUP):
                k = n * GROUP + g
                tile = steps[number, 7, k].astype(jnp.int32)
                local = jnp.minimum(k - tile, blocks - 1)
                block = local + number * blocks
                wanted = jnp.where(k < pairs, tile, -1).astype(F32)
                got = lax.dot_general(parts[tile], weights[block], NN, preferred_element_type=F32)
                got = got[:rows] + got[HALF : HALF + rows]
                got = got[:, :LANES] + got[:, LANES:]
                got = jnp.where(tiles[block][:1] == wanted, got, 0.0)
                place = pl.ds(pl.multiple_of(local * LANES, LANES), LANES)
                outs[number][:, place] += got
        return 0

    lax.fori_loop(0, -(-pairs // GROUP), step, 0)


def project_call(means, sources, table, bins, per_tile, ntiles, state_rows=0):
    rows, count = means[0].shape[0], sources[0].shape[1]
    lists = len(sources)
    blocks = count // LANES
    pairs = blocks + ntiles - 1
    return pl.pallas_call(
        functools.partial(project_kernel, bins, per_tile, pairs, lists, state_rows),
        out_shape=[jax.ShapeDtypeStruct((rows, count), F32)] * lists
        + [jax.ShapeDtypeStruct((state_rows, LANES), F32)] * bool(state_rows),
        in_specs=[VMEM] * (lists + 4),
        out_specs=[VMEM] * (lists + bool(state_rows)),
        scratch_shapes=[
            pltpu.VMEM((lists * blocks, TILE, 2 * LANES), BF16),
            pltpu.VMEM((lists * blocks, 16, LANES), F32),
            pltpu.VMEM((ntiles, 2 * HALF, TILE), BF16),
            pltpu.SMEM((lists, 8, LANES), F32),
            pltpu.SemaphoreType.DMA((lists,)),
        ] + [pltpu.VMEM((rows * means[0].shape[1] // LANES, LANES), F32), pltpu.VMEM((LANES, LANES), F32)] * bool(state_rows),
        compiler_params=params(19),
        cost_estimate=pl.CostEstimate(flops=lists * pairs * 2 * LANES * TILE * TILE, bytes_accessed=0, transcendentals=0),
        name="project",
    )(*means, *sources, table)


def middle_kernel(species, bins, chunk, refs_in, refs_out, scratch):
    *accs, cmc_ref, diss_ref, rate_ref, count_ref, matrix_ref = refs_in
    fresh_ref, next_ref, far_ref = refs_out
    nat, quads, turned, side_out, load, outward, hopped, summed, got, state_ref, edge_out, edge_in, side_in, pick_ref, third_ref, send, recv, side_send, side_recv = scratch
    rows, width = fresh_ref.shape
    steps = width // chunk
    slab, nslab = lax.axis_index("slab"), lax.axis_size("slab")
    cross, ncross = lax.axis_index("cross"), lax.axis_size("cross")
    parity = lax.rem(slab, 2)
    outer = slab + 4 * parity - 2
    inner = slab - 4 * parity + 2
    partner = slab + 1 - 2 * parity
    has_outer = (outer >= 0) & (outer < nslab)
    has_inner = (inner >= 0) & (inner < nslab)
    has_before, has_after = cross > 0, cross < ncross - 1
    has_down, has_up = slab > 0, slab < nslab - 1
    mesh = pl.DeviceIdType.MESH

    def partial_sum(piece):
        total = accs[0][:, piece]
        for more in accs[1:]:
            total = total + more[:, piece]
        return total

    loads, start = [], 0
    for n, source in enumerate((cmc_ref, diss_ref, rate_ref)):
        target = nat.at[start : start + source.shape[0]]
        loads.append(pltpu.make_async_copy(source, target, load.at[n]))
        loads[-1].start()
        start += source.shape[0]
    if start < nat.shape[0]:
        nat[start:, :] = jnp.zeros((nat.shape[0] - start, LANES), F32)
    outward[...] = partial_sum(slice(0, width))

    @pl.when(jnp.logical_not(has_inner))
    def _():
        hopped[...] = jnp.zeros_like(hopped)

    @pl.when(jnp.logical_not(has_outer))
    def _():
        far_ref[...] = jnp.zeros_like(far_ref)

    @pl.when(jnp.logical_not(has_before))
    def _():
        edge_in[:, :, :LANES] = jnp.zeros(edge_in.shape[:2] + (LANES,), F32)

    @pl.when(jnp.logical_not(has_after))
    def _():
        edge_in[:, :, LANES:] = jnp.zeros(edge_in.shape[:2] + (LANES,), F32)

    @pl.when(jnp.logical_not(has_down))
    def _():
        side_in[0] = jnp.zeros(side_in.shape[1:], F32)

    @pl.when(jnp.logical_not(has_up))
    def _():
        side_in[1] = jnp.zeros(side_in.shape[1:], F32)

    barrier = pltpu.get_barrier_semaphore()
    greet = lambda where: pl.semaphore_signal(barrier, inc=1, device_id=where, device_id_type=mesh)
    pl.when(has_down)(lambda: greet({"slab": slab - 1}))
    pl.when(has_up)(lambda: greet({"slab": slab + 1}))
    pl.when(has_outer)(lambda: greet({"slab": outer}))
    pl.when(has_inner)(lambda: greet({"slab": inner}))
    pl.when(has_before)(lambda: greet({"cross": cross - 1}))
    pl.when(has_after)(lambda: greet({"cross": cross + 1}))
    number = lambda flag: jnp.where(flag, 1, 0)
    flags = (has_down, has_up, has_outer, has_inner, has_before, has_after)
    pl.semaphore_wait(barrier, sum(number(flag) for flag in flags))

    def lanes(c, base=0):
        return pl.ds(pl.multiple_of(base + c * chunk, chunk), chunk)

    def remote(kind, c, source, target, where):
        return pltpu.make_async_remote_copy(
            src_ref=source, dst_ref=target, send_sem=send.at[kind, c], recv_sem=recv.at[kind, c],
            device_id=where, device_id_type=mesh,
        )

    to_outer = lambda c: remote(0, c, outward.at[:, lanes(c)], hopped.at[:, lanes(c)], {"slab": outer})
    to_partner = lambda c: remote(1, c, summed.at[:, lanes(c)], got.at[:, lanes(c)], {"slab": partner})
    to_after = lambda c: remote(2, c, edge_out.at[c, :, LANES:], edge_in.at[c, :, :LANES], {"cross": cross + 1})
    to_before = lambda c: remote(3, c, edge_out.at[c, :, :LANES], edge_in.at[c, :, LANES:], {"cross": cross - 1})
    give = lambda c: remote(4, c, fresh_ref.at[:, lanes(c)], next_ref.at[:, lanes(c)], {"slab": partner})
    pass_on = lambda c: remote(5, c, next_ref.at[:, lanes(c)], far_ref.at[:, lanes(c)], {"slab": inner})

    def side(n, source, where):
        return pltpu.make_async_remote_copy(
            src_ref=source, dst_ref=side_in.at[n], send_sem=side_send.at[n], recv_sem=side_recv.at[n],
            device_id=where, device_id_type=mesh,
        )

    to_up = side(0, side_out.at[0], {"slab": slab + 1})
    to_down = side(1, side_out.at[1], {"slab": slab - 1})

    def start_hops(chunks):
        @pl.when(has_outer)
        def _():
            for c in chunks:
                to_outer(c).start()

    start_hops(range(2))
    for copy in loads:
        copy.wait()
    lines = width // LANES
    fold = LANES // bins
    blocked = lax.broadcasted_iota(jnp.int32, (LANES // fold, LANES), 1) // bins

    def turn(g, _):
        turned[...] = nat[pl.ds(pl.multiple_of(g * LANES, LANES), LANES), :].T
        parts = [turned[pl.ds(r, LANES // fold, stride=fold), :] for r in range(fold)]
        for k in range(fold):
            out = parts[k]
            for r in range(fold):
                if r != k:
                    out = jnp.where(blocked == r, pltpu.roll(parts[r], (r - k) * bins % LANES, 1), out)
            place = pl.multiple_of(g * LANES + k * lines, lines)
            quads[pl.ds(place, lines), :] = out
        return 0

    lax.fori_loop(0, nat.shape[0] // LANES, turn, 0)
    tile = lambda q: quads[pl.ds(q, rows, stride=lines), :]
    side_out[0] = tile(lines - 1)
    side_out[1] = tile(0)

    lane = lax.broadcasted_iota(jnp.int32, (2 * LANES, chunk), 1)
    row = lax.broadcasted_iota(jnp.int32, (2 * LANES, chunk), 0)
    target = jnp.where(row < LANES, row * bins, (row - LANES) * bins + bins - 1)
    pick_ref[...] = rows_equal(target, lane)
    third = matrix_ref.shape[1] // 3
    high, low = halves(matrix_ref[...])
    column = lax.broadcasted_iota(jnp.int32, matrix_ref.shape, 1)
    third_ref[...] = jnp.where(column < 2 * third, high.astype(F32), low.astype(F32)).astype(BF16)
    line = lax.broadcasted_iota(jnp.int32, (rows, chunk), 0)
    slot = lax.broadcasted_iota(jnp.int32, (rows, chunk), 1) % bins
    gap = [jnp.zeros((third - rows, chunk), F32)] * (third > rows)

    pl.when(has_up)(to_up.start)
    pl.when(has_down)(to_down.start)
    start_hops(range(2, steps))

    def stacked(x):
        high = x.astype(BF16).astype(F32)
        return jnp.concatenate([high, x - high], axis=0).astype(BF16)

    def add_hop(c):
        pl.when(has_inner)(lambda: to_outer(c).wait_recv())
        summed[:, lanes(c)] = partial_sum(lanes(c, 2 * width)) + hopped[:, lanes(c)]

    per = chunk // LANES

    def advect(c):
        here = jnp.concatenate([tile(c * per + n) for n in range(per)], axis=1)
        low = jnp.where(c == 0, side_in[0], tile(jnp.maximum(c * per - 1, 0)))
        high = jnp.where(c == steps - 1, side_in[1], tile(jnp.minimum((c + 1) * per, lines - 1)))
        left = pltpu.roll(jnp.concatenate([low, here], axis=1), bins, 1)[:, LANES:]
        right = pltpu.roll(jnp.concatenate([here, high], axis=1), chunk + LANES - bins, 1)[:, :chunk]
        return here - 0.4 * (here - left) + 0.1 * (right - 2.0 * here + left)

    def cell_row(n, c):
        start = (species + n) * lines + c * per
        return jnp.concatenate([quads[pl.ds(start + k, 1), :] for k in range(per)], axis=1)

    def blend(c):
        total = partial_sum(lanes(c, width)) + got[:, lanes(c)]
        blended = (total + advect(c)) / (total[species : species + 1] + 1.0)
        state_ref[:, lanes(c)] = blended
        edge = lax.dot_general(stacked(blended), pick_ref[...], NT, preferred_element_type=F32)
        edge_out[c] = edge[:rows] + edge[rows:]

    def send_edges(c):
        pl.when(has_after)(lambda: to_after(c).start())
        pl.when(has_before)(lambda: to_before(c).start())

    def wait_edges(c):
        pl.when(has_before)(lambda: to_after(c).wait_recv())
        pl.when(has_after)(lambda: to_before(c).wait_recv())

    def react(c):
        here = state_ref[:, lanes(c)]
        around = lax.dot_general(stacked(edge_in[c]), pick_ref[...], NN, preferred_element_type=F32)
        around = around[:rows] + around[rows:]
        before = jnp.where(slot == 0, around, pltpu.roll(here, 1, 1))
        after = jnp.where(slot == bins - 1, around, pltpu.roll(here, chunk - 1, 1))
        state = here + cell_row(0, c) * (after - 2.0 * here + before)
        half = 0.5 * cell_row(1, c)
        count = count_ref[:, lanes(c)]
        for k in range(KMAX):
            high, low = (part.astype(F32) for part in halves(state))
            stack = jnp.concatenate([high, *gap, low, *gap, high, *gap], axis=0).astype(BF16)
            rate = lax.dot_general(third_ref[...], stack, NN, preferred_element_type=F32)
            state = jnp.where(k < count, state + half * jnp.tanh(rate), state)
        fresh_ref[:, lanes(c)] = jnp.where(line == species, 1.0, state)

    def step(t, _):
        def when(lag, body):
            c = t - lag
            pl.when((c >= 0) & (c < steps))(lambda: body(c))

        def second(c):
            pl.when((c == 0) & has_down)(to_up.wait_recv)
            pl.when((c == 0) & has_up)(to_down.wait_recv)
            to_partner(c).wait_recv()
            blend(c)

        def third_stage(c):
            wait_edges(c)
            react(c)

        def fourth(c):
            give(c).wait_recv()
            pl.when(has_inner)(lambda: pass_on(c).start())

        when(0, add_hop)
        when(LAG[0], second)
        when(0, lambda c: to_partner(c).start())
        when(LAG[1], third_stage)
        when(LAG[0], send_edges)
        when(LAG[2], fourth)
        when(LAG[1], lambda c: give(c).start())
        return 0

    lax.fori_loop(0, steps + LAG[2], step, 0)

    def finish(c, _):
        pl.when(has_outer)(lambda: to_outer(c).wait_send())
        to_partner(c).wait_send()
        pl.when(has_after)(lambda: to_after(c).wait_send())
        pl.when(has_before)(lambda: to_before(c).wait_send())
        give(c).wait_send()
        pl.when(has_inner)(lambda: pass_on(c).wait_send())
        pl.when(has_outer)(lambda: pass_on(c).wait_recv())
        return 0

    lax.fori_loop(0, steps, finish, 0)
    pl.when(has_up)(to_up.wait_send)
    pl.when(has_down)(to_down.wait_send)


def middle_call(accs, cmc, diss, rate, count, matrix, species, bins, chunk=512):
    rows, width = accs[0].shape[0], count.shape[1]
    steps = width // chunk
    given = len(accs) + 5

    def kernel(*refs):
        middle_kernel(species, bins, chunk, refs[:given], refs[given : given + 3], refs[given + 3 :])

    return pl.pallas_call(
        kernel,
        out_shape=[jax.ShapeDtypeStruct((rows, width), F32)] * 3,
        in_specs=[VMEM] * len(accs) + [pl.BlockSpec(memory_space=pl.ANY)] * 3 + [VMEM] * 2,
        out_specs=[VMEM] * 3,
        scratch_shapes=[pltpu.VMEM((rows * bins, LANES), F32), pltpu.VMEM((rows * width // LANES, LANES), F32)]
        + [pltpu.VMEM((LANES, LANES), F32), pltpu.VMEM((2, rows, LANES), F32), pltpu.SemaphoreType.DMA((3,))]
        + [pltpu.VMEM((rows, width), F32)] * 5
        + [pltpu.VMEM((steps, rows, 2 * LANES), F32)] * 2
        + [pltpu.VMEM((2, rows, LANES), F32), pltpu.VMEM((2 * LANES, chunk), BF16), pltpu.VMEM(matrix.shape, BF16)]
        + [pltpu.SemaphoreType.DMA((6, steps))] * 2
        + [pltpu.SemaphoreType.DMA((2,))] * 2,
        compiler_params=pltpu.CompilerParams(vmem_limit_bytes=20 << 20, collective_id=1, has_side_effects=True),
        name="middle",
    )(*accs, cmc, diss, rate, count, matrix)


def on_device(
    les_state, cmc_state, cmc_map, pdf_index, pdf_table, diffusion, chem_matrix, dissipation, reaction_rate, substeps
):
    species = les_state.shape[0]
    rows = -(-(species + 2) // 8) * 8
    bins, cells = cmc_state.shape[1:]
    nshape = pdf_table.shape[0]
    count = cmc_map.size
    ncross = lax.axis_size("cross")
    per_tile = TILE // bins
    ntiles = 3 * cells // per_tile
    flat, rank, parts, low = head_call(
        les_state, cmc_map, pdf_index, diffusion, rows, cells, nshape, ntiles, nshape * per_tile
    )
    bits = [1 << k for k in range(ncross.bit_length() - 1)]
    low_there = swap(low, "cross", bits[-1])
    high = sort_call(parts, rank)
    high_there = swap(high, "cross", bits[-1])
    near_lists = [(low, high)] + [(swap(low, "cross", bit), swap(high, "cross", bit)) for bit in bits[:-1]]
    low_far = [low_there] + [swap(low_there, "cross", bit) for bit in bits[:-1]]

    table = lax.dynamic_slice_in_dim(pdf_table.T, lax.axis_index("cross") * bins, bins, axis=0)

    extra = rows - species
    matrix = jnp.tile(jnp.pad(chem_matrix, ((0, extra), (0, -(-rows // 16) * 16 - species))), (1, 3))
    terms = (cmc_state.reshape(species * bins, cells), dissipation, reaction_rate, jnp.repeat(substeps, bins)[None, :], matrix)
    acc, *near_keys = collect_call(near_lists, table, species, bins, per_tile, ntiles)
    acc, high_there, terms = lax.optimization_barrier((acc, high_there, terms))
    high_far = [high_there] + [swap(high_there, "cross", bit) for bit in bits[:-1]]
    more, *far_keys = collect_call(list(zip(low_far, high_far)), table, species, bins, per_tile, ntiles)
    accs = [acc, more]
    means = middle_call(accs, *terms, species, bins)
    means = [means[2], means[0], means[1]]
    there, *pieces = project_call(means, far_keys, table, bins, per_tile, ntiles)
    pieces = [swap(piece, "cross", bit) for bit, piece in zip(bits[:-1], pieces)]
    part = count // 2
    low, high = there[:, :part], there[:, part:]
    for piece in pieces:
        low, high = low + piece[:, :part], high + piece[:, part:]
    low, means = lax.optimization_barrier((low, means))
    low = swap(low, "cross", bits[-1])
    high = swap(high, "cross", bits[-1])
    *here, cmc_out = project_call(means, near_keys, table, bins, per_tile, ntiles, species * bins)
    total = [here[0]] + [swap(piece, "cross", bit) for bit, piece in zip(bits[:-1], here[1:])]
    before = unsort_call(total, low, rank, None, None)
    les_out = unsort_call(total, high, rank, before, flat)
    return (les_out.reshape(les_state.shape), cmc_out.reshape(species, bins, cells))


def solution(mesh):
    return jax.shard_map(
        on_device,
        mesh=mesh,
        in_specs=(
            P(None, "slab", "cross", None),
            P(None, "cross", "slab"),
            P("slab", "cross", None),
            P("slab", "cross", None),
            P(),
            P(),
            P(),
            P("cross", "slab"),
            P("cross", "slab"),
            P("slab"),
        ),
        out_specs=(P(None, "slab", "cross", None), P(None, "cross", "slab")),
        check_vma=False,
    )
```

```python
import functools


import jax
import jax.numpy as jnp
from jax import lax
from jax.experimental import pallas as pl
from jax.experimental.pallas import tpu as pltpu
from jax.sharding import PartitionSpec as P

KMAX = 4
F32 = jnp.float32
BF16 = jnp.bfloat16
NT = (((1,), (1,)), ((), ()))
NN = (((1,), (0,)), ((), ()))
LANES = 128
TILE = 256
HALF = 64
GROUP = 16
LAG = (2, 4, 6)


def swap(array, axis, bit):
    count = lax.axis_size(axis)
    return lax.ppermute(array, axis, [(i, i ^ bit) for i in range(count)])


def halves(x):
    high = x.astype(BF16)
    return high, (x - high.astype(F32)).astype(BF16)


def padded_halves(x):
    gap = jnp.zeros((HALF - x.shape[0], x.shape[1]), F32)
    high = x.astype(BF16).astype(F32)
    return jnp.concatenate([high, gap, x - high, gap], axis=0).astype(BF16)


def rows_equal(targets, row):
    return jnp.where(targets == row, 1.0, 0.0).astype(BF16)


def whole(shape):
    return pl.BlockSpec(shape, lambda *_: (0,) * len(shape))


VMEM = pl.BlockSpec(memory_space=pltpu.VMEM)
SMEM = pl.BlockSpec(memory_space=pltpu.SMEM)


def params(mib):
    return pltpu.CompilerParams(vmem_limit_bytes=mib << 20)


def fetch_rows(sources, steps, sems):
    copies = []
    for number, source in enumerate(sources):
        last = source.at[source.shape[0] - 8 : source.shape[0], :LANES]
        copies.append(pltpu.make_async_copy(last, steps.at[number], sems.at[number]))
        copies[-1].start()
    return copies


def ranks(tiles, span, key_ref, rank_ref, table_ref):
    count = rank_ref.shape[1]
    ids = lax.broadcasted_iota(jnp.int32, (tiles, TILE), 0).astype(F32)
    tile_of = lambda n: jnp.floor((key_ref[:1, n * TILE : (n + 1) * TILE] + 0.5) * (1.0 / span))
    total = jnp.zeros((tiles, TILE), F32)
    for n in range(count // TILE):
        total = total + jnp.where(ids == tile_of(n), 1.0, 0.0)
    total = jnp.sum(total, axis=1, keepdims=True)
    total = jnp.broadcast_to(total, (tiles, LANES))
    big = jnp.floor(total * (1.0 / HALF))
    row = lax.broadcasted_iota(jnp.int32, (tiles, tiles), 0)
    below = rows_equal(jnp.where(lax.broadcasted_iota(jnp.int32, (tiles, tiles), 1) < row, 1, 0), 1)
    add = lambda part: lax.dot_general(below, part.astype(BF16), NN, preferred_element_type=F32)
    base = add(big) * HALF + add(total - big * HALF)
    order = lax.broadcasted_iota(jnp.int32, (tiles, LANES), 0).astype(F32)
    lane = lax.broadcasted_iota(jnp.int32, (tiles, LANES), 1).astype(F32)
    last = jnp.maximum(jnp.ceil((base + total) * (1.0 / LANES)) - 1.0, 0.0) + order
    passed = jnp.where((last < lane) & (order < tiles - 1), 1.0, 0.0)
    table_ref[...] = jnp.sum(passed, axis=0, keepdims=True)
    ahead = jnp.where(
        lax.broadcasted_iota(jnp.int32, (TILE, TILE), 0) < lax.broadcasted_iota(jnp.int32, (TILE, TILE), 1), 1.0, 0.0
    ).astype(BF16)
    carry = base[:, :1]
    for n in range(count // TILE):
        hot = jnp.where(ids == tile_of(n), 1.0, 0.0)
        before = lax.dot_general(hot.astype(BF16), ahead, NN, preferred_element_type=F32) + carry
        rank_ref[:, n * TILE : (n + 1) * TILE] = jnp.sum(hot * before, axis=0, keepdims=True)
        carry = carry + jnp.sum(hot, axis=1, keepdims=True)


HALO_ORDER = {2: lambda n: (), 3: lambda n: range(1, n - 1), 0: lambda n: (), 1: lambda n: sorted({0, n - 1})}


def head_kernel(grid_shape, cells, nshape, tiles, span, *refs):
    given, (t_ref, rank_ref, parts_ref, half_ref), refs = refs[:4], refs[4:8], refs[8:]
    les_ref, map_ref, shape_ref, diff_ref, key_ref, table_ref, *refs = refs
    faces, halos, (send, recv, load) = refs[:4], refs[4:8], refs[8:]
    loads = [
        pltpu.make_async_copy(source, target, load.at[n])
        for n, (source, target) in enumerate(zip(given, (les_ref, map_ref, shape_ref, diff_ref)))
    ]
    for copy in loads:
        copy.start()
    species, nx, ny = grid_shape
    count = rank_ref.shape[1]
    slab, nslab = lax.axis_index("slab"), lax.axis_size("slab")
    cross, ncross = lax.axis_index("cross"), lax.axis_size("cross")
    mesh = pl.DeviceIdType.MESH
    sides = [
        (slab > 0, {"slab": slab - 1}),
        (slab < nslab - 1, {"slab": slab + 1}),
        (cross > 0, {"cross": cross - 1}),
        (cross < ncross - 1, {"cross": cross + 1}),
    ]
    barrier = pltpu.get_barrier_semaphore()
    for n, (there, where) in enumerate(sides):

        @pl.when(jnp.logical_not(there))
        def _(n=n):
            halos[n][...] = jnp.zeros_like(halos[n])

    for copy in loads:
        copy.wait()
    line = lambda x, y: les_ref[pl.ds(x * ny + y, species, stride=nx * ny), :]
    for n, x in enumerate((0, nx - 1)):
        for y in range(ny):
            faces[n][y, :species] = line(x, y)
    for n, y in enumerate((0, ny - 1)):
        for x in range(nx):
            faces[2 + n][x, :species] = line(x, y)
    for there, where in sides:

        @pl.when(there)
        def _(where=where):
            pl.semaphore_signal(barrier, inc=1, device_id=where, device_id_type=mesh)

    pl.semaphore_wait(barrier, sum(jnp.where(there, 1, 0) for there, _ in sides))
    copies = []
    for n, (there, where) in enumerate(sides):
        copy = pltpu.make_async_remote_copy(
            src_ref=faces[n], dst_ref=halos[n ^ 1], send_sem=send.at[n], recv_sem=recv.at[n ^ 1],
            device_id=where, device_id_type=mesh,
        )
        pl.when(there)(copy.start)
        copies.append(copy)
    offset = map_ref[...] - (slab - 1) * cells
    block = jnp.where(offset >= cells, 1, 0) + jnp.where(offset >= 2 * cells, 1, 0)
    offset = jnp.where(lax.rem(slab, 2) == 1, (2 - block) * cells + offset - block * cells, offset)
    key = (offset * nshape + shape_ref[...]).astype(F32)
    key_ref[:1, :] = key
    t_ref[species:, :] = jnp.concatenate([key] + [jnp.zeros((t_ref.shape[0] - species - 1, count), F32)], axis=0)
    ranks(tiles, span, key_ref, rank_ref, table_ref)
    row = lax.broadcasted_iota(jnp.int32, (species, species), 0)
    number = jnp.where(row == lax.broadcasted_iota(jnp.int32, (species, species), 1), diff_ref[...], 0.0)
    number = jnp.sum(number, axis=1, keepdims=True)
    lane = lax.broadcasted_iota(jnp.int32, (species, LANES), 1)
    for n in (2, 3, 0, 1):
        pl.when(sides[n ^ 1][0])(copies[n].wait_recv)
        for x, y in [(x, y) for x in HALO_ORDER[n](nx) for y in range(ny)]:
            here = line(x, y)
            around = line(x + 1, y) if x < nx - 1 else halos[1][y, :species]
            around = around + (line(x - 1, y) if x else halos[0][y, :species])
            around = around + (line(x, y + 1) if y < ny - 1 else halos[3][x, :species])
            around = around + (line(x, y - 1) if y else halos[2][x, :species])
            around = around + jnp.where(lane < LANES - 1, pltpu.roll(here, LANES - 1, 1), 0.0)
            around = around + jnp.where(lane > 0, pltpu.roll(here, 1, 1), 0.0)
            place = (x * ny + y) * LANES
            t_ref[:species, place : place + LANES] = here + number * (around - 6.0 * here)
    x = t_ref[...]
    high = x.astype(BF16).astype(F32)
    parts_ref[...] = jnp.concatenate([high, x - high], axis=0).astype(BF16)
    sort_tiles(parts_ref, rank_ref, table_ref[...], half_ref, 0)
    for n, (there, _) in enumerate(sides):
        pl.when(there)(copies[n].wait_send)


def head_call(les_state, cmc_map, pdf_index, diffusion, rows, cells, nshape, tiles, span):
    species, nx, ny, nz = les_state.shape
    count = nx * ny * nz
    halo = [pltpu.VMEM((n, rows, LANES), F32) for n in (ny, ny, nx, nx)]
    return pl.pallas_call(
        functools.partial(head_kernel, (species, nx, ny), cells, nshape, tiles, span),
        out_shape=[
            jax.ShapeDtypeStruct((rows, count), F32),
            jax.ShapeDtypeStruct((1, count), F32),
            jax.ShapeDtypeStruct((2 * rows, count), BF16),
            jax.ShapeDtypeStruct((rows, count // 2), F32),
        ],
        in_specs=[pl.BlockSpec(memory_space=pltpu.HBM)] * 4,
        out_specs=[VMEM] * 4,
        scratch_shapes=[
            pltpu.VMEM((species * nx * ny, nz), F32),
            pltpu.VMEM((1, count), jnp.int32),
            pltpu.VMEM((1, count), jnp.int32),
            pltpu.VMEM((1, species), F32),
            pltpu.VMEM((8, count), F32),
            pltpu.VMEM((1, LANES), F32),
        ] + halo * 2 + [pltpu.SemaphoreType.DMA((4,))] * 3,
        compiler_params=pltpu.CompilerParams(vmem_limit_bytes=60 << 20, collective_id=2, has_side_effects=True),
        name="head",
    )(
        les_state.reshape(species * nx * ny, nz), cmc_map.reshape(1, count), pdf_index.reshape(1, count),
        diffusion.reshape(1, species),
    )


CHUNK = 2 * TILE


def sort_tiles(parts, rank_ref, steps, out_ref, first):
    rows = out_ref.shape[0]
    count = rank_ref.shape[1]

    def step(n, _):
        here = (first + n) * TILE
        total = jnp.zeros((2 * rows, TILE), F32)
        for k in range(count // CHUNK):
            piece = slice(k * CHUNK, (k + 1) * CHUNK)
            ids = lax.broadcasted_iota(jnp.int32, (TILE, CHUNK), 0) + here
            hot = rows_equal(ids.astype(F32), rank_ref[:, piece])
            total = total + lax.dot_general(parts[:, piece], hot, NT, preferred_element_type=F32)
        total = total[:rows] + total[rows:]
        if steps is not None:
            line = lax.broadcasted_iota(jnp.int32, (rows, TILE), 0)
            total = jnp.where(line == rows - 1, jnp.concatenate([steps] * (TILE // LANES), axis=1), total)
        out_ref[:, pl.ds(pl.multiple_of(n * TILE, TILE), TILE)] = total
        return 0

    lax.fori_loop(0, out_ref.shape[1] // TILE, step, 0)


def sort_kernel(parts_ref, rank_ref, out_ref):
    sort_tiles(parts_ref, rank_ref, None, out_ref, out_ref.shape[1] // TILE)


def sort_call(parts, rank):
    rows, count = parts.shape[0] // 2, parts.shape[1]
    return pl.pallas_call(
        sort_kernel,
        out_shape=jax.ShapeDtypeStruct((rows, count // 2), F32),
        in_specs=[VMEM] * 2,
        out_specs=VMEM,
        compiler_params=params(8),
        cost_estimate=pl.CostEstimate(flops=2 * rows * count * count, bytes_accessed=4 * rows * count, transcendentals=0),
        name="sort",
    )(parts, rank)


def unsort_kernel(half, given, rank_ref, *refs):
    xs, refs = refs[:given], refs[given:]
    before, (flat_ref,) = (refs[:1], refs[1:2]) if half else ((), (None,))
    out_ref, parts = refs[-2:]
    rows, count = xs[0].shape[0], rank_ref.shape[1]
    width = xs[0].shape[1]

    @pl.when(pl.program_id(0) == 0)
    def _():
        x = xs[0][...]
        for more in xs[1:]:
            x = x + more[...]
        high = x.astype(BF16).astype(F32)
        parts[...] = jnp.concatenate([high, x - high], axis=0).astype(BF16)

    total = jnp.zeros((2 * rows, TILE), F32)
    for k in range(width // CHUNK):
        ids = lax.broadcasted_iota(jnp.int32, (CHUNK, TILE), 0) + (half * width + k * CHUNK)
        hot = rows_equal(ids.astype(F32), rank_ref[:, pl.ds(pl.multiple_of(pl.program_id(0) * TILE, TILE), TILE)])
        piece = parts[:, k * CHUNK : (k + 1) * CHUNK]
        total = total + lax.dot_general(piece, hot, NN, preferred_element_type=F32)
    total = total[:rows] + total[rows:]
    if not half:
        out_ref[...] = total
        return
    total = total + before[0][...]
    species = rows - 2
    ratio = 0.5 / total[species : species + 1]
    for n in range(TILE // LANES):
        piece = slice(n * LANES, (n + 1) * LANES)
        line = pl.program_id(0) * (TILE // LANES) + n
        value = 0.5 * flat_ref[:species, piece] + total[:species, piece] * ratio[:, piece]
        out_ref[pl.ds(line, species, stride=count // LANES), :] = value


def unsort_call(wholes, piece, rank, before, flat):
    half = int(before is not None)
    rows, count = wholes[0].shape
    part = pl.BlockSpec((rows, count // 2), lambda i: (0, half))
    column = pl.BlockSpec((rows, TILE), lambda i: (0, i))
    args = [rank, *wholes, piece]
    specs = [whole(rank.shape)] + [part] * len(wholes) + [whole(piece.shape)]
    out_shape, out_spec = (rows, count), column
    if half:
        args += [before, flat]
        specs += [column, column]
        lines = (rows - 2) * count // LANES
        out_shape, out_spec = (lines, LANES), whole((lines, LANES))
    return pl.pallas_call(
        functools.partial(unsort_kernel, half, len(wholes) + 1),
        grid=(count // TILE,),
        out_shape=jax.ShapeDtypeStruct(out_shape, F32),
        in_specs=specs,
        out_specs=out_spec,
        scratch_shapes=[pltpu.VMEM((2 * rows, count // 2), BF16)],
        compiler_params=params(12),
        cost_estimate=pl.CostEstimate(flops=2 * rows * count * count, bytes_accessed=4 * rows * count, transcendentals=0),
        name="unsort",
    )(*args)


def weights_of(key, table, bins, per_tile):
    nshape = table.shape[1]
    cell = jnp.floor((key + 0.5) * (1.0 / nshape))
    shape = key - cell * nshape
    tile = jnp.floor((cell + 0.5) * (1.0 / per_tile))
    within = cell - tile * per_tile
    ids = lax.broadcasted_iota(jnp.int32, (nshape, key.shape[1]), 0).astype(F32).astype(BF16)
    hot = jnp.where(ids == shape.astype(BF16), jnp.ones((), BF16), jnp.zeros((), BF16))
    picked = lax.dot_general(table, hot, NN, preferred_element_type=F32).astype(BF16)
    masks = [jnp.where(within == m, 1.0, 0.0).astype(BF16) for m in range(per_tile)]
    columns = []
    for part in (picked[:bins], picked[bins:]):
        columns.append(jnp.concatenate([part * mask for mask in masks], axis=0))
    return jnp.concatenate(columns, axis=1), tile


def split_table(table):
    high = table.astype(BF16).astype(F32)
    return jnp.concatenate([high, table - high], axis=0).astype(BF16)


def prepare_weights(source, index, key_row, table, bins, per_tile, weights, tiles):
    def step(n, _):
        key = source[key_row : key_row + 1, pl.ds(pl.multiple_of(n * LANES, LANES), LANES)]
        block, tile = weights_of(key, table, bins, per_tile)
        weights[index + n] = block
        tiles[index + n] = jnp.broadcast_to(tile, tiles.shape[1:])
        return 0

    lax.fori_loop(0, source.shape[1] // LANES, step, 0, unroll=4)


def collect_kernel(species, bins, per_tile, pairs, lists, *refs):
    sources, refs = [refs[2 * n : 2 * n + 2] for n in range(lists)], refs[2 * lists :]
    table_ref, out_ref, *refs = refs
    weights, tiles, *refs = refs
    keys, (parts, steps, sems) = refs[:lists], refs[lists:]
    copies = fetch_rows([source[0] for source in sources], steps, sems)
    rows, part = sources[0][0].shape
    count = 2 * part
    for key, source in zip(keys, sources):
        key[...] = source[0][rows - 8 :, :LANES]
    blocks = count // LANES
    out_ref[...] = jnp.zeros_like(out_ref)
    table = split_table(table_ref[...])
    line = lax.broadcasted_iota(jnp.int32, (rows, LANES), 0)
    for number in range(2 * lists):
        source = sources[number // 2][number % 2]
        start = number * blocks // 2
        prepare_weights(source, start, species, table, bins, per_tile, weights, tiles)

        def split(n, _, source=source, start=start):
            x = source[:, pl.ds(pl.multiple_of(n * LANES, LANES), LANES)]
            x = jnp.where(line < species, x, jnp.where(line == species, 1.0, 0.0))
            parts[start + n] = padded_halves(x)
            return 0

        lax.fori_loop(0, blocks // 2, split, 0, unroll=4)

    for copy in copies:
        copy.wait()

    def step(n, _):
        for number in range(lists):
            for g in range(GROUP):
                k = n * GROUP + g
                tile = steps[number, 7, k].astype(jnp.int32)
                block = jnp.minimum(k - tile, blocks - 1) + number * blocks
                wanted = jnp.where(k < pairs, tile, -1).astype(F32)
                mask = jnp.where(tiles[block] == wanted, 1.0, 0.0).astype(BF16)
                mask = jnp.concatenate([mask] * (2 * HALF // mask.shape[0]), axis=0)
                x = parts[block] * mask
                both = jnp.concatenate([x, x], axis=1)
                got = lax.dot_general(both, weights[block], NT, preferred_element_type=F32)
                place = pl.ds(pl.multiple_of(tile * TILE, TILE), TILE)
                out_ref[:, place] += got[:rows] + got[HALF : HALF + rows]
        return 0

    lax.fori_loop(0, -(-pairs // GROUP), step, 0)


def collect_call(sources, table, species, bins, per_tile, ntiles):
    rows, count = sources[0][0].shape[0], 2 * sources[0][0].shape[1]
    lists, blocks = len(sources), count // LANES
    pairs = blocks + ntiles - 1
    args = [half for source in sources for half in source] + [table]
    specs = [VMEM] * (2 * lists + 1)
    return pl.pallas_call(
        functools.partial(collect_kernel, species, bins, per_tile, pairs, lists),
        out_shape=[
            jax.ShapeDtypeStruct((rows, ntiles * TILE), F32),
            jax.ShapeDtypeStruct((lists * blocks, TILE, 2 * LANES), BF16),
            jax.ShapeDtypeStruct((lists * blocks, 16, LANES), F32),
        ]
        + [jax.ShapeDtypeStruct((8, LANES), F32)] * lists,
        in_specs=specs,
        out_specs=[VMEM] * (lists + 3),
        scratch_shapes=[
            pltpu.VMEM((lists * blocks, 2 * HALF, LANES), BF16),
            pltpu.SMEM((lists, 8, LANES), F32),
            pltpu.SemaphoreType.DMA((lists,)),
        ],
        compiler_params=params(19),
        cost_estimate=pl.CostEstimate(flops=lists * pairs * 2 * LANES * TILE * TILE, bytes_accessed=0, transcendentals=0),
        name="collect",
    )(*args)


def turn_back(mean, out_ref, bins, quads, turned):
    rows, width = mean.shape
    lines = width // LANES
    fold = LANES // bins
    for q in range(lines):
        quads[pl.ds(q, rows, stride=lines), :] = mean[:, q * LANES : (q + 1) * LANES]
    blocked = lax.broadcasted_iota(jnp.int32, (lines, LANES), 1) // bins

    def turn(g):
        source = [quads[pl.ds(pl.multiple_of(g * LANES + k * lines, lines), lines), :] for k in range(fold)]
        for r in range(fold):
            out = source[r]
            for k in range(fold):
                if k != r:
                    out = jnp.where(blocked == k, pltpu.roll(source[k], (k - r) * bins % LANES, 1), out)
            turned[pl.ds(r, lines, stride=fold), :] = out
        return turned[...].T

    full, rest = out_ref.shape[0] // LANES, out_ref.shape[0] % LANES

    def step(g, _):
        out_ref[pl.ds(pl.multiple_of(g * LANES, LANES), LANES), :] = turn(g)
        return 0

    lax.fori_loop(0, full, step, 0)
    if rest:
        out_ref[full * LANES :, :] = turn(full)[:rest]


def project_kernel(bins, pairs, lists, state_rows, *refs):
    parts, weights, tiles, *refs = refs
    sources, refs = refs[:lists], refs[lists:]
    mean = refs.pop(0) if state_rows else None
    outs, refs = refs[:lists], refs[lists:]
    state_ref = refs.pop(0) if state_rows else None
    steps, sems, *turning = refs
    copies = fetch_rows(sources, steps, sems)
    rows, count = outs[0].shape
    blocks = count // LANES
    for out in outs:
        out[...] = jnp.zeros_like(out)
    if state_rows:
        turn_back(mean, state_ref, bins, *turning)
    for copy in copies:
        copy.wait()

    def step(n, _):
        for number in range(lists):
            for g in range(GROUP):
                k = n * GROUP + g
                tile = steps[number, 7, k].astype(jnp.int32)
                local = jnp.minimum(k - tile, blocks - 1)
                block = local + number * blocks
                wanted = jnp.where(k < pairs, tile, -1).astype(F32)
                got = lax.dot_general(parts[tile], weights[block], NN, preferred_element_type=F32)
                got = got[:rows] + got[HALF : HALF + rows]
                got = got[:, :LANES] + got[:, LANES:]
                got = jnp.where(tiles[block][:1] == wanted, got, 0.0)
                place = pl.ds(pl.multiple_of(local * LANES, LANES), LANES)
                outs[number][:, place] += got
        return 0

    lax.fori_loop(0, -(-pairs // GROUP), step, 0)


def project_call(parts, collected, rows, count, bins, ntiles, mean=None, state_rows=0):
    weights, tiles, *sources = collected
    lists = len(sources)
    pairs = count // LANES + ntiles - 1
    extra = [] if mean is None else [mean]
    scratch = [pltpu.SMEM((lists, 8, LANES), F32), pltpu.SemaphoreType.DMA((lists,))]
    if extra:
        scratch += [pltpu.VMEM((mean.size // LANES, LANES), F32), pltpu.VMEM((LANES, LANES), F32)]
    return pl.pallas_call(
        functools.partial(project_kernel, bins, pairs, lists, state_rows),
        out_shape=[jax.ShapeDtypeStruct((rows, count), F32)] * lists
        + [jax.ShapeDtypeStruct((state_rows, LANES), F32)] * len(extra),
        in_specs=[VMEM] * (3 + lists + len(extra)),
        out_specs=[VMEM] * (lists + len(extra)),
        scratch_shapes=scratch,
        compiler_params=params(20),
        cost_estimate=pl.CostEstimate(flops=lists * pairs * 2 * LANES * TILE * TILE, bytes_accessed=0, transcendentals=0),
        name="project",
    )(parts, weights, tiles, *sources, *extra)


def middle_kernel(species, bins, chunk, refs_in, refs_out, scratch):
    *accs, cmc_ref, diss_ref, rate_ref, count_ref, matrix_ref = refs_in
    fresh_ref, parts_ref = refs_out
    next_ref, far_ref, nat, quads, turned, side_out, load, outward, hopped, summed, got, state_ref, edge_out, edge_in, side_in, pick_ref, third_ref, send, recv, side_send, side_recv = scratch
    rows, width = fresh_ref.shape
    steps = width // chunk
    slab, nslab = lax.axis_index("slab"), lax.axis_size("slab")
    cross, ncross = lax.axis_index("cross"), lax.axis_size("cross")
    parity = lax.rem(slab, 2)
    outer = slab + 4 * parity - 2
    inner = slab - 4 * parity + 2
    partner = slab + 1 - 2 * parity
    has_outer = (outer >= 0) & (outer < nslab)
    has_inner = (inner >= 0) & (inner < nslab)
    has_before, has_after = cross > 0, cross < ncross - 1
    has_down, has_up = slab > 0, slab < nslab - 1
    mesh = pl.DeviceIdType.MESH

    def partial_sum(piece):
        total = accs[0][:, piece]
        for more in accs[1:]:
            total = total + more[:, piece]
        return total

    loads, start = [], 0
    for n, source in enumerate((cmc_ref, diss_ref, rate_ref)):
        target = nat.at[start : start + source.shape[0]]
        loads.append(pltpu.make_async_copy(source, target, load.at[n]))
        loads[-1].start()
        start += source.shape[0]
    if start < nat.shape[0]:
        nat[start:, :] = jnp.zeros((nat.shape[0] - start, LANES), F32)
    outward[...] = partial_sum(slice(0, width))

    @pl.when(jnp.logical_not(has_inner))
    def _():
        hopped[...] = jnp.zeros_like(hopped)

    @pl.when(jnp.logical_not(has_outer))
    def _():
        far_ref[...] = jnp.zeros_like(far_ref)

    @pl.when(jnp.logical_not(has_before))
    def _():
        edge_in[:, :, :LANES] = jnp.zeros(edge_in.shape[:2] + (LANES,), F32)

    @pl.when(jnp.logical_not(has_after))
    def _():
        edge_in[:, :, LANES:] = jnp.zeros(edge_in.shape[:2] + (LANES,), F32)

    @pl.when(jnp.logical_not(has_down))
    def _():
        side_in[0] = jnp.zeros(side_in.shape[1:], F32)

    @pl.when(jnp.logical_not(has_up))
    def _():
        side_in[1] = jnp.zeros(side_in.shape[1:], F32)

    barrier = pltpu.get_barrier_semaphore()
    greet = lambda where: pl.semaphore_signal(barrier, inc=1, device_id=where, device_id_type=mesh)
    pl.when(has_down)(lambda: greet({"slab": slab - 1}))
    pl.when(has_up)(lambda: greet({"slab": slab + 1}))
    pl.when(has_outer)(lambda: greet({"slab": outer}))
    pl.when(has_inner)(lambda: greet({"slab": inner}))
    pl.when(has_before)(lambda: greet({"cross": cross - 1}))
    pl.when(has_after)(lambda: greet({"cross": cross + 1}))
    number = lambda flag: jnp.where(flag, 1, 0)
    flags = (has_down, has_up, has_outer, has_inner, has_before, has_after)
    pl.semaphore_wait(barrier, sum(number(flag) for flag in flags))

    def lanes(c, base=0):
        return pl.ds(pl.multiple_of(base + c * chunk, chunk), chunk)

    def remote(kind, c, source, target, where):
        return pltpu.make_async_remote_copy(
            src_ref=source, dst_ref=target, send_sem=send.at[kind, c], recv_sem=recv.at[kind, c],
            device_id=where, device_id_type=mesh,
        )

    to_outer = lambda c: remote(0, c, outward.at[:, lanes(c)], hopped.at[:, lanes(c)], {"slab": outer})
    to_partner = lambda c: remote(1, c, summed.at[:, lanes(c)], got.at[:, lanes(c)], {"slab": partner})
    to_after = lambda c: remote(2, c, edge_out.at[c, :, LANES:], edge_in.at[c, :, :LANES], {"cross": cross + 1})
    to_before = lambda c: remote(3, c, edge_out.at[c, :, :LANES], edge_in.at[c, :, LANES:], {"cross": cross - 1})
    give = lambda c: remote(4, c, fresh_ref.at[:, lanes(c)], next_ref.at[:, lanes(c)], {"slab": partner})
    pass_on = lambda c: remote(5, c, next_ref.at[:, lanes(c)], far_ref.at[:, lanes(c)], {"slab": inner})

    def side(n, source, where):
        return pltpu.make_async_remote_copy(
            src_ref=source, dst_ref=side_in.at[n], send_sem=side_send.at[n], recv_sem=side_recv.at[n],
            device_id=where, device_id_type=mesh,
        )

    to_up = side(0, side_out.at[0], {"slab": slab + 1})
    to_down = side(1, side_out.at[1], {"slab": slab - 1})

    def start_hops(chunks):
        @pl.when(has_outer)
        def _():
            for c in chunks:
                to_outer(c).start()

    start_hops(range(2))
    for copy in loads:
        copy.wait()
    lines = width // LANES
    fold = LANES // bins
    blocked = lax.broadcasted_iota(jnp.int32, (LANES // fold, LANES), 1) // bins

    def turn(g, _):
        turned[...] = nat[pl.ds(pl.multiple_of(g * LANES, LANES), LANES), :].T
        parts = [turned[pl.ds(r, LANES // fold, stride=fold), :] for r in range(fold)]
        for k in range(fold):
            out = parts[k]
            for r in range(fold):
                if r != k:
                    out = jnp.where(blocked == r, pltpu.roll(parts[r], (r - k) * bins % LANES, 1), out)
            place = pl.multiple_of(g * LANES + k * lines, lines)
            quads[pl.ds(place, lines), :] = out
        return 0

    lax.fori_loop(0, nat.shape[0] // LANES, turn, 0)
    tile = lambda q: quads[pl.ds(q, rows, stride=lines), :]
    side_out[0] = tile(lines - 1)
    side_out[1] = tile(0)

    lane = lax.broadcasted_iota(jnp.int32, (2 * LANES, chunk), 1)
    row = lax.broadcasted_iota(jnp.int32, (2 * LANES, chunk), 0)
    target = jnp.where(row < LANES, row * bins, (row - LANES) * bins + bins - 1)
    pick_ref[...] = rows_equal(target, lane)
    third = matrix_ref.shape[1] // 3
    high, low = halves(matrix_ref[...])
    column = lax.broadcasted_iota(jnp.int32, matrix_ref.shape, 1)
    third_ref[...] = jnp.where(column < 2 * third, high.astype(F32), low.astype(F32)).astype(BF16)
    line = lax.broadcasted_iota(jnp.int32, (rows, chunk), 0)
    slot = lax.broadcasted_iota(jnp.int32, (rows, chunk), 1) % bins
    gap = [jnp.zeros((third - rows, chunk), F32)] * (third > rows)

    pl.when(has_up)(to_up.start)
    pl.when(has_down)(to_down.start)
    start_hops(range(2, steps))

    def stacked(x):
        high = x.astype(BF16).astype(F32)
        return jnp.concatenate([high, x - high], axis=0).astype(BF16)

    def add_hop(c):
        pl.when(has_inner)(lambda: to_outer(c).wait_recv())
        summed[:, lanes(c)] = partial_sum(lanes(c, 2 * width)) + hopped[:, lanes(c)]

    per = chunk // LANES

    def advect(c):
        here = jnp.concatenate([tile(c * per + n) for n in range(per)], axis=1)
        low = jnp.where(c == 0, side_in[0], tile(jnp.maximum(c * per - 1, 0)))
        high = jnp.where(c == steps - 1, side_in[1], tile(jnp.minimum((c + 1) * per, lines - 1)))
        left = pltpu.roll(jnp.concatenate([low, here], axis=1), bins, 1)[:, LANES:]
        right = pltpu.roll(jnp.concatenate([here, high], axis=1), chunk + LANES - bins, 1)[:, :chunk]
        return here - 0.4 * (here - left) + 0.1 * (right - 2.0 * here + left)

    def cell_row(n, c):
        start = (species + n) * lines + c * per
        return jnp.concatenate([quads[pl.ds(start + k, 1), :] for k in range(per)], axis=1)

    def blend(c):
        total = partial_sum(lanes(c, width)) + got[:, lanes(c)]
        blended = (total + advect(c)) / (total[species : species + 1] + 1.0)
        state_ref[:, lanes(c)] = blended
        edge = lax.dot_general(stacked(blended), pick_ref[...], NT, preferred_element_type=F32)
        edge_out[c] = edge[:rows] + edge[rows:]

    def send_edges(c):
        pl.when(has_after)(lambda: to_after(c).start())
        pl.when(has_before)(lambda: to_before(c).start())

    def wait_edges(c):
        pl.when(has_before)(lambda: to_after(c).wait_recv())
        pl.when(has_after)(lambda: to_before(c).wait_recv())

    def react(c):
        here = state_ref[:, lanes(c)]
        around = lax.dot_general(stacked(edge_in[c]), pick_ref[...], NN, preferred_element_type=F32)
        around = around[:rows] + around[rows:]
        before = jnp.where(slot == 0, around, pltpu.roll(here, 1, 1))
        after = jnp.where(slot == bins - 1, around, pltpu.roll(here, chunk - 1, 1))
        state = here + cell_row(0, c) * (after - 2.0 * here + before)
        half = 0.5 * cell_row(1, c)
        count = count_ref[:, lanes(c)]
        for k in range(KMAX):
            high, low = (part.astype(F32) for part in halves(state))
            stack = jnp.concatenate([high, *gap, low, *gap, high, *gap], axis=0).astype(BF16)
            rate = lax.dot_general(third_ref[...], stack, NN, preferred_element_type=F32)
            state = jnp.where(k < count, state + half * jnp.tanh(rate), state)
        state = jnp.where(line == species, 1.0, state)
        fresh_ref[:, lanes(c)] = state
        keep(1, c, state)

    def keep(which, c, mean):
        for n in range(chunk // TILE):
            index = which * (width // TILE) + c * (chunk // TILE) + n
            parts_ref[index] = padded_halves(mean[:, n * TILE : (n + 1) * TILE])

    def step(t, _):
        def when(lag, body):
            c = t - lag
            pl.when((c >= 0) & (c < steps))(lambda: body(c))

        def second(c):
            pl.when((c == 0) & has_down)(to_up.wait_recv)
            pl.when((c == 0) & has_up)(to_down.wait_recv)
            to_partner(c).wait_recv()
            blend(c)

        def third_stage(c):
            wait_edges(c)
            react(c)

        def fourth(c):
            give(c).wait_recv()
            pl.when(has_inner)(lambda: pass_on(c).start())
            keep(2, c, next_ref[:, lanes(c)])

        when(0, add_hop)
        when(LAG[0], second)
        when(0, lambda c: to_partner(c).start())
        when(LAG[1], third_stage)
        when(LAG[0], send_edges)
        when(LAG[2], fourth)
        when(LAG[1], lambda c: give(c).start())
        return 0

    lax.fori_loop(0, steps + LAG[2], step, 0)

    def finish(c, _):
        pl.when(has_outer)(lambda: to_outer(c).wait_send())
        to_partner(c).wait_send()
        pl.when(has_after)(lambda: to_after(c).wait_send())
        pl.when(has_before)(lambda: to_before(c).wait_send())
        give(c).wait_send()
        pl.when(has_inner)(lambda: pass_on(c).wait_send())
        pl.when(has_outer)(lambda: pass_on(c).wait_recv())
        keep(0, c, far_ref[:, lanes(c)])
        return 0

    lax.fori_loop(0, steps, finish, 0)
    pl.when(has_up)(to_up.wait_send)
    pl.when(has_down)(to_down.wait_send)


def middle_call(accs, cmc, diss, rate, count, matrix, species, bins, chunk=256):
    rows, width = accs[0].shape[0], count.shape[1]
    steps = width // chunk
    given = len(accs) + 5

    def kernel(*refs):
        middle_kernel(species, bins, chunk, refs[:given], refs[given : given + 2], refs[given + 2 :])

    return pl.pallas_call(
        kernel,
        out_shape=[
            jax.ShapeDtypeStruct((rows, width), F32),
            jax.ShapeDtypeStruct((3 * width // TILE, 2 * HALF, TILE), BF16),
        ],
        in_specs=[VMEM] * len(accs) + [pl.BlockSpec(memory_space=pl.ANY)] * 3 + [VMEM] * 2,
        out_specs=[VMEM] * 2,
        scratch_shapes=[pltpu.VMEM((rows, width), F32)] * 2
        + [pltpu.VMEM((rows * bins, LANES), F32), pltpu.VMEM((rows * width // LANES, LANES), F32)]
        + [pltpu.VMEM((LANES, LANES), F32), pltpu.VMEM((2, rows, LANES), F32), pltpu.SemaphoreType.DMA((3,))]
        + [pltpu.VMEM((rows, width), F32)] * 5
        + [pltpu.VMEM((steps, rows, 2 * LANES), F32)] * 2
        + [pltpu.VMEM((2, rows, LANES), F32), pltpu.VMEM((2 * LANES, chunk), BF16), pltpu.VMEM(matrix.shape, BF16)]
        + [pltpu.SemaphoreType.DMA((6, steps))] * 2
        + [pltpu.SemaphoreType.DMA((2,))] * 2,
        compiler_params=pltpu.CompilerParams(vmem_limit_bytes=22 << 20, collective_id=1, has_side_effects=True),
        name="middle",
    )(*accs, cmc, diss, rate, count, matrix)


def on_device(
    les_state, cmc_state, cmc_map, pdf_index, pdf_table, diffusion, chem_matrix, dissipation, reaction_rate, substeps
):
    species = les_state.shape[0]
    rows = -(-(species + 2) // 8) * 8
    bins, cells = cmc_state.shape[1:]
    nshape = pdf_table.shape[0]
    count = cmc_map.size
    ncross = lax.axis_size("cross")
    per_tile = TILE // bins
    ntiles = 3 * cells // per_tile
    flat, rank, parts, low = head_call(
        les_state, cmc_map, pdf_index, diffusion, rows, cells, nshape, ntiles, nshape * per_tile
    )
    bits = [1 << k for k in range(ncross.bit_length() - 1)]
    low_there = swap(low, "cross", bits[-1])
    high = sort_call(parts, rank)
    high_there = swap(high, "cross", bits[-1])
    near_lists = [(low, high)] + [(swap(low, "cross", bit), swap(high, "cross", bit)) for bit in bits[:-1]]
    low_far = [low_there] + [swap(low_there, "cross", bit) for bit in bits[:-1]]

    table = lax.dynamic_slice_in_dim(pdf_table.T, lax.axis_index("cross") * bins, bins, axis=0)

    extra = rows - species
    matrix = jnp.tile(jnp.pad(chem_matrix, ((0, extra), (0, -(-rows // 16) * 16 - species))), (1, 3))
    terms = (cmc_state.reshape(species * bins, cells), dissipation, reaction_rate, jnp.repeat(substeps, bins)[None, :], matrix)
    acc, *near = collect_call(near_lists, table, species, bins, per_tile, ntiles)
    acc, high_there, terms = lax.optimization_barrier((acc, high_there, terms))
    high_far = [high_there] + [swap(high_there, "cross", bit) for bit in bits[:-1]]
    accs, far = [acc], []
    for pair in zip(low_far, high_far):
        acc, *collected = collect_call([pair], table, species, bins, per_tile, ntiles)
        accs.append(acc)
        far.append(collected)
    fresh, parts = middle_call(accs, *terms, species, bins)

    pieces = []
    for bit, collected in zip(bits[:-1], far[1:]):
        (piece,) = project_call(parts, collected, rows, count, bins, ntiles)
        piece, parts = lax.optimization_barrier((piece, parts))
        pieces.append(swap(piece, "cross", bit))
    (there,) = project_call(parts, far[0], rows, count, bins, ntiles)
    part = count // 2
    low, high = there[:, :part], there[:, part:]
    for piece in pieces:
        low, high = low + piece[:, :part], high + piece[:, part:]
    low, parts = lax.optimization_barrier((low, parts))
    low = swap(low, "cross", bits[-1])
    high = swap(high, "cross", bits[-1])
    *here, cmc_out = project_call(parts, near, rows, count, bins, ntiles, fresh, species * bins)
    total = [here[0]] + [swap(piece, "cross", bit) for bit, piece in zip(bits[:-1], here[1:])]
    before = unsort_call(total, low, rank, None, None)
    les_out = unsort_call(total, high, rank, before, flat)
    return (les_out.reshape(les_state.shape), cmc_out.reshape(species, bins, cells))


def solution(mesh):
    return jax.shard_map(
        on_device,
        mesh=mesh,
        in_specs=(
            P(None, "slab", "cross", None),
            P(None, "cross", "slab"),
            P("slab", "cross", None),
            P("slab", "cross", None),
            P(),
            P(),
            P(),
            P("cross", "slab"),
            P("cross", "slab"),
            P("slab"),
        ),
        out_specs=(P(None, "slab", "cross", None), P(None, "cross", "slab")),
        check_vma=False,
    )
```

```python
import functools


import jax
import jax.numpy as jnp
from jax import lax
from jax.experimental import pallas as pl
from jax.experimental.pallas import tpu as pltpu
from jax.sharding import PartitionSpec as P

KMAX = 4
F32 = jnp.float32
BF16 = jnp.bfloat16
NT = (((1,), (1,)), ((), ()))
NN = (((1,), (0,)), ((), ()))
LANES = 128
TILE = 256
HALF = 64
GROUP = 16
LAG = (3, 6, 9)


def swap(array, axis, bit):
    count = lax.axis_size(axis)
    return lax.ppermute(array, axis, [(i, i ^ bit) for i in range(count)])


def halves(x):
    high = x.astype(BF16)
    return high, (x - high.astype(F32)).astype(BF16)


def padded_halves(x):
    gap = jnp.zeros((HALF - x.shape[0], x.shape[1]), F32)
    high = x.astype(BF16).astype(F32)
    return jnp.concatenate([high, gap, x - high, gap], axis=0).astype(BF16)


def rows_equal(targets, row):
    return jnp.where(targets == row, 1.0, 0.0).astype(BF16)


def whole(shape):
    return pl.BlockSpec(shape, lambda *_: (0,) * len(shape))


VMEM = pl.BlockSpec(memory_space=pltpu.VMEM)
SMEM = pl.BlockSpec(memory_space=pltpu.SMEM)


def params(mib):
    return pltpu.CompilerParams(vmem_limit_bytes=mib << 20)


def fetch_rows(sources, steps, sems):
    copies = []
    for number, source in enumerate(sources):
        last = source.at[source.shape[0] - 8 : source.shape[0], :LANES]
        copies.append(pltpu.make_async_copy(last, steps.at[number], sems.at[number]))
        copies[-1].start()
    return copies


def ranks(tiles, span, key_ref, rank_ref, table_ref):
    count = rank_ref.shape[1]
    ids = lax.broadcasted_iota(jnp.int32, (tiles, TILE), 0).astype(F32)
    tile_of = lambda n: jnp.floor((key_ref[:1, n * TILE : (n + 1) * TILE] + 0.5) * (1.0 / span))
    total = jnp.zeros((tiles, TILE), F32)
    for n in range(count // TILE):
        total = total + jnp.where(ids == tile_of(n), 1.0, 0.0)
    total = jnp.sum(total, axis=1, keepdims=True)
    total = jnp.broadcast_to(total, (tiles, LANES))
    big = jnp.floor(total * (1.0 / HALF))
    row = lax.broadcasted_iota(jnp.int32, (tiles, tiles), 0)
    below = rows_equal(jnp.where(lax.broadcasted_iota(jnp.int32, (tiles, tiles), 1) < row, 1, 0), 1)
    add = lambda part: lax.dot_general(below, part.astype(BF16), NN, preferred_element_type=F32)
    base = add(big) * HALF + add(total - big * HALF)
    order = lax.broadcasted_iota(jnp.int32, (tiles, LANES), 0).astype(F32)
    lane = lax.broadcasted_iota(jnp.int32, (tiles, LANES), 1).astype(F32)
    last = jnp.maximum(jnp.ceil((base + total) * (1.0 / LANES)) - 1.0, 0.0) + order
    passed = jnp.where((last < lane) & (order < tiles - 1), 1.0, 0.0)
    table_ref[...] = jnp.sum(passed, axis=0, keepdims=True)
    ahead = jnp.where(
        lax.broadcasted_iota(jnp.int32, (TILE, TILE), 0) < lax.broadcasted_iota(jnp.int32, (TILE, TILE), 1), 1.0, 0.0
    ).astype(BF16)
    carry = base[:, :1]
    for n in range(count // TILE):
        hot = jnp.where(ids == tile_of(n), 1.0, 0.0)
        before = lax.dot_general(hot.astype(BF16), ahead, NN, preferred_element_type=F32) + carry
        rank_ref[:, n * TILE : (n + 1) * TILE] = jnp.sum(hot * before, axis=0, keepdims=True)
        carry = carry + jnp.sum(hot, axis=1, keepdims=True)


HALO_ORDER = {2: lambda n: (), 3: lambda n: range(1, n - 1), 0: lambda n: (), 1: lambda n: sorted({0, n - 1})}


def head_kernel(grid_shape, cells, nshape, tiles, span, *refs):
    given, (t_ref, rank_ref, parts_ref, half_ref), refs = refs[:4], refs[4:8], refs[8:]
    les_ref, map_ref, shape_ref, diff_ref, key_ref, table_ref, *refs = refs
    faces, halos, (send, recv, load) = refs[:4], refs[4:8], refs[8:]
    loads = [
        pltpu.make_async_copy(source, target, load.at[n])
        for n, (source, target) in enumerate(zip(given, (les_ref, map_ref, shape_ref, diff_ref)))
    ]
    for copy in loads:
        copy.start()
    species, nx, ny = grid_shape
    count = rank_ref.shape[1]
    slab, nslab = lax.axis_index("slab"), lax.axis_size("slab")
    cross, ncross = lax.axis_index("cross"), lax.axis_size("cross")
    mesh = pl.DeviceIdType.MESH
    sides = [
        (slab > 0, {"slab": slab - 1}),
        (slab < nslab - 1, {"slab": slab + 1}),
        (cross > 0, {"cross": cross - 1}),
        (cross < ncross - 1, {"cross": cross + 1}),
    ]
    barrier = pltpu.get_barrier_semaphore()
    for n, (there, where) in enumerate(sides):

        @pl.when(jnp.logical_not(there))
        def _(n=n):
            halos[n][...] = jnp.zeros_like(halos[n])

    for copy in loads:
        copy.wait()
    line = lambda x, y: les_ref[pl.ds(x * ny + y, species, stride=nx * ny), :]
    for n, x in enumerate((0, nx - 1)):
        for y in range(ny):
            faces[n][y, :species] = line(x, y)
    for n, y in enumerate((0, ny - 1)):
        for x in range(nx):
            faces[2 + n][x, :species] = line(x, y)
    for there, where in sides:

        @pl.when(there)
        def _(where=where):
            pl.semaphore_signal(barrier, inc=1, device_id=where, device_id_type=mesh)

    pl.semaphore_wait(barrier, sum(jnp.where(there, 1, 0) for there, _ in sides))
    copies = []
    for n, (there, where) in enumerate(sides):
        copy = pltpu.make_async_remote_copy(
            src_ref=faces[n], dst_ref=halos[n ^ 1], send_sem=send.at[n], recv_sem=recv.at[n ^ 1],
            device_id=where, device_id_type=mesh,
        )
        pl.when(there)(copy.start)
        copies.append(copy)
    offset = map_ref[...] - (slab - 1) * cells
    block = jnp.where(offset >= cells, 1, 0) + jnp.where(offset >= 2 * cells, 1, 0)
    offset = jnp.where(lax.rem(slab, 2) == 1, (2 - block) * cells + offset - block * cells, offset)
    key = (offset * nshape + shape_ref[...]).astype(F32)
    key_ref[:1, :] = key
    t_ref[species:, :] = jnp.concatenate([key] + [jnp.zeros((t_ref.shape[0] - species - 1, count), F32)], axis=0)
    ranks(tiles, span, key_ref, rank_ref, table_ref)
    row = lax.broadcasted_iota(jnp.int32, (species, species), 0)
    number = jnp.where(row == lax.broadcasted_iota(jnp.int32, (species, species), 1), diff_ref[...], 0.0)
    number = jnp.sum(number, axis=1, keepdims=True)
    lane = lax.broadcasted_iota(jnp.int32, (species, LANES), 1)
    for n in (2, 3, 0, 1):
        pl.when(sides[n ^ 1][0])(copies[n].wait_recv)
        for x, y in [(x, y) for x in HALO_ORDER[n](nx) for y in range(ny)]:
            here = line(x, y)
            around = line(x + 1, y) if x < nx - 1 else halos[1][y, :species]
            around = around + (line(x - 1, y) if x else halos[0][y, :species])
            around = around + (line(x, y + 1) if y < ny - 1 else halos[3][x, :species])
            around = around + (line(x, y - 1) if y else halos[2][x, :species])
            around = around + jnp.where(lane < LANES - 1, pltpu.roll(here, LANES - 1, 1), 0.0)
            around = around + jnp.where(lane > 0, pltpu.roll(here, 1, 1), 0.0)
            place = (x * ny + y) * LANES
            t_ref[:species, place : place + LANES] = here + number * (around - 6.0 * here)
        planes = list(HALO_ORDER[n](nx))
        for x in planes:
            piece = slice(x * ny * LANES, (x + 1) * ny * LANES)
            value = t_ref[:, piece]
            high = value.astype(BF16).astype(F32)
            parts_ref[:, piece] = jnp.concatenate([high, value - high], axis=0).astype(BF16)
        if planes and ny * LANES == CHUNK:
            last = n == 1
            sort_tiles(parts_ref, rank_ref, table_ref[...] if last else None, half_ref, 0, planes, last and nx > 2)
    if ny * LANES != CHUNK:
        sort_tiles(parts_ref, rank_ref, table_ref[...], half_ref, 0)
    for n, (there, _) in enumerate(sides):
        pl.when(there)(copies[n].wait_send)


def head_call(les_state, cmc_map, pdf_index, diffusion, rows, cells, nshape, tiles, span):
    species, nx, ny, nz = les_state.shape
    count = nx * ny * nz
    halo = [pltpu.VMEM((n, rows, LANES), F32) for n in (ny, ny, nx, nx)]
    return pl.pallas_call(
        functools.partial(head_kernel, (species, nx, ny), cells, nshape, tiles, span),
        out_shape=[
            jax.ShapeDtypeStruct((rows, count), F32),
            jax.ShapeDtypeStruct((1, count), F32),
            jax.ShapeDtypeStruct((2 * rows, count), BF16),
            jax.ShapeDtypeStruct((rows, count // 2), F32),
        ],
        in_specs=[pl.BlockSpec(memory_space=pltpu.HBM)] * 4,
        out_specs=[VMEM] * 4,
        scratch_shapes=[
            pltpu.VMEM((species * nx * ny, nz), F32),
            pltpu.VMEM((1, count), jnp.int32),
            pltpu.VMEM((1, count), jnp.int32),
            pltpu.VMEM((1, species), F32),
            pltpu.VMEM((8, count), F32),
            pltpu.VMEM((1, LANES), F32),
        ] + halo * 2 + [pltpu.SemaphoreType.DMA((4,))] * 3,
        compiler_params=pltpu.CompilerParams(vmem_limit_bytes=60 << 20, collective_id=2, has_side_effects=True),
        name="head",
    )(
        les_state.reshape(species * nx * ny, nz), cmc_map.reshape(1, count), pdf_index.reshape(1, count),
        diffusion.reshape(1, species),
    )


CHUNK = 2 * TILE


def sort_tiles(parts, rank_ref, steps, out_ref, first, pieces=None, more=False):
    rows = out_ref.shape[0]
    count = rank_ref.shape[1]

    def step(n, _):
        here = (first + n) * TILE
        total = jnp.zeros((2 * rows, TILE), F32)
        for k in range(count // CHUNK) if pieces is None else pieces:
            piece = slice(k * CHUNK, (k + 1) * CHUNK)
            ids = lax.broadcasted_iota(jnp.int32, (TILE, CHUNK), 0) + here
            hot = rows_equal(ids.astype(F32), rank_ref[:, piece])
            total = total + lax.dot_general(parts[:, piece], hot, NT, preferred_element_type=F32)
        total = total[:rows] + total[rows:]
        place = pl.ds(pl.multiple_of(n * TILE, TILE), TILE)
        if more:
            total = total + out_ref[:, place]
        if steps is not None:
            line = lax.broadcasted_iota(jnp.int32, (rows, TILE), 0)
            total = jnp.where(line == rows - 1, jnp.concatenate([steps] * (TILE // LANES), axis=1), total)
        out_ref[:, place] = total
        return 0

    lax.fori_loop(0, out_ref.shape[1] // TILE, step, 0)


def sort_kernel(parts_ref, rank_ref, out_ref):
    sort_tiles(parts_ref, rank_ref, None, out_ref, out_ref.shape[1] // TILE)


def sort_call(parts, rank):
    rows, count = parts.shape[0] // 2, parts.shape[1]
    return pl.pallas_call(
        sort_kernel,
        out_shape=jax.ShapeDtypeStruct((rows, count // 2), F32),
        in_specs=[VMEM] * 2,
        out_specs=VMEM,
        compiler_params=params(8),
        cost_estimate=pl.CostEstimate(flops=2 * rows * count * count, bytes_accessed=4 * rows * count, transcendentals=0),
        name="sort",
    )(parts, rank)


def unsort_kernel(half, given, rank_ref, *refs):
    xs, refs = refs[:given], refs[given:]
    before, (flat_ref,) = (refs[:1], refs[1:2]) if half else ((), (None,))
    out_ref, parts = refs[-2:]
    rows, count = xs[0].shape[0], rank_ref.shape[1]
    width = xs[0].shape[1]

    @pl.when(pl.program_id(0) == 0)
    def _():
        x = xs[0][...]
        for more in xs[1:]:
            x = x + more[...]
        high = x.astype(BF16).astype(F32)
        parts[...] = jnp.concatenate([high, x - high], axis=0).astype(BF16)

    total = jnp.zeros((2 * rows, TILE), F32)
    for k in range(width // CHUNK):
        ids = lax.broadcasted_iota(jnp.int32, (CHUNK, TILE), 0) + (half * width + k * CHUNK)
        hot = rows_equal(ids.astype(F32), rank_ref[:, pl.ds(pl.multiple_of(pl.program_id(0) * TILE, TILE), TILE)])
        piece = parts[:, k * CHUNK : (k + 1) * CHUNK]
        total = total + lax.dot_general(piece, hot, NN, preferred_element_type=F32)
    total = total[:rows] + total[rows:]
    if not half:
        out_ref[...] = total
        return
    total = total + before[0][...]
    species = rows - 2
    ratio = 0.5 / total[species : species + 1]
    for n in range(TILE // LANES):
        piece = slice(n * LANES, (n + 1) * LANES)
        line = pl.program_id(0) * (TILE // LANES) + n
        value = 0.5 * flat_ref[:species, piece] + total[:species, piece] * ratio[:, piece]
        out_ref[pl.ds(line, species, stride=count // LANES), :] = value


def unsort_call(wholes, piece, rank, before, flat):
    half = int(before is not None)
    rows, count = wholes[0].shape
    part = pl.BlockSpec((rows, count // 2), lambda i: (0, half))
    column = pl.BlockSpec((rows, TILE), lambda i: (0, i))
    args = [rank, *wholes, piece]
    specs = [whole(rank.shape)] + [part] * len(wholes) + [whole(piece.shape)]
    out_shape, out_spec = (rows, count), column
    if half:
        args += [before, flat]
        specs += [column, column]
        lines = (rows - 2) * count // LANES
        out_shape, out_spec = (lines, LANES), whole((lines, LANES))
    return pl.pallas_call(
        functools.partial(unsort_kernel, half, len(wholes) + 1),
        grid=(count // TILE,),
        out_shape=jax.ShapeDtypeStruct(out_shape, F32),
        in_specs=specs,
        out_specs=out_spec,
        scratch_shapes=[pltpu.VMEM((2 * rows, count // 2), BF16)],
        compiler_params=params(12),
        cost_estimate=pl.CostEstimate(flops=2 * rows * count * count, bytes_accessed=4 * rows * count, transcendentals=0),
        name="unsort",
    )(*args)


def weights_of(key, table, bins, per_tile):
    nshape = table.shape[1]
    cell = jnp.floor((key + 0.5) * (1.0 / nshape))
    shape = key - cell * nshape
    tile = jnp.floor((cell + 0.5) * (1.0 / per_tile))
    within = cell - tile * per_tile
    ids = lax.broadcasted_iota(jnp.int32, (nshape, key.shape[1]), 0).astype(F32).astype(BF16)
    hot = jnp.where(ids == shape.astype(BF16), jnp.ones((), BF16), jnp.zeros((), BF16))
    picked = lax.dot_general(table, hot, NN, preferred_element_type=F32).astype(BF16)
    masks = [jnp.where(within == m, 1.0, 0.0).astype(BF16) for m in range(per_tile)]
    columns = []
    for part in (picked[:bins], picked[bins:]):
        columns.append(jnp.concatenate([part * mask for mask in masks], axis=0))
    return jnp.concatenate(columns, axis=1), tile


def split_table(table):
    high = table.astype(BF16).astype(F32)
    return jnp.concatenate([high, table - high], axis=0).astype(BF16)


def prepare_weights(source, index, key_row, table, bins, per_tile, weights, tiles):
    def step(n, _):
        key = source[key_row : key_row + 1, pl.ds(pl.multiple_of(n * LANES, LANES), LANES)]
        block, tile = weights_of(key, table, bins, per_tile)
        weights[index + n] = block
        tiles[index + n] = jnp.broadcast_to(tile, tiles.shape[1:])
        return 0

    lax.fori_loop(0, source.shape[1] // LANES, step, 0, unroll=4)


def collect_kernel(species, bins, per_tile, pairs, lists, *refs):
    sources, refs = [refs[2 * n : 2 * n + 2] for n in range(lists)], refs[2 * lists :]
    table_ref, out_ref, *refs = refs
    weights, tiles, *refs = refs
    keys, (parts, steps, sems) = refs[:lists], refs[lists:]
    copies = fetch_rows([source[0] for source in sources], steps, sems)
    rows, part = sources[0][0].shape
    count = 2 * part
    for key, source in zip(keys, sources):
        key[...] = source[0][rows - 8 :, :LANES]
    blocks = count // LANES
    out_ref[...] = jnp.zeros_like(out_ref)
    table = split_table(table_ref[...])
    line = lax.broadcasted_iota(jnp.int32, (rows, LANES), 0)
    for number in range(2 * lists):
        source = sources[number // 2][number % 2]
        start = number * blocks // 2
        prepare_weights(source, start, species, table, bins, per_tile, weights, tiles)

        def split(n, _, source=source, start=start):
            x = source[:, pl.ds(pl.multiple_of(n * LANES, LANES), LANES)]
            x = jnp.where(line < species, x, jnp.where(line == species, 1.0, 0.0))
            parts[start + n] = padded_halves(x)
            return 0

        lax.fori_loop(0, blocks // 2, split, 0, unroll=4)

    for copy in copies:
        copy.wait()

    def step(n, _):
        for number in range(lists):
            for g in range(GROUP):
                k = n * GROUP + g
                tile = steps[number, 7, k].astype(jnp.int32)
                block = jnp.minimum(k - tile, blocks - 1) + number * blocks
                wanted = jnp.where(k < pairs, tile, -1).astype(F32)
                mask = jnp.where(tiles[block] == wanted, 1.0, 0.0).astype(BF16)
                mask = jnp.concatenate([mask] * (2 * HALF // mask.shape[0]), axis=0)
                x = parts[block] * mask
                both = jnp.concatenate([x, x], axis=1)
                got = lax.dot_general(both, weights[block], NT, preferred_element_type=F32)
                place = pl.ds(pl.multiple_of(tile * TILE, TILE), TILE)
                out_ref[:, place] += got[:rows] + got[HALF : HALF + rows]
        return 0

    lax.fori_loop(0, -(-pairs // GROUP), step, 0)


def collect_call(sources, table, species, bins, per_tile, ntiles):
    rows, count = sources[0][0].shape[0], 2 * sources[0][0].shape[1]
    lists, blocks = len(sources), count // LANES
    pairs = blocks + ntiles - 1
    args = [half for source in sources for half in source] + [table]
    specs = [VMEM] * (2 * lists + 1)
    return pl.pallas_call(
        functools.partial(collect_kernel, species, bins, per_tile, pairs, lists),
        out_shape=[
            jax.ShapeDtypeStruct((rows, ntiles * TILE), F32),
            jax.ShapeDtypeStruct((lists * blocks, TILE, 2 * LANES), BF16),
            jax.ShapeDtypeStruct((lists * blocks, 16, LANES), F32),
        ]
        + [jax.ShapeDtypeStruct((8, LANES), F32)] * lists,
        in_specs=specs,
        out_specs=[VMEM] * (lists + 3),
        scratch_shapes=[
            pltpu.VMEM((lists * blocks, 2 * HALF, LANES), BF16),
            pltpu.SMEM((lists, 8, LANES), F32),
            pltpu.SemaphoreType.DMA((lists,)),
        ],
        compiler_params=params(19),
        cost_estimate=pl.CostEstimate(flops=lists * pairs * 2 * LANES * TILE * TILE, bytes_accessed=0, transcendentals=0),
        name="collect",
    )(*args)


def turn_back(mean, out_ref, bins, quads, turned):
    rows, width = mean.shape
    lines = width // LANES
    fold = LANES // bins
    for q in range(lines):
        quads[pl.ds(q, rows, stride=lines), :] = mean[:, q * LANES : (q + 1) * LANES]
    blocked = lax.broadcasted_iota(jnp.int32, (lines, LANES), 1) // bins

    def turn(g):
        source = [quads[pl.ds(pl.multiple_of(g * LANES + k * lines, lines), lines), :] for k in range(fold)]
        for r in range(fold):
            out = source[r]
            for k in range(fold):
                if k != r:
                    out = jnp.where(blocked == k, pltpu.roll(source[k], (k - r) * bins % LANES, 1), out)
            turned[pl.ds(r, lines, stride=fold), :] = out
        return turned[...].T

    full, rest = out_ref.shape[0] // LANES, out_ref.shape[0] % LANES

    def step(g, _):
        out_ref[pl.ds(pl.multiple_of(g * LANES, LANES), LANES), :] = turn(g)
        return 0

    lax.fori_loop(0, full, step, 0)
    if rest:
        out_ref[full * LANES :, :] = turn(full)[:rest]


def project_kernel(bins, pairs, lists, state_rows, *refs):
    parts, weights, tiles, *refs = refs
    sources, refs = refs[:lists], refs[lists:]
    mean = refs.pop(0) if state_rows else None
    outs, refs = refs[:lists], refs[lists:]
    state_ref = refs.pop(0) if state_rows else None
    steps, sems, *turning = refs
    copies = fetch_rows(sources, steps, sems)
    rows, count = outs[0].shape
    blocks = count // LANES
    for out in outs:
        out[...] = jnp.zeros_like(out)
    if state_rows:
        turn_back(mean, state_ref, bins, *turning)
    for copy in copies:
        copy.wait()

    def step(n, _):
        for number in range(lists):
            for g in range(GROUP):
                k = n * GROUP + g
                tile = steps[number, 7, k].astype(jnp.int32)
                local = jnp.minimum(k - tile, blocks - 1)
                block = local + number * blocks
                wanted = jnp.where(k < pairs, tile, -1).astype(F32)
                got = lax.dot_general(parts[tile], weights[block], NN, preferred_element_type=F32)
                got = got[:rows] + got[HALF : HALF + rows]
                got = got[:, :LANES] + got[:, LANES:]
                got = jnp.where(tiles[block][:1] == wanted, got, 0.0)
                place = pl.ds(pl.multiple_of(local * LANES, LANES), LANES)
                outs[number][:, place] += got
        return 0

    lax.fori_loop(0, -(-pairs // GROUP), step, 0)


def project_call(parts, collected, rows, count, bins, ntiles, mean=None, state_rows=0):
    weights, tiles, *sources = collected
    lists = len(sources)
    pairs = count // LANES + ntiles - 1
    extra = [] if mean is None else [mean]
    scratch = [pltpu.SMEM((lists, 8, LANES), F32), pltpu.SemaphoreType.DMA((lists,))]
    if extra:
        scratch += [pltpu.VMEM((mean.size // LANES, LANES), F32), pltpu.VMEM((LANES, LANES), F32)]
    return pl.pallas_call(
        functools.partial(project_kernel, bins, pairs, lists, state_rows),
        out_shape=[jax.ShapeDtypeStruct((rows, count), F32)] * lists
        + [jax.ShapeDtypeStruct((state_rows, LANES), F32)] * len(extra),
        in_specs=[VMEM] * (3 + lists + len(extra)),
        out_specs=[VMEM] * (lists + len(extra)),
        scratch_shapes=scratch,
        compiler_params=params(20),
        cost_estimate=pl.CostEstimate(flops=lists * pairs * 2 * LANES * TILE * TILE, bytes_accessed=0, transcendentals=0),
        name="project",
    )(parts, weights, tiles, *sources, *extra)


def middle_kernel(species, bins, chunk, refs_in, refs_out, scratch):
    *accs, cmc_ref, diss_ref, rate_ref, count_ref, matrix_ref = refs_in
    fresh_ref, parts_ref = refs_out
    next_ref, far_ref, nat, quads, turned, side_out, load, outward, hopped, summed, got, state_ref, edge_out, edge_in, side_in, pick_ref, third_ref, send, recv, side_send, side_recv = scratch
    rows, width = fresh_ref.shape
    steps = width // chunk
    slab, nslab = lax.axis_index("slab"), lax.axis_size("slab")
    cross, ncross = lax.axis_index("cross"), lax.axis_size("cross")
    parity = lax.rem(slab, 2)
    outer = slab + 4 * parity - 2
    inner = slab - 4 * parity + 2
    partner = slab + 1 - 2 * parity
    has_outer = (outer >= 0) & (outer < nslab)
    has_inner = (inner >= 0) & (inner < nslab)
    has_before, has_after = cross > 0, cross < ncross - 1
    has_down, has_up = slab > 0, slab < nslab - 1
    mesh = pl.DeviceIdType.MESH

    def partial_sum(piece):
        total = accs[0][:, piece]
        for more in accs[1:]:
            total = total + more[:, piece]
        return total

    loads, start = [], 0
    for n, source in enumerate((cmc_ref, diss_ref, rate_ref)):
        target = nat.at[start : start + source.shape[0]]
        loads.append(pltpu.make_async_copy(source, target, load.at[n]))
        loads[-1].start()
        start += source.shape[0]
    if start < nat.shape[0]:
        nat[start:, :] = jnp.zeros((nat.shape[0] - start, LANES), F32)
    outward[...] = partial_sum(slice(0, width))

    @pl.when(jnp.logical_not(has_inner))
    def _():
        hopped[...] = jnp.zeros_like(hopped)

    @pl.when(jnp.logical_not(has_outer))
    def _():
        far_ref[...] = jnp.zeros_like(far_ref)

    @pl.when(jnp.logical_not(has_before))
    def _():
        edge_in[:, :, :LANES] = jnp.zeros(edge_in.shape[:2] + (LANES,), F32)

    @pl.when(jnp.logical_not(has_after))
    def _():
        edge_in[:, :, LANES:] = jnp.zeros(edge_in.shape[:2] + (LANES,), F32)

    @pl.when(jnp.logical_not(has_down))
    def _():
        side_in[0] = jnp.zeros(side_in.shape[1:], F32)

    @pl.when(jnp.logical_not(has_up))
    def _():
        side_in[1] = jnp.zeros(side_in.shape[1:], F32)

    barrier = pltpu.get_barrier_semaphore()
    greet = lambda where: pl.semaphore_signal(barrier, inc=1, device_id=where, device_id_type=mesh)
    pl.when(has_down)(lambda: greet({"slab": slab - 1}))
    pl.when(has_up)(lambda: greet({"slab": slab + 1}))
    pl.when(has_outer)(lambda: greet({"slab": outer}))
    pl.when(has_inner)(lambda: greet({"slab": inner}))
    pl.when(has_before)(lambda: greet({"cross": cross - 1}))
    pl.when(has_after)(lambda: greet({"cross": cross + 1}))
    number = lambda flag: jnp.where(flag, 1, 0)
    flags = (has_down, has_up, has_outer, has_inner, has_before, has_after)
    pl.semaphore_wait(barrier, sum(number(flag) for flag in flags))

    def lanes(c, base=0):
        return pl.ds(pl.multiple_of(base + c * chunk, chunk), chunk)

    def remote(kind, c, source, target, where):
        return pltpu.make_async_remote_copy(
            src_ref=source, dst_ref=target, send_sem=send.at[kind, c], recv_sem=recv.at[kind, c],
            device_id=where, device_id_type=mesh,
        )

    to_outer = lambda c: remote(0, c, outward.at[:, lanes(c)], hopped.at[:, lanes(c)], {"slab": outer})
    to_partner = lambda c: remote(1, c, summed.at[:, lanes(c)], got.at[:, lanes(c)], {"slab": partner})
    to_after = lambda c: remote(2, c, edge_out.at[c, :, LANES:], edge_in.at[c, :, :LANES], {"cross": cross + 1})
    to_before = lambda c: remote(3, c, edge_out.at[c, :, :LANES], edge_in.at[c, :, LANES:], {"cross": cross - 1})
    give = lambda c: remote(4, c, fresh_ref.at[:, lanes(c)], next_ref.at[:, lanes(c)], {"slab": partner})
    pass_on = lambda c: remote(5, c, next_ref.at[:, lanes(c)], far_ref.at[:, lanes(c)], {"slab": inner})

    def side(n, source, where):
        return pltpu.make_async_remote_copy(
            src_ref=source, dst_ref=side_in.at[n], send_sem=side_send.at[n], recv_sem=side_recv.at[n],
            device_id=where, device_id_type=mesh,
        )

    to_up = side(0, side_out.at[0], {"slab": slab + 1})
    to_down = side(1, side_out.at[1], {"slab": slab - 1})

    def start_hops(chunks):
        @pl.when(has_outer)
        def _():
            for c in chunks:
                to_outer(c).start()

    start_hops(range(2))
    for copy in loads:
        copy.wait()
    lines = width // LANES
    fold = LANES // bins
    blocked = lax.broadcasted_iota(jnp.int32, (LANES // fold, LANES), 1) // bins

    def turn(g, _):
        turned[...] = nat[pl.ds(pl.multiple_of(g * LANES, LANES), LANES), :].T
        parts = [turned[pl.ds(r, LANES // fold, stride=fold), :] for r in range(fold)]
        for k in range(fold):
            out = parts[k]
            for r in range(fold):
                if r != k:
                    out = jnp.where(blocked == r, pltpu.roll(parts[r], (r - k) * bins % LANES, 1), out)
            place = pl.multiple_of(g * LANES + k * lines, lines)
            quads[pl.ds(place, lines), :] = out
        return 0

    lax.fori_loop(0, nat.shape[0] // LANES, turn, 0)
    tile = lambda q: quads[pl.ds(q, rows, stride=lines), :]
    side_out[0] = tile(lines - 1)
    side_out[1] = tile(0)

    lane = lax.broadcasted_iota(jnp.int32, (2 * LANES, chunk), 1)
    row = lax.broadcasted_iota(jnp.int32, (2 * LANES, chunk), 0)
    target = jnp.where(row < LANES, row * bins, (row - LANES) * bins + bins - 1)
    pick_ref[...] = rows_equal(target, lane)
    third = matrix_ref.shape[1] // 3
    high, low = halves(matrix_ref[...])
    column = lax.broadcasted_iota(jnp.int32, matrix_ref.shape, 1)
    third_ref[...] = jnp.where(column < 2 * third, high.astype(F32), low.astype(F32)).astype(BF16)
    line = lax.broadcasted_iota(jnp.int32, (rows, chunk), 0)
    slot = lax.broadcasted_iota(jnp.int32, (rows, chunk), 1) % bins
    gap = [jnp.zeros((third - rows, chunk), F32)] * (third > rows)

    pl.when(has_up)(to_up.start)
    pl.when(has_down)(to_down.start)
    start_hops(range(2, steps))

    def stacked(x):
        high = x.astype(BF16).astype(F32)
        return jnp.concatenate([high, x - high], axis=0).astype(BF16)

    def add_hop(c):
        pl.when(has_inner)(lambda: to_outer(c).wait_recv())
        summed[:, lanes(c)] = partial_sum(lanes(c, 2 * width)) + hopped[:, lanes(c)]

    per = chunk // LANES

    def advect(c):
        here = jnp.concatenate([tile(c * per + n) for n in range(per)], axis=1)
        low = jnp.where(c == 0, side_in[0], tile(jnp.maximum(c * per - 1, 0)))
        high = jnp.where(c == steps - 1, side_in[1], tile(jnp.minimum((c + 1) * per, lines - 1)))
        left = pltpu.roll(jnp.concatenate([low, here], axis=1), bins, 1)[:, LANES:]
        right = pltpu.roll(jnp.concatenate([here, high], axis=1), chunk + LANES - bins, 1)[:, :chunk]
        return here - 0.4 * (here - left) + 0.1 * (right - 2.0 * here + left)

    def cell_row(n, c):
        start = (species + n) * lines + c * per
        return jnp.concatenate([quads[pl.ds(start + k, 1), :] for k in range(per)], axis=1)

    def blend(c):
        total = partial_sum(lanes(c, width)) + got[:, lanes(c)]
        blended = (total + advect(c)) / (total[species : species + 1] + 1.0)
        state_ref[:, lanes(c)] = blended
        edge = lax.dot_general(stacked(blended), pick_ref[...], NT, preferred_element_type=F32)
        edge_out[c] = edge[:rows] + edge[rows:]

    def send_edges(c):
        pl.when(has_after)(lambda: to_after(c).start())
        pl.when(has_before)(lambda: to_before(c).start())

    def wait_edges(c):
        pl.when(has_before)(lambda: to_after(c).wait_recv())
        pl.when(has_after)(lambda: to_before(c).wait_recv())

    def react(c):
        here = state_ref[:, lanes(c)]
        around = lax.dot_general(stacked(edge_in[c]), pick_ref[...], NN, preferred_element_type=F32)
        around = around[:rows] + around[rows:]
        before = jnp.where(slot == 0, around, pltpu.roll(here, 1, 1))
        after = jnp.where(slot == bins - 1, around, pltpu.roll(here, chunk - 1, 1))
        state = here + cell_row(0, c) * (after - 2.0 * here + before)
        half = 0.5 * cell_row(1, c)
        count = count_ref[:, lanes(c)]
        for k in range(KMAX):
            high, low = (part.astype(F32) for part in halves(state))
            stack = jnp.concatenate([high, *gap, low, *gap, high, *gap], axis=0).astype(BF16)
            rate = lax.dot_general(third_ref[...], stack, NN, preferred_element_type=F32)
            state = jnp.where(k < count, state + half * jnp.tanh(rate), state)
        state = jnp.where(line == species, 1.0, state)
        fresh_ref[:, lanes(c)] = state
        keep(1, c, state)

    def keep(which, c, mean):
        for n in range(chunk // TILE):
            index = which * (width // TILE) + c * (chunk // TILE) + n
            parts_ref[index] = padded_halves(mean[:, n * TILE : (n + 1) * TILE])

    def step(t, _):
        def when(lag, body):
            c = t - lag
            pl.when((c >= 0) & (c < steps))(lambda: body(c))

        def second(c):
            pl.when((c == 0) & has_down)(to_up.wait_recv)
            pl.when((c == 0) & has_up)(to_down.wait_recv)
            to_partner(c).wait_recv()
            blend(c)

        def third_stage(c):
            wait_edges(c)
            react(c)

        def fourth(c):
            give(c).wait_recv()
            pl.when(has_inner)(lambda: pass_on(c).start())
            keep(2, c, next_ref[:, lanes(c)])

        when(0, add_hop)
        when(LAG[0], second)
        when(0, lambda c: to_partner(c).start())
        when(LAG[1], third_stage)
        when(LAG[0], send_edges)
        when(LAG[2], fourth)
        when(LAG[1], lambda c: give(c).start())
        return 0

    lax.fori_loop(0, steps + LAG[2], step, 0)

    def finish(c, _):
        pl.when(has_outer)(lambda: to_outer(c).wait_send())
        to_partner(c).wait_send()
        pl.when(has_after)(lambda: to_after(c).wait_send())
        pl.when(has_before)(lambda: to_before(c).wait_send())
        give(c).wait_send()
        pl.when(has_inner)(lambda: pass_on(c).wait_send())
        pl.when(has_outer)(lambda: pass_on(c).wait_recv())
        keep(0, c, far_ref[:, lanes(c)])
        return 0

    lax.fori_loop(0, steps, finish, 0)
    pl.when(has_up)(to_up.wait_send)
    pl.when(has_down)(to_down.wait_send)


def middle_call(accs, cmc, diss, rate, count, matrix, species, bins, chunk=512):
    rows, width = accs[0].shape[0], count.shape[1]
    steps = width // chunk
    given = len(accs) + 5

    def kernel(*refs):
        middle_kernel(species, bins, chunk, refs[:given], refs[given : given + 2], refs[given + 2 :])

    return pl.pallas_call(
        kernel,
        out_shape=[
            jax.ShapeDtypeStruct((rows, width), F32),
            jax.ShapeDtypeStruct((3 * width // TILE, 2 * HALF, TILE), BF16),
        ],
        in_specs=[VMEM] * len(accs) + [pl.BlockSpec(memory_space=pl.ANY)] * 3 + [VMEM] * 2,
        out_specs=[VMEM] * 2,
        scratch_shapes=[pltpu.VMEM((rows, width), F32)] * 2
        + [pltpu.VMEM((rows * bins, LANES), F32), pltpu.VMEM((rows * width // LANES, LANES), F32)]
        + [pltpu.VMEM((LANES, LANES), F32), pltpu.VMEM((2, rows, LANES), F32), pltpu.SemaphoreType.DMA((3,))]
        + [pltpu.VMEM((rows, width), F32)] * 5
        + [pltpu.VMEM((steps, rows, 2 * LANES), F32)] * 2
        + [pltpu.VMEM((2, rows, LANES), F32), pltpu.VMEM((2 * LANES, chunk), BF16), pltpu.VMEM(matrix.shape, BF16)]
        + [pltpu.SemaphoreType.DMA((6, steps))] * 2
        + [pltpu.SemaphoreType.DMA((2,))] * 2,
        compiler_params=pltpu.CompilerParams(vmem_limit_bytes=22 << 20, collective_id=1, has_side_effects=True),
        name="middle",
    )(*accs, cmc, diss, rate, count, matrix)


def on_device(
    les_state, cmc_state, cmc_map, pdf_index, pdf_table, diffusion, chem_matrix, dissipation, reaction_rate, substeps
):
    species = les_state.shape[0]
    rows = -(-(species + 2) // 8) * 8
    bins, cells = cmc_state.shape[1:]
    nshape = pdf_table.shape[0]
    count = cmc_map.size
    ncross = lax.axis_size("cross")
    per_tile = TILE // bins
    ntiles = 3 * cells // per_tile
    flat, rank, parts, low = head_call(
        les_state, cmc_map, pdf_index, diffusion, rows, cells, nshape, ntiles, nshape * per_tile
    )
    bits = [1 << k for k in range(ncross.bit_length() - 1)]
    low_there = swap(low, "cross", bits[-1])
    high = sort_call(parts, rank)
    high_there = swap(high, "cross", bits[-1])
    near_lists = [(low, high)] + [(swap(low, "cross", bit), swap(high, "cross", bit)) for bit in bits[:-1]]
    low_far = [low_there] + [swap(low_there, "cross", bit) for bit in bits[:-1]]

    table = lax.dynamic_slice_in_dim(pdf_table.T, lax.axis_index("cross") * bins, bins, axis=0)

    extra = rows - species
    matrix = jnp.tile(jnp.pad(chem_matrix, ((0, extra), (0, -(-rows // 16) * 16 - species))), (1, 3))
    terms = (cmc_state.reshape(species * bins, cells), dissipation, reaction_rate, jnp.repeat(substeps, bins)[None, :], matrix)
    acc, *near = collect_call(near_lists, table, species, bins, per_tile, ntiles)
    acc, high_there, terms = lax.optimization_barrier((acc, high_there, terms))
    high_far = [high_there] + [swap(high_there, "cross", bit) for bit in bits[:-1]]
    accs, far = [acc], []
    for pair in zip(low_far, high_far):
        acc, *collected = collect_call([pair], table, species, bins, per_tile, ntiles)
        accs.append(acc)
        far.append(collected)
    fresh, parts = middle_call(accs, *terms, species, bins)

    pieces = []
    for bit, collected in zip(bits[:-1], far[1:]):
        (piece,) = project_call(parts, collected, rows, count, bins, ntiles)
        piece, parts = lax.optimization_barrier((piece, parts))
        pieces.append(swap(piece, "cross", bit))
    (there,) = project_call(parts, far[0], rows, count, bins, ntiles)
    part = count // 2
    low, high = there[:, :part], there[:, part:]
    for piece in pieces:
        low, high = low + piece[:, :part], high + piece[:, part:]
    low, parts = lax.optimization_barrier((low, parts))
    low = swap(low, "cross", bits[-1])
    high = swap(high, "cross", bits[-1])
    *here, cmc_out = project_call(parts, near, rows, count, bins, ntiles, fresh, species * bins)
    total = [here[0]] + [swap(piece, "cross", bit) for bit, piece in zip(bits[:-1], here[1:])]
    before = unsort_call(total, low, rank, None, None)
    les_out = unsort_call(total, high, rank, before, flat)
    return (les_out.reshape(les_state.shape), cmc_out.reshape(species, bins, cells))


def solution(mesh):
    return jax.shard_map(
        on_device,
        mesh=mesh,
        in_specs=(
            P(None, "slab", "cross", None),
            P(None, "cross", "slab"),
            P("slab", "cross", None),
            P("slab", "cross", None),
            P(),
            P(),
            P(),
            P("cross", "slab"),
            P("cross", "slab"),
            P("slab"),
        ),
        out_specs=(P(None, "slab", "cross", None), P(None, "cross", "slab")),
        check_vma=False,
    )
```

```python
import functools


import jax
import jax.numpy as jnp
from jax import lax
from jax.experimental import pallas as pl
from jax.experimental.pallas import tpu as pltpu
from jax.sharding import PartitionSpec as P

KMAX = 4
F32 = jnp.float32
BF16 = jnp.bfloat16
NT = (((1,), (1,)), ((), ()))
NN = (((1,), (0,)), ((), ()))
LANES = 128
TILE = 256
HALF = 64
GROUP = 16
LAG = (3, 6, 9)


def swap(array, axis, bit):
    count = lax.axis_size(axis)
    return lax.ppermute(array, axis, [(i, i ^ bit) for i in range(count)])


def halves(x):
    high = x.astype(BF16)
    return high, (x - high.astype(F32)).astype(BF16)


def padded_halves(x):
    gap = jnp.zeros((HALF - x.shape[0], x.shape[1]), F32)
    high = x.astype(BF16).astype(F32)
    return jnp.concatenate([high, gap, x - high, gap], axis=0).astype(BF16)


def rows_equal(targets, row):
    return jnp.where(targets == row, 1.0, 0.0).astype(BF16)


def whole(shape):
    return pl.BlockSpec(shape, lambda *_: (0,) * len(shape))


VMEM = pl.BlockSpec(memory_space=pltpu.VMEM)
SMEM = pl.BlockSpec(memory_space=pltpu.SMEM)


def params(mib):
    return pltpu.CompilerParams(vmem_limit_bytes=mib << 20)


def fetch_rows(sources, steps, sems):
    copies = []
    for number, source in enumerate(sources):
        last = source.at[source.shape[0] - 8 : source.shape[0], :LANES]
        copies.append(pltpu.make_async_copy(last, steps.at[number], sems.at[number]))
        copies[-1].start()
    return copies


def ranks(tiles, span, key_ref, rank_ref, table_ref):
    count = rank_ref.shape[1]
    ids = lax.broadcasted_iota(jnp.int32, (tiles, TILE), 0).astype(F32)
    tile_of = lambda n: jnp.floor((key_ref[:1, n * TILE : (n + 1) * TILE] + 0.5) * (1.0 / span))
    total = jnp.zeros((tiles, TILE), F32)
    for n in range(count // TILE):
        total = total + jnp.where(ids == tile_of(n), 1.0, 0.0)
    total = jnp.sum(total, axis=1, keepdims=True)
    total = jnp.broadcast_to(total, (tiles, LANES))
    big = jnp.floor(total * (1.0 / HALF))
    row = lax.broadcasted_iota(jnp.int32, (tiles, tiles), 0)
    below = rows_equal(jnp.where(lax.broadcasted_iota(jnp.int32, (tiles, tiles), 1) < row, 1, 0), 1)
    add = lambda part: lax.dot_general(below, part.astype(BF16), NN, preferred_element_type=F32)
    base = add(big) * HALF + add(total - big * HALF)
    order = lax.broadcasted_iota(jnp.int32, (tiles, LANES), 0).astype(F32)
    lane = lax.broadcasted_iota(jnp.int32, (tiles, LANES), 1).astype(F32)
    last = jnp.maximum(jnp.ceil((base + total) * (1.0 / LANES)) - 1.0, 0.0) + order
    passed = jnp.where((last < lane) & (order < tiles - 1), 1.0, 0.0)
    table = jnp.sum(passed, axis=0, keepdims=True)
    number = lane[:1]
    blocks = count // LANES
    early = jnp.where((number - table < blocks // 2) & (number < blocks + tiles - 1), 1.0, 0.0)
    table_ref[...] = jnp.where(number == LANES - 1, jnp.sum(early, axis=1, keepdims=True), table)
    ahead = jnp.where(
        lax.broadcasted_iota(jnp.int32, (TILE, TILE), 0) < lax.broadcasted_iota(jnp.int32, (TILE, TILE), 1), 1.0, 0.0
    ).astype(BF16)
    carry = base[:, :1]
    for n in range(count // TILE):
        hot = jnp.where(ids == tile_of(n), 1.0, 0.0)
        before = lax.dot_general(hot.astype(BF16), ahead, NN, preferred_element_type=F32) + carry
        rank_ref[:, n * TILE : (n + 1) * TILE] = jnp.sum(hot * before, axis=0, keepdims=True)
        carry = carry + jnp.sum(hot, axis=1, keepdims=True)


HALO_ORDER = {2: lambda n: (), 3: lambda n: range(1, n - 1), 0: lambda n: (), 1: lambda n: sorted({0, n - 1})}


def head_kernel(grid_shape, cells, nshape, tiles, span, *refs):
    given, (t_ref, rank_ref, parts_ref, half_ref), refs = refs[:4], refs[4:8], refs[8:]
    les_ref, map_ref, shape_ref, diff_ref, key_ref, table_ref, *refs = refs
    faces, halos, (send, recv, load) = refs[:4], refs[4:8], refs[8:]
    loads = [
        pltpu.make_async_copy(source, target, load.at[n])
        for n, (source, target) in enumerate(zip(given, (les_ref, map_ref, shape_ref, diff_ref)))
    ]
    for copy in loads:
        copy.start()
    species, nx, ny = grid_shape
    count = rank_ref.shape[1]
    slab, nslab = lax.axis_index("slab"), lax.axis_size("slab")
    cross, ncross = lax.axis_index("cross"), lax.axis_size("cross")
    mesh = pl.DeviceIdType.MESH
    sides = [
        (slab > 0, {"slab": slab - 1}),
        (slab < nslab - 1, {"slab": slab + 1}),
        (cross > 0, {"cross": cross - 1}),
        (cross < ncross - 1, {"cross": cross + 1}),
    ]
    barrier = pltpu.get_barrier_semaphore()
    for n, (there, where) in enumerate(sides):

        @pl.when(jnp.logical_not(there))
        def _(n=n):
            halos[n][...] = jnp.zeros_like(halos[n])

    for copy in loads:
        copy.wait()
    line = lambda x, y: les_ref[pl.ds(x * ny + y, species, stride=nx * ny), :]
    for n, x in enumerate((0, nx - 1)):
        for y in range(ny):
            faces[n][y, :species] = line(x, y)
    for n, y in enumerate((0, ny - 1)):
        for x in range(nx):
            faces[2 + n][x, :species] = line(x, y)
    for there, where in sides:

        @pl.when(there)
        def _(where=where):
            pl.semaphore_signal(barrier, inc=1, device_id=where, device_id_type=mesh)

    pl.semaphore_wait(barrier, sum(jnp.where(there, 1, 0) for there, _ in sides))
    copies = {}
    for n in (2, 3, 0, 1):
        there, where = sides[n]
        copy = pltpu.make_async_remote_copy(
            src_ref=faces[n], dst_ref=halos[n ^ 1], send_sem=send.at[n], recv_sem=recv.at[n ^ 1],
            device_id=where, device_id_type=mesh,
        )
        pl.when(there)(copy.start)
        copies[n] = copy
    offset = map_ref[...] - (slab - 1) * cells
    block = jnp.where(offset >= cells, 1, 0) + jnp.where(offset >= 2 * cells, 1, 0)
    offset = jnp.where(lax.rem(slab, 2) == 1, (2 - block) * cells + offset - block * cells, offset)
    key = (offset * nshape + shape_ref[...]).astype(F32)
    key_ref[:1, :] = key
    t_ref[species:, :] = jnp.concatenate([key] + [jnp.zeros((t_ref.shape[0] - species - 1, count), F32)], axis=0)
    ranks(tiles, span, key_ref, rank_ref, table_ref)
    row = lax.broadcasted_iota(jnp.int32, (species, species), 0)
    number = jnp.where(row == lax.broadcasted_iota(jnp.int32, (species, species), 1), diff_ref[...], 0.0)
    number = jnp.sum(number, axis=1, keepdims=True)
    lane = lax.broadcasted_iota(jnp.int32, (species, LANES), 1)
    for n in (2, 3, 0, 1):
        pl.when(sides[n ^ 1][0])(copies[n].wait_recv)
        for x, y in [(x, y) for x in HALO_ORDER[n](nx) for y in range(ny)]:
            here = line(x, y)
            around = line(x + 1, y) if x < nx - 1 else halos[1][y, :species]
            around = around + (line(x - 1, y) if x else halos[0][y, :species])
            around = around + (line(x, y + 1) if y < ny - 1 else halos[3][x, :species])
            around = around + (line(x, y - 1) if y else halos[2][x, :species])
            around = around + jnp.where(lane < LANES - 1, pltpu.roll(here, LANES - 1, 1), 0.0)
            around = around + jnp.where(lane > 0, pltpu.roll(here, 1, 1), 0.0)
            place = (x * ny + y) * LANES
            t_ref[:species, place : place + LANES] = here + number * (around - 6.0 * here)
        planes = list(HALO_ORDER[n](nx))
        for x in planes:
            piece = slice(x * ny * LANES, (x + 1) * ny * LANES)
            value = t_ref[:, piece]
            high = value.astype(BF16).astype(F32)
            parts_ref[:, piece] = jnp.concatenate([high, value - high], axis=0).astype(BF16)
        if planes and ny * LANES == CHUNK:
            last = n == 1
            sort_tiles(parts_ref, rank_ref, table_ref[...] if last else None, half_ref, 0, planes, last and nx > 2)
    if ny * LANES != CHUNK:
        sort_tiles(parts_ref, rank_ref, table_ref[...], half_ref, 0)
    for n, (there, _) in enumerate(sides):
        pl.when(there)(copies[n].wait_send)


def head_call(les_state, cmc_map, pdf_index, diffusion, rows, cells, nshape, tiles, span):
    species, nx, ny, nz = les_state.shape
    count = nx * ny * nz
    halo = [pltpu.VMEM((n, rows, LANES), F32) for n in (ny, ny, nx, nx)]
    return pl.pallas_call(
        functools.partial(head_kernel, (species, nx, ny), cells, nshape, tiles, span),
        out_shape=[
            jax.ShapeDtypeStruct((rows, count), F32),
            jax.ShapeDtypeStruct((1, count), F32),
            jax.ShapeDtypeStruct((2 * rows, count), BF16),
            jax.ShapeDtypeStruct((rows, count // 2), F32),
        ],
        in_specs=[pl.BlockSpec(memory_space=pltpu.HBM)] * 4,
        out_specs=[VMEM] * 4,
        scratch_shapes=[
            pltpu.VMEM((species * nx * ny, nz), F32),
            pltpu.VMEM((1, count), jnp.int32),
            pltpu.VMEM((1, count), jnp.int32),
            pltpu.VMEM((1, species), F32),
            pltpu.VMEM((8, count), F32),
            pltpu.VMEM((1, LANES), F32),
        ] + halo * 2 + [pltpu.SemaphoreType.DMA((4,))] * 3,
        compiler_params=pltpu.CompilerParams(vmem_limit_bytes=60 << 20, collective_id=2, has_side_effects=True),
        name="head",
    )(
        les_state.reshape(species * nx * ny, nz), cmc_map.reshape(1, count), pdf_index.reshape(1, count),
        diffusion.reshape(1, species),
    )


CHUNK = 2 * TILE


def sort_tiles(parts, rank_ref, steps, out_ref, first, pieces=None, more=False):
    rows = out_ref.shape[0]
    count = rank_ref.shape[1]

    def step(n, _):
        here = (first + n) * TILE
        total = jnp.zeros((2 * rows, TILE), F32)
        for k in range(count // CHUNK) if pieces is None else pieces:
            piece = slice(k * CHUNK, (k + 1) * CHUNK)
            ids = lax.broadcasted_iota(jnp.int32, (TILE, CHUNK), 0) + here
            hot = rows_equal(ids.astype(F32), rank_ref[:, piece])
            total = total + lax.dot_general(parts[:, piece], hot, NT, preferred_element_type=F32)
        total = total[:rows] + total[rows:]
        place = pl.ds(pl.multiple_of(n * TILE, TILE), TILE)
        if more:
            total = total + out_ref[:, place]
        if steps is not None:
            line = lax.broadcasted_iota(jnp.int32, (rows, TILE), 0)
            total = jnp.where(line == rows - 1, jnp.concatenate([steps] * (TILE // LANES), axis=1), total)
        out_ref[:, place] = total
        return 0

    lax.fori_loop(0, out_ref.shape[1] // TILE, step, 0)


def sort_kernel(parts_ref, rank_ref, out_ref):
    sort_tiles(parts_ref, rank_ref, None, out_ref, out_ref.shape[1] // TILE)


def sort_call(parts, rank):
    rows, count = parts.shape[0] // 2, parts.shape[1]
    return pl.pallas_call(
        sort_kernel,
        out_shape=jax.ShapeDtypeStruct((rows, count // 2), F32),
        in_specs=[VMEM] * 2,
        out_specs=VMEM,
        compiler_params=params(8),
        cost_estimate=pl.CostEstimate(flops=2 * rows * count * count, bytes_accessed=4 * rows * count, transcendentals=0),
        name="sort",
    )(parts, rank)


def unsort_kernel(half, given, rank_ref, *refs):
    xs, refs = refs[:given], refs[given:]
    before, (flat_ref,) = (refs[:1], refs[1:2]) if half else ((), (None,))
    out_ref, parts = refs[-2:]
    rows, count = xs[0].shape[0], rank_ref.shape[1]
    width = xs[0].shape[1]

    @pl.when(pl.program_id(0) == 0)
    def _():
        x = xs[0][...]
        for more in xs[1:]:
            x = x + more[...]
        high = x.astype(BF16).astype(F32)
        parts[...] = jnp.concatenate([high, x - high], axis=0).astype(BF16)

    total = jnp.zeros((2 * rows, TILE), F32)
    for k in range(width // CHUNK):
        ids = lax.broadcasted_iota(jnp.int32, (CHUNK, TILE), 0) + (half * width + k * CHUNK)
        hot = rows_equal(ids.astype(F32), rank_ref[:, pl.ds(pl.multiple_of(pl.program_id(0) * TILE, TILE), TILE)])
        piece = parts[:, k * CHUNK : (k + 1) * CHUNK]
        total = total + lax.dot_general(piece, hot, NN, preferred_element_type=F32)
    total = total[:rows] + total[rows:]
    if not half:
        out_ref[...] = total
        return
    total = total + before[0][...]
    species = rows - 2
    ratio = 0.5 / total[species : species + 1]
    for n in range(TILE // LANES):
        piece = slice(n * LANES, (n + 1) * LANES)
        line = pl.program_id(0) * (TILE // LANES) + n
        value = 0.5 * flat_ref[:species, piece] + total[:species, piece] * ratio[:, piece]
        out_ref[pl.ds(line, species, stride=count // LANES), :] = value


def unsort_call(wholes, piece, rank, before, flat):
    half = int(before is not None)
    rows, count = wholes[0].shape
    part = pl.BlockSpec((rows, count // 2), lambda i: (0, half))
    column = pl.BlockSpec((rows, TILE), lambda i: (0, i))
    args = [rank, *wholes, piece]
    specs = [whole(rank.shape)] + [part] * len(wholes) + [whole(piece.shape)]
    out_shape, out_spec = (rows, count), column
    if half:
        args += [before, flat]
        specs += [column, column]
        lines = (rows - 2) * count // LANES
        out_shape, out_spec = (lines, LANES), whole((lines, LANES))
    return pl.pallas_call(
        functools.partial(unsort_kernel, half, len(wholes) + 1),
        grid=(count // TILE,),
        out_shape=jax.ShapeDtypeStruct(out_shape, F32),
        in_specs=specs,
        out_specs=out_spec,
        scratch_shapes=[pltpu.VMEM((2 * rows, count // 2), BF16)],
        compiler_params=params(12),
        cost_estimate=pl.CostEstimate(flops=2 * rows * count * count, bytes_accessed=4 * rows * count, transcendentals=0),
        name="unsort",
    )(*args)


def weights_of(key, table, bins, per_tile):
    nshape = table.shape[1]
    cell = jnp.floor((key + 0.5) * (1.0 / nshape))
    shape = key - cell * nshape
    tile = jnp.floor((cell + 0.5) * (1.0 / per_tile))
    within = cell - tile * per_tile
    ids = lax.broadcasted_iota(jnp.int32, (nshape, key.shape[1]), 0).astype(F32).astype(BF16)
    hot = jnp.where(ids == shape.astype(BF16), jnp.ones((), BF16), jnp.zeros((), BF16))
    picked = lax.dot_general(table, hot, NN, preferred_element_type=F32).astype(BF16)
    masks = [jnp.where(within == m, 1.0, 0.0).astype(BF16) for m in range(per_tile)]
    columns = []
    for part in (picked[:bins], picked[bins:]):
        columns.append(jnp.concatenate([part * mask for mask in masks], axis=0))
    return jnp.concatenate(columns, axis=1), tile


def split_table(table):
    high = table.astype(BF16).astype(F32)
    return jnp.concatenate([high, table - high], axis=0).astype(BF16)


def prepare_weights(source, index, key_row, table, bins, per_tile, weights, tiles):
    def step(n, _):
        key = source[key_row : key_row + 1, pl.ds(pl.multiple_of(n * LANES, LANES), LANES)]
        block, tile = weights_of(key, table, bins, per_tile)
        weights[index + n] = block
        tiles[index + n] = jnp.broadcast_to(tile, tiles.shape[1:])
        return 0

    lax.fori_loop(0, source.shape[1] // LANES, step, 0, unroll=4)


def collect_kernel(species, bins, per_tile, pairs, lists, *refs):
    sources, refs = [refs[2 * n : 2 * n + 2] for n in range(lists)], refs[2 * lists :]
    table_ref, out_ref, *refs = refs
    weights, tiles, *refs = refs
    keys, (parts, steps, sems) = refs[:lists], refs[lists:]
    copies = fetch_rows([source[0] for source in sources], steps, sems)
    rows, part = sources[0][0].shape
    count = 2 * part
    for key, source in zip(keys, sources):
        key[...] = source[0][rows - 8 :, :LANES]
    blocks = count // LANES
    out_ref[...] = jnp.zeros_like(out_ref)
    table = split_table(table_ref[...])
    line = lax.broadcasted_iota(jnp.int32, (rows, LANES), 0)
    for number in range(2 * lists):
        source = sources[number // 2][number % 2]
        start = number * blocks // 2
        prepare_weights(source, start, species, table, bins, per_tile, weights, tiles)

        def split(n, _, source=source, start=start):
            x = source[:, pl.ds(pl.multiple_of(n * LANES, LANES), LANES)]
            x = jnp.where(line < species, x, jnp.where(line == species, 1.0, 0.0))
            parts[start + n] = padded_halves(x)
            return 0

        lax.fori_loop(0, blocks // 2, split, 0, unroll=4)

    for copy in copies:
        copy.wait()

    def step(n, _):
        for number in range(lists):
            for g in range(GROUP):
                k = n * GROUP + g
                tile = steps[number, 7, k].astype(jnp.int32)
                block = jnp.minimum(k - tile, blocks - 1) + number * blocks
                wanted = jnp.where(k < pairs, tile, -1).astype(F32)
                mask = jnp.where(tiles[block] == wanted, 1.0, 0.0).astype(BF16)
                mask = jnp.concatenate([mask] * (2 * HALF // mask.shape[0]), axis=0)
                x = parts[block] * mask
                both = jnp.concatenate([x, x], axis=1)
                got = lax.dot_general(both, weights[block], NT, preferred_element_type=F32)
                place = pl.ds(pl.multiple_of(tile * TILE, TILE), TILE)
                out_ref[:, place] += got[:rows] + got[HALF : HALF + rows]
        return 0

    lax.fori_loop(0, -(-pairs // GROUP), step, 0)


def collect_call(sources, table, species, bins, per_tile, ntiles):
    rows, count = sources[0][0].shape[0], 2 * sources[0][0].shape[1]
    lists, blocks = len(sources), count // LANES
    pairs = blocks + ntiles - 1
    args = [half for source in sources for half in source] + [table]
    specs = [VMEM] * (2 * lists + 1)
    return pl.pallas_call(
        functools.partial(collect_kernel, species, bins, per_tile, pairs, lists),
        out_shape=[
            jax.ShapeDtypeStruct((rows, ntiles * TILE), F32),
            jax.ShapeDtypeStruct((lists * blocks, TILE, 2 * LANES), BF16),
            jax.ShapeDtypeStruct((lists * blocks, 16, LANES), F32),
        ]
        + [jax.ShapeDtypeStruct((8, LANES), F32)] * lists,
        in_specs=specs,
        out_specs=[VMEM] * (lists + 3),
        scratch_shapes=[
            pltpu.VMEM((lists * blocks, 2 * HALF, LANES), BF16),
            pltpu.SMEM((lists, 8, LANES), F32),
            pltpu.SemaphoreType.DMA((lists,)),
        ],
        compiler_params=params(19),
        cost_estimate=pl.CostEstimate(flops=lists * pairs * 2 * LANES * TILE * TILE, bytes_accessed=0, transcendentals=0),
        name="collect",
    )(*args)


def turn_back(mean, out_ref, bins, quads, turned):
    rows, width = mean.shape
    lines = width // LANES
    fold = LANES // bins
    for q in range(lines):
        quads[pl.ds(q, rows, stride=lines), :] = mean[:, q * LANES : (q + 1) * LANES]
    blocked = lax.broadcasted_iota(jnp.int32, (lines, LANES), 1) // bins

    def turn(g):
        source = [quads[pl.ds(pl.multiple_of(g * LANES + k * lines, lines), lines), :] for k in range(fold)]
        for r in range(fold):
            out = source[r]
            for k in range(fold):
                if k != r:
                    out = jnp.where(blocked == k, pltpu.roll(source[k], (k - r) * bins % LANES, 1), out)
            turned[pl.ds(r, lines, stride=fold), :] = out
        return turned[...].T

    full, rest = out_ref.shape[0] // LANES, out_ref.shape[0] % LANES

    def step(g, _):
        out_ref[pl.ds(pl.multiple_of(g * LANES, LANES), LANES), :] = turn(g)
        return 0

    lax.fori_loop(0, full, step, 0)
    if rest:
        out_ref[full * LANES :, :] = turn(full)[:rest]


def project_kernel(bins, pairs, lists, state_rows, part, *refs):
    parts, weights, tiles, *refs = refs
    sources, refs = refs[:lists], refs[lists:]
    mean = refs.pop(0) if state_rows else None
    outs, refs = refs[:lists], refs[lists:]
    state_ref = refs.pop(0) if state_rows else None
    steps, sems, *turning = refs
    copies = fetch_rows(sources, steps, sems)
    rows, count = outs[0].shape
    blocks = count // LANES
    whole_blocks = blocks if part is None else 2 * blocks
    base = blocks * (part or 0)
    group = GROUP if part is None else GROUP // 2
    for out in outs:
        out[...] = jnp.zeros_like(out)
    if state_rows:
        turn_back(mean, state_ref, bins, *turning)
    for copy in copies:
        copy.wait()

    def step(n, _):
        for number in range(lists):
            for g in range(group):
                k = n * group + g
                tile = steps[number, 7, k].astype(jnp.int32)
                block = jnp.minimum(k - tile, whole_blocks - 1)
                local = jnp.clip(block - base, 0, blocks - 1)
                block = block + number * whole_blocks
                valid = k < pairs
                if part is not None:
                    valid = valid & ((k < middle) == (part == 0))
                wanted = jnp.where(valid, tile, -1).astype(F32)
                got = lax.dot_general(parts[tile], weights[block], NN, preferred_element_type=F32)
                got = got[:rows] + got[HALF : HALF + rows]
                got = got[:, :LANES] + got[:, LANES:]
                got = jnp.where(tiles[block][:1] == wanted, got, 0.0)
                place = pl.ds(pl.multiple_of(local * LANES, LANES), LANES)
                outs[number][:, place] += got
        return 0

    start, stop = 0, -(-pairs // group)
    if part is not None:
        middle = steps[0, 7, LANES - 1].astype(jnp.int32)
        start, stop = (0, (middle + group - 1) // group) if part == 0 else (middle // group, stop)
    lax.fori_loop(start, stop, step, 0)


def project_call(parts, collected, rows, count, bins, ntiles, mean=None, state_rows=0, part=None):
    weights, tiles, *sources = collected
    lists = len(sources)
    pairs = count // LANES + ntiles - 1
    extra = [] if mean is None else [mean]
    scratch = [pltpu.SMEM((lists, 8, LANES), F32), pltpu.SemaphoreType.DMA((lists,))]
    if extra:
        scratch += [pltpu.VMEM((mean.size // LANES, LANES), F32), pltpu.VMEM((LANES, LANES), F32)]
    return pl.pallas_call(
        functools.partial(project_kernel, bins, pairs, lists, state_rows, part),
        out_shape=[jax.ShapeDtypeStruct((rows, count if part is None else count // 2), F32)] * lists
        + [jax.ShapeDtypeStruct((state_rows, LANES), F32)] * len(extra),
        in_specs=[VMEM] * (3 + lists + len(extra)),
        out_specs=[VMEM] * (lists + len(extra)),
        scratch_shapes=scratch,
        compiler_params=params(20),
        cost_estimate=pl.CostEstimate(flops=lists * pairs * 2 * LANES * TILE * TILE, bytes_accessed=0, transcendentals=0),
        name="project",
    )(parts, weights, tiles, *sources, *extra)


def middle_kernel(species, bins, chunk, refs_in, refs_out, scratch):
    *accs, cmc_ref, diss_ref, rate_ref, count_ref, matrix_ref = refs_in
    fresh_ref, parts_ref = refs_out
    next_ref, far_ref, nat, quads, turned, side_out, load, outward, hopped, summed, got, state_ref, edge_out, edge_in, side_in, pick_ref, third_ref, send, recv, side_send, side_recv = scratch
    rows, width = fresh_ref.shape
    steps = width // chunk
    slab, nslab = lax.axis_index("slab"), lax.axis_size("slab")
    cross, ncross = lax.axis_index("cross"), lax.axis_size("cross")
    parity = lax.rem(slab, 2)
    outer = slab + 4 * parity - 2
    inner = slab - 4 * parity + 2
    partner = slab + 1 - 2 * parity
    has_outer = (outer >= 0) & (outer < nslab)
    has_inner = (inner >= 0) & (inner < nslab)
    has_before, has_after = cross > 0, cross < ncross - 1
    has_down, has_up = slab > 0, slab < nslab - 1
    mesh = pl.DeviceIdType.MESH

    def partial_sum(piece):
        total = accs[0][:, piece]
        for more in accs[1:]:
            total = total + more[:, piece]
        return total

    loads, start = [], 0
    for n, source in enumerate((cmc_ref, diss_ref, rate_ref)):
        target = nat.at[start : start + source.shape[0]]
        loads.append(pltpu.make_async_copy(source, target, load.at[n]))
        loads[-1].start()
        start += source.shape[0]
    if start < nat.shape[0]:
        nat[start:, :] = jnp.zeros((nat.shape[0] - start, LANES), F32)
    outward[...] = partial_sum(slice(0, width))

    @pl.when(jnp.logical_not(has_inner))
    def _():
        hopped[...] = jnp.zeros_like(hopped)

    @pl.when(jnp.logical_not(has_outer))
    def _():
        far_ref[...] = jnp.zeros_like(far_ref)

    @pl.when(jnp.logical_not(has_before))
    def _():
        edge_in[:, :, :LANES] = jnp.zeros(edge_in.shape[:2] + (LANES,), F32)

    @pl.when(jnp.logical_not(has_after))
    def _():
        edge_in[:, :, LANES:] = jnp.zeros(edge_in.shape[:2] + (LANES,), F32)

    @pl.when(jnp.logical_not(has_down))
    def _():
        side_in[0] = jnp.zeros(side_in.shape[1:], F32)

    @pl.when(jnp.logical_not(has_up))
    def _():
        side_in[1] = jnp.zeros(side_in.shape[1:], F32)

    barrier = pltpu.get_barrier_semaphore()
    greet = lambda where: pl.semaphore_signal(barrier, inc=1, device_id=where, device_id_type=mesh)
    pl.when(has_down)(lambda: greet({"slab": slab - 1}))
    pl.when(has_up)(lambda: greet({"slab": slab + 1}))
    pl.when(has_outer)(lambda: greet({"slab": outer}))
    pl.when(has_inner)(lambda: greet({"slab": inner}))
    pl.when(has_before)(lambda: greet({"cross": cross - 1}))
    pl.when(has_after)(lambda: greet({"cross": cross + 1}))
    number = lambda flag: jnp.where(flag, 1, 0)
    flags = (has_down, has_up, has_outer, has_inner, has_before, has_after)
    pl.semaphore_wait(barrier, sum(number(flag) for flag in flags))

    def lanes(c, base=0):
        return pl.ds(pl.multiple_of(base + c * chunk, chunk), chunk)

    def remote(kind, c, source, target, where):
        return pltpu.make_async_remote_copy(
            src_ref=source, dst_ref=target, send_sem=send.at[kind, c], recv_sem=recv.at[kind, c],
            device_id=where, device_id_type=mesh,
        )

    to_outer = lambda c: remote(0, c, outward.at[:, lanes(c)], hopped.at[:, lanes(c)], {"slab": outer})
    to_partner = lambda c: remote(1, c, summed.at[:, lanes(c)], got.at[:, lanes(c)], {"slab": partner})
    to_after = lambda c: remote(2, c, edge_out.at[c, :, LANES:], edge_in.at[c, :, :LANES], {"cross": cross + 1})
    to_before = lambda c: remote(3, c, edge_out.at[c, :, :LANES], edge_in.at[c, :, LANES:], {"cross": cross - 1})
    give = lambda c: remote(4, c, fresh_ref.at[:, lanes(c)], next_ref.at[:, lanes(c)], {"slab": partner})
    pass_on = lambda c: remote(5, c, next_ref.at[:, lanes(c)], far_ref.at[:, lanes(c)], {"slab": inner})

    def side(n, source, where):
        return pltpu.make_async_remote_copy(
            src_ref=source, dst_ref=side_in.at[n], send_sem=side_send.at[n], recv_sem=side_recv.at[n],
            device_id=where, device_id_type=mesh,
        )

    to_up = side(0, side_out.at[0], {"slab": slab + 1})
    to_down = side(1, side_out.at[1], {"slab": slab - 1})

    def start_hops(chunks):
        @pl.when(has_outer)
        def _():
            for c in chunks:
                to_outer(c).start()

    start_hops(range(2))
    for copy in loads:
        copy.wait()
    lines = width // LANES
    fold = LANES // bins
    blocked = lax.broadcasted_iota(jnp.int32, (LANES // fold, LANES), 1) // bins

    def turn(g, _):
        turned[...] = nat[pl.ds(pl.multiple_of(g * LANES, LANES), LANES), :].T
        parts = [turned[pl.ds(r, LANES // fold, stride=fold), :] for r in range(fold)]
        for k in range(fold):
            out = parts[k]
            for r in range(fold):
                if r != k:
                    out = jnp.where(blocked == r, pltpu.roll(parts[r], (r - k) * bins % LANES, 1), out)
            place = pl.multiple_of(g * LANES + k * lines, lines)
            quads[pl.ds(place, lines), :] = out
        return 0

    lax.fori_loop(0, nat.shape[0] // LANES, turn, 0)
    tile = lambda q: quads[pl.ds(q, rows, stride=lines), :]
    side_out[0] = tile(lines - 1)
    side_out[1] = tile(0)

    lane = lax.broadcasted_iota(jnp.int32, (2 * LANES, chunk), 1)
    row = lax.broadcasted_iota(jnp.int32, (2 * LANES, chunk), 0)
    target = jnp.where(row < LANES, row * bins, (row - LANES) * bins + bins - 1)
    pick_ref[...] = rows_equal(target, lane)
    third = matrix_ref.shape[1] // 3
    high, low = halves(matrix_ref[...])
    column = lax.broadcasted_iota(jnp.int32, matrix_ref.shape, 1)
    third_ref[...] = jnp.where(column < 2 * third, high.astype(F32), low.astype(F32)).astype(BF16)
    line = lax.broadcasted_iota(jnp.int32, (rows, chunk), 0)
    slot = lax.broadcasted_iota(jnp.int32, (rows, chunk), 1) % bins
    gap = [jnp.zeros((third - rows, chunk), F32)] * (third > rows)

    pl.when(has_up)(to_up.start)
    pl.when(has_down)(to_down.start)
    start_hops(range(2, steps))

    def stacked(x):
        high = x.astype(BF16).astype(F32)
        return jnp.concatenate([high, x - high], axis=0).astype(BF16)

    def add_hop(c):
        pl.when(has_inner)(lambda: to_outer(c).wait_recv())
        summed[:, lanes(c)] = partial_sum(lanes(c, 2 * width)) + hopped[:, lanes(c)]

    per = chunk // LANES

    def advect(c):
        here = jnp.concatenate([tile(c * per + n) for n in range(per)], axis=1)
        low = jnp.where(c == 0, side_in[0], tile(jnp.maximum(c * per - 1, 0)))
        high = jnp.where(c == steps - 1, side_in[1], tile(jnp.minimum((c + 1) * per, lines - 1)))
        left = pltpu.roll(jnp.concatenate([low, here], axis=1), bins, 1)[:, LANES:]
        right = pltpu.roll(jnp.concatenate([here, high], axis=1), chunk + LANES - bins, 1)[:, :chunk]
        return here - 0.4 * (here - left) + 0.1 * (right - 2.0 * here + left)

    def cell_row(n, c):
        start = (species + n) * lines + c * per
        return jnp.concatenate([quads[pl.ds(start + k, 1), :] for k in range(per)], axis=1)

    def blend(c):
        total = partial_sum(lanes(c, width)) + got[:, lanes(c)]
        blended = (total + advect(c)) / (total[species : species + 1] + 1.0)
        state_ref[:, lanes(c)] = blended
        edge = lax.dot_general(stacked(blended), pick_ref[...], NT, preferred_element_type=F32)
        edge_out[c] = edge[:rows] + edge[rows:]

    def send_edges(c):
        pl.when(has_after)(lambda: to_after(c).start())
        pl.when(has_before)(lambda: to_before(c).start())

    def wait_edges(c):
        pl.when(has_before)(lambda: to_after(c).wait_recv())
        pl.when(has_after)(lambda: to_before(c).wait_recv())

    def react(c):
        here = state_ref[:, lanes(c)]
        around = lax.dot_general(stacked(edge_in[c]), pick_ref[...], NN, preferred_element_type=F32)
        around = around[:rows] + around[rows:]
        before = jnp.where(slot == 0, around, pltpu.roll(here, 1, 1))
        after = jnp.where(slot == bins - 1, around, pltpu.roll(here, chunk - 1, 1))
        state = here + cell_row(0, c) * (after - 2.0 * here + before)
        half = 0.5 * cell_row(1, c)
        count = count_ref[:, lanes(c)]
        for k in range(KMAX):
            high, low = (part.astype(F32) for part in halves(state))
            stack = jnp.concatenate([high, *gap, low, *gap, high, *gap], axis=0).astype(BF16)
            rate = lax.dot_general(third_ref[...], stack, NN, preferred_element_type=F32)
            state = jnp.where(k < count, state + half * jnp.tanh(rate), state)
        state = jnp.where(line == species, 1.0, state)
        fresh_ref[:, lanes(c)] = state
        keep(1, c, state)

    def keep(which, c, mean):
        for n in range(chunk // TILE):
            index = which * (width // TILE) + c * (chunk // TILE) + n
            parts_ref[index] = padded_halves(mean[:, n * TILE : (n + 1) * TILE])

    def step(t, _):
        def when(lag, body):
            c = t - lag
            pl.when((c >= 0) & (c < steps))(lambda: body(c))

        def second(c):
            pl.when((c == 0) & has_down)(to_up.wait_recv)
            pl.when((c == 0) & has_up)(to_down.wait_recv)
            to_partner(c).wait_recv()
            blend(c)

        def third_stage(c):
            wait_edges(c)
            react(c)

        def fourth(c):
            give(c).wait_recv()
            pl.when(has_inner)(lambda: pass_on(c).start())
            keep(2, c, next_ref[:, lanes(c)])

        when(0, add_hop)
        when(LAG[0], second)
        when(0, lambda c: to_partner(c).start())
        when(LAG[1], third_stage)
        when(LAG[0], send_edges)
        when(LAG[2], fourth)
        when(LAG[1], lambda c: give(c).start())
        return 0

    lax.fori_loop(0, steps + LAG[2], step, 0)

    def finish(c, _):
        pl.when(has_outer)(lambda: to_outer(c).wait_send())
        to_partner(c).wait_send()
        pl.when(has_after)(lambda: to_after(c).wait_send())
        pl.when(has_before)(lambda: to_before(c).wait_send())
        give(c).wait_send()
        pl.when(has_inner)(lambda: pass_on(c).wait_send())
        pl.when(has_outer)(lambda: pass_on(c).wait_recv())
        keep(0, c, far_ref[:, lanes(c)])
        return 0

    lax.fori_loop(0, steps, finish, 0)
    pl.when(has_up)(to_up.wait_send)
    pl.when(has_down)(to_down.wait_send)


def middle_call(accs, cmc, diss, rate, count, matrix, species, bins, chunk=512):
    rows, width = accs[0].shape[0], count.shape[1]
    steps = width // chunk
    given = len(accs) + 5

    def kernel(*refs):
        middle_kernel(species, bins, chunk, refs[:given], refs[given : given + 2], refs[given + 2 :])

    return pl.pallas_call(
        kernel,
        out_shape=[
            jax.ShapeDtypeStruct((rows, width), F32),
            jax.ShapeDtypeStruct((3 * width // TILE, 2 * HALF, TILE), BF16),
        ],
        in_specs=[VMEM] * len(accs) + [pl.BlockSpec(memory_space=pl.ANY)] * 3 + [VMEM] * 2,
        out_specs=[VMEM] * 2,
        scratch_shapes=[pltpu.VMEM((rows, width), F32)] * 2
        + [pltpu.VMEM((rows * bins, LANES), F32), pltpu.VMEM((rows * width // LANES, LANES), F32)]
        + [pltpu.VMEM((LANES, LANES), F32), pltpu.VMEM((2, rows, LANES), F32), pltpu.SemaphoreType.DMA((3,))]
        + [pltpu.VMEM((rows, width), F32)] * 5
        + [pltpu.VMEM((steps, rows, 2 * LANES), F32)] * 2
        + [pltpu.VMEM((2, rows, LANES), F32), pltpu.VMEM((2 * LANES, chunk), BF16), pltpu.VMEM(matrix.shape, BF16)]
        + [pltpu.SemaphoreType.DMA((6, steps))] * 2
        + [pltpu.SemaphoreType.DMA((2,))] * 2,
        compiler_params=pltpu.CompilerParams(vmem_limit_bytes=22 << 20, collective_id=1, has_side_effects=True),
        name="middle",
    )(*accs, cmc, diss, rate, count, matrix)


def on_device(
    les_state, cmc_state, cmc_map, pdf_index, pdf_table, diffusion, chem_matrix, dissipation, reaction_rate, substeps
):
    species = les_state.shape[0]
    rows = -(-(species + 2) // 8) * 8
    bins, cells = cmc_state.shape[1:]
    nshape = pdf_table.shape[0]
    count = cmc_map.size
    ncross = lax.axis_size("cross")
    per_tile = TILE // bins
    ntiles = 3 * cells // per_tile
    flat, rank, parts, low = head_call(
        les_state, cmc_map, pdf_index, diffusion, rows, cells, nshape, ntiles, nshape * per_tile
    )
    bits = [1 << k for k in range(ncross.bit_length() - 1)]
    low_there = swap(low, "cross", bits[-1])
    high = sort_call(parts, rank)
    high_there = swap(high, "cross", bits[-1])
    near_lists = [(low, high)] + [(swap(low, "cross", bit), swap(high, "cross", bit)) for bit in bits[:-1]]
    low_far = [low_there] + [swap(low_there, "cross", bit) for bit in bits[:-1]]

    table = lax.dynamic_slice_in_dim(pdf_table.T, lax.axis_index("cross") * bins, bins, axis=0)

    extra = rows - species
    matrix = jnp.tile(jnp.pad(chem_matrix, ((0, extra), (0, -(-rows // 16) * 16 - species))), (1, 3))
    terms = (cmc_state.reshape(species * bins, cells), dissipation, reaction_rate, jnp.repeat(substeps, bins)[None, :], matrix)
    acc, *near = collect_call(near_lists, table, species, bins, per_tile, ntiles)
    acc, high_there, terms = lax.optimization_barrier((acc, high_there, terms))
    high_far = [high_there] + [swap(high_there, "cross", bit) for bit in bits[:-1]]
    accs, far = [acc], []
    for pair in zip(low_far, high_far):
        acc, *collected = collect_call([pair], table, species, bins, per_tile, ntiles)
        accs.append(acc)
        far.append(collected)
    fresh, parts = middle_call(accs, *terms, species, bins)

    ends = []
    for part in range(2):
        pieces = []
        for bit, collected in zip(bits[:-1], far[1:]):
            (piece,) = project_call(parts, collected, rows, count, bins, ntiles, part=part)
            piece, parts = lax.optimization_barrier((piece, parts))
            pieces.append(swap(piece, "cross", bit))
        (there,) = project_call(parts, far[0], rows, count, bins, ntiles, part=part)
        there = sum(pieces, there)
        there, parts = lax.optimization_barrier((there, parts))
        ends.append(swap(there, "cross", bits[-1]))
    low, high = ends
    *here, cmc_out = project_call(parts, near, rows, count, bins, ntiles, fresh, species * bins)
    total = [here[0]] + [swap(piece, "cross", bit) for bit, piece in zip(bits[:-1], here[1:])]
    before = unsort_call(total, low, rank, None, None)
    les_out = unsort_call(total, high, rank, before, flat)
    return (les_out.reshape(les_state.shape), cmc_out.reshape(species, bins, cells))


def solution(mesh):
    return jax.shard_map(
        on_device,
        mesh=mesh,
        in_specs=(
            P(None, "slab", "cross", None),
            P(None, "cross", "slab"),
            P("slab", "cross", None),
            P("slab", "cross", None),
            P(),
            P(),
            P(),
            P("cross", "slab"),
            P("cross", "slab"),
            P("slab"),
        ),
        out_specs=(P(None, "slab", "cross", None), P(None, "cross", "slab")),
        check_vma=False,
    )
```

```python
import functools


import jax
import jax.numpy as jnp
from jax import lax
from jax.experimental import pallas as pl
from jax.experimental.pallas import tpu as pltpu
from jax.sharding import PartitionSpec as P

KMAX = 4
F32 = jnp.float32
BF16 = jnp.bfloat16
NT = (((1,), (1,)), ((), ()))
NN = (((1,), (0,)), ((), ()))
LANES = 128
TILE = 256
HALF = 64
GROUP = 16
LAG = (3, 6, 9)


def swap(array, axis, bit):
    count = lax.axis_size(axis)
    return lax.ppermute(array, axis, [(i, i ^ bit) for i in range(count)])


def halves(x):
    high = x.astype(BF16)
    return high, (x - high.astype(F32)).astype(BF16)


def padded_halves(x):
    gap = jnp.zeros((HALF - x.shape[0], x.shape[1]), F32)
    high = x.astype(BF16).astype(F32)
    return jnp.concatenate([high, gap, x - high, gap], axis=0).astype(BF16)


def rows_equal(targets, row):
    return jnp.where(targets == row, 1.0, 0.0).astype(BF16)


def whole(shape):
    return pl.BlockSpec(shape, lambda *_: (0,) * len(shape))


VMEM = pl.BlockSpec(memory_space=pltpu.VMEM)
SMEM = pl.BlockSpec(memory_space=pltpu.SMEM)


def params(mib):
    return pltpu.CompilerParams(vmem_limit_bytes=mib << 20)


def fetch_rows(sources, steps, sems):
    copies = []
    for number, source in enumerate(sources):
        last = source.at[source.shape[0] - 8 : source.shape[0], :LANES]
        copies.append(pltpu.make_async_copy(last, steps.at[number], sems.at[number]))
        copies[-1].start()
    return copies


def ranks(tiles, span, key_ref, rank_ref, table_ref):
    count = rank_ref.shape[1]
    ids = lax.broadcasted_iota(jnp.int32, (tiles, TILE), 0).astype(F32)
    tile_of = lambda n: jnp.floor((key_ref[:1, n * TILE : (n + 1) * TILE] + 0.5) * (1.0 / span))
    total = jnp.zeros((tiles, TILE), F32)
    for n in range(count // TILE):
        total = total + jnp.where(ids == tile_of(n), 1.0, 0.0)
    total = jnp.sum(total, axis=1, keepdims=True)
    total = jnp.broadcast_to(total, (tiles, LANES))
    big = jnp.floor(total * (1.0 / HALF))
    row = lax.broadcasted_iota(jnp.int32, (tiles, tiles), 0)
    below = rows_equal(jnp.where(lax.broadcasted_iota(jnp.int32, (tiles, tiles), 1) < row, 1, 0), 1)
    add = lambda part: lax.dot_general(below, part.astype(BF16), NN, preferred_element_type=F32)
    base = add(big) * HALF + add(total - big * HALF)
    order = lax.broadcasted_iota(jnp.int32, (tiles, LANES), 0).astype(F32)
    lane = lax.broadcasted_iota(jnp.int32, (tiles, LANES), 1).astype(F32)
    last = jnp.maximum(jnp.ceil((base + total) * (1.0 / LANES)) - 1.0, 0.0) + order
    passed = jnp.where((last < lane) & (order < tiles - 1), 1.0, 0.0)
    table = jnp.sum(passed, axis=0, keepdims=True)
    number = lane[:1]
    blocks = count // LANES
    early = jnp.where((number - table < blocks // 2) & (number < blocks + tiles - 1), 1.0, 0.0)
    table_ref[...] = jnp.where(number == LANES - 1, jnp.sum(early, axis=1, keepdims=True), table)
    ahead = jnp.where(
        lax.broadcasted_iota(jnp.int32, (TILE, TILE), 0) < lax.broadcasted_iota(jnp.int32, (TILE, TILE), 1), 1.0, 0.0
    ).astype(BF16)
    carry = base[:, :1]
    for n in range(count // TILE):
        hot = jnp.where(ids == tile_of(n), 1.0, 0.0)
        before = lax.dot_general(hot.astype(BF16), ahead, NN, preferred_element_type=F32) + carry
        rank_ref[:, n * TILE : (n + 1) * TILE] = jnp.sum(hot * before, axis=0, keepdims=True)
        carry = carry + jnp.sum(hot, axis=1, keepdims=True)


def head_kernel(grid_shape, cells, nshape, tiles, span, *refs):
    given, (t_ref, rank_ref, parts_ref, half_ref), refs = refs[:4], refs[4:8], refs[8:]
    les_ref, map_ref, shape_ref, diff_ref, key_ref, table_ref, *refs = refs
    faces, halos, (send, recv, load) = refs[:4], refs[4:8], refs[8:]
    loads = [
        pltpu.make_async_copy(source, target, load.at[n])
        for n, (source, target) in enumerate(zip(given, (les_ref, map_ref, shape_ref, diff_ref)))
    ]
    for copy in loads:
        copy.start()
    species, nx, ny = grid_shape
    count = rank_ref.shape[1]
    slab, nslab = lax.axis_index("slab"), lax.axis_size("slab")
    cross, ncross = lax.axis_index("cross"), lax.axis_size("cross")
    mesh = pl.DeviceIdType.MESH
    sides = [
        (slab > 0, {"slab": slab - 1}),
        (slab < nslab - 1, {"slab": slab + 1}),
        (cross > 0, {"cross": cross - 1}),
        (cross < ncross - 1, {"cross": cross + 1}),
    ]
    barrier = pltpu.get_barrier_semaphore()
    for n, (there, where) in enumerate(sides):

        @pl.when(jnp.logical_not(there))
        def _(n=n):
            halos[n][...] = jnp.zeros_like(halos[n])

    for copy in loads:
        copy.wait()
    line = lambda x, y: les_ref[pl.ds(x * ny + y, species, stride=nx * ny), :]
    for n, x in enumerate((0, nx - 1)):
        for y in range(ny):
            faces[n][y, :species] = line(x, y)
    for n, y in enumerate((0, ny - 1)):
        for x in range(nx):
            faces[2 + n][x, :species] = line(x, y)
    for there, where in sides:

        @pl.when(there)
        def _(where=where):
            pl.semaphore_signal(barrier, inc=1, device_id=where, device_id_type=mesh)

    pl.semaphore_wait(barrier, sum(jnp.where(there, 1, 0) for there, _ in sides))
    copies = {}
    for n in (2, 3, 0, 1):
        there, where = sides[n]
        copy = pltpu.make_async_remote_copy(
            src_ref=faces[n], dst_ref=halos[n ^ 1], send_sem=send.at[n], recv_sem=recv.at[n ^ 1],
            device_id=where, device_id_type=mesh,
        )
        pl.when(there)(copy.start)
        copies[n] = copy
    offset = map_ref[...] - (slab - 1) * cells
    block = jnp.where(offset >= cells, 1, 0) + jnp.where(offset >= 2 * cells, 1, 0)
    offset = jnp.where(lax.rem(slab, 2) == 1, (2 - block) * cells + offset - block * cells, offset)
    key = (offset * nshape + shape_ref[...]).astype(F32)
    key_ref[:1, :] = key
    t_ref[species:, :] = jnp.concatenate([key] + [jnp.zeros((t_ref.shape[0] - species - 1, count), F32)], axis=0)
    ranks(tiles, span, key_ref, rank_ref, table_ref)
    row = lax.broadcasted_iota(jnp.int32, (species, species), 0)
    number = jnp.where(row == lax.broadcasted_iota(jnp.int32, (species, species), 1), diff_ref[...], 0.0)
    number = jnp.sum(number, axis=1, keepdims=True)
    lane = lax.broadcasted_iota(jnp.int32, (species, LANES), 1)
    edge_y, edge_x = sorted({0, ny - 1}), sorted({0, nx - 1})
    phases = [
        ((), [(x, y) for x in range(1, nx - 1) for y in range(1, ny - 1)]),
        ((2, 3), [(x, y) for x in range(1, nx - 1) for y in edge_y]),
        ((0, 1), [(x, y) for x in edge_x for y in range(ny)]),
    ]
    done = 0
    for sources, places in phases:
        for n in sources:
            pl.when(sides[n ^ 1][0])(copies[n].wait_recv)
        for x, y in places:
            here = line(x, y)
            around = line(x + 1, y) if x < nx - 1 else halos[1][y, :species]
            around = around + (line(x - 1, y) if x else halos[0][y, :species])
            around = around + (line(x, y + 1) if y < ny - 1 else halos[3][x, :species])
            around = around + (line(x, y - 1) if y else halos[2][x, :species])
            around = around + jnp.where(lane < LANES - 1, pltpu.roll(here, LANES - 1, 1), 0.0)
            around = around + jnp.where(lane > 0, pltpu.roll(here, 1, 1), 0.0)
            place = (x * ny + y) * LANES
            t_ref[:species, place : place + LANES] = here + number * (around - 6.0 * here)
        for x, y in places:
            piece = slice((x * ny + y) * LANES, (x * ny + y + 1) * LANES)
            value = t_ref[:, piece]
            high = value.astype(BF16).astype(F32)
            parts_ref[:, piece] = jnp.concatenate([high, value - high], axis=0).astype(BF16)
        if places:
            done += len(places)
            table = table_ref[...] if done == nx * ny else None
            sort_tiles(parts_ref, rank_ref, table, half_ref, 0, [x * ny + y for x, y in places], done > len(places))
    for n, (there, _) in enumerate(sides):
        pl.when(there)(copies[n].wait_send)


def head_call(les_state, cmc_map, pdf_index, diffusion, rows, cells, nshape, tiles, span):
    species, nx, ny, nz = les_state.shape
    count = nx * ny * nz
    halo = [pltpu.VMEM((n, rows, LANES), F32) for n in (ny, ny, nx, nx)]
    return pl.pallas_call(
        functools.partial(head_kernel, (species, nx, ny), cells, nshape, tiles, span),
        out_shape=[
            jax.ShapeDtypeStruct((rows, count), F32),
            jax.ShapeDtypeStruct((1, count), F32),
            jax.ShapeDtypeStruct((2 * rows, count), BF16),
            jax.ShapeDtypeStruct((rows, count // 2), F32),
        ],
        in_specs=[pl.BlockSpec(memory_space=pltpu.HBM)] * 4,
        out_specs=[VMEM] * 4,
        scratch_shapes=[
            pltpu.VMEM((species * nx * ny, nz), F32),
            pltpu.VMEM((1, count), jnp.int32),
            pltpu.VMEM((1, count), jnp.int32),
            pltpu.VMEM((1, species), F32),
            pltpu.VMEM((8, count), F32),
            pltpu.VMEM((1, LANES), F32),
        ] + halo * 2 + [pltpu.SemaphoreType.DMA((4,))] * 3,
        compiler_params=pltpu.CompilerParams(vmem_limit_bytes=60 << 20, collective_id=2, has_side_effects=True),
        name="head",
    )(
        les_state.reshape(species * nx * ny, nz), cmc_map.reshape(1, count), pdf_index.reshape(1, count),
        diffusion.reshape(1, species),
    )


CHUNK = 2 * TILE


def sort_tiles(parts, rank_ref, steps, out_ref, first, lines=None, more=False):
    rows = out_ref.shape[0]
    lines = list(range(rank_ref.shape[1] // LANES)) if lines is None else lines
    groups = [lines[n : n + CHUNK // LANES] for n in range(0, len(lines), CHUNK // LANES)]

    def pick(ref, group):
        if group == list(range(group[0], group[-1] + 1)):
            return ref[:, group[0] * LANES : (group[-1] + 1) * LANES]
        return jnp.concatenate([ref[:, n * LANES : (n + 1) * LANES] for n in group], axis=1)

    def step(n, _):
        here = (first + n) * TILE
        total = jnp.zeros((2 * rows, TILE), F32)
        for group in groups:
            ids = lax.broadcasted_iota(jnp.int32, (TILE, len(group) * LANES), 0) + here
            hot = rows_equal(ids.astype(F32), pick(rank_ref, group))
            total = total + lax.dot_general(pick(parts, group), hot, NT, preferred_element_type=F32)
        total = total[:rows] + total[rows:]
        place = pl.ds(pl.multiple_of(n * TILE, TILE), TILE)
        if more:
            total = total + out_ref[:, place]
        if steps is not None:
            line = lax.broadcasted_iota(jnp.int32, (rows, TILE), 0)
            total = jnp.where(line == rows - 1, jnp.concatenate([steps] * (TILE // LANES), axis=1), total)
        out_ref[:, place] = total
        return 0

    lax.fori_loop(0, out_ref.shape[1] // TILE, step, 0)


def sort_kernel(parts_ref, rank_ref, out_ref):
    sort_tiles(parts_ref, rank_ref, None, out_ref, out_ref.shape[1] // TILE)


def sort_call(parts, rank):
    rows, count = parts.shape[0] // 2, parts.shape[1]
    return pl.pallas_call(
        sort_kernel,
        out_shape=jax.ShapeDtypeStruct((rows, count // 2), F32),
        in_specs=[VMEM] * 2,
        out_specs=VMEM,
        compiler_params=params(8),
        cost_estimate=pl.CostEstimate(flops=2 * rows * count * count, bytes_accessed=4 * rows * count, transcendentals=0),
        name="sort",
    )(parts, rank)


def unsort_kernel(half, given, rank_ref, *refs):
    xs, refs = refs[:given], refs[given:]
    before, (flat_ref,) = (refs[:1], refs[1:2]) if half else ((), (None,))
    out_ref, parts = refs[-2:]
    rows, count = xs[0].shape[0], rank_ref.shape[1]
    width = xs[0].shape[1]

    @pl.when(pl.program_id(0) == 0)
    def _():
        x = xs[0][...]
        for more in xs[1:]:
            x = x + more[...]
        high = x.astype(BF16).astype(F32)
        parts[...] = jnp.concatenate([high, x - high], axis=0).astype(BF16)

    total = jnp.zeros((2 * rows, TILE), F32)
    for k in range(width // CHUNK):
        ids = lax.broadcasted_iota(jnp.int32, (CHUNK, TILE), 0) + (half * width + k * CHUNK)
        hot = rows_equal(ids.astype(F32), rank_ref[:, pl.ds(pl.multiple_of(pl.program_id(0) * TILE, TILE), TILE)])
        piece = parts[:, k * CHUNK : (k + 1) * CHUNK]
        total = total + lax.dot_general(piece, hot, NN, preferred_element_type=F32)
    total = total[:rows] + total[rows:]
    if not half:
        out_ref[...] = total
        return
    total = total + before[0][...]
    species = rows - 2
    ratio = 0.5 / total[species : species + 1]
    for n in range(TILE // LANES):
        piece = slice(n * LANES, (n + 1) * LANES)
        line = pl.program_id(0) * (TILE // LANES) + n
        value = 0.5 * flat_ref[:species, piece] + total[:species, piece] * ratio[:, piece]
        out_ref[pl.ds(line, species, stride=count // LANES), :] = value


def unsort_call(wholes, piece, rank, before, flat):
    half = int(before is not None)
    rows, count = wholes[0].shape
    part = pl.BlockSpec((rows, count // 2), lambda i: (0, half))
    column = pl.BlockSpec((rows, TILE), lambda i: (0, i))
    args = [rank, *wholes, piece]
    specs = [whole(rank.shape)] + [part] * len(wholes) + [whole(piece.shape)]
    out_shape, out_spec = (rows, count), column
    if half:
        args += [before, flat]
        specs += [column, column]
        lines = (rows - 2) * count // LANES
        out_shape, out_spec = (lines, LANES), whole((lines, LANES))
    return pl.pallas_call(
        functools.partial(unsort_kernel, half, len(wholes) + 1),
        grid=(count // TILE,),
        out_shape=jax.ShapeDtypeStruct(out_shape, F32),
        in_specs=specs,
        out_specs=out_spec,
        scratch_shapes=[pltpu.VMEM((2 * rows, count // 2), BF16)],
        compiler_params=params(12),
        cost_estimate=pl.CostEstimate(flops=2 * rows * count * count, bytes_accessed=4 * rows * count, transcendentals=0),
        name="unsort",
    )(*args)


def weights_of(key, table, bins, per_tile):
    nshape = table.shape[1]
    cell = jnp.floor((key + 0.5) * (1.0 / nshape))
    shape = key - cell * nshape
    tile = jnp.floor((cell + 0.5) * (1.0 / per_tile))
    within = cell - tile * per_tile
    ids = lax.broadcasted_iota(jnp.int32, (nshape, key.shape[1]), 0).astype(F32).astype(BF16)
    hot = jnp.where(ids == shape.astype(BF16), jnp.ones((), BF16), jnp.zeros((), BF16))
    picked = lax.dot_general(table, hot, NN, preferred_element_type=F32).astype(BF16)
    masks = [jnp.where(within == m, 1.0, 0.0).astype(BF16) for m in range(per_tile)]
    columns = []
    for part in (picked[:bins], picked[bins:]):
        columns.append(jnp.concatenate([part * mask for mask in masks], axis=0))
    return jnp.concatenate(columns, axis=1), tile


def split_table(table):
    high = table.astype(BF16).astype(F32)
    return jnp.concatenate([high, table - high], axis=0).astype(BF16)


def prepare_weights(source, index, key_row, table, bins, per_tile, weights, tiles):
    def step(n, _):
        key = source[key_row : key_row + 1, pl.ds(pl.multiple_of(n * LANES, LANES), LANES)]
        block, tile = weights_of(key, table, bins, per_tile)
        weights[index + n] = block
        tiles[index + n] = jnp.broadcast_to(tile, tiles.shape[1:])
        return 0

    lax.fori_loop(0, source.shape[1] // LANES, step, 0, unroll=4)


def collect_kernel(species, bins, per_tile, pairs, lists, *refs):
    sources, refs = [refs[2 * n : 2 * n + 2] for n in range(lists)], refs[2 * lists :]
    table_ref, out_ref, *refs = refs
    weights, tiles, *refs = refs
    keys, (parts, steps, sems) = refs[:lists], refs[lists:]
    copies = fetch_rows([source[0] for source in sources], steps, sems)
    rows, part = sources[0][0].shape
    count = 2 * part
    for key, source in zip(keys, sources):
        key[...] = source[0][rows - 8 :, :LANES]
    blocks = count // LANES
    out_ref[...] = jnp.zeros_like(out_ref)
    table = split_table(table_ref[...])
    line = lax.broadcasted_iota(jnp.int32, (rows, LANES), 0)
    for number in range(2 * lists):
        source = sources[number // 2][number % 2]
        start = number * blocks // 2
        prepare_weights(source, start, species, table, bins, per_tile, weights, tiles)

        def split(n, _, source=source, start=start):
            x = source[:, pl.ds(pl.multiple_of(n * LANES, LANES), LANES)]
            x = jnp.where(line < species, x, jnp.where(line == species, 1.0, 0.0))
            parts[start + n] = padded_halves(x)
            return 0

        lax.fori_loop(0, blocks // 2, split, 0, unroll=4)

    for copy in copies:
        copy.wait()

    def step(n, _):
        for number in range(lists):
            for g in range(GROUP):
                k = n * GROUP + g
                tile = steps[number, 7, k].astype(jnp.int32)
                block = jnp.minimum(k - tile, blocks - 1) + number * blocks
                wanted = jnp.where(k < pairs, tile, -1).astype(F32)
                mask = jnp.where(tiles[block] == wanted, 1.0, 0.0).astype(BF16)
                mask = jnp.concatenate([mask] * (2 * HALF // mask.shape[0]), axis=0)
                x = parts[block] * mask
                both = jnp.concatenate([x, x], axis=1)
                got = lax.dot_general(both, weights[block], NT, preferred_element_type=F32)
                place = pl.ds(pl.multiple_of(tile * TILE, TILE), TILE)
                out_ref[:, place] += got[:rows] + got[HALF : HALF + rows]
        return 0

    lax.fori_loop(0, -(-pairs // GROUP), step, 0)


def collect_call(sources, table, species, bins, per_tile, ntiles):
    rows, count = sources[0][0].shape[0], 2 * sources[0][0].shape[1]
    lists, blocks = len(sources), count // LANES
    pairs = blocks + ntiles - 1
    args = [half for source in sources for half in source] + [table]
    specs = [VMEM] * (2 * lists + 1)
    return pl.pallas_call(
        functools.partial(collect_kernel, species, bins, per_tile, pairs, lists),
        out_shape=[
            jax.ShapeDtypeStruct((rows, ntiles * TILE), F32),
            jax.ShapeDtypeStruct((lists * blocks, TILE, 2 * LANES), BF16),
            jax.ShapeDtypeStruct((lists * blocks, 16, LANES), F32),
        ]
        + [jax.ShapeDtypeStruct((8, LANES), F32)] * lists,
        in_specs=specs,
        out_specs=[VMEM] * (lists + 3),
        scratch_shapes=[
            pltpu.VMEM((lists * blocks, 2 * HALF, LANES), BF16),
            pltpu.SMEM((lists, 8, LANES), F32),
            pltpu.SemaphoreType.DMA((lists,)),
        ],
        compiler_params=params(19),
        cost_estimate=pl.CostEstimate(flops=lists * pairs * 2 * LANES * TILE * TILE, bytes_accessed=0, transcendentals=0),
        name="collect",
    )(*args)


def turn_back(mean, out_ref, bins, quads, turned):
    rows, width = mean.shape
    lines = width // LANES
    fold = LANES // bins
    for q in range(lines):
        quads[pl.ds(q, rows, stride=lines), :] = mean[:, q * LANES : (q + 1) * LANES]
    blocked = lax.broadcasted_iota(jnp.int32, (lines, LANES), 1) // bins

    def turn(g):
        source = [quads[pl.ds(pl.multiple_of(g * LANES + k * lines, lines), lines), :] for k in range(fold)]
        for r in range(fold):
            out = source[r]
            for k in range(fold):
                if k != r:
                    out = jnp.where(blocked == k, pltpu.roll(source[k], (k - r) * bins % LANES, 1), out)
            turned[pl.ds(r, lines, stride=fold), :] = out
        return turned[...].T

    full, rest = out_ref.shape[0] // LANES, out_ref.shape[0] % LANES

    def step(g, _):
        out_ref[pl.ds(pl.multiple_of(g * LANES, LANES), LANES), :] = turn(g)
        return 0

    lax.fori_loop(0, full, step, 0)
    if rest:
        out_ref[full * LANES :, :] = turn(full)[:rest]


def project_kernel(bins, pairs, lists, state_rows, part, first, *refs):
    parts, weights, tiles, *refs = refs
    sources, refs = refs[:lists], refs[lists:]
    mean = refs.pop(0) if state_rows else None
    outs, refs = refs[:lists], refs[lists:]
    state_ref = refs.pop(0) if state_rows else None
    steps, sems, *turning = refs
    copies = fetch_rows(sources, steps, sems)
    rows, count = outs[0].shape
    blocks = count // LANES
    whole_blocks = blocks if part is None else 2 * blocks
    base = blocks * (part or 0)
    group = GROUP if part is None else GROUP // 2
    for out in outs:
        out[...] = jnp.zeros_like(out)
    if state_rows:
        turn_back(mean, state_ref, bins, *turning)
    for copy in copies:
        copy.wait()

    def step(n, _):
        for number in range(lists):
            for g in range(group):
                k = n * group + g
                tile = steps[number, 7, k].astype(jnp.int32)
                block = jnp.minimum(k - tile, whole_blocks - 1)
                local = jnp.clip(block - base, 0, blocks - 1)
                block = block + (first + number) * whole_blocks
                valid = k < pairs
                if part is not None:
                    valid = valid & ((k < middle) == (part == 0))
                wanted = jnp.where(valid, tile, -1).astype(F32)
                got = lax.dot_general(parts[tile], weights[block], NN, preferred_element_type=F32)
                got = got[:rows] + got[HALF : HALF + rows]
                got = got[:, :LANES] + got[:, LANES:]
                got = jnp.where(tiles[block][:1] == wanted, got, 0.0)
                place = pl.ds(pl.multiple_of(local * LANES, LANES), LANES)
                outs[number][:, place] += got
        return 0

    start, stop = 0, -(-pairs // group)
    if part is not None:
        middle = steps[0, 7, LANES - 1].astype(jnp.int32)
        start, stop = (0, (middle + group - 1) // group) if part == 0 else (middle // group, stop)
    lax.fori_loop(start, stop, step, 0)


def project_call(parts, collected, rows, count, bins, ntiles, mean=None, state_rows=0, part=None, first=0):
    weights, tiles, *sources = collected
    lists = len(sources)
    pairs = count // LANES + ntiles - 1
    extra = [] if mean is None else [mean]
    scratch = [pltpu.SMEM((lists, 8, LANES), F32), pltpu.SemaphoreType.DMA((lists,))]
    if extra:
        scratch += [pltpu.VMEM((mean.size // LANES, LANES), F32), pltpu.VMEM((LANES, LANES), F32)]
    return pl.pallas_call(
        functools.partial(project_kernel, bins, pairs, lists, state_rows, part, first),
        out_shape=[jax.ShapeDtypeStruct((rows, count if part is None else count // 2), F32)] * lists
        + [jax.ShapeDtypeStruct((state_rows, LANES), F32)] * len(extra),
        in_specs=[VMEM] * (3 + lists + len(extra)),
        out_specs=[VMEM] * (lists + len(extra)),
        scratch_shapes=scratch,
        compiler_params=params(20),
        cost_estimate=pl.CostEstimate(flops=lists * pairs * 2 * LANES * TILE * TILE, bytes_accessed=0, transcendentals=0),
        name="project",
    )(parts, weights, tiles, *sources, *extra)


def middle_kernel(species, bins, chunk, refs_in, refs_out, scratch):
    *accs, cmc_ref, diss_ref, rate_ref, count_ref, matrix_ref = refs_in
    fresh_ref, parts_ref = refs_out
    next_ref, far_ref, nat, quads, turned, side_out, load, outward, hopped, summed, got, state_ref, edge_out, edge_in, side_in, pick_ref, third_ref, send, recv, side_send, side_recv = scratch
    rows, width = fresh_ref.shape
    steps = width // chunk
    slab, nslab = lax.axis_index("slab"), lax.axis_size("slab")
    cross, ncross = lax.axis_index("cross"), lax.axis_size("cross")
    parity = lax.rem(slab, 2)
    outer = slab + 4 * parity - 2
    inner = slab - 4 * parity + 2
    partner = slab + 1 - 2 * parity
    has_outer = (outer >= 0) & (outer < nslab)
    has_inner = (inner >= 0) & (inner < nslab)
    has_before, has_after = cross > 0, cross < ncross - 1
    has_down, has_up = slab > 0, slab < nslab - 1
    mesh = pl.DeviceIdType.MESH

    def partial_sum(piece):
        total = accs[0][:, piece]
        for more in accs[1:]:
            total = total + more[:, piece]
        return total

    loads, start = [], 0
    for n, source in enumerate((cmc_ref, diss_ref, rate_ref)):
        target = nat.at[start : start + source.shape[0]]
        loads.append(pltpu.make_async_copy(source, target, load.at[n]))
        loads[-1].start()
        start += source.shape[0]
    if start < nat.shape[0]:
        nat[start:, :] = jnp.zeros((nat.shape[0] - start, LANES), F32)
    outward[...] = partial_sum(slice(0, width))

    @pl.when(jnp.logical_not(has_inner))
    def _():
        hopped[...] = jnp.zeros_like(hopped)

    @pl.when(jnp.logical_not(has_outer))
    def _():
        far_ref[...] = jnp.zeros_like(far_ref)

    @pl.when(jnp.logical_not(has_before))
    def _():
        edge_in[:, :, :LANES] = jnp.zeros(edge_in.shape[:2] + (LANES,), F32)

    @pl.when(jnp.logical_not(has_after))
    def _():
        edge_in[:, :, LANES:] = jnp.zeros(edge_in.shape[:2] + (LANES,), F32)

    @pl.when(jnp.logical_not(has_down))
    def _():
        side_in[0] = jnp.zeros(side_in.shape[1:], F32)

    @pl.when(jnp.logical_not(has_up))
    def _():
        side_in[1] = jnp.zeros(side_in.shape[1:], F32)

    barrier = pltpu.get_barrier_semaphore()
    greet = lambda where: pl.semaphore_signal(barrier, inc=1, device_id=where, device_id_type=mesh)
    pl.when(has_down)(lambda: greet({"slab": slab - 1}))
    pl.when(has_up)(lambda: greet({"slab": slab + 1}))
    pl.when(has_outer)(lambda: greet({"slab": outer}))
    pl.when(has_inner)(lambda: greet({"slab": inner}))
    pl.when(has_before)(lambda: greet({"cross": cross - 1}))
    pl.when(has_after)(lambda: greet({"cross": cross + 1}))
    number = lambda flag: jnp.where(flag, 1, 0)
    flags = (has_down, has_up, has_outer, has_inner, has_before, has_after)
    pl.semaphore_wait(barrier, sum(number(flag) for flag in flags))

    def lanes(c, base=0):
        return pl.ds(pl.multiple_of(base + c * chunk, chunk), chunk)

    def remote(kind, c, source, target, where):
        return pltpu.make_async_remote_copy(
            src_ref=source, dst_ref=target, send_sem=send.at[kind, c], recv_sem=recv.at[kind, c],
            device_id=where, device_id_type=mesh,
        )

    to_outer = lambda c: remote(0, c, outward.at[:, lanes(c)], hopped.at[:, lanes(c)], {"slab": outer})
    to_partner = lambda c: remote(1, c, summed.at[:, lanes(c)], got.at[:, lanes(c)], {"slab": partner})
    to_after = lambda c: remote(2, c, edge_out.at[c, :, LANES:], edge_in.at[c, :, :LANES], {"cross": cross + 1})
    to_before = lambda c: remote(3, c, edge_out.at[c, :, :LANES], edge_in.at[c, :, LANES:], {"cross": cross - 1})
    give = lambda c: remote(4, c, fresh_ref.at[:, lanes(c)], next_ref.at[:, lanes(c)], {"slab": partner})
    pass_on = lambda c: remote(5, c, next_ref.at[:, lanes(c)], far_ref.at[:, lanes(c)], {"slab": inner})

    def side(n, source, where):
        return pltpu.make_async_remote_copy(
            src_ref=source, dst_ref=side_in.at[n], send_sem=side_send.at[n], recv_sem=side_recv.at[n],
            device_id=where, device_id_type=mesh,
        )

    to_up = side(0, side_out.at[0], {"slab": slab + 1})
    to_down = side(1, side_out.at[1], {"slab": slab - 1})

    def start_hops(chunks):
        @pl.when(has_outer)
        def _():
            for c in chunks:
                to_outer(c).start()

    start_hops(range(2))
    for copy in loads:
        copy.wait()
    lines = width // LANES
    fold = LANES // bins
    blocked = lax.broadcasted_iota(jnp.int32, (LANES // fold, LANES), 1) // bins

    def turn(g, _):
        turned[...] = nat[pl.ds(pl.multiple_of(g * LANES, LANES), LANES), :].T
        parts = [turned[pl.ds(r, LANES // fold, stride=fold), :] for r in range(fold)]
        for k in range(fold):
            out = parts[k]
            for r in range(fold):
                if r != k:
                    out = jnp.where(blocked == r, pltpu.roll(parts[r], (r - k) * bins % LANES, 1), out)
            place = pl.multiple_of(g * LANES + k * lines, lines)
            quads[pl.ds(place, lines), :] = out
        return 0

    lax.fori_loop(0, nat.shape[0] // LANES, turn, 0)
    tile = lambda q: quads[pl.ds(q, rows, stride=lines), :]
    side_out[0] = tile(lines - 1)
    side_out[1] = tile(0)

    lane = lax.broadcasted_iota(jnp.int32, (2 * LANES, chunk), 1)
    row = lax.broadcasted_iota(jnp.int32, (2 * LANES, chunk), 0)
    target = jnp.where(row < LANES, row * bins, (row - LANES) * bins + bins - 1)
    pick_ref[...] = rows_equal(target, lane)
    third = matrix_ref.shape[1] // 3
    high, low = halves(matrix_ref[...])
    column = lax.broadcasted_iota(jnp.int32, matrix_ref.shape, 1)
    third_ref[...] = jnp.where(column < 2 * third, high.astype(F32), low.astype(F32)).astype(BF16)
    line = lax.broadcasted_iota(jnp.int32, (rows, chunk), 0)
    slot = lax.broadcasted_iota(jnp.int32, (rows, chunk), 1) % bins
    gap = [jnp.zeros((third - rows, chunk), F32)] * (third > rows)

    pl.when(has_up)(to_up.start)
    pl.when(has_down)(to_down.start)
    start_hops(range(2, steps))

    def stacked(x):
        high = x.astype(BF16).astype(F32)
        return jnp.concatenate([high, x - high], axis=0).astype(BF16)

    def add_hop(c):
        pl.when(has_inner)(lambda: to_outer(c).wait_recv())
        summed[:, lanes(c)] = partial_sum(lanes(c, 2 * width)) + hopped[:, lanes(c)]

    per = chunk // LANES

    def advect(c):
        here = jnp.concatenate([tile(c * per + n) for n in range(per)], axis=1)
        low = jnp.where(c == 0, side_in[0], tile(jnp.maximum(c * per - 1, 0)))
        high = jnp.where(c == steps - 1, side_in[1], tile(jnp.minimum((c + 1) * per, lines - 1)))
        left = pltpu.roll(jnp.concatenate([low, here], axis=1), bins, 1)[:, LANES:]
        right = pltpu.roll(jnp.concatenate([here, high], axis=1), chunk + LANES - bins, 1)[:, :chunk]
        return here - 0.4 * (here - left) + 0.1 * (right - 2.0 * here + left)

    def cell_row(n, c):
        start = (species + n) * lines + c * per
        return jnp.concatenate([quads[pl.ds(start + k, 1), :] for k in range(per)], axis=1)

    def blend(c):
        total = partial_sum(lanes(c, width)) + got[:, lanes(c)]
        blended = (total + advect(c)) / (total[species : species + 1] + 1.0)
        state_ref[:, lanes(c)] = blended
        edge = lax.dot_general(stacked(blended), pick_ref[...], NT, preferred_element_type=F32)
        edge_out[c] = edge[:rows] + edge[rows:]

    def send_edges(c):
        pl.when(has_after)(lambda: to_after(c).start())
        pl.when(has_before)(lambda: to_before(c).start())

    def wait_edges(c):
        pl.when(has_before)(lambda: to_after(c).wait_recv())
        pl.when(has_after)(lambda: to_before(c).wait_recv())

    def react(c):
        here = state_ref[:, lanes(c)]
        around = lax.dot_general(stacked(edge_in[c]), pick_ref[...], NN, preferred_element_type=F32)
        around = around[:rows] + around[rows:]
        before = jnp.where(slot == 0, around, pltpu.roll(here, 1, 1))
        after = jnp.where(slot == bins - 1, around, pltpu.roll(here, chunk - 1, 1))
        state = here + cell_row(0, c) * (after - 2.0 * here + before)
        half = 0.5 * cell_row(1, c)
        count = count_ref[:, lanes(c)]
        for k in range(KMAX):
            high, low = (part.astype(F32) for part in halves(state))
            stack = jnp.concatenate([high, *gap, low, *gap, high, *gap], axis=0).astype(BF16)
            rate = lax.dot_general(third_ref[...], stack, NN, preferred_element_type=F32)
            state = jnp.where(k < count, state + half * jnp.tanh(rate), state)
        state = jnp.where(line == species, 1.0, state)
        fresh_ref[:, lanes(c)] = state
        keep(1, c, state)

    def keep(which, c, mean):
        for n in range(chunk // TILE):
            index = which * (width // TILE) + c * (chunk // TILE) + n
            parts_ref[index] = padded_halves(mean[:, n * TILE : (n + 1) * TILE])

    def step(t, _):
        def when(lag, body):
            c = t - lag
            pl.when((c >= 0) & (c < steps))(lambda: body(c))

        def second(c):
            pl.when((c == 0) & has_down)(to_up.wait_recv)
            pl.when((c == 0) & has_up)(to_down.wait_recv)
            to_partner(c).wait_recv()
            blend(c)

        def third_stage(c):
            wait_edges(c)
            react(c)

        def fourth(c):
            give(c).wait_recv()
            pl.when(has_inner)(lambda: pass_on(c).start())
            keep(2, c, next_ref[:, lanes(c)])

        when(0, add_hop)
        when(LAG[0], second)
        when(0, lambda c: to_partner(c).start())
        when(LAG[1], third_stage)
        when(LAG[0], send_edges)
        when(LAG[2], fourth)
        when(LAG[1], lambda c: give(c).start())
        return 0

    lax.fori_loop(0, steps + LAG[2], step, 0)

    def finish(c, _):
        pl.when(has_outer)(lambda: to_outer(c).wait_send())
        to_partner(c).wait_send()
        pl.when(has_after)(lambda: to_after(c).wait_send())
        pl.when(has_before)(lambda: to_before(c).wait_send())
        give(c).wait_send()
        pl.when(has_inner)(lambda: pass_on(c).wait_send())
        pl.when(has_outer)(lambda: pass_on(c).wait_recv())
        keep(0, c, far_ref[:, lanes(c)])
        return 0

    lax.fori_loop(0, steps, finish, 0)
    pl.when(has_up)(to_up.wait_send)
    pl.when(has_down)(to_down.wait_send)


def middle_call(accs, cmc, diss, rate, count, matrix, species, bins, chunk=512):
    rows, width = accs[0].shape[0], count.shape[1]
    steps = width // chunk
    given = len(accs) + 5

    def kernel(*refs):
        middle_kernel(species, bins, chunk, refs[:given], refs[given : given + 2], refs[given + 2 :])

    return pl.pallas_call(
        kernel,
        out_shape=[
            jax.ShapeDtypeStruct((rows, width), F32),
            jax.ShapeDtypeStruct((3 * width // TILE, 2 * HALF, TILE), BF16),
        ],
        in_specs=[VMEM] * len(accs) + [pl.BlockSpec(memory_space=pl.ANY)] * 3 + [VMEM] * 2,
        out_specs=[VMEM] * 2,
        scratch_shapes=[pltpu.VMEM((rows, width), F32)] * 2
        + [pltpu.VMEM((rows * bins, LANES), F32), pltpu.VMEM((rows * width // LANES, LANES), F32)]
        + [pltpu.VMEM((LANES, LANES), F32), pltpu.VMEM((2, rows, LANES), F32), pltpu.SemaphoreType.DMA((3,))]
        + [pltpu.VMEM((rows, width), F32)] * 5
        + [pltpu.VMEM((steps, rows, 2 * LANES), F32)] * 2
        + [pltpu.VMEM((2, rows, LANES), F32), pltpu.VMEM((2 * LANES, chunk), BF16), pltpu.VMEM(matrix.shape, BF16)]
        + [pltpu.SemaphoreType.DMA((6, steps))] * 2
        + [pltpu.SemaphoreType.DMA((2,))] * 2,
        compiler_params=pltpu.CompilerParams(vmem_limit_bytes=22 << 20, collective_id=1, has_side_effects=True),
        name="middle",
    )(*accs, cmc, diss, rate, count, matrix)


def on_device(
    les_state, cmc_state, cmc_map, pdf_index, pdf_table, diffusion, chem_matrix, dissipation, reaction_rate, substeps
):
    species = les_state.shape[0]
    rows = -(-(species + 2) // 8) * 8
    bins, cells = cmc_state.shape[1:]
    nshape = pdf_table.shape[0]
    count = cmc_map.size
    ncross = lax.axis_size("cross")
    per_tile = TILE // bins
    ntiles = 3 * cells // per_tile
    flat, rank, parts, low = head_call(
        les_state, cmc_map, pdf_index, diffusion, rows, cells, nshape, ntiles, nshape * per_tile
    )
    bits = [1 << k for k in range(ncross.bit_length() - 1)]
    low_there = swap(low, "cross", bits[-1])
    high = sort_call(parts, rank)
    high_there = swap(high, "cross", bits[-1])
    near_lists = [(low, high)] + [(swap(low, "cross", bit), swap(high, "cross", bit)) for bit in bits[:-1]]
    low_far = [low_there] + [swap(low_there, "cross", bit) for bit in bits[:-1]]

    table = lax.dynamic_slice_in_dim(pdf_table.T, lax.axis_index("cross") * bins, bins, axis=0)

    extra = rows - species
    matrix = jnp.tile(jnp.pad(chem_matrix, ((0, extra), (0, -(-rows // 16) * 16 - species))), (1, 3))
    terms = (cmc_state.reshape(species * bins, cells), dissipation, reaction_rate, jnp.repeat(substeps, bins)[None, :], matrix)
    acc, *near = collect_call(near_lists, table, species, bins, per_tile, ntiles)
    acc, high_there, terms = lax.optimization_barrier((acc, high_there, terms))
    high_far = [high_there] + [swap(high_there, "cross", bit) for bit in bits[:-1]]
    accs, far = [acc], []
    for pair in zip(low_far, high_far):
        acc, *collected = collect_call([pair], table, species, bins, per_tile, ntiles)
        accs.append(acc)
        far.append(collected)
    fresh, parts = middle_call(accs, *terms, species, bins)

    ends = []
    for part in range(2):
        pieces = []
        for bit, collected in zip(bits[:-1], far[1:]):
            (piece,) = project_call(parts, collected, rows, count, bins, ntiles, part=part)
            piece, parts = lax.optimization_barrier((piece, parts))
            pieces.append(swap(piece, "cross", bit))
        (there,) = project_call(parts, far[0], rows, count, bins, ntiles, part=part)
        there = sum(pieces, there)
        there, parts = lax.optimization_barrier((there, parts))
        ends.append(swap(there, "cross", bits[-1]))
    low, high = ends
    weights, tiles, *keys = near
    pieces = []
    for n, bit in enumerate(bits[:-1], 1):
        (piece,) = project_call(parts, [weights, tiles, keys[n]], rows, count, bins, ntiles, first=n)
        pieces.append(swap(piece, "cross", bit))
    here, cmc_out = project_call(
        parts, [weights, tiles, keys[0]], rows, count, bins, ntiles, fresh, species * bins
    )
    total = [here] + pieces
    before = unsort_call(total, low, rank, None, None)
    les_out = unsort_call(total, high, rank, before, flat)
    return (les_out.reshape(les_state.shape), cmc_out.reshape(species, bins, cells))


def solution(mesh):
    return jax.shard_map(
        on_device,
        mesh=mesh,
        in_specs=(
            P(None, "slab", "cross", None),
            P(None, "cross", "slab"),
            P("slab", "cross", None),
            P("slab", "cross", None),
            P(),
            P(),
            P(),
            P("cross", "slab"),
            P("cross", "slab"),
            P("slab"),
        ),
        out_specs=(P(None, "slab", "cross", None), P(None, "cross", "slab")),
        check_vma=False,
    )
```

```python
import functools


import jax
import jax.numpy as jnp
from jax import lax
from jax.experimental import pallas as pl
from jax.experimental.pallas import tpu as pltpu
from jax.sharding import PartitionSpec as P

KMAX = 4
F32 = jnp.float32
BF16 = jnp.bfloat16
NT = (((1,), (1,)), ((), ()))
NN = (((1,), (0,)), ((), ()))
LANES = 128
TILE = 256
HALF = 64
GROUP = 16
LAG = (5, 9, 14)


def swap(array, axis, bit):
    count = lax.axis_size(axis)
    return lax.ppermute(array, axis, [(i, i ^ bit) for i in range(count)])


def halves(x):
    high = x.astype(BF16)
    return high, (x - high.astype(F32)).astype(BF16)


def padded_halves(x):
    gap = jnp.zeros((HALF - x.shape[0], x.shape[1]), F32)
    high = x.astype(BF16).astype(F32)
    return jnp.concatenate([high, gap, x - high, gap], axis=0).astype(BF16)


def rows_equal(targets, row):
    return jnp.where(targets == row, 1.0, 0.0).astype(BF16)


def whole(shape):
    return pl.BlockSpec(shape, lambda *_: (0,) * len(shape))


VMEM = pl.BlockSpec(memory_space=pltpu.VMEM)
SMEM = pl.BlockSpec(memory_space=pltpu.SMEM)


def params(mib):
    return pltpu.CompilerParams(vmem_limit_bytes=mib << 20)


def fetch_rows(sources, steps, sems):
    copies = []
    for number, source in enumerate(sources):
        last = source.at[source.shape[0] - 8 : source.shape[0], :LANES]
        copies.append(pltpu.make_async_copy(last, steps.at[number], sems.at[number]))
        copies[-1].start()
    return copies


def ranks(tiles, span, key_ref, rank_ref, table_ref):
    count = rank_ref.shape[1]
    ids = lax.broadcasted_iota(jnp.int32, (tiles, TILE), 0).astype(F32)
    tile_of = lambda n: jnp.floor((key_ref[:1, n * TILE : (n + 1) * TILE] + 0.5) * (1.0 / span))
    total = jnp.zeros((tiles, TILE), F32)
    for n in range(count // TILE):
        total = total + jnp.where(ids == tile_of(n), 1.0, 0.0)
    total = jnp.sum(total, axis=1, keepdims=True)
    total = jnp.broadcast_to(total, (tiles, LANES))
    big = jnp.floor(total * (1.0 / HALF))
    row = lax.broadcasted_iota(jnp.int32, (tiles, tiles), 0)
    below = rows_equal(jnp.where(lax.broadcasted_iota(jnp.int32, (tiles, tiles), 1) < row, 1, 0), 1)
    add = lambda part: lax.dot_general(below, part.astype(BF16), NN, preferred_element_type=F32)
    base = add(big) * HALF + add(total - big * HALF)
    order = lax.broadcasted_iota(jnp.int32, (tiles, LANES), 0).astype(F32)
    lane = lax.broadcasted_iota(jnp.int32, (tiles, LANES), 1).astype(F32)
    last = jnp.maximum(jnp.ceil((base + total) * (1.0 / LANES)) - 1.0, 0.0) + order
    passed = jnp.where((last < lane) & (order < tiles - 1), 1.0, 0.0)
    table = jnp.sum(passed, axis=0, keepdims=True)
    number = lane[:1]
    blocks = count // LANES
    early = jnp.where((number - table < blocks // 2) & (number < blocks + tiles - 1), 1.0, 0.0)
    table_ref[...] = jnp.where(number == LANES - 1, jnp.sum(early, axis=1, keepdims=True), table)
    ahead = jnp.where(
        lax.broadcasted_iota(jnp.int32, (TILE, TILE), 0) < lax.broadcasted_iota(jnp.int32, (TILE, TILE), 1), 1.0, 0.0
    ).astype(BF16)
    carry = base[:, :1]
    for n in range(count // TILE):
        hot = jnp.where(ids == tile_of(n), 1.0, 0.0)
        before = lax.dot_general(hot.astype(BF16), ahead, NN, preferred_element_type=F32) + carry
        rank_ref[:, n * TILE : (n + 1) * TILE] = jnp.sum(hot * before, axis=0, keepdims=True)
        carry = carry + jnp.sum(hot, axis=1, keepdims=True)


def head_kernel(grid_shape, cells, nshape, tiles, span, *refs):
    given, (t_ref, rank_ref, parts_ref, half_ref), refs = refs[:4], refs[4:8], refs[8:]
    les_ref, map_ref, shape_ref, diff_ref, key_ref, table_ref, *refs = refs
    faces, halos, (send, recv, load) = refs[:4], refs[4:8], refs[8:]
    loads = [
        pltpu.make_async_copy(source, target, load.at[n])
        for n, (source, target) in enumerate(zip(given, (les_ref, map_ref, shape_ref, diff_ref)))
    ]
    for copy in loads:
        copy.start()
    species, nx, ny = grid_shape
    count = rank_ref.shape[1]
    slab, nslab = lax.axis_index("slab"), lax.axis_size("slab")
    cross, ncross = lax.axis_index("cross"), lax.axis_size("cross")
    mesh = pl.DeviceIdType.MESH
    sides = [
        (slab > 0, {"slab": slab - 1}),
        (slab < nslab - 1, {"slab": slab + 1}),
        (cross > 0, {"cross": cross - 1}),
        (cross < ncross - 1, {"cross": cross + 1}),
    ]
    barrier = pltpu.get_barrier_semaphore()
    for n, (there, where) in enumerate(sides):

        @pl.when(jnp.logical_not(there))
        def _(n=n):
            halos[n][...] = jnp.zeros_like(halos[n])

    for copy in loads:
        copy.wait()
    line = lambda x, y: les_ref[pl.ds(x * ny + y, species, stride=nx * ny), :]
    for n, x in enumerate((0, nx - 1)):
        for y in range(ny):
            faces[n][y, :species] = line(x, y)
    for n, y in enumerate((0, ny - 1)):
        for x in range(nx):
            faces[2 + n][x, :species] = line(x, y)
    for there, where in sides:

        @pl.when(there)
        def _(where=where):
            pl.semaphore_signal(barrier, inc=1, device_id=where, device_id_type=mesh)

    pl.semaphore_wait(barrier, sum(jnp.where(there, 1, 0) for there, _ in sides))
    copies = {}
    for n in (2, 3, 0, 1):
        there, where = sides[n]
        copy = pltpu.make_async_remote_copy(
            src_ref=faces[n], dst_ref=halos[n ^ 1], send_sem=send.at[n], recv_sem=recv.at[n ^ 1],
            device_id=where, device_id_type=mesh,
        )
        pl.when(there)(copy.start)
        copies[n] = copy
    offset = map_ref[...] - (slab - 1) * cells
    block = jnp.where(offset >= cells, 1, 0) + jnp.where(offset >= 2 * cells, 1, 0)
    offset = jnp.where(lax.rem(slab, 2) == 1, (2 - block) * cells + offset - block * cells, offset)
    key = (offset * nshape + shape_ref[...]).astype(F32)
    key_ref[:1, :] = key
    t_ref[species:, :] = jnp.concatenate([key] + [jnp.zeros((t_ref.shape[0] - species - 1, count), F32)], axis=0)
    ranks(tiles, span, key_ref, rank_ref, table_ref)
    row = lax.broadcasted_iota(jnp.int32, (species, species), 0)
    number = jnp.where(row == lax.broadcasted_iota(jnp.int32, (species, species), 1), diff_ref[...], 0.0)
    number = jnp.sum(number, axis=1, keepdims=True)
    lane = lax.broadcasted_iota(jnp.int32, (species, LANES), 1)
    edge_y, edge_x = sorted({0, ny - 1}), sorted({0, nx - 1})
    phases = [
        ((), [(x, y) for x in range(1, nx - 1) for y in range(1, ny - 1)]),
        ((2, 3), [(x, y) for x in range(1, nx - 1) for y in edge_y]),
        ((0, 1), [(x, y) for x in edge_x for y in range(ny)]),
    ]
    done = 0
    for sources, places in phases:
        for n in sources:
            pl.when(sides[n ^ 1][0])(copies[n].wait_recv)
        for x, y in places:
            here = line(x, y)
            around = line(x + 1, y) if x < nx - 1 else halos[1][y, :species]
            around = around + (line(x - 1, y) if x else halos[0][y, :species])
            around = around + (line(x, y + 1) if y < ny - 1 else halos[3][x, :species])
            around = around + (line(x, y - 1) if y else halos[2][x, :species])
            around = around + jnp.where(lane < LANES - 1, pltpu.roll(here, LANES - 1, 1), 0.0)
            around = around + jnp.where(lane > 0, pltpu.roll(here, 1, 1), 0.0)
            place = (x * ny + y) * LANES
            t_ref[:species, place : place + LANES] = here + number * (around - 6.0 * here)
        for x, y in places:
            piece = slice((x * ny + y) * LANES, (x * ny + y + 1) * LANES)
            value = t_ref[:, piece]
            high = value.astype(BF16).astype(F32)
            parts_ref[:, piece] = jnp.concatenate([high, value - high], axis=0).astype(BF16)
        if places:
            done += len(places)
            table = table_ref[...] if done == nx * ny else None
            sort_tiles(parts_ref, rank_ref, table, half_ref, 0, [x * ny + y for x, y in places], done > len(places))
    for n, (there, _) in enumerate(sides):
        pl.when(there)(copies[n].wait_send)


def head_call(les_state, cmc_map, pdf_index, diffusion, rows, cells, nshape, tiles, span):
    species, nx, ny, nz = les_state.shape
    count = nx * ny * nz
    halo = [pltpu.VMEM((n, rows, LANES), F32) for n in (ny, ny, nx, nx)]
    return pl.pallas_call(
        functools.partial(head_kernel, (species, nx, ny), cells, nshape, tiles, span),
        out_shape=[
            jax.ShapeDtypeStruct((rows, count), F32),
            jax.ShapeDtypeStruct((1, count), F32),
            jax.ShapeDtypeStruct((2 * rows, count), BF16),
            jax.ShapeDtypeStruct((rows, count // 2), F32),
        ],
        in_specs=[pl.BlockSpec(memory_space=pltpu.HBM)] * 4,
        out_specs=[VMEM] * 4,
        scratch_shapes=[
            pltpu.VMEM((species * nx * ny, nz), F32),
            pltpu.VMEM((1, count), jnp.int32),
            pltpu.VMEM((1, count), jnp.int32),
            pltpu.VMEM((1, species), F32),
            pltpu.VMEM((8, count), F32),
            pltpu.VMEM((1, LANES), F32),
        ] + halo * 2 + [pltpu.SemaphoreType.DMA((4,))] * 3,
        compiler_params=pltpu.CompilerParams(vmem_limit_bytes=60 << 20, collective_id=2, has_side_effects=True),
        name="head",
    )(
        les_state.reshape(species * nx * ny, nz), cmc_map.reshape(1, count), pdf_index.reshape(1, count),
        diffusion.reshape(1, species),
    )


CHUNK = 2 * TILE


def sort_tiles(parts, rank_ref, steps, out_ref, first, lines=None, more=False):
    rows = out_ref.shape[0]
    lines = list(range(rank_ref.shape[1] // LANES)) if lines is None else lines
    groups = [lines[n : n + CHUNK // LANES] for n in range(0, len(lines), CHUNK // LANES)]

    def pick(ref, group):
        if group == list(range(group[0], group[-1] + 1)):
            return ref[:, group[0] * LANES : (group[-1] + 1) * LANES]
        return jnp.concatenate([ref[:, n * LANES : (n + 1) * LANES] for n in group], axis=1)

    def step(n, _):
        here = (first + n) * TILE
        total = jnp.zeros((2 * rows, TILE), F32)
        for group in groups:
            ids = lax.broadcasted_iota(jnp.int32, (TILE, len(group) * LANES), 0) + here
            hot = rows_equal(ids.astype(F32), pick(rank_ref, group))
            total = total + lax.dot_general(pick(parts, group), hot, NT, preferred_element_type=F32)
        total = total[:rows] + total[rows:]
        place = pl.ds(pl.multiple_of(n * TILE, TILE), TILE)
        if more:
            total = total + out_ref[:, place]
        if steps is not None:
            line = lax.broadcasted_iota(jnp.int32, (rows, TILE), 0)
            total = jnp.where(line == rows - 1, jnp.concatenate([steps] * (TILE // LANES), axis=1), total)
        out_ref[:, place] = total
        return 0

    lax.fori_loop(0, out_ref.shape[1] // TILE, step, 0)


def sort_kernel(parts_ref, rank_ref, out_ref):
    sort_tiles(parts_ref, rank_ref, None, out_ref, out_ref.shape[1] // TILE)


def sort_call(parts, rank):
    rows, count = parts.shape[0] // 2, parts.shape[1]
    return pl.pallas_call(
        sort_kernel,
        out_shape=jax.ShapeDtypeStruct((rows, count // 2), F32),
        in_specs=[VMEM] * 2,
        out_specs=VMEM,
        compiler_params=params(8),
        cost_estimate=pl.CostEstimate(flops=2 * rows * count * count, bytes_accessed=4 * rows * count, transcendentals=0),
        name="sort",
    )(parts, rank)


def unsort_kernel(half, given, rank_ref, *refs):
    xs, refs = refs[:given], refs[given:]
    before, (flat_ref,) = (refs[:1], refs[1:2]) if half else ((), (None,))
    out_ref, parts = refs[-2:]
    rows, count = xs[0].shape[0], rank_ref.shape[1]
    width = xs[0].shape[1]

    @pl.when(pl.program_id(0) == 0)
    def _():
        x = xs[0][...]
        for more in xs[1:]:
            x = x + more[...]
        high = x.astype(BF16).astype(F32)
        parts[...] = jnp.concatenate([high, x - high], axis=0).astype(BF16)

    total = jnp.zeros((2 * rows, TILE), F32)
    for k in range(width // CHUNK):
        ids = lax.broadcasted_iota(jnp.int32, (CHUNK, TILE), 0) + (half * width + k * CHUNK)
        hot = rows_equal(ids.astype(F32), rank_ref[:, pl.ds(pl.multiple_of(pl.program_id(0) * TILE, TILE), TILE)])
        piece = parts[:, k * CHUNK : (k + 1) * CHUNK]
        total = total + lax.dot_general(piece, hot, NN, preferred_element_type=F32)
    total = total[:rows] + total[rows:]
    if not half:
        out_ref[...] = total
        return
    total = total + before[0][...]
    species = rows - 2
    ratio = 0.5 / total[species : species + 1]
    for n in range(TILE // LANES):
        piece = slice(n * LANES, (n + 1) * LANES)
        line = pl.program_id(0) * (TILE // LANES) + n
        value = 0.5 * flat_ref[:species, piece] + total[:species, piece] * ratio[:, piece]
        out_ref[pl.ds(line, species, stride=count // LANES), :] = value


def unsort_call(wholes, piece, rank, before, flat):
    half = int(before is not None)
    rows, count = wholes[0].shape
    part = pl.BlockSpec((rows, count // 2), lambda i: (0, half))
    column = pl.BlockSpec((rows, TILE), lambda i: (0, i))
    args = [rank, *wholes, piece]
    specs = [whole(rank.shape)] + [part] * len(wholes) + [whole(piece.shape)]
    out_shape, out_spec = (rows, count), column
    if half:
        args += [before, flat]
        specs += [column, column]
        lines = (rows - 2) * count // LANES
        out_shape, out_spec = (lines, LANES), whole((lines, LANES))
    return pl.pallas_call(
        functools.partial(unsort_kernel, half, len(wholes) + 1),
        grid=(count // TILE,),
        out_shape=jax.ShapeDtypeStruct(out_shape, F32),
        in_specs=specs,
        out_specs=out_spec,
        scratch_shapes=[pltpu.VMEM((2 * rows, count // 2), BF16)],
        compiler_params=params(12),
        cost_estimate=pl.CostEstimate(flops=2 * rows * count * count, bytes_accessed=4 * rows * count, transcendentals=0),
        name="unsort",
    )(*args)


def weights_of(key, table, bins, per_tile):
    nshape = table.shape[1]
    cell = jnp.floor((key + 0.5) * (1.0 / nshape))
    shape = key - cell * nshape
    tile = jnp.floor((cell + 0.5) * (1.0 / per_tile))
    within = cell - tile * per_tile
    ids = lax.broadcasted_iota(jnp.int32, (nshape, key.shape[1]), 0).astype(F32).astype(BF16)
    hot = jnp.where(ids == shape.astype(BF16), jnp.ones((), BF16), jnp.zeros((), BF16))
    picked = lax.dot_general(table, hot, NN, preferred_element_type=F32).astype(BF16)
    masks = [jnp.where(within == m, 1.0, 0.0).astype(BF16) for m in range(per_tile)]
    columns = []
    for part in (picked[:bins], picked[bins:]):
        columns.append(jnp.concatenate([part * mask for mask in masks], axis=0))
    return jnp.concatenate(columns, axis=1), tile


def split_table(table):
    high = table.astype(BF16).astype(F32)
    return jnp.concatenate([high, table - high], axis=0).astype(BF16)


def prepare_weights(source, index, key_row, table, bins, per_tile, weights, tiles):
    def step(n, _):
        key = source[key_row : key_row + 1, pl.ds(pl.multiple_of(n * LANES, LANES), LANES)]
        block, tile = weights_of(key, table, bins, per_tile)
        weights[index + n] = block
        tiles[index + n] = jnp.broadcast_to(tile, tiles.shape[1:])
        return 0

    lax.fori_loop(0, source.shape[1] // LANES, step, 0, unroll=4)


def collect_kernel(species, bins, per_tile, pairs, lists, *refs):
    sources, refs = [refs[2 * n : 2 * n + 2] for n in range(lists)], refs[2 * lists :]
    table_ref, out_ref, *refs = refs
    weights, tiles, *refs = refs
    keys, (parts, steps, sems) = refs[:lists], refs[lists:]
    copies = fetch_rows([source[0] for source in sources], steps, sems)
    rows, part = sources[0][0].shape
    count = 2 * part
    for key, source in zip(keys, sources):
        key[...] = source[0][rows - 8 :, :LANES]
    blocks = count // LANES
    out_ref[...] = jnp.zeros_like(out_ref)
    table = split_table(table_ref[...])
    line = lax.broadcasted_iota(jnp.int32, (rows, LANES), 0)
    for number in range(2 * lists):
        source = sources[number // 2][number % 2]
        start = number * blocks // 2
        prepare_weights(source, start, species, table, bins, per_tile, weights, tiles)

        def split(n, _, source=source, start=start):
            x = source[:, pl.ds(pl.multiple_of(n * LANES, LANES), LANES)]
            x = jnp.where(line < species, x, jnp.where(line == species, 1.0, 0.0))
            parts[start + n] = padded_halves(x)
            return 0

        lax.fori_loop(0, blocks // 2, split, 0, unroll=4)

    for copy in copies:
        copy.wait()

    def step(n, _):
        for number in range(lists):
            for g in range(GROUP):
                k = n * GROUP + g
                tile = steps[number, 7, k].astype(jnp.int32)
                block = jnp.minimum(k - tile, blocks - 1) + number * blocks
                wanted = jnp.where(k < pairs, tile, -1).astype(F32)
                mask = jnp.where(tiles[block] == wanted, 1.0, 0.0).astype(BF16)
                mask = jnp.concatenate([mask] * (2 * HALF // mask.shape[0]), axis=0)
                x = parts[block] * mask
                both = jnp.concatenate([x, x], axis=1)
                got = lax.dot_general(both, weights[block], NT, preferred_element_type=F32)
                place = pl.ds(pl.multiple_of(tile * TILE, TILE), TILE)
                out_ref[:, place] += got[:rows] + got[HALF : HALF + rows]
        return 0

    lax.fori_loop(0, -(-pairs // GROUP), step, 0)


def collect_call(sources, table, species, bins, per_tile, ntiles):
    rows, count = sources[0][0].shape[0], 2 * sources[0][0].shape[1]
    lists, blocks = len(sources), count // LANES
    pairs = blocks + ntiles - 1
    args = [half for source in sources for half in source] + [table]
    specs = [VMEM] * (2 * lists + 1)
    return pl.pallas_call(
        functools.partial(collect_kernel, species, bins, per_tile, pairs, lists),
        out_shape=[
            jax.ShapeDtypeStruct((rows, ntiles * TILE), F32),
            jax.ShapeDtypeStruct((lists * blocks, TILE, 2 * LANES), BF16),
            jax.ShapeDtypeStruct((lists * blocks, 16, LANES), F32),
        ]
        + [jax.ShapeDtypeStruct((8, LANES), F32)] * lists,
        in_specs=specs,
        out_specs=[VMEM] * (lists + 3),
        scratch_shapes=[
            pltpu.VMEM((lists * blocks, 2 * HALF, LANES), BF16),
            pltpu.SMEM((lists, 8, LANES), F32),
            pltpu.SemaphoreType.DMA((lists,)),
        ],
        compiler_params=params(19),
        cost_estimate=pl.CostEstimate(flops=lists * pairs * 2 * LANES * TILE * TILE, bytes_accessed=0, transcendentals=0),
        name="collect",
    )(*args)


def turn_back(mean, out_ref, bins, quads, turned):
    rows, width = mean.shape
    lines = width // LANES
    fold = LANES // bins
    for q in range(lines):
        quads[pl.ds(q, rows, stride=lines), :] = mean[:, q * LANES : (q + 1) * LANES]
    blocked = lax.broadcasted_iota(jnp.int32, (lines, LANES), 1) // bins

    def turn(g):
        source = [quads[pl.ds(pl.multiple_of(g * LANES + k * lines, lines), lines), :] for k in range(fold)]
        for r in range(fold):
            out = source[r]
            for k in range(fold):
                if k != r:
                    out = jnp.where(blocked == k, pltpu.roll(source[k], (k - r) * bins % LANES, 1), out)
            turned[pl.ds(r, lines, stride=fold), :] = out
        return turned[...].T

    full, rest = out_ref.shape[0] // LANES, out_ref.shape[0] % LANES

    def step(g, _):
        out_ref[pl.ds(pl.multiple_of(g * LANES, LANES), LANES), :] = turn(g)
        return 0

    lax.fori_loop(0, full, step, 0)
    if rest:
        out_ref[full * LANES :, :] = turn(full)[:rest]


def project_kernel(pairs, lists, state_rows, part, first, *refs):
    parts, weights, tiles, *refs = refs
    sources, refs = refs[:lists], refs[lists:]
    mean = refs.pop(0) if state_rows else None
    outs, refs = refs[:lists], refs[lists:]
    state_ref = refs.pop(0) if state_rows else None
    steps, sems = refs
    copies = fetch_rows(sources, steps, sems)
    rows, count = outs[0].shape
    blocks = count // LANES
    whole_blocks = blocks if part is None else 2 * blocks
    base = blocks * (part or 0)
    group = GROUP if part is None else GROUP // 2
    for out in outs:
        out[...] = jnp.zeros_like(out)
    if state_rows:
        state_ref[...] = mean[...]
    for copy in copies:
        copy.wait()

    def step(n, _):
        for number in range(lists):
            for g in range(group):
                k = n * group + g
                tile = steps[number, 7, k].astype(jnp.int32)
                block = jnp.minimum(k - tile, whole_blocks - 1)
                local = jnp.clip(block - base, 0, blocks - 1)
                block = block + (first + number) * whole_blocks
                valid = k < pairs
                if part is not None:
                    valid = valid & ((k < middle) == (part == 0))
                wanted = jnp.where(valid, tile, -1).astype(F32)
                got = lax.dot_general(parts[tile], weights[block], NN, preferred_element_type=F32)
                got = got[:rows] + got[HALF : HALF + rows]
                got = got[:, :LANES] + got[:, LANES:]
                got = jnp.where(tiles[block][:1] == wanted, got, 0.0)
                place = pl.ds(pl.multiple_of(local * LANES, LANES), LANES)
                outs[number][:, place] += got
        return 0

    start, stop = 0, -(-pairs // group)
    if part is not None:
        middle = steps[0, 7, LANES - 1].astype(jnp.int32)
        start, stop = (0, (middle + group - 1) // group) if part == 0 else (middle // group, stop)
    lax.fori_loop(start, stop, step, 0)


def project_call(parts, collected, rows, count, ntiles, mean=None, state_rows=0, part=None, first=0):
    weights, tiles, *sources = collected
    lists = len(sources)
    pairs = count // LANES + ntiles - 1
    extra = [] if mean is None else [mean]
    scratch = [pltpu.SMEM((lists, 8, LANES), F32), pltpu.SemaphoreType.DMA((lists,))]
    return pl.pallas_call(
        functools.partial(project_kernel, pairs, lists, state_rows, part, first),
        out_shape=[jax.ShapeDtypeStruct((rows, count if part is None else count // 2), F32)] * lists
        + [jax.ShapeDtypeStruct((state_rows, LANES), F32)] * len(extra),
        in_specs=[VMEM] * (3 + lists + len(extra)),
        out_specs=[VMEM] * (lists + len(extra)),
        scratch_shapes=scratch,
        compiler_params=params(20),
        cost_estimate=pl.CostEstimate(flops=lists * pairs * 2 * LANES * TILE * TILE, bytes_accessed=0, transcendentals=0),
        name="project",
    )(parts, weights, tiles, *sources, *extra)


def middle_kernel(species, bins, chunk, refs_in, refs_out, scratch):
    *accs, cmc_ref, diss_ref, rate_ref, count_ref, matrix_ref = refs_in
    state_out, parts_ref = refs_out
    fresh_ref, next_ref, far_ref, nat, quads, turned, side_out, load, outward, hopped, summed, got, state_ref, edge_out, edge_in, side_in, pick_ref, third_ref, send, recv, side_send, side_recv = scratch
    rows, width = fresh_ref.shape
    steps = width // chunk
    slab, nslab = lax.axis_index("slab"), lax.axis_size("slab")
    cross, ncross = lax.axis_index("cross"), lax.axis_size("cross")
    parity = lax.rem(slab, 2)
    outer = slab + 4 * parity - 2
    inner = slab - 4 * parity + 2
    partner = slab + 1 - 2 * parity
    has_outer = (outer >= 0) & (outer < nslab)
    has_inner = (inner >= 0) & (inner < nslab)
    has_before, has_after = cross > 0, cross < ncross - 1
    has_down, has_up = slab > 0, slab < nslab - 1
    mesh = pl.DeviceIdType.MESH

    def partial_sum(piece):
        total = accs[0][:, piece]
        for more in accs[1:]:
            total = total + more[:, piece]
        return total

    loads, start = [], 0
    for n, source in enumerate((cmc_ref, diss_ref, rate_ref)):
        target = nat.at[start : start + source.shape[0]]
        loads.append(pltpu.make_async_copy(source, target, load.at[n]))
        loads[-1].start()
        start += source.shape[0]
    if start < nat.shape[0]:
        nat[start:, :] = jnp.zeros((nat.shape[0] - start, LANES), F32)
    outward[...] = partial_sum(slice(0, width))

    @pl.when(jnp.logical_not(has_inner))
    def _():
        hopped[...] = jnp.zeros_like(hopped)

    @pl.when(jnp.logical_not(has_outer))
    def _():
        far_ref[...] = jnp.zeros_like(far_ref)

    @pl.when(jnp.logical_not(has_before))
    def _():
        edge_in[:, :, :LANES] = jnp.zeros(edge_in.shape[:2] + (LANES,), F32)

    @pl.when(jnp.logical_not(has_after))
    def _():
        edge_in[:, :, LANES:] = jnp.zeros(edge_in.shape[:2] + (LANES,), F32)

    @pl.when(jnp.logical_not(has_down))
    def _():
        side_in[0] = jnp.zeros(side_in.shape[1:], F32)

    @pl.when(jnp.logical_not(has_up))
    def _():
        side_in[1] = jnp.zeros(side_in.shape[1:], F32)

    barrier = pltpu.get_barrier_semaphore()
    greet = lambda where: pl.semaphore_signal(barrier, inc=1, device_id=where, device_id_type=mesh)
    pl.when(has_down)(lambda: greet({"slab": slab - 1}))
    pl.when(has_up)(lambda: greet({"slab": slab + 1}))
    pl.when(has_outer)(lambda: greet({"slab": outer}))
    pl.when(has_inner)(lambda: greet({"slab": inner}))
    pl.when(has_before)(lambda: greet({"cross": cross - 1}))
    pl.when(has_after)(lambda: greet({"cross": cross + 1}))
    number = lambda flag: jnp.where(flag, 1, 0)
    flags = (has_down, has_up, has_outer, has_inner, has_before, has_after)
    pl.semaphore_wait(barrier, sum(number(flag) for flag in flags))

    def lanes(c, base=0):
        return pl.ds(pl.multiple_of(base + c * chunk, chunk), chunk)

    def remote(kind, c, source, target, where):
        return pltpu.make_async_remote_copy(
            src_ref=source, dst_ref=target, send_sem=send.at[kind, c], recv_sem=recv.at[kind, c],
            device_id=where, device_id_type=mesh,
        )

    to_outer = lambda c: remote(0, c, outward.at[:, lanes(c)], hopped.at[:, lanes(c)], {"slab": outer})
    to_partner = lambda c: remote(1, c, summed.at[:, lanes(c)], got.at[:, lanes(c)], {"slab": partner})
    to_after = lambda c: remote(2, c, edge_out.at[c, :, LANES:], edge_in.at[c, :, :LANES], {"cross": cross + 1})
    to_before = lambda c: remote(3, c, edge_out.at[c, :, :LANES], edge_in.at[c, :, LANES:], {"cross": cross - 1})
    give = lambda c: remote(4, c, fresh_ref.at[:, lanes(c)], next_ref.at[:, lanes(c)], {"slab": partner})
    pass_on = lambda c: remote(5, c, next_ref.at[:, lanes(c)], far_ref.at[:, lanes(c)], {"slab": inner})

    def side(n, source, where):
        return pltpu.make_async_remote_copy(
            src_ref=source, dst_ref=side_in.at[n], send_sem=side_send.at[n], recv_sem=side_recv.at[n],
            device_id=where, device_id_type=mesh,
        )

    to_up = side(0, side_out.at[0], {"slab": slab + 1})
    to_down = side(1, side_out.at[1], {"slab": slab - 1})

    def start_hops(chunks):
        @pl.when(has_outer)
        def _():
            for c in chunks:
                to_outer(c).start()

    start_hops(range(2))
    for copy in loads:
        copy.wait()
    lines = width // LANES
    fold = LANES // bins
    blocked = lax.broadcasted_iota(jnp.int32, (LANES // fold, LANES), 1) // bins

    def turn(g, _):
        turned[...] = nat[pl.ds(pl.multiple_of(g * LANES, LANES), LANES), :].T
        parts = [turned[pl.ds(r, LANES // fold, stride=fold), :] for r in range(fold)]
        for k in range(fold):
            out = parts[k]
            for r in range(fold):
                if r != k:
                    out = jnp.where(blocked == r, pltpu.roll(parts[r], (r - k) * bins % LANES, 1), out)
            place = pl.multiple_of(g * LANES + k * lines, lines)
            quads[pl.ds(place, lines), :] = out
        return 0

    lax.fori_loop(0, nat.shape[0] // LANES, turn, 0)
    tile = lambda q: quads[pl.ds(q, rows, stride=lines), :]
    side_out[0] = tile(lines - 1)
    side_out[1] = tile(0)

    lane = lax.broadcasted_iota(jnp.int32, (2 * LANES, chunk), 1)
    row = lax.broadcasted_iota(jnp.int32, (2 * LANES, chunk), 0)
    target = jnp.where(row < LANES, row * bins, (row - LANES) * bins + bins - 1)
    pick_ref[...] = rows_equal(target, lane)
    third = matrix_ref.shape[1] // 3
    high, low = halves(matrix_ref[...])
    column = lax.broadcasted_iota(jnp.int32, matrix_ref.shape, 1)
    third_ref[...] = jnp.where(column < 2 * third, high.astype(F32), low.astype(F32)).astype(BF16)
    line = lax.broadcasted_iota(jnp.int32, (rows, chunk), 0)
    slot = lax.broadcasted_iota(jnp.int32, (rows, chunk), 1) % bins
    gap = [jnp.zeros((third - rows, chunk), F32)] * (third > rows)

    pl.when(has_up)(to_up.start)
    pl.when(has_down)(to_down.start)
    start_hops(range(2, steps))

    def stacked(x):
        high = x.astype(BF16).astype(F32)
        return jnp.concatenate([high, x - high], axis=0).astype(BF16)

    def add_hop(c):
        pl.when(has_inner)(lambda: to_outer(c).wait_recv())
        summed[:, lanes(c)] = partial_sum(lanes(c, 2 * width)) + hopped[:, lanes(c)]

    per = chunk // LANES

    def advect(c):
        here = jnp.concatenate([tile(c * per + n) for n in range(per)], axis=1)
        low = jnp.where(c == 0, side_in[0], tile(jnp.maximum(c * per - 1, 0)))
        high = jnp.where(c == steps - 1, side_in[1], tile(jnp.minimum((c + 1) * per, lines - 1)))
        left = pltpu.roll(jnp.concatenate([low, here], axis=1), bins, 1)[:, LANES:]
        right = pltpu.roll(jnp.concatenate([here, high], axis=1), chunk + LANES - bins, 1)[:, :chunk]
        return here - 0.4 * (here - left) + 0.1 * (right - 2.0 * here + left)

    def cell_row(n, c):
        start = (species + n) * lines + c * per
        return jnp.concatenate([quads[pl.ds(start + k, 1), :] for k in range(per)], axis=1)

    def blend(c):
        total = partial_sum(lanes(c, width)) + got[:, lanes(c)]
        blended = (total + advect(c)) / (total[species : species + 1] + 1.0)
        state_ref[:, lanes(c)] = blended
        edge = lax.dot_general(stacked(blended), pick_ref[...], NT, preferred_element_type=F32)
        edge_out[c] = edge[:rows] + edge[rows:]

    def send_edges(c):
        pl.when(has_after)(lambda: to_after(c).start())
        pl.when(has_before)(lambda: to_before(c).start())

    def wait_edges(c):
        pl.when(has_before)(lambda: to_after(c).wait_recv())
        pl.when(has_after)(lambda: to_before(c).wait_recv())

    def react(c):
        here = state_ref[:, lanes(c)]
        around = lax.dot_general(stacked(edge_in[c]), pick_ref[...], NN, preferred_element_type=F32)
        around = around[:rows] + around[rows:]
        before = jnp.where(slot == 0, around, pltpu.roll(here, 1, 1))
        after = jnp.where(slot == bins - 1, around, pltpu.roll(here, chunk - 1, 1))
        state = here + cell_row(0, c) * (after - 2.0 * here + before)
        half = 0.5 * cell_row(1, c)
        count = count_ref[:, lanes(c)]
        for k in range(KMAX):
            high, low = (part.astype(F32) for part in halves(state))
            stack = jnp.concatenate([high, *gap, low, *gap, high, *gap], axis=0).astype(BF16)
            rate = lax.dot_general(third_ref[...], stack, NN, preferred_element_type=F32)
            state = jnp.where(k < count, state + half * jnp.tanh(rate), state)
        state = jnp.where(line == species, 1.0, state)
        fresh_ref[:, lanes(c)] = state
        keep(1, c, state)

    def keep(which, c, mean):
        for n in range(chunk // TILE):
            index = which * (width // TILE) + c * (chunk // TILE) + n
            parts_ref[index] = padded_halves(mean[:, n * TILE : (n + 1) * TILE])

    def step(t, _):
        def when(lag, body):
            c = t - lag
            pl.when((c >= 0) & (c < steps))(lambda: body(c))

        def second(c):
            pl.when((c == 0) & has_down)(to_up.wait_recv)
            pl.when((c == 0) & has_up)(to_down.wait_recv)
            to_partner(c).wait_recv()
            blend(c)

        def third_stage(c):
            wait_edges(c)
            react(c)

        def fourth(c):
            give(c).wait_recv()
            pl.when(has_inner)(lambda: pass_on(c).start())
            keep(2, c, next_ref[:, lanes(c)])

        when(0, add_hop)
        when(LAG[0], second)
        when(0, lambda c: to_partner(c).start())
        when(LAG[1], third_stage)
        when(LAG[0], send_edges)
        when(LAG[2], fourth)
        when(LAG[1], lambda c: give(c).start())
        return 0

    lax.fori_loop(0, steps + LAG[2], step, 0)
    turn_back(fresh_ref, state_out, bins, quads, turned)

    def finish(c, _):
        pl.when(has_outer)(lambda: to_outer(c).wait_send())
        to_partner(c).wait_send()
        pl.when(has_after)(lambda: to_after(c).wait_send())
        pl.when(has_before)(lambda: to_before(c).wait_send())
        give(c).wait_send()
        pl.when(has_inner)(lambda: pass_on(c).wait_send())
        pl.when(has_outer)(lambda: pass_on(c).wait_recv())
        keep(0, c, far_ref[:, lanes(c)])
        return 0

    lax.fori_loop(0, steps, finish, 0)
    pl.when(has_up)(to_up.wait_send)
    pl.when(has_down)(to_down.wait_send)


def middle_call(accs, cmc, diss, rate, count, matrix, species, bins, chunk=256):
    rows, width = accs[0].shape[0], count.shape[1]
    steps = width // chunk
    given = len(accs) + 5

    def kernel(*refs):
        middle_kernel(species, bins, chunk, refs[:given], refs[given : given + 2], refs[given + 2 :])

    return pl.pallas_call(
        kernel,
        out_shape=[
            jax.ShapeDtypeStruct(cmc.shape, F32),
            jax.ShapeDtypeStruct((3 * width // TILE, 2 * HALF, TILE), BF16),
        ],
        in_specs=[VMEM] * len(accs) + [pl.BlockSpec(memory_space=pl.ANY)] * 3 + [VMEM] * 2,
        out_specs=[VMEM] * 2,
        scratch_shapes=[pltpu.VMEM((rows, width), F32)] * 3
        + [pltpu.VMEM((rows * bins, LANES), F32), pltpu.VMEM((rows * width // LANES, LANES), F32)]
        + [pltpu.VMEM((LANES, LANES), F32), pltpu.VMEM((2, rows, LANES), F32), pltpu.SemaphoreType.DMA((3,))]
        + [pltpu.VMEM((rows, width), F32)] * 5
        + [pltpu.VMEM((steps, rows, 2 * LANES), F32)] * 2
        + [pltpu.VMEM((2, rows, LANES), F32), pltpu.VMEM((2 * LANES, chunk), BF16), pltpu.VMEM(matrix.shape, BF16)]
        + [pltpu.SemaphoreType.DMA((6, steps))] * 2
        + [pltpu.SemaphoreType.DMA((2,))] * 2,
        compiler_params=pltpu.CompilerParams(vmem_limit_bytes=22 << 20, collective_id=1, has_side_effects=True),
        name="middle",
    )(*accs, cmc, diss, rate, count, matrix)


def on_device(
    les_state, cmc_state, cmc_map, pdf_index, pdf_table, diffusion, chem_matrix, dissipation, reaction_rate, substeps
):
    species = les_state.shape[0]
    rows = -(-(species + 2) // 8) * 8
    bins, cells = cmc_state.shape[1:]
    nshape = pdf_table.shape[0]
    count = cmc_map.size
    ncross = lax.axis_size("cross")
    per_tile = TILE // bins
    ntiles = 3 * cells // per_tile
    flat, rank, parts, low = head_call(
        les_state, cmc_map, pdf_index, diffusion, rows, cells, nshape, ntiles, nshape * per_tile
    )
    bits = [1 << k for k in range(ncross.bit_length() - 1)]
    low_there = swap(low, "cross", bits[-1])
    high = sort_call(parts, rank)
    high_there = swap(high, "cross", bits[-1])
    near_lists = [(low, high)] + [(swap(low, "cross", bit), swap(high, "cross", bit)) for bit in bits[:-1]]
    low_far = [low_there] + [swap(low_there, "cross", bit) for bit in bits[:-1]]

    table = lax.dynamic_slice_in_dim(pdf_table.T, lax.axis_index("cross") * bins, bins, axis=0)

    extra = rows - species
    matrix = jnp.tile(jnp.pad(chem_matrix, ((0, extra), (0, -(-rows // 16) * 16 - species))), (1, 3))
    terms = (cmc_state.reshape(species * bins, cells), dissipation, reaction_rate, jnp.repeat(substeps, bins)[None, :], matrix)
    acc, *near = collect_call(near_lists, table, species, bins, per_tile, ntiles)
    acc, high_there, terms = lax.optimization_barrier((acc, high_there, terms))
    high_far = [high_there] + [swap(high_there, "cross", bit) for bit in bits[:-1]]
    accs, far = [acc], []
    for pair in zip(low_far, high_far):
        acc, *collected = collect_call([pair], table, species, bins, per_tile, ntiles)
        accs.append(acc)
        far.append(collected)
    state, parts = middle_call(accs, *terms, species, bins)

    ends = []
    for part in range(2):
        pieces = []
        for bit, collected in zip(bits[:-1], far[1:]):
            (piece,) = project_call(parts, collected, rows, count, ntiles, part=part)
            piece, parts = lax.optimization_barrier((piece, parts))
            pieces.append(swap(piece, "cross", bit))
        (there,) = project_call(parts, far[0], rows, count, ntiles, part=part)
        there = sum(pieces, there)
        there, parts = lax.optimization_barrier((there, parts))
        ends.append(swap(there, "cross", bits[-1]))
    low, high = ends
    weights, tiles, *keys = near
    pieces = []
    for n, bit in enumerate(bits[:-1], 1):
        (piece,) = project_call(parts, [weights, tiles, keys[n]], rows, count, ntiles, first=n)
        pieces.append(swap(piece, "cross", bit))
    here, cmc_out = project_call(parts, [weights, tiles, keys[0]], rows, count, ntiles, state, species * bins)
    total = [here] + pieces
    before = unsort_call(total, low, rank, None, None)
    les_out = unsort_call(total, high, rank, before, flat)
    return (les_out.reshape(les_state.shape), cmc_out.reshape(species, bins, cells))


def solution(mesh):
    return jax.shard_map(
        on_device,
        mesh=mesh,
        in_specs=(
            P(None, "slab", "cross", None),
            P(None, "cross", "slab"),
            P("slab", "cross", None),
            P("slab", "cross", None),
            P(),
            P(),
            P(),
            P("cross", "slab"),
            P("cross", "slab"),
            P("slab"),
        ),
        out_specs=(P(None, "slab", "cross", None), P(None, "cross", "slab")),
        check_vma=False,
    )
```
